32 devices in a mesh: dp: 8 (over y, x, core), tensor: 4 (over z).
Axes of the slice: x: 2, y: 2, z: 4, core: 2. Of those that a mesh axis runs over, the one named last changes fastest.
Arguments:
- tokens: bfloat16 [16384, 2048], P(('dp', 'tensor')), may hold values from -6 to 6
- upstream: bfloat16 [16384, 2048], P(('dp', 'tensor')), may hold values from -6 to 6
- lengths: int32 [8, 4], P('dp'), may hold values from 1 to 1024, as said below
- positions: int32 [8, 2048], P('dp'), may hold values from 0 to 9214, as said below
- pages: int32 [256], replicated, may hold values from 0 to 255, as said below
- attn_gain: bfloat16 [2048], P('dp'), may hold values from 0.099609375 to 1.8984375
- w_query: bfloat16 [2048, 2048], P('dp', 'tensor'), may hold values from -0.125 to 0.125
- w_key: bfloat16 [2048, 512], P('dp', 'tensor'), may hold values from -0.125 to 0.125
- w_value: bfloat16 [2048, 512], P('dp', 'tensor'), may hold values from -0.125 to 0.125
- w_out: bfloat16 [2048, 2048], P('tensor', 'dp'), may hold values from -1 to 1
- mlp_gain: bfloat16 [2048], P('dp'), may hold values from 0.099609375 to 1.8984375
- w_gate: bfloat16 [2048, 8192], P('dp', 'tensor'), may hold values from -0.125 to 0.125
- w_up: bfloat16 [2048, 8192], P('dp', 'tensor'), may hold values from -0.125 to 0.125
- w_down: bfloat16 [8192, 2048], P('tensor', 'dp'), may hold values from -0.0625 to 0.0625
Outputs:
- output: bfloat16 [16384, 2048], P(('dp', 'tensor'))
- grad_tokens: bfloat16 [16384, 2048], P(('dp', 'tensor'))
- grad_attn_gain: float32 [2048], P('dp')
- grad_w_query: float32 [2048, 2048], P('dp', 'tensor')
- grad_w_key: float32 [2048, 512], P('dp', 'tensor')
- grad_w_value: float32 [2048, 512], P('dp', 'tensor')
- grad_w_out: float32 [2048, 2048], P('tensor', 'dp')
- grad_mlp_gain: float32 [2048], P('dp')
- grad_w_gate: float32 [2048, 8192], P('dp', 'tensor')
- grad_w_up: float32 [2048, 8192], P('dp', 'tensor')
- grad_w_down: float32 [8192, 2048], P('tensor', 'dp')
The draws below stay inside these ranges and needn't reach their ends.
Inputs may be any that keep to these rules, and one draw needn't show every extreme that they name: `lengths`: each row sums to 1920; the rows of a group past that sum are padding; the largest length in every row is exactly 1024. The rows of one sequence hold consecutive positions rising by one from its first position, which is below 8192; the longest sequence of each group starts at 8191; padding rows hold 0. A permutation; dealt page j and given page pages[j] lie on devices with the same tensor index, and the 8 dealt pages of one device come one from each dp index.
All inputs are finite; a program needn't handle non-finite values.
Results may differ from the reference program's by a relative error of at most 0.025.
Values may be sent and summed in bfloat16 or wider, within the bound.
A program may use at most 320 MiB of HBM per device.

```python
import jax
import jax.numpy as jnp
from jax import lax

D = 2048
HQ = 32
KV = 8
HD = 64
FF = 8192
TOK_DP = 2048
MAXLEN = 1024
POS_START = 8192
NSEQ = 4
DP_GROUPS = 8
TP_GROUP = 4
TOKENS = 16384
N_DP = 8
N_TENSOR = 4


def layout(key):
    groups = DP_GROUPS
    seq_count = NSEQ
    remain_rows = TOK_DP - TOK_DP // 16 - MAXLEN
    part_count = seq_count - 1
    base_len = remain_rows // part_count
    extra_len = remain_rows - base_len * part_count
    part_ids = jnp.arange(part_count, dtype=jnp.int32)
    others = base_len + (part_ids < extra_len).astype(jnp.int32)
    others = jnp.broadcast_to(others[None, :], (groups, part_count))
    spread_max = max(0, min(base_len - 1, MAXLEN - base_len - 1))
    if part_count >= 2:
        pair_count = part_count // 2
        shifts = jax.random.randint(jax.random.fold_in(key, 1), (groups, pair_count), -spread_max, spread_max + 1)
        pair_shift = jnp.zeros((groups, part_count), jnp.int32)
        pair_shift = pair_shift.at[:, 0:2 * pair_count:2].add(shifts).at[:, 1:2 * pair_count:2].add(-shifts)
        others = others + pair_shift
    long_slot = jax.random.randint(jax.random.fold_in(key, 2), (groups, 1), 0, seq_count)
    column = jnp.arange(seq_count, dtype=jnp.int32)[None, :]
    take_index = jnp.clip(column - (column > long_slot).astype(jnp.int32), 0, part_count - 1)
    lengths = jnp.where(column == long_slot, MAXLEN, jnp.take_along_axis(others, take_index, axis=1)).astype(jnp.int32)
    seq_ends = jnp.cumsum(lengths, axis=1)
    begins = seq_ends - lengths
    starts = jax.random.randint(jax.random.fold_in(key, 3), (groups, seq_count), 0, POS_START)
    starts = jnp.where(column == long_slot, POS_START - 1, starts).astype(jnp.int32)
    row_ids = jnp.arange(TOK_DP, dtype=jnp.int32)
    segment = jnp.sum((row_ids[None, :, None] >= seq_ends[:, None, :]).astype(jnp.int32), axis=2)
    onehot = (segment[:, :, None] == jnp.arange(seq_count, dtype=jnp.int32)[None, None, :]).astype(jnp.int32)
    offset = jnp.sum(onehot * (starts - begins)[:, None, :], axis=2)
    positions = jnp.where(segment < seq_count, row_ids[None, :] + offset, 0).astype(jnp.int32)
    return (lengths, positions)


def draw_lengths(key, part):
    return layout(key)[0]


def draw_positions(key, part):
    return layout(key)[1]


def draw_pages(key, part):
    groups = DP_GROUPS
    splits = TP_GROUP
    row_keys = jax.random.split(jax.random.fold_in(key, 11), groups * splits)
    col_keys = jax.random.split(jax.random.fold_in(key, 12), groups * splits)
    source_of = jax.vmap(lambda sub_key: jax.random.permutation(sub_key, groups))(row_keys).reshape(groups, splits, groups)
    slot_of = jax.vmap(lambda sub_key: jax.random.permutation(sub_key, groups))(col_keys).reshape(groups, splits, groups)
    dest_ids = jnp.arange(groups, dtype=jnp.int32)[:, None, None]
    tensor_ids = jnp.arange(splits, dtype=jnp.int32)[None, :, None]
    slot_ids = slot_of[source_of, tensor_ids, dest_ids]
    page_map = (source_of * splits + tensor_ids) * groups + slot_ids
    return page_map.reshape(-1).astype(jnp.int32)


def level_of(stream_key, extent, pieces, least, largest):
    def one(axis_at, blocks):
        draws = jax.random.uniform(jax.random.fold_in(jax.random.fold_in(stream_key, 6), axis_at), (blocks,), jnp.float32, least / len(pieces), largest / len(pieces))
        return jnp.repeat(jnp.exp(draws), extent[axis_at] // blocks).reshape((-1,) + (1,) * (len(extent) - axis_at - 1))

    factor_of = one(*pieces[0])
    for cut in pieces[1:]:
        factor_of = factor_of * one(*cut)
    return factor_of


def noise(rng, extent, deviation, most, cuts=(), kind=jnp.bfloat16):
    factor_of = level_of(rng, extent, cuts, -0.22, 0.18) if cuts else 1.0
    values = jax.random.normal(rng, extent, jnp.float32) * deviation * factor_of
    return jnp.minimum(jnp.maximum(values, -most), most).astype(kind)


def setup_inputs(seed: int = 0) -> dict:
    key_of = jax.random.split(jax.random.key(seed), 15)
    tokens = noise(key_of[0], (TOKENS, D), 1.0, 6.0, ((0, 32),))
    upstream = noise(key_of[1], (TOKENS, D), 1.0, 6.0, ((0, 32),))
    lengths = draw_lengths(jax.random.fold_in(key_of[14], 71), 0)
    positions = draw_positions(jax.random.fold_in(key_of[14], 71), 0)
    pages = draw_pages(jax.random.fold_in(key_of[14], 71), 0)
    attn_gain = jnp.clip(1.0 + 0.18 * jax.random.normal(key_of[5], (D,), jnp.float32), 0.099609375, 1.8984375).astype(jnp.bfloat16)
    w_query = noise(key_of[6], (D, HQ * HD), D ** -0.5, 0.125, ((0, 8), (1, 4)))
    w_key = noise(key_of[7], (D, KV * HD), D ** -0.5, 0.125, ((0, 8), (1, 4)))
    w_value = noise(key_of[8], (D, KV * HD), D ** -0.5, 0.125, ((0, 8), (1, 4)))
    w_out = noise(key_of[9], (HQ * HD, D), (HQ * HD // 64) ** -0.5, 1.0, ((0, 4), (1, 8)))
    mlp_gain = jnp.clip(1.0 + 0.18 * jax.random.normal(key_of[10], (D,), jnp.float32), 0.099609375, 1.8984375).astype(jnp.bfloat16)
    w_gate = noise(key_of[11], (D, FF), D ** -0.5, 0.125, ((0, 8), (1, 4)))
    w_up = noise(key_of[12], (D, FF), D ** -0.5, 0.125, ((0, 8), (1, 4)))
    w_down = noise(key_of[13], (FF, D), FF ** -0.5, 0.0625, ((0, 4), (1, 8)))
    return {"tokens": tokens, "upstream": upstream, "lengths": lengths, "positions": positions, "pages": pages, "attn_gain": attn_gain, "w_query": w_query, "w_key": w_key, "w_value": w_value, "w_out": w_out, "mlp_gain": mlp_gain, "w_gate": w_gate, "w_up": w_up, "w_down": w_down}


@jax.custom_vjp
def low(v):
    return lax.optimization_barrier(v.astype(jnp.bfloat16)).astype(jnp.float32)

@jax.custom_vjp
def low_back(v):
    return v

def low_keep(v):
    return (low(v), None)

def low_pass(kept, grad):
    return (grad,)

def back_keep(v):
    return (v, None)

def back_low(kept, grad):
    return (low(grad),)
low.defvjp(low_keep, low_pass)
low_back.defvjp(back_keep, back_low)
epsilon = 1e-05
theta_base = 500000.0
masked_score = -1e+30
highest = lax.Precision.HIGHEST
block_rows = 512

def matmul(left, right):
    return jnp.dot(left, right, precision=highest, preferred_element_type=jnp.float32)

def rms_norm(hidden, gain):
    return hidden * lax.rsqrt(lax.optimization_barrier(jnp.mean(hidden * hidden, axis=-1, keepdims=True)) + epsilon) * gain

def rope_tables(positions, head_dim):
    half_dim = head_dim // 2
    inverse_freq = theta_base ** (-(jnp.arange(half_dim, dtype=jnp.float32) * 2.0) / head_dim)
    angles = positions.astype(jnp.float32)[:, None] * inverse_freq[None, :]
    cos_table = jnp.concatenate([jnp.cos(angles), jnp.cos(angles)], axis=1)
    sine_table = jnp.concatenate([jnp.sin(angles), jnp.sin(angles)], axis=1)
    return (cos_table, sine_table)

def rotate(values, cos_table, sine_table):
    half_dim = values.shape[-1] // 2
    turned = jnp.concatenate([-values[..., half_dim:], values[..., :half_dim]], axis=-1)
    return values * cos_table[:, None, :] + turned * sine_table[:, None, :]

def attention_shard(queries, keys_rot, values, segment):
    total_rows, q_heads, head_dim = queries.shape
    kv_heads = keys_rot.shape[1]
    groups = q_heads // kv_heads
    block_len = min(block_rows, total_rows)
    row_ids = jnp.arange(total_rows, dtype=jnp.int32)

    def one_block(row_start):
        q_block = lax.dynamic_slice_in_dim(queries, row_start, block_len, 0).reshape(block_len, kv_heads, groups, head_dim)
        raw_scores = low_back(jnp.einsum('qkgd,rkd->kgqr', q_block, keys_rot, precision=highest) * head_dim ** (-0.5))
        seg_rows = lax.dynamic_slice_in_dim(segment, row_start, block_len, 0)
        query_ids = row_start + jnp.arange(block_len, dtype=jnp.int32)
        allowed = (seg_rows[:, None] == segment[None, :]) & (row_ids[None, :] <= query_ids[:, None])
        probs_low = low(jax.nn.softmax(jnp.where(allowed[None, None], raw_scores, masked_score), axis=-1))
        mixed = jnp.einsum('kgqr,rkd->qkgd', probs_low, values, precision=highest)
        return mixed.reshape(block_len, q_heads * head_dim)
    block_starts = jnp.arange(total_rows // block_len, dtype=jnp.int32) * block_len
    return lax.map(jax.checkpoint(one_block), block_starts).reshape(total_rows, q_heads * head_dim)

def group_forward(params, hidden_in, segment, positions):
    gain_one, w_query, w_key, w_value, w_out, gain_two, w_gate, w_up, w_down = params
    tok_group = hidden_in.shape[0]
    q_cols = HQ * HD // N_TENSOR
    kv_cols = KV * HD // N_TENSOR
    ff_cols = FF // N_TENSOR
    cos_table, sine_table = rope_tables(positions, HD)
    normed_one = low(rms_norm(hidden_in, gain_one))
    branch_one = jnp.zeros_like(hidden_in)
    for shard in range(N_TENSOR):
        rows_in = low_back(normed_one)
        query_pre = low_back(matmul(rows_in, w_query[:, shard * q_cols:(shard + 1) * q_cols]))
        key_pre = low_back(matmul(rows_in, w_key[:, shard * kv_cols:(shard + 1) * kv_cols]))
        value_pre = low_back(matmul(rows_in, w_value[:, shard * kv_cols:(shard + 1) * kv_cols]))
        queries = low(rotate(query_pre.reshape(tok_group, -1, HD), cos_table, sine_table))
        keys_rot = low(rotate(key_pre.reshape(tok_group, -1, HD), cos_table, sine_table))
        values = low(value_pre).reshape(tok_group, -1, HD)
        mixed = low(low_back(attention_shard(queries, keys_rot, values, segment)))
        branch_one = branch_one + low(matmul(mixed, w_out[shard * q_cols:(shard + 1) * q_cols, :]))
    hidden_mid = hidden_in + low_back(branch_one)
    normed_two = low(rms_norm(hidden_mid, gain_two))
    branch_two = jnp.zeros_like(hidden_in)
    for shard in range(N_TENSOR):
        rows_in = low_back(normed_two)
        gate_pre = low_back(matmul(rows_in, w_gate[:, shard * ff_cols:(shard + 1) * ff_cols]))
        up_pre = low_back(matmul(rows_in, w_up[:, shard * ff_cols:(shard + 1) * ff_cols]))
        inner_act = low(jax.nn.silu(gate_pre) * up_pre)
        branch_two = branch_two + low(matmul(inner_act, w_down[shard * ff_cols:(shard + 1) * ff_cols, :]))
    return hidden_mid + low_back(branch_two)

def reference(tokens, upstream, lengths, positions, pages, attn_gain, w_query, w_key, w_value, w_out, mlp_gain, w_gate, w_up, w_down):
    page_rows = TOK_DP // (N_TENSOR * N_DP)
    deal_order = (pages[:, None] * page_rows + jnp.arange(page_rows, dtype=jnp.int32)[None, :]).reshape(-1).astype(jnp.int32)
    dealt_in = tokens.astype(jnp.float32)[deal_order].reshape(N_DP, TOK_DP, D)
    dealt_grad = upstream.astype(jnp.float32)[deal_order].reshape(N_DP, TOK_DP, D)
    seq_ends = jnp.cumsum(lengths, axis=1)
    row_ids = jnp.arange(TOK_DP, dtype=jnp.int32)
    segment = lax.optimization_barrier(jnp.sum((row_ids[None, :, None] >= seq_ends[:, None, :]).astype(jnp.int32), axis=2))
    valid_rows = (segment < NSEQ).astype(jnp.float32)[..., None]
    params = tuple((weight_arg.astype(jnp.float32) for weight_arg in (attn_gain, w_query, w_key, w_value, w_out, mlp_gain, w_gate, w_up, w_down)))

    def forward(dealt, weights):

        def one_group(group_item):
            hidden_in, seg_rows, pos_rows, mask_rows = group_item
            return group_forward(weights, hidden_in, seg_rows, pos_rows) * mask_rows
        return lax.map(jax.checkpoint(one_group), (dealt, segment, positions, valid_rows))
    result, pullback = jax.vjp(forward, dealt_in, params)
    grad_dealt, grad_params = pullback(dealt_grad)
    output = jnp.zeros((TOKENS, D), jnp.float32).at[deal_order].set(result.reshape(-1, D)).astype(jnp.bfloat16)
    grad_tokens = jnp.zeros((TOKENS, D), jnp.float32).at[deal_order].set(grad_dealt.reshape(-1, D)).astype(jnp.bfloat16)
    return (output, grad_tokens, grad_params[0], grad_params[1], grad_params[2], grad_params[3], grad_params[4], grad_params[5], grad_params[6], grad_params[7], grad_params[8])
```

```python
import functools

import jax
import jax.numpy as jnp
from jax import lax
from jax.experimental import pallas as pl
from jax.experimental.pallas import tpu as pltpu
from jax.sharding import PartitionSpec as P

HD = 64
HALF = HD // 2

epsilon = 1e-05
theta_base = 500000.0
masked_score = -1e30
score_scale = HD**-0.5
block_rows = 256
MESH = pl.DeviceIdType.MESH
f32 = jnp.float32
bf16 = jnp.bfloat16


def dot_nn(left, right):
    return lax.dot_general(left, right, (((1,), (0,)), ((), ())), preferred_element_type=f32)


def dot_nt(left, right):
    return lax.dot_general(left, right, (((1,), (1,)), ((), ())), preferred_element_type=f32)


def dot_tn(left, right):
    return lax.dot_general(left, right, (((0,), (0,)), ((), ())), preferred_element_type=f32)


def exchange_kernel(dp_count, tp_count, page_rows, to_heads, src, dst, send_sem, recv_sem, own_sem):
    count = dp_count * tp_count
    my_dp = lax.axis_index("dp")
    my_tp = lax.axis_index("tensor")
    me = my_dp * tp_count + my_tp

    def split(peer):
        return lax.div(peer, tp_count), lax.rem(peer, tp_count)

    barrier = pltpu.get_barrier_semaphore()

    def greet(j, carry):
        p_dp, p_tp = split(lax.rem(me + j, count))
        pl.semaphore_signal(
            barrier, inc=1, device_id={"dp": p_dp, "tensor": p_tp}, device_id_type=MESH
        )
        return carry

    lax.fori_loop(1, count, greet, 0)
    pl.semaphore_wait(barrier, count - 1)

    def ends(p_dp, p_tp, peer):
        if to_heads:
            return src.at[p_tp, pl.ds(p_dp * page_rows, page_rows), :], dst.at[me]
        return src.at[peer], dst.at[my_tp, pl.ds(my_dp * page_rows, page_rows), :]

    own_src, own_dst = ends(my_dp, my_tp, me)
    own = pltpu.make_async_copy(own_src, own_dst, own_sem)
    own.start()

    def copy_to(j):
        peer = lax.rem(me + j, count)
        p_dp, p_tp = split(peer)
        block_src, block_dst = ends(p_dp, p_tp, peer)
        return pltpu.make_async_remote_copy(
            src_ref=block_src,
            dst_ref=block_dst,
            send_sem=send_sem.at[j],
            recv_sem=recv_sem.at[j],
            device_id={"dp": p_dp, "tensor": p_tp},
            device_id_type=MESH,
        )

    def start(j, carry):
        copy_to(j).start()
        return carry

    def finish(j, carry):
        copy_to(j).wait()
        return carry

    lax.fori_loop(1, count, start, 0)
    own.wait()
    lax.fori_loop(1, count, finish, 0)


def exchange(array, dp_count, tp_count, page_rows, to_heads, collective_id):
    cols = array.shape[-1]
    count = dp_count * tp_count
    if to_heads:
        out_shape = (count, page_rows, cols)
    else:
        out_shape = (tp_count, dp_count * page_rows, cols)
    nbytes = array.size * 2
    return pl.pallas_call(
        functools.partial(exchange_kernel, dp_count, tp_count, page_rows, to_heads),
        out_shape=jax.ShapeDtypeStruct(out_shape, array.dtype),
        in_specs=[pl.BlockSpec(memory_space=pl.ANY)],
        out_specs=pl.BlockSpec(memory_space=pl.ANY),
        scratch_shapes=[
            pltpu.SemaphoreType.DMA((count,)),
            pltpu.SemaphoreType.DMA((count,)),
            pltpu.SemaphoreType.DMA,
        ],
        compiler_params=pltpu.CompilerParams(collective_id=collective_id, has_side_effects=True),
        cost_estimate=pl.CostEstimate(flops=0, bytes_accessed=40 * nbytes, transcendentals=0),
        name="exchange",
    )(array)


def prep_kernel(pages_per, q_heads, kv_heads, perm, *refs):
    page_refs = refs[:pages_per]
    cos_ref, sin_ref, q_t, k_t, k_rows, v_t, v_rows = refs[pages_per:]
    rows = jnp.concatenate([r[0].astype(f32) for r in page_refs], axis=0)
    turned = rows.T
    cos, sin = cos_ref[...], sin_ref[...]

    def rope(base):
        first, second = turned[base : base + HALF], turned[base + HALF : base + HD]
        return jnp.concatenate([first * cos - second * sin, second * cos + first * sin], axis=0)

    for h in range(q_heads):
        roped = rope(h * HD).astype(bf16)
        q_t[h * HD : (h + 1) * HD, :] = (roped.astype(f32) * score_scale).astype(bf16)
    k_base = q_heads * HD
    v_base = k_base + kv_heads * HD
    for g in range(kv_heads):
        roped = rope(k_base + g * HD)
        k_t[g * HD : (g + 1) * HD, :] = roped.astype(bf16)
        k_rows[g] = roped.T.astype(bf16)
        v_t[g * HD : (g + 1) * HD, :] = turned[v_base + g * HD : v_base + (g + 1) * HD].astype(bf16)
        v_rows[g] = rows[:, v_base + g * HD : v_base + (g + 1) * HD].astype(bf16)


def prepare(slots, perm, cos_t, sin_t, q_heads, kv_heads):
    page_rows, cols = slots.shape[1:]
    total_rows = slots.shape[0] * page_rows
    lanes = 128
    pages_per = lanes // page_rows

    def page_spec(a):
        return pl.BlockSpec(
            (1, page_rows, cols), lambda i, perm_ref, a=a: (perm_ref[i * pages_per + a], 0, 0)
        )

    table = pl.BlockSpec((HALF, lanes), lambda i, perm_ref: (0, i))
    return pl.pallas_call(
        functools.partial(prep_kernel, pages_per, q_heads, kv_heads),
        grid_spec=pltpu.PrefetchScalarGridSpec(
            num_scalar_prefetch=1,
            grid=(total_rows // lanes,),
            in_specs=[page_spec(a) for a in range(pages_per)] + [table, table],
            out_specs=[
                pl.BlockSpec((q_heads * HD, lanes), lambda i, perm_ref: (0, i)),
                pl.BlockSpec((kv_heads * HD, lanes), lambda i, perm_ref: (0, i)),
                pl.BlockSpec((kv_heads, lanes, HD), lambda i, perm_ref: (0, i, 0)),
                pl.BlockSpec((kv_heads * HD, lanes), lambda i, perm_ref: (0, i)),
                pl.BlockSpec((kv_heads, lanes, HD), lambda i, perm_ref: (0, i, 0)),
            ],
        ),
        out_shape=[
            jax.ShapeDtypeStruct((q_heads * HD, total_rows), bf16),
            jax.ShapeDtypeStruct((kv_heads * HD, total_rows), bf16),
            jax.ShapeDtypeStruct((kv_heads, total_rows, HD), bf16),
            jax.ShapeDtypeStruct((kv_heads * HD, total_rows), bf16),
            jax.ShapeDtypeStruct((kv_heads, total_rows, HD), bf16),
        ],
        cost_estimate=pl.CostEstimate(
            flops=8 * slots.size, bytes_accessed=6 * slots.size, transcendentals=0
        ),
        name="prepare",
    )(perm, *([slots] * pages_per), cos_t, sin_t)


def block_bias(i, j, begin_row, block_len):
    keys = j * block_len + lax.broadcasted_iota(jnp.int32, (block_len, block_len), 0)
    queries = i * block_len + lax.broadcasted_iota(jnp.int32, (block_len, block_len), 1)
    allowed = (keys >= begin_row) & (keys <= queries)
    return jnp.where(allowed, 0.0, masked_score)


def forward_kernel(
    q_heads, kv_heads, page_rows, first_block, perm,
    q_t, k_rows, v_t, begin, o_t, lse, o_slots, acc, top, total, stage, sems,
):
    i = pl.program_id(0)
    block_len = q_t.shape[1]
    per_group = q_heads // kv_heads
    acc[...] = jnp.zeros_like(acc)
    top[...] = jnp.full_like(top, masked_score)
    total[...] = jnp.zeros_like(total)
    begin_row = begin[...]

    def visit(j, carry):
        bias = block_bias(i, j, begin_row, block_len)
        at = pl.ds(pl.multiple_of(j * block_len, block_len), block_len)
        for h in range(q_heads):
            g = h // per_group
            span = slice(h * HD, (h + 1) * HD)
            scores = dot_nn(k_rows[g, at, :], q_t[span, :]) + bias
            old = top[h : h + 1, :]
            new = jnp.maximum(old, jnp.max(scores, axis=0, keepdims=True))
            weights = jnp.exp(scores - new)
            fade = jnp.exp(old - new)
            total[h : h + 1, :] = total[h : h + 1, :] * fade + jnp.sum(
                weights, axis=0, keepdims=True
            )
            top[h : h + 1, :] = new
            acc[span, :] = acc[span, :] * fade + dot_nn(
                v_t[g * HD : (g + 1) * HD, at], weights.astype(bf16)
            )
        return carry

    lax.fori_loop(first_block[i], i + 1, visit, 0)
    lse[...] = top[...] + jnp.log(total[...])
    scaled = [
        acc[h * HD : (h + 1) * HD, :] / total[h : h + 1, :] for h in range(q_heads)
    ]
    mixed = jnp.concatenate(scaled, axis=0)
    o_t[...] = mixed.astype(bf16)
    pages = block_len // page_rows
    stage[...] = mixed.T.astype(bf16).reshape(pages, page_rows, q_heads * HD)
    copies = [
        pltpu.make_async_copy(stage.at[a], o_slots.at[perm[i * pages + a]], sems.at[a])
        for a in range(pages)
    ]
    for copy in copies:
        copy.start()
    for copy in copies:
        copy.wait()


def attend_forward(q_t, k_rows, v_t, begin, first_block, perm, page_rows, block_len):
    total_rows = q_t.shape[1]
    kv_heads = k_rows.shape[0]
    q_heads = q_t.shape[0] // HD
    pages = block_len // page_rows
    return pl.pallas_call(
        functools.partial(forward_kernel, q_heads, kv_heads, page_rows),
        grid_spec=pltpu.PrefetchScalarGridSpec(
            num_scalar_prefetch=2,
            grid=(total_rows // block_len,),
            in_specs=[
                pl.BlockSpec((q_heads * HD, block_len), lambda i, *_: (0, i)),
                pl.BlockSpec((kv_heads, total_rows, HD), lambda i, *_: (0, 0, 0)),
                pl.BlockSpec((kv_heads * HD, total_rows), lambda i, *_: (0, 0)),
                pl.BlockSpec((1, block_len), lambda i, *_: (0, i)),
            ],
            out_specs=[
                pl.BlockSpec((q_heads * HD, block_len), lambda i, *_: (0, i)),
                pl.BlockSpec((q_heads, block_len), lambda i, *_: (0, i)),
                pl.BlockSpec(memory_space=pl.ANY),
            ],
            scratch_shapes=[
                pltpu.VMEM((q_heads * HD, block_len), f32),
                pltpu.VMEM((q_heads, block_len), f32),
                pltpu.VMEM((q_heads, block_len), f32),
                pltpu.VMEM((pages, page_rows, q_heads * HD), bf16),
                pltpu.SemaphoreType.DMA((pages,)),
            ],
        ),
        out_shape=[
            jax.ShapeDtypeStruct((q_heads * HD, total_rows), bf16),
            jax.ShapeDtypeStruct((q_heads, total_rows), f32),
            jax.ShapeDtypeStruct((total_rows // page_rows, page_rows, q_heads * HD), bf16),
        ],
        cost_estimate=pl.CostEstimate(
            flops=q_heads * total_rows * total_rows * HD,
            bytes_accessed=8 * q_t.size,
            transcendentals=q_heads * total_rows * total_rows // 4,
        ),
        name="attend_forward",
    )(first_block, perm, q_t, k_rows, v_t, begin)


def backward_kernel(
    q_heads, kv_heads, page_rows, pages, first_block, perm, *refs
):
    grad_pages = refs[:pages]
    (
        q_t, k_rows, k_t, v_rows, o_t, lse, begin, cos_ref, sin_ref, cos_all, sin_all,
        out, grad_q, grad_k, grad_v, stage, kv_stage, sems, kv_sems,
    ) = refs[pages:]
    i = pl.program_id(0)
    steps = pl.num_programs(0)
    block_len = q_t.shape[1]
    per_group = q_heads // kv_heads
    q_cols = q_heads * HD
    kv_cols = kv_heads * HD

    @pl.when(i == 0)
    def _():
        grad_k[...] = jnp.zeros_like(grad_k)
        grad_v[...] = jnp.zeros_like(grad_v)

    grad_rows = jnp.concatenate([r[0].astype(f32) for r in grad_pages], axis=0)
    grad_t = grad_rows.T
    grad_low = grad_t.astype(bf16)
    inner = [
        jnp.sum(
            grad_t[h * HD : (h + 1) * HD] * o_t[h * HD : (h + 1) * HD, :].astype(f32),
            axis=0,
            keepdims=True,
        )
        for h in range(q_heads)
    ]
    grad_q[...] = jnp.zeros_like(grad_q)
    begin_row = begin[...]

    def visit(j, carry):
        bias = block_bias(i, j, begin_row, block_len)
        at = pl.ds(pl.multiple_of(j * block_len, block_len), block_len)
        for g in range(kv_heads):
            kv_span = slice(g * HD, (g + 1) * HD)
            keys, vals, keys_t = k_rows[g, at, :], v_rows[g, at, :], k_t[kv_span, at]
            add_k = jnp.zeros((HD, block_len), f32)
            add_v = jnp.zeros((HD, block_len), f32)
            for h in range(g * per_group, (g + 1) * per_group):
                span = slice(h * HD, (h + 1) * HD)
                queries = q_t[span, :]
                probs = jnp.exp(dot_nn(keys, queries) + bias - lse[h : h + 1, :])
                grad_h = grad_low[span]
                grad_probs = dot_nn(vals, grad_h)
                grad_scores = (probs * (grad_probs - inner[h])).astype(bf16)
                add_v = add_v + dot_nt(grad_h, probs.astype(bf16))
                add_k = add_k + dot_nt(queries, grad_scores)
                grad_q[span, :] = grad_q[span, :] + dot_nn(keys_t, grad_scores)
            grad_k[kv_span, at] = grad_k[kv_span, at] + add_k
            grad_v[kv_span, at] = grad_v[kv_span, at] + add_v
        return carry

    lax.fori_loop(first_block[i], i + 1, visit, 0)

    def unrope(value, cos, sin):
        first, second = value[:HALF], value[HALF:]
        return jnp.concatenate([first * cos + second * sin, second * cos - first * sin], axis=0)

    cos, sin = cos_ref[...], sin_ref[...]
    parts = [
        unrope(grad_q[h * HD : (h + 1) * HD, :] * score_scale, cos, sin) for h in range(q_heads)
    ]
    stage[...] = jnp.concatenate(parts, axis=0).T.astype(bf16).reshape(pages, page_rows, q_cols)
    copies = [
        pltpu.make_async_copy(
            stage.at[a], out.at[perm[i * pages + a], :, pl.ds(0, q_cols)], sems.at[a]
        )
        for a in range(pages)
    ]
    for copy in copies:
        copy.start()
    for copy in copies:
        copy.wait()

    @pl.when(i == steps - 1)
    def _():
        all_pages = kv_stage.shape[0]
        cos, sin = cos_all[...], sin_all[...]
        parts = [unrope(grad_k[g * HD : (g + 1) * HD, :], cos, sin) for g in range(kv_heads)]
        both = jnp.concatenate(parts + [grad_v[...]], axis=0)
        kv_stage[...] = both.T.astype(bf16).reshape(all_pages, page_rows, 2 * kv_cols)
        copies = [
            pltpu.make_async_copy(
                kv_stage.at[a], out.at[perm[a], :, pl.ds(q_cols, 2 * kv_cols)], kv_sems.at[a]
            )
            for a in range(all_pages)
        ]
        for copy in copies:
            copy.start()
        for copy in copies:
            copy.wait()


def attend_backward(
    grad_slots, q_t, k_rows, k_t, v_rows, o_t, lse, begin, cos_t, sin_t, first_block, perm,
    page_rows, block_len,
):
    total_rows = q_t.shape[1]
    kv_heads = k_rows.shape[0]
    q_heads = q_t.shape[0] // HD
    pages = block_len // page_rows
    all_pages = total_rows // page_rows
    q_cols = q_heads * HD
    kv_cols = kv_heads * HD

    def page_spec(a):
        return pl.BlockSpec(
            (1, page_rows, q_cols),
            lambda i, first_ref, perm_ref, a=a: (perm_ref[i * pages + a], 0, 0),
        )

    def whole(shape):
        return pl.BlockSpec(shape, lambda i, *_: (0,) * len(shape))

    def column(rows):
        return pl.BlockSpec((rows, block_len), lambda i, *_: (0, i))

    return pl.pallas_call(
        functools.partial(backward_kernel, q_heads, kv_heads, page_rows, pages),
        grid_spec=pltpu.PrefetchScalarGridSpec(
            num_scalar_prefetch=2,
            grid=(total_rows // block_len,),
            in_specs=[page_spec(a) for a in range(pages)]
            + [
                column(q_cols),
                whole((kv_heads, total_rows, HD)),
                whole((kv_cols, total_rows)),
                whole((kv_heads, total_rows, HD)),
                column(q_cols),
                column(q_heads),
                column(1),
                column(HALF),
                column(HALF),
                whole((HALF, total_rows)),
                whole((HALF, total_rows)),
            ],
            out_specs=pl.BlockSpec(memory_space=pl.ANY),
            scratch_shapes=[
                pltpu.VMEM((q_cols, block_len), f32),
                pltpu.VMEM((kv_cols, total_rows), f32),
                pltpu.VMEM((kv_cols, total_rows), f32),
                pltpu.VMEM((pages, page_rows, q_cols), bf16),
                pltpu.VMEM((all_pages, page_rows, 2 * kv_cols), bf16),
                pltpu.SemaphoreType.DMA((pages,)),
                pltpu.SemaphoreType.DMA((all_pages,)),
            ],
        ),
        out_shape=jax.ShapeDtypeStruct((all_pages, page_rows, q_cols + 2 * kv_cols), bf16),
        cost_estimate=pl.CostEstimate(
            flops=3 * q_heads * total_rows * total_rows * HD,
            bytes_accessed=12 * q_t.size,
            transcendentals=q_heads * total_rows * total_rows // 4,
        ),
        name="attend_backward",
    )(
        first_block, perm, *([grad_slots] * pages), q_t, k_rows, k_t, v_rows, o_t, lse, begin,
        cos_t, sin_t, cos_t, sin_t,
    )


def rms_scale(hidden):
    return lax.rsqrt(jnp.mean(hidden * hidden, axis=1, keepdims=True) + epsilon)


def norm_back(grad_norm, hidden, scale_rows, gain):
    normed = hidden * scale_rows
    gain_part = jnp.sum(grad_norm * normed, axis=0)
    inner = grad_norm * gain
    grad_hidden = scale_rows * (inner - normed * jnp.mean(inner * normed, axis=1, keepdims=True))
    return (grad_hidden, gain_part)


def local(
    tokens,
    upstream,
    lengths,
    positions,
    pages,
    attn_gain,
    w_query,
    w_key,
    w_value,
    w_out,
    mlp_gain,
    w_gate,
    w_up,
    w_down,
):
    dp_count = lax.axis_size("dp")
    tp_count = lax.axis_size("tensor")
    dp_index = lax.axis_index("dp")
    tp_index = lax.axis_index("tensor")
    tok_dev, width = tokens.shape
    tok_group = tok_dev * tp_count
    page_rows = tok_dev // dp_count
    group_pages = tp_count * dp_count
    page_count = pages.shape[0]
    device = dp_index * tp_count + tp_index
    everyone = ("tensor", "dp")

    local_ids = jnp.arange(dp_count, dtype=jnp.int32)
    inverse = (
        jnp.zeros((page_count,), jnp.int32).at[pages].set(jnp.arange(page_count, dtype=jnp.int32))
    )
    dealt = lax.dynamic_slice_in_dim(inverse, device * dp_count, dp_count)
    dest_group = dealt // group_pages
    send_order = jnp.zeros((dp_count,), jnp.int32).at[dest_group].set(local_ids)
    group_sources = lax.dynamic_slice_in_dim(pages, dp_index * group_pages, group_pages)
    perm = (
        (group_sources // group_pages) * tp_count
        + jnp.arange(group_pages, dtype=jnp.int32) // dp_count
    ).astype(jnp.int32)

    def reorder(rows, order):
        blocks = rows.reshape(dp_count, page_rows, rows.shape[1])
        return jnp.take(blocks, order, axis=0).reshape(rows.shape)

    hidden_in = reorder(tokens, send_order).astype(f32)
    grad_top = reorder(upstream, send_order).astype(f32)
    seq_lens = lengths[0]
    seq_ends = jnp.cumsum(seq_lens)
    place = (jnp.take(dealt, send_order) % group_pages) * page_rows
    place_rows = (place[:, None] + jnp.arange(page_rows, dtype=jnp.int32)[None, :]).reshape(-1)
    valid_rows = (place_rows < seq_ends[-1]).astype(f32)[:, None]

    row_ids = jnp.arange(tok_group, dtype=jnp.int32)
    begin = jnp.max(
        jnp.where(row_ids[:, None] >= seq_ends[None, :], seq_ends[None, :], 0), axis=1
    ).astype(jnp.int32)
    block_len = min(block_rows, tok_group)
    first_block = begin[::block_len] // block_len
    begin = begin[None, :]
    inverse_freq = theta_base ** (-(jnp.arange(HALF, dtype=f32) * 2.0) / HD)
    angles = inverse_freq[:, None] * positions.astype(f32)
    cos_t, sin_t = jnp.cos(angles), jnp.sin(angles)

    q_cols, kv_cols = w_query.shape[1], w_key.shape[1]
    q_heads, kv_heads = q_cols // HD, kv_cols // HD
    qkv_shard = jnp.concatenate([w_query, w_key, w_value], axis=1)
    row_shard = qkv_shard.shape[0]

    def gather_all(shard):
        full = lax.all_gather(shard, everyone, axis=0, tiled=False)
        return full.reshape(tp_count, dp_count * shard.shape[0], shard.shape[1])

    def scatter_all(full):
        blocks = full.reshape(tp_count * dp_count, row_shard, full.shape[2])
        return lax.psum_scatter(blocks, everyone, scatter_dimension=0, tiled=False)

    w_qkv = gather_all(qkv_shard)
    w_out_t = gather_all(w_out.T)
    gains = lax.all_gather(jnp.stack([attn_gain, mlp_gain]), "dp", axis=1, tiled=True)
    gain_one, gain_two = gains[0].astype(f32), gains[1].astype(f32)
    full_gate = lax.all_gather(w_gate, "dp", axis=0, tiled=True)
    full_up = lax.all_gather(w_up, "dp", axis=0, tiled=True)
    full_down = lax.all_gather(w_down, "dp", axis=1, tiled=True)

    scale_one = rms_scale(hidden_in)
    normed_one = (hidden_in * scale_one * gain_one).astype(bf16)
    qkv = jnp.einsum("rk,tkc->trc", normed_one, w_qkv, preferred_element_type=f32).astype(bf16)
    trade = functools.partial(
        exchange, dp_count=dp_count, tp_count=tp_count, page_rows=page_rows
    )
    qkv_slots = trade(qkv, to_heads=True, collective_id=0)
    q_t, k_t, k_rows, v_t, v_rows = prepare(qkv_slots, perm, cos_t, sin_t, q_heads, kv_heads)
    o_t, lse, o_slots = attend_forward(
        q_t, k_rows, v_t, begin, first_block, perm, page_rows, block_len
    )
    mixed = trade(o_slots, to_heads=False, collective_id=1)
    branch_one = jnp.einsum("trc,tkc->rk", mixed, w_out_t, preferred_element_type=f32)
    hidden_mid = hidden_in + branch_one

    scale_two = rms_scale(hidden_mid)
    normed_two = (hidden_mid * scale_two * gain_two).astype(bf16)
    mlp_rows = lax.all_gather(normed_two, "tensor", axis=0, tiled=True)
    grad_out = grad_top * valid_rows
    grad_mlp = lax.all_gather(grad_out.astype(bf16), "tensor", axis=0, tiled=True)
    gate_pre = dot_nn(mlp_rows, full_gate)
    up_pre = dot_nn(mlp_rows, full_up)
    sigmoid_gate = jax.nn.sigmoid(gate_pre)
    activated = gate_pre * sigmoid_gate
    inner_act = (activated * up_pre).astype(bf16)
    branch_two = lax.psum_scatter(
        dot_nn(inner_act, full_down).astype(bf16), "tensor", scatter_dimension=0, tiled=True
    ).astype(f32)
    result = ((hidden_mid + branch_two) * valid_rows).astype(bf16)

    grad_down = dot_tn(inner_act, grad_mlp)
    grad_inner = dot_nt(grad_mlp, full_down)
    grad_upre = (grad_inner * activated).astype(bf16)
    grad_gpre = (
        grad_inner * up_pre * sigmoid_gate * (1.0 + gate_pre * (1.0 - sigmoid_gate))
    ).astype(bf16)
    grad_gate = dot_tn(mlp_rows, grad_gpre)
    grad_up = dot_tn(mlp_rows, grad_upre)
    grad_normed_two = lax.psum_scatter(
        (dot_nt(grad_gpre, full_gate) + dot_nt(grad_upre, full_up)).astype(bf16),
        "tensor",
        scatter_dimension=0,
        tiled=True,
    ).astype(f32)
    grad_mid_norm, gain_two_part = norm_back(grad_normed_two, hidden_mid, scale_two, gain_two)
    grad_mid = grad_out + grad_mid_norm

    grad_z = grad_mid.astype(bf16)
    grad_mixed = jnp.einsum("rk,tkc->trc", grad_z, w_out_t, preferred_element_type=f32).astype(
        bf16
    )
    grad_slots = trade(grad_mixed, to_heads=True, collective_id=2)
    grad_wout_t = jnp.einsum("rk,trc->tkc", grad_z, mixed, preferred_element_type=f32)
    grad_qkv_slots = attend_backward(
        grad_slots, q_t, k_rows, k_t, v_rows, o_t, lse, begin, cos_t, sin_t, first_block, perm,
        page_rows, block_len,
    )
    grad_qkv = trade(grad_qkv_slots, to_heads=False, collective_id=3)
    grad_wqkv = jnp.einsum("rk,trc->tkc", normed_one, grad_qkv, preferred_element_type=f32)
    grad_normed_one = jnp.einsum("trc,tkc->rk", grad_qkv, w_qkv, preferred_element_type=f32)
    grad_in_norm, gain_one_part = norm_back(grad_normed_one, hidden_in, scale_one, gain_one)
    grad_in = (grad_mid + grad_in_norm).astype(bf16)

    def reduce_dp(grad, axis):
        return lax.psum_scatter(
            grad.astype(bf16), "dp", scatter_dimension=axis, tiled=True
        ).astype(f32)

    sum_down = reduce_dp(grad_down, 1)
    sum_gate = reduce_dp(grad_gate, 0)
    sum_up = reduce_dp(grad_up, 0)
    sum_out = scatter_all(grad_wout_t.astype(bf16)).astype(f32).T
    sum_qkv = scatter_all(grad_wqkv.astype(bf16)).astype(f32)
    gain_sums = lax.psum(jnp.stack([gain_one_part, gain_two_part]), everyone)
    gain_shard = attn_gain.shape[0]
    gain_sums = lax.dynamic_slice_in_dim(gain_sums, dp_index * gain_shard, gain_shard, 1)
    return (
        reorder(result, dest_group),
        reorder(grad_in, dest_group),
        gain_sums[0],
        sum_qkv[:, :q_cols],
        sum_qkv[:, q_cols : q_cols + kv_cols],
        sum_qkv[:, q_cols + kv_cols :],
        sum_out,
        gain_sums[1],
        sum_gate,
        sum_up,
        sum_down,
    )


def solution(mesh):
    rows = P(("dp", "tensor"), None)
    weight = P("dp", "tensor")
    weight_t = P("tensor", "dp")
    return jax.shard_map(
        local,
        mesh=mesh,
        in_specs=(
            rows,
            rows,
            P("dp", None),
            P("dp", None),
            P(),
            P("dp"),
            weight,
            weight,
            weight,
            weight_t,
            P("dp"),
            weight,
            weight,
            weight_t,
        ),
        out_specs=(
            rows,
            rows,
            P("dp"),
            weight,
            weight,
            weight,
            weight_t,
            P("dp"),
            weight,
            weight,
            weight_t,
        ),
        check_vma=False,
    )
```

```python
import functools

import jax
import jax.numpy as jnp
from jax import lax
from jax.experimental import pallas as pl
from jax.experimental.layout import Layout, with_layout_constraint
from jax.experimental.pallas import tpu as pltpu
from jax.sharding import PartitionSpec as P

HD = 64
HALF = HD // 2

epsilon = 1e-05
theta_base = 500000.0
masked_score = -1e30
score_scale = HD**-0.5
block_rows = 256
MESH = pl.DeviceIdType.MESH
f32 = jnp.float32
bf16 = jnp.bfloat16


def dot_nn(left, right):
    return lax.dot_general(left, right, (((1,), (0,)), ((), ())), preferred_element_type=f32)


def dot_nt(left, right):
    return lax.dot_general(left, right, (((1,), (1,)), ((), ())), preferred_element_type=f32)


def dot_tn(left, right):
    return lax.dot_general(left, right, (((0,), (0,)), ((), ())), preferred_element_type=f32)


def prep_kernel(pages_per, q_heads, kv_heads, perm, *refs):
    page_refs = refs[:pages_per]
    cos_ref, sin_ref, q_t, k_t, k_rows, v_t, v_rows = refs[pages_per:]
    rows = jnp.concatenate([r[0].astype(f32) for r in page_refs], axis=0)
    turned = rows.T
    cos, sin = cos_ref[...], sin_ref[...]

    def rope(base):
        first, second = turned[base : base + HALF], turned[base + HALF : base + HD]
        return jnp.concatenate([first * cos - second * sin, second * cos + first * sin], axis=0)

    for h in range(q_heads):
        roped = rope(h * HD).astype(bf16)
        q_t[h * HD : (h + 1) * HD, :] = (roped.astype(f32) * score_scale).astype(bf16)
    k_base = q_heads * HD
    v_base = k_base + kv_heads * HD
    for g in range(kv_heads):
        roped = rope(k_base + g * HD)
        k_t[g * HD : (g + 1) * HD, :] = roped.astype(bf16)
        k_rows[g] = roped.T.astype(bf16)
        v_t[g * HD : (g + 1) * HD, :] = turned[v_base + g * HD : v_base + (g + 1) * HD].astype(bf16)
        v_rows[g] = rows[:, v_base + g * HD : v_base + (g + 1) * HD].astype(bf16)


def prepare(slots, perm, cos_t, sin_t, q_heads, kv_heads):
    page_rows, cols = slots.shape[1:]
    total_rows = slots.shape[0] * page_rows
    lanes = 128
    pages_per = lanes // page_rows

    def page_spec(a):
        return pl.BlockSpec(
            (1, page_rows, cols), lambda i, perm_ref, a=a: (perm_ref[i * pages_per + a], 0, 0)
        )

    table = pl.BlockSpec((HALF, lanes), lambda i, perm_ref: (0, i))
    return pl.pallas_call(
        functools.partial(prep_kernel, pages_per, q_heads, kv_heads),
        grid_spec=pltpu.PrefetchScalarGridSpec(
            num_scalar_prefetch=1,
            grid=(total_rows // lanes,),
            in_specs=[page_spec(a) for a in range(pages_per)] + [table, table],
            out_specs=[
                pl.BlockSpec((q_heads * HD, lanes), lambda i, perm_ref: (0, i)),
                pl.BlockSpec((kv_heads * HD, lanes), lambda i, perm_ref: (0, i)),
                pl.BlockSpec((kv_heads, lanes, HD), lambda i, perm_ref: (0, i, 0)),
                pl.BlockSpec((kv_heads * HD, lanes), lambda i, perm_ref: (0, i)),
                pl.BlockSpec((kv_heads, lanes, HD), lambda i, perm_ref: (0, i, 0)),
            ],
        ),
        out_shape=[
            jax.ShapeDtypeStruct((q_heads * HD, total_rows), bf16),
            jax.ShapeDtypeStruct((kv_heads * HD, total_rows), bf16),
            jax.ShapeDtypeStruct((kv_heads, total_rows, HD), bf16),
            jax.ShapeDtypeStruct((kv_heads * HD, total_rows), bf16),
            jax.ShapeDtypeStruct((kv_heads, total_rows, HD), bf16),
        ],
        cost_estimate=pl.CostEstimate(
            flops=8 * slots.size, bytes_accessed=6 * slots.size, transcendentals=0
        ),
        name="prepare",
    )(perm, *([slots] * pages_per), cos_t, sin_t)


def block_bias(i, j, begin_row, block_len):
    keys = j * block_len + lax.broadcasted_iota(jnp.int32, (block_len, block_len), 0)
    queries = i * block_len + lax.broadcasted_iota(jnp.int32, (block_len, block_len), 1)
    allowed = (keys >= begin_row) & (keys <= queries)
    return jnp.where(allowed, 0.0, masked_score)


def forward_kernel(
    q_heads, kv_heads, page_rows, first_block, perm,
    q_t, k_rows, v_t, begin, o_t, lse, o_slots, acc, top, total, stage, sems,
):
    i = pl.program_id(0)
    block_len = q_t.shape[1]
    per_group = q_heads // kv_heads
    acc[...] = jnp.zeros_like(acc)
    top[...] = jnp.full_like(top, masked_score)
    total[...] = jnp.zeros_like(total)
    begin_row = begin[...]

    def visit(j, carry):
        bias = block_bias(i, j, begin_row, block_len)
        at = pl.ds(pl.multiple_of(j * block_len, block_len), block_len)
        for h in range(q_heads):
            g = h // per_group
            span = slice(h * HD, (h + 1) * HD)
            scores = dot_nn(k_rows[g, at, :], q_t[span, :]) + bias
            old = top[h : h + 1, :]
            new = jnp.maximum(old, jnp.max(scores, axis=0, keepdims=True))
            weights = jnp.exp(scores - new)
            fade = jnp.exp(old - new)
            total[h : h + 1, :] = total[h : h + 1, :] * fade + jnp.sum(
                weights, axis=0, keepdims=True
            )
            top[h : h + 1, :] = new
            acc[span, :] = acc[span, :] * fade + dot_nn(
                v_t[g * HD : (g + 1) * HD, at], weights.astype(bf16)
            )
        return carry

    lax.fori_loop(first_block[i], i + 1, visit, 0)
    lse[...] = top[...] + jnp.log(total[...])
    scaled = [
        acc[h * HD : (h + 1) * HD, :] / total[h : h + 1, :] for h in range(q_heads)
    ]
    mixed = jnp.concatenate(scaled, axis=0)
    o_t[...] = mixed.astype(bf16)
    pages = block_len // page_rows
    stage[...] = mixed.T.astype(bf16).reshape(pages, page_rows, q_heads * HD)
    copies = [
        pltpu.make_async_copy(stage.at[a], o_slots.at[perm[i * pages + a]], sems.at[a])
        for a in range(pages)
    ]
    for copy in copies:
        copy.start()
    for copy in copies:
        copy.wait()


def attend_forward(q_t, k_rows, v_t, begin, first_block, perm, page_rows, block_len):
    total_rows = q_t.shape[1]
    kv_heads = k_rows.shape[0]
    q_heads = q_t.shape[0] // HD
    pages = block_len // page_rows
    return pl.pallas_call(
        functools.partial(forward_kernel, q_heads, kv_heads, page_rows),
        grid_spec=pltpu.PrefetchScalarGridSpec(
            num_scalar_prefetch=2,
            grid=(total_rows // block_len,),
            in_specs=[
                pl.BlockSpec((q_heads * HD, block_len), lambda i, *_: (0, i)),
                pl.BlockSpec((kv_heads, total_rows, HD), lambda i, *_: (0, 0, 0)),
                pl.BlockSpec((kv_heads * HD, total_rows), lambda i, *_: (0, 0)),
                pl.BlockSpec((1, block_len), lambda i, *_: (0, i)),
            ],
            out_specs=[
                pl.BlockSpec((q_heads * HD, block_len), lambda i, *_: (0, i)),
                pl.BlockSpec((q_heads, block_len), lambda i, *_: (0, i)),
                pl.BlockSpec(memory_space=pl.ANY),
            ],
            scratch_shapes=[
                pltpu.VMEM((q_heads * HD, block_len), f32),
                pltpu.VMEM((q_heads, block_len), f32),
                pltpu.VMEM((q_heads, block_len), f32),
                pltpu.VMEM((pages, page_rows, q_heads * HD), bf16),
                pltpu.SemaphoreType.DMA((pages,)),
            ],
        ),
        out_shape=[
            jax.ShapeDtypeStruct((q_heads * HD, total_rows), bf16),
            jax.ShapeDtypeStruct((q_heads, total_rows), f32),
            jax.ShapeDtypeStruct((total_rows // page_rows, page_rows, q_heads * HD), bf16),
        ],
        cost_estimate=pl.CostEstimate(
            flops=q_heads * total_rows * total_rows * HD,
            bytes_accessed=8 * q_t.size,
            transcendentals=q_heads * total_rows * total_rows // 4,
        ),
        name="attend_forward",
    )(first_block, perm, q_t, k_rows, v_t, begin)


def backward_kernel(
    q_heads, kv_heads, page_rows, pages, first_block, perm, *refs
):
    grad_pages = refs[:pages]
    (
        q_t, k_rows, k_t, v_rows, o_t, lse, begin, cos_ref, sin_ref, cos_all, sin_all,
        out, grad_q, grad_k, grad_v, stage, kv_stage, sems, kv_sems,
    ) = refs[pages:]
    i = pl.program_id(0)
    steps = pl.num_programs(0)
    block_len = q_t.shape[1]
    per_group = q_heads // kv_heads
    q_cols = q_heads * HD
    kv_cols = kv_heads * HD

    @pl.when(i == 0)
    def _():
        grad_k[...] = jnp.zeros_like(grad_k)
        grad_v[...] = jnp.zeros_like(grad_v)

    grad_rows = jnp.concatenate([r[0].astype(f32) for r in grad_pages], axis=0)
    grad_t = grad_rows.T
    grad_low = grad_t.astype(bf16)
    inner = [
        jnp.sum(
            grad_t[h * HD : (h + 1) * HD] * o_t[h * HD : (h + 1) * HD, :].astype(f32),
            axis=0,
            keepdims=True,
        )
        for h in range(q_heads)
    ]
    grad_q[...] = jnp.zeros_like(grad_q)
    begin_row = begin[...]

    def visit(j, carry):
        bias = block_bias(i, j, begin_row, block_len)
        at = pl.ds(pl.multiple_of(j * block_len, block_len), block_len)
        for g in range(kv_heads):
            kv_span = slice(g * HD, (g + 1) * HD)
            keys, vals, keys_t = k_rows[g, at, :], v_rows[g, at, :], k_t[kv_span, at]
            add_k = jnp.zeros((HD, block_len), f32)
            add_v = jnp.zeros((HD, block_len), f32)
            for h in range(g * per_group, (g + 1) * per_group):
                span = slice(h * HD, (h + 1) * HD)
                queries = q_t[span, :]
                probs = jnp.exp(dot_nn(keys, queries) + bias - lse[h : h + 1, :])
                grad_h = grad_low[span]
                grad_probs = dot_nn(vals, grad_h)
                grad_scores = (probs * (grad_probs - inner[h])).astype(bf16)
                add_v = add_v + dot_nt(grad_h, probs.astype(bf16))
                add_k = add_k + dot_nt(queries, grad_scores)
                grad_q[span, :] = grad_q[span, :] + dot_nn(keys_t, grad_scores)
            grad_k[kv_span, at] = grad_k[kv_span, at] + add_k
            grad_v[kv_span, at] = grad_v[kv_span, at] + add_v
        return carry

    lax.fori_loop(first_block[i], i + 1, visit, 0)

    def unrope(value, cos, sin):
        first, second = value[:HALF], value[HALF:]
        return jnp.concatenate([first * cos + second * sin, second * cos - first * sin], axis=0)

    cos, sin = cos_ref[...], sin_ref[...]
    parts = [
        unrope(grad_q[h * HD : (h + 1) * HD, :] * score_scale, cos, sin) for h in range(q_heads)
    ]
    stage[...] = jnp.concatenate(parts, axis=0).T.astype(bf16).reshape(pages, page_rows, q_cols)
    copies = [
        pltpu.make_async_copy(
            stage.at[a], out.at[perm[i * pages + a], :, pl.ds(0, q_cols)], sems.at[a]
        )
        for a in range(pages)
    ]
    for copy in copies:
        copy.start()
    for copy in copies:
        copy.wait()

    @pl.when(i == steps - 1)
    def _():
        all_pages = kv_stage.shape[0]
        cos, sin = cos_all[...], sin_all[...]
        parts = [unrope(grad_k[g * HD : (g + 1) * HD, :], cos, sin) for g in range(kv_heads)]
        both = jnp.concatenate(parts + [grad_v[...]], axis=0)
        kv_stage[...] = both.T.astype(bf16).reshape(all_pages, page_rows, 2 * kv_cols)
        copies = [
            pltpu.make_async_copy(
                kv_stage.at[a], out.at[perm[a], :, pl.ds(q_cols, 2 * kv_cols)], kv_sems.at[a]
            )
            for a in range(all_pages)
        ]
        for copy in copies:
            copy.start()
        for copy in copies:
            copy.wait()


def attend_backward(
    grad_slots, q_t, k_rows, k_t, v_rows, o_t, lse, begin, cos_t, sin_t, first_block, perm,
    page_rows, block_len,
):
    total_rows = q_t.shape[1]
    kv_heads = k_rows.shape[0]
    q_heads = q_t.shape[0] // HD
    pages = block_len // page_rows
    all_pages = total_rows // page_rows
    q_cols = q_heads * HD
    kv_cols = kv_heads * HD

    def page_spec(a):
        return pl.BlockSpec(
            (1, page_rows, q_cols),
            lambda i, first_ref, perm_ref, a=a: (perm_ref[i * pages + a], 0, 0),
        )

    def whole(shape):
        return pl.BlockSpec(shape, lambda i, *_: (0,) * len(shape))

    def column(rows):
        return pl.BlockSpec((rows, block_len), lambda i, *_: (0, i))

    return pl.pallas_call(
        functools.partial(backward_kernel, q_heads, kv_heads, page_rows, pages),
        grid_spec=pltpu.PrefetchScalarGridSpec(
            num_scalar_prefetch=2,
            grid=(total_rows // block_len,),
            in_specs=[page_spec(a) for a in range(pages)]
            + [
                column(q_cols),
                whole((kv_heads, total_rows, HD)),
                whole((kv_cols, total_rows)),
                whole((kv_heads, total_rows, HD)),
                column(q_cols),
                column(q_heads),
                column(1),
                column(HALF),
                column(HALF),
                whole((HALF, total_rows)),
                whole((HALF, total_rows)),
            ],
            out_specs=pl.BlockSpec(memory_space=pl.ANY),
            scratch_shapes=[
                pltpu.VMEM((q_cols, block_len), f32),
                pltpu.VMEM((kv_cols, total_rows), f32),
                pltpu.VMEM((kv_cols, total_rows), f32),
                pltpu.VMEM((pages, page_rows, q_cols), bf16),
                pltpu.VMEM((all_pages, page_rows, 2 * kv_cols), bf16),
                pltpu.SemaphoreType.DMA((pages,)),
                pltpu.SemaphoreType.DMA((all_pages,)),
            ],
        ),
        out_shape=jax.ShapeDtypeStruct((all_pages, page_rows, q_cols + 2 * kv_cols), bf16),
        cost_estimate=pl.CostEstimate(
            flops=3 * q_heads * total_rows * total_rows * HD,
            bytes_accessed=12 * q_t.size,
            transcendentals=q_heads * total_rows * total_rows // 4,
        ),
        name="attend_backward",
    )(
        first_block, perm, *([grad_slots] * pages), q_t, k_rows, k_t, v_rows, o_t, lse, begin,
        cos_t, sin_t, cos_t, sin_t,
    )


def feed_kernel(
    ring, tile, own_rows, *refs
):
    grad_rows = refs[:ring]
    (
        weights, grad_all, rows_all, act_all, grads_all, mixed_all, grad_own,
    held, grads_held, acc_n, acc_m, first_part, arrived, outgoing, mixed_stage, final_stage,
    load_sem, keep_sem, grad_sem, mixed_sem, final_sem,
    row_send, row_recv, sum_send, sum_recv, all_sem,
    ) = refs[ring:]
    me = lax.axis_index("tensor")
    right = lax.rem(me + 1, ring)
    left = lax.rem(me + ring - 1, ring)
    hidden = weights.shape[1] // 3
    tiles = hidden // tile

    barrier = pltpu.get_barrier_semaphore()
    for neighbour in (left, right):
        pl.semaphore_signal(barrier, inc=1, device_id={"tensor": neighbour}, device_id_type=MESH)
    pl.semaphore_wait(barrier, 2)

    load = pltpu.make_async_copy(own_rows, held.at[0], load_sem)
    load.start()

    def grad_load(s):
        return pltpu.make_async_copy(grad_rows[s], grads_held.at[s % 2], grad_sem.at[s % 2])

    def grad_keep(s):
        return pltpu.make_async_copy(
            grads_held.at[lax.rem(s, 2)], grad_all.at[s], all_sem.at[lax.rem(s, 2)]
        )

    grad_load(0).start()
    load.wait()

    def pass_rows(s):
        return pltpu.make_async_remote_copy(
            src_ref=held.at[s],
            dst_ref=held.at[s + 1],
            send_sem=row_send.at[s],
            recv_sem=row_recv.at[s],
            device_id={"tensor": right},
            device_id_type=MESH,
        )

    def pass_sum(s):
        return pltpu.make_async_remote_copy(
            src_ref=outgoing.at[s - 1],
            dst_ref=arrived.at[s - 1],
            send_sem=sum_send.at[s - 1],
            recv_sem=sum_recv.at[s - 1],
            device_id={"tensor": right},
            device_id_type=MESH,
        )

    def keep(s):
        return pltpu.make_async_copy(held.at[s], rows_all.at[s], keep_sem.at[s])

    def mixed_store(s):
        return pltpu.make_async_copy(mixed_stage, mixed_all.at[s], mixed_sem)

    def chunk(s, carry):
        @pl.when(s > 0)
        def _():
            pass_rows(s - 1).wait_recv()

        @pl.when(s < ring - 1)
        def _():
            pass_rows(s).start()

        keep(s).start()

        @pl.when(s > 0)
        def _():
            grad_keep(s - 1).wait()

        for k in range(ring):

            @pl.when(s == k)
            def _(k=k):
                grad_load(k).wait()
                if k < ring - 1:
                    grad_load(k + 1).start()

        grad_keep(s).start()
        slot = lax.rem(s, 2)
        acc_n[...] = jnp.zeros_like(acc_n)
        acc_m[...] = jnp.zeros_like(acc_m)

        def body(w_gate, w_up, w_down, act, grad_gate, grad_up):
            rows = held[s]
            gate = dot_nn(rows, w_gate[...])
            up = dot_nn(rows, w_up[...])
            grad_act = dot_nn(grads_held[slot], w_down[...])
            sig = 1.0 / (1.0 + jnp.exp(-gate))
            silu = gate * sig
            low_act = (silu * up).astype(bf16)
            low_up = (grad_act * silu).astype(bf16)
            low_gate = (grad_act * up * sig * (1.0 + gate * (1.0 - sig))).astype(bf16)
            act[...] = low_act
            grad_gate[...] = low_gate
            grad_up[...] = low_up
            acc_m[...] += dot_nt(low_act, w_down[...])
            acc_n[...] += dot_nt(low_gate, w_gate[...]) + dot_nt(low_up, w_up[...])

        width, count = own_rows.shape[1], own_rows.shape[0]
        pltpu.emit_pipeline(
            body,
            grid=(tiles,),
            in_specs=[
                pl.BlockSpec((width, tile), lambda k: (0, k)),
                pl.BlockSpec((width, tile), lambda k: (0, k + tiles)),
                pl.BlockSpec((width, tile), lambda k: (0, k + 2 * tiles)),
            ],
            out_specs=[
                pl.BlockSpec((count, tile), lambda k: (0, k)),
                pl.BlockSpec((count, tile), lambda k: (0, k)),
                pl.BlockSpec((count, tile), lambda k: (0, k + tiles)),
            ],
        )(weights, weights, weights, act_all.at[s], grads_all.at[s], grads_all.at[s])

        @pl.when(s > 0)
        def _():
            mixed_store(s - 1).wait()

        mixed_stage[...] = acc_m[...].astype(bf16)
        mixed_store(s).start()

        @pl.when(s == 0)
        def _():
            first_part[...] = acc_n[...]

        @pl.when(s == 1)
        def _():
            outgoing[0] = acc_n[...].astype(bf16)

        @pl.when(s > 1)
        def _():
            pass_sum(s - 1).wait_recv()
            outgoing[s - 1] = (acc_n[...] + arrived[s - 2].astype(f32)).astype(bf16)

        @pl.when(s > 0)
        def _():
            pass_sum(s).start()

        return carry

    lax.fori_loop(0, ring, chunk, 0)
    mixed_store(ring - 1).wait()
    pass_sum(ring - 1).wait_recv()
    final_stage[...] = (first_part[...] + arrived[ring - 2].astype(f32)).astype(bf16)
    final = pltpu.make_async_copy(final_stage, grad_own, final_sem)
    final.start()

    def settle(s, carry):
        keep(s).wait()

        @pl.when(s < ring - 1)
        def _():
            pass_rows(s).wait_send()

        @pl.when(s > 0)
        def _():
            pass_sum(s).wait_send()

        return carry

    lax.fori_loop(0, ring, settle, 0)
    grad_keep(ring - 1).wait()
    final.wait()


def feed(own_rows, grad_rows, weights, ring, tile=256, collective_id=7):
    count, width = own_rows.shape
    hidden = weights.shape[1] // 3
    any_spec = pl.BlockSpec(memory_space=pl.ANY)
    dma = pltpu.SemaphoreType.DMA
    return pl.pallas_call(
        functools.partial(feed_kernel, ring, min(tile, hidden)),
        out_shape=[
            jax.ShapeDtypeStruct((ring, count, width), bf16),
            jax.ShapeDtypeStruct((ring, count, width), bf16),
            jax.ShapeDtypeStruct((ring, count, hidden), bf16),
            jax.ShapeDtypeStruct((ring, count, 2 * hidden), bf16),
            jax.ShapeDtypeStruct((ring, count, width), bf16),
            jax.ShapeDtypeStruct((count, width), bf16),
        ],
        in_specs=[any_spec] * (2 + ring),
        out_specs=[any_spec] * 6,
        scratch_shapes=[
            pltpu.VMEM((ring, count, width), bf16),
            pltpu.VMEM((2, count, width), bf16),
            pltpu.VMEM((count, width), f32),
            pltpu.VMEM((count, width), f32),
            pltpu.VMEM((count, width), f32),
            pltpu.VMEM((ring - 1, count, width), bf16),
            pltpu.VMEM((ring - 1, count, width), bf16),
            pltpu.VMEM((count, width), bf16),
            pltpu.VMEM((count, width), bf16),
            dma,
            dma((ring,)),
            dma((2,)),
            dma,
            dma,
            dma((ring - 1,)),
            dma((ring - 1,)),
            dma((ring - 1,)),
            dma((ring - 1,)),
            dma((2,)),
        ],
        compiler_params=pltpu.CompilerParams(
            collective_id=collective_id, has_side_effects=True, vmem_limit_bytes=64 * 1024 * 1024 - 65536,
        ),
        cost_estimate=pl.CostEstimate(
            flops=12 * ring * count * width * hidden,
            bytes_accessed=8 * ring * count * width,
            transcendentals=ring * count * hidden,
        ),
        name="feed_forward",
    )(own_rows, *grad_rows, weights)


def spread_kernel(rows, weight, out):
    out[0] = dot_nn(rows[...], weight[0]).astype(out.dtype)


def spread(rows, weights, part, cols):
    shards, width, _ = weights.shape
    count = rows.shape[0]
    return pl.pallas_call(
        spread_kernel,
        grid=(shards,),
        in_specs=[
            pl.BlockSpec((count, width), lambda t: (0, 0)),
            pl.BlockSpec((1, width, cols), lambda t: (t, 0, part)),
        ],
        out_specs=pl.BlockSpec((1, count, cols), lambda t: (t, 0, 0)),
        out_shape=jax.ShapeDtypeStruct((shards, count, cols), bf16),
        cost_estimate=pl.CostEstimate(
            flops=2 * shards * count * width * cols,
            bytes_accessed=2 * shards * width * cols,
            transcendentals=0,
        ),
        name="spread",
    )(rows, weights)


def gather_kernel(part, weight, begin, out):
    @pl.when(pl.program_id(0) == 0)
    def _():
        out[...] = begin[...]

    out[...] += dot_nt(part[0], weight[0])


def gather_sum(parts, weights, part, begin):
    shards, count, cols = parts.shape
    width = weights.shape[1]
    return pl.pallas_call(
        gather_kernel,
        grid=(shards,),
        in_specs=[
            pl.BlockSpec((1, count, cols), lambda t: (t, 0, 0)),
            pl.BlockSpec((1, width, cols), lambda t: (t, 0, part)),
            pl.BlockSpec((count, width), lambda t: (0, 0)),
        ],
        out_specs=pl.BlockSpec((count, width), lambda t: (0, 0)),
        out_shape=jax.ShapeDtypeStruct((count, width), f32),
        cost_estimate=pl.CostEstimate(
            flops=2 * shards * count * width * cols,
            bytes_accessed=2 * shards * width * cols,
            transcendentals=0,
        ),
        name="gather_sum",
    )(parts, weights, begin)


def outer_kernel(rows, part, out, turned):
    @pl.when(pl.program_id(0) == 0)
    def _():
        turned[...] = rows[...].T

    out[...] = dot_nn(turned[...], part[0]).astype(out.dtype)


def outer(rows, parts):
    shards, count, cols = parts.shape
    width = rows.shape[1]
    return pl.pallas_call(
        outer_kernel,
        grid=(shards,),
        in_specs=[
            pl.BlockSpec((count, width), lambda t: (0, 0)),
            pl.BlockSpec((1, count, cols), lambda t: (t, 0, 0)),
        ],
        out_specs=pl.BlockSpec((width, cols), lambda t: (0, t)),
        out_shape=jax.ShapeDtypeStruct((width, shards * cols), bf16),
        scratch_shapes=[pltpu.VMEM((width, count), bf16)],
        cost_estimate=pl.CostEstimate(
            flops=2 * shards * count * width * cols,
            bytes_accessed=2 * shards * width * cols,
            transcendentals=0,
        ),
        name="outer",
    )(rows, parts)


def rms_scale(hidden):
    return lax.rsqrt(jnp.mean(hidden * hidden, axis=1, keepdims=True) + epsilon)


def norm_back(grad_norm, hidden, scale_rows, gain):
    normed = hidden * scale_rows
    gain_part = jnp.sum(grad_norm * normed, axis=0)
    inner = grad_norm * gain
    grad_hidden = scale_rows * (inner - normed * jnp.mean(inner * normed, axis=1, keepdims=True))
    return (grad_hidden, gain_part)


def after(value, other):
    return lax.optimization_barrier((value, other))[0]


def local(
    tokens,
    upstream,
    lengths,
    positions,
    pages,
    attn_gain,
    w_query,
    w_key,
    w_value,
    w_out,
    mlp_gain,
    w_gate,
    w_up,
    w_down,
):
    dp_count = lax.axis_size("dp")
    tp_count = lax.axis_size("tensor")
    dp_index = lax.axis_index("dp")
    tp_index = lax.axis_index("tensor")
    tok_dev, width = tokens.shape
    tok_group = tok_dev * tp_count
    page_rows = tok_dev // dp_count
    group_pages = tp_count * dp_count
    page_count = pages.shape[0]
    device = dp_index * tp_count + tp_index
    everyone = ("tensor", "dp")

    local_ids = jnp.arange(dp_count, dtype=jnp.int32)
    inverse = (
        jnp.zeros((page_count,), jnp.int32).at[pages].set(jnp.arange(page_count, dtype=jnp.int32))
    )
    dealt = lax.dynamic_slice_in_dim(inverse, device * dp_count, dp_count)
    dest_group = dealt // group_pages
    send_order = jnp.zeros((dp_count,), jnp.int32).at[dest_group].set(local_ids)
    group_sources = lax.dynamic_slice_in_dim(pages, dp_index * group_pages, group_pages)
    perm = (
        (jnp.arange(group_pages, dtype=jnp.int32) // dp_count) * dp_count
        + group_sources // group_pages
    ).astype(jnp.int32)

    def reorder(rows, order):
        blocks = rows.reshape(dp_count, page_rows, rows.shape[1])
        return jnp.take(blocks, order, axis=0).reshape(rows.shape)

    hidden_in = reorder(tokens, send_order).astype(f32)
    grad_top = reorder(upstream, send_order).astype(f32)
    seq_lens = lengths[0]
    seq_ends = jnp.cumsum(seq_lens)
    place = (jnp.take(dealt, send_order) % group_pages) * page_rows
    place_rows = (place[:, None] + jnp.arange(page_rows, dtype=jnp.int32)[None, :]).reshape(-1)
    valid_rows = (place_rows < seq_ends[-1]).astype(f32)[:, None]

    row_ids = jnp.arange(tok_group, dtype=jnp.int32)
    begin = jnp.max(
        jnp.where(row_ids[:, None] >= seq_ends[None, :], seq_ends[None, :], 0), axis=1
    ).astype(jnp.int32)
    block_len = min(block_rows, tok_group)
    first_block = begin[::block_len] // block_len
    begin = begin[None, :]
    inverse_freq = theta_base ** (-(jnp.arange(HALF, dtype=f32) * 2.0) / HD)
    angles = inverse_freq[:, None] * positions.astype(f32)
    cos_t, sin_t = jnp.cos(angles), jnp.sin(angles)

    q_cols, kv_cols = w_query.shape[1], w_key.shape[1]
    kv_heads = kv_cols // HD
    per_group = q_cols // kv_cols
    group_q = per_group * HD
    groups = range(kv_heads)
    qkv_shards = [
        jnp.concatenate(
            [
                w_query[:, g * group_q : (g + 1) * group_q],
                w_key[:, g * HD : (g + 1) * HD],
                w_value[:, g * HD : (g + 1) * HD],
            ],
            axis=1,
        )
        for g in groups
    ]

    def gather_all(shard):
        full = lax.all_gather(shard, everyone, axis=0, tiled=False)
        return full.reshape(tp_count, dp_count * shard.shape[0], shard.shape[1])

    def trade(value):
        blocks = value.reshape(group_pages, page_rows, value.shape[-1])
        return lax.all_to_all(blocks, everyone, split_axis=0, concat_axis=0, tiled=True)

    def trade_back(value):
        return trade(value).reshape(tp_count, tok_dev, value.shape[-1])

    ring_next = [(t, (t + 1) % tp_count) for t in range(tp_count)]

    def pass_on(value):
        return lax.ppermute(value, "tensor", ring_next)

    gains = lax.all_gather(jnp.stack([attn_gain, mlp_gain]), "dp", axis=1, tiled=True)
    gain_one, gain_two = gains[0].astype(f32), gains[1].astype(f32)

    grad_out = grad_top * valid_rows
    grad_chunks = [grad_out.astype(bf16)]
    for _ in range(tp_count - 1):
        grad_chunks.append(pass_on(grad_chunks[-1]))

    scale_one = rms_scale(hidden_in)
    normed_one = (hidden_in * scale_one * gain_one).astype(bf16)
    w_qkv, qkv, slots = [], [], []
    for g in groups:
        if g == 0:
            w_qkv.append(gather_all(qkv_shards[g]))
            weight = after(w_qkv[g], grad_chunks[1])
        else:
            w_qkv.append(gather_all(after(qkv_shards[g], qkv[-1])))
            weight = after(w_qkv[g], slots[-1])
        qkv.append(spread(normed_one, weight, 0, group_q + 2 * HD))
        slots.append(trade(qkv[g]))
    out_shard = with_layout_constraint(w_out.T, Layout(major_to_minor=(0, 1)))
    w_out_t = gather_all(after(out_shard, qkv[-1]))
    mlp_shard = jnp.concatenate([w_gate, w_up, w_down.T], axis=1)
    saved, mixed = [], []
    last = qkv[-1]
    for g in groups:
        q_t, k_t, k_rows, v_t, v_rows = prepare(
            after(slots[g], last), perm, cos_t, sin_t, per_group, 1
        )
        if g == 0:
            w_mlp = lax.all_gather(after(mlp_shard, q_t), "dp", axis=0, tiled=True)
        o_t, lse, last = attend_forward(
            q_t, k_rows, v_t, begin, first_block, perm, page_rows, block_len
        )
        saved.append((q_t, k_rows, k_t, v_rows, o_t, lse))
        mixed.append(trade_back(last))
    hidden_mid = hidden_in
    for g in groups:
        hidden_mid = gather_sum(mixed[g], w_out_t, g, hidden_mid)

    scale_two = rms_scale(hidden_mid)
    normed_two = (hidden_mid * scale_two * gain_two).astype(bf16)
    grad_mlp, mlp_rows, inner_act, grad_gate_up, partial_two, grad_normed_two = feed(
        normed_two, grad_chunks, w_mlp, tp_count
    )
    grad_normed_two = grad_normed_two.astype(f32)
    grad_mid_norm, gain_two_part = norm_back(grad_normed_two, hidden_mid, scale_two, gain_two)
    grad_mid = grad_out + grad_mid_norm
    branch_two = partial_two[1]
    for s in range(2, tp_count):
        branch_two = (pass_on(branch_two).astype(f32) + partial_two[s].astype(f32)).astype(bf16)
    branch_two = pass_on(branch_two)

    def reduce_dp(grad):
        return lax.psum_scatter(grad.astype(bf16), "dp", scatter_dimension=0, tiled=True)

    def reduce_tensor(value):
        cols = value.shape[1] // tp_count
        total = lax.dynamic_slice_in_dim(value, tp_index * cols, cols, 1).astype(f32)
        for s in range(1, tp_count):
            target = lax.rem(tp_index + s, tp_count)
            block = lax.dynamic_slice_in_dim(value, target * cols, cols, 1)
            pairs = [(t, (t + s) % tp_count) for t in range(tp_count)]
            total = total + lax.ppermute(block, "tensor", pairs).astype(f32)
        return total

    def flat(value):
        return value.reshape(tok_group, value.shape[-1])

    grad_down_t = dot_tn(flat(grad_mlp), flat(inner_act)).astype(bf16)
    sum_down = reduce_dp(grad_down_t)
    grad_gate_up = dot_tn(flat(mlp_rows), flat(after(grad_gate_up, grad_down_t))).astype(bf16)
    sum_gate_up = reduce_dp(grad_gate_up)
    grad_z = after(grad_mid.astype(bf16), grad_gate_up)
    grad_slots = [trade(spread(grad_z, w_out_t, g, group_q)) for g in groups]
    grad_qkv = []
    last = grad_z
    for g in groups:
        q_t, k_rows, k_t, v_rows, o_t, lse = saved[g]
        back = attend_backward(
            after(grad_slots[g], last), q_t, k_rows, k_t, v_rows, o_t, lse, begin, cos_t, sin_t,
            first_block, perm, page_rows, block_len,
        )
        grad_qkv.append(trade_back(back))
        last = (back, sum_down)
    grad_wout = outer(after(grad_z, back), jnp.concatenate(mixed, axis=2))
    sum_out = reduce_dp(grad_wout)
    normed_late = after(normed_one, (sum_gate_up, grad_wout))
    hidden = sum_gate_up.shape[1] // 2
    grad_wqkv = outer(normed_late, jnp.concatenate(grad_qkv, axis=2))
    sum_qkv = reduce_tensor(reduce_dp(grad_wqkv))
    grad_normed_one = jnp.zeros((tok_dev, width), f32)
    for g in groups:
        grad_normed_one = gather_sum(grad_qkv[g], w_qkv[g], 0, grad_normed_one)
    sum_out = reduce_tensor(sum_out)
    each = group_q + 2 * HD
    sum_qkv = [sum_qkv[:, g * each : (g + 1) * each] for g in groups]
    result = (
        (after(hidden_mid, back) + branch_two.astype(f32) + partial_two[0].astype(f32)) * valid_rows
    ).astype(bf16)
    grad_in_norm, gain_one_part = norm_back(grad_normed_one, hidden_in, scale_one, gain_one)
    grad_in = (grad_mid + grad_in_norm).astype(bf16)

    gain_sums = lax.psum(jnp.stack([gain_one_part, gain_two_part]), everyone)
    gain_shard = attn_gain.shape[0]
    gain_sums = lax.dynamic_slice_in_dim(gain_sums, dp_index * gain_shard, gain_shard, 1)
    return (
        reorder(result, dest_group),
        reorder(grad_in, dest_group),
        gain_sums[0],
        jnp.concatenate([part[:, :group_q] for part in sum_qkv], axis=1),
        jnp.concatenate([part[:, group_q : group_q + HD] for part in sum_qkv], axis=1),
        jnp.concatenate([part[:, group_q + HD :] for part in sum_qkv], axis=1),
        sum_out.T,
        gain_sums[1],
        sum_gate_up[:, :hidden].astype(f32),
        sum_gate_up[:, hidden:].astype(f32),
        sum_down.astype(f32).T,
    )


def solution(mesh):
    rows = P(("dp", "tensor"), None)
    weight = P("dp", "tensor")
    weight_t = P("tensor", "dp")
    return jax.shard_map(
        local,
        mesh=mesh,
        in_specs=(
            rows,
            rows,
            P("dp", None),
            P("dp", None),
            P(),
            P("dp"),
            weight,
            weight,
            weight,
            weight_t,
            P("dp"),
            weight,
            weight,
            weight_t,
        ),
        out_specs=(
            rows,
            rows,
            P("dp"),
            weight,
            weight,
            weight,
            weight_t,
            P("dp"),
            weight,
            weight,
            weight_t,
        ),
        check_vma=False,
    )
```

```python
import functools

import jax
import jax.numpy as jnp
from jax import lax
from jax.experimental import pallas as pl
from jax.experimental.layout import Layout, with_layout_constraint
from jax.experimental.pallas import tpu as pltpu
from jax.sharding import PartitionSpec as P

HD = 64
HALF = HD // 2

epsilon = 1e-05
theta_base = 500000.0
masked_score = -1e30
score_scale = HD**-0.5
block_rows = 256
MESH = pl.DeviceIdType.MESH
f32 = jnp.float32
bf16 = jnp.bfloat16


def dot_nn(left, right):
    return lax.dot_general(left, right, (((1,), (0,)), ((), ())), preferred_element_type=f32)


def dot_nt(left, right):
    return lax.dot_general(left, right, (((1,), (1,)), ((), ())), preferred_element_type=f32)


def dot_tn(left, right):
    return lax.dot_general(left, right, (((0,), (0,)), ((), ())), preferred_element_type=f32)


def prep_kernel(pages_per, q_heads, kv_heads, perm, *refs):
    page_refs = refs[:pages_per]
    cos_ref, sin_ref, q_t, k_t, k_rows, v_t, v_rows = refs[pages_per:]
    rows = jnp.concatenate([r[0].astype(f32) for r in page_refs], axis=0)
    turned = rows.T
    cos, sin = cos_ref[...], sin_ref[...]

    def rope(base):
        first, second = turned[base : base + HALF], turned[base + HALF : base + HD]
        return jnp.concatenate([first * cos - second * sin, second * cos + first * sin], axis=0)

    for h in range(q_heads):
        roped = rope(h * HD).astype(bf16)
        q_t[h * HD : (h + 1) * HD, :] = (roped.astype(f32) * score_scale).astype(bf16)
    k_base = q_heads * HD
    v_base = k_base + kv_heads * HD
    for g in range(kv_heads):
        roped = rope(k_base + g * HD)
        k_t[g * HD : (g + 1) * HD, :] = roped.astype(bf16)
        k_rows[g] = roped.T.astype(bf16)
        v_t[g * HD : (g + 1) * HD, :] = turned[v_base + g * HD : v_base + (g + 1) * HD].astype(bf16)
        v_rows[g] = rows[:, v_base + g * HD : v_base + (g + 1) * HD].astype(bf16)


def prepare(slots, perm, cos_t, sin_t, q_heads, kv_heads):
    page_rows, cols = slots.shape[1:]
    total_rows = slots.shape[0] * page_rows
    lanes = 128
    pages_per = lanes // page_rows

    def page_spec(a):
        return pl.BlockSpec(
            (1, page_rows, cols), lambda i, perm_ref, a=a: (perm_ref[i * pages_per + a], 0, 0)
        )

    table = pl.BlockSpec((HALF, lanes), lambda i, perm_ref: (0, i))
    return pl.pallas_call(
        functools.partial(prep_kernel, pages_per, q_heads, kv_heads),
        grid_spec=pltpu.PrefetchScalarGridSpec(
            num_scalar_prefetch=1,
            grid=(total_rows // lanes,),
            in_specs=[page_spec(a) for a in range(pages_per)] + [table, table],
            out_specs=[
                pl.BlockSpec((q_heads * HD, lanes), lambda i, perm_ref: (0, i)),
                pl.BlockSpec((kv_heads * HD, lanes), lambda i, perm_ref: (0, i)),
                pl.BlockSpec((kv_heads, lanes, HD), lambda i, perm_ref: (0, i, 0)),
                pl.BlockSpec((kv_heads * HD, lanes), lambda i, perm_ref: (0, i)),
                pl.BlockSpec((kv_heads, lanes, HD), lambda i, perm_ref: (0, i, 0)),
            ],
        ),
        out_shape=[
            jax.ShapeDtypeStruct((q_heads * HD, total_rows), bf16),
            jax.ShapeDtypeStruct((kv_heads * HD, total_rows), bf16),
            jax.ShapeDtypeStruct((kv_heads, total_rows, HD), bf16),
            jax.ShapeDtypeStruct((kv_heads * HD, total_rows), bf16),
            jax.ShapeDtypeStruct((kv_heads, total_rows, HD), bf16),
        ],
        cost_estimate=pl.CostEstimate(
            flops=8 * slots.size, bytes_accessed=6 * slots.size, transcendentals=0
        ),
        name="prepare",
    )(perm, *([slots] * pages_per), cos_t, sin_t)


def block_bias(i, j, begin_row, block_len):
    keys = j * block_len + lax.broadcasted_iota(jnp.int32, (block_len, block_len), 0)
    queries = i * block_len + lax.broadcasted_iota(jnp.int32, (block_len, block_len), 1)
    allowed = (keys >= begin_row) & (keys <= queries)
    return jnp.where(allowed, 0.0, masked_score)


def forward_kernel(
    q_heads, kv_heads, page_rows, first_block, perm,
    q_t, k_rows, v_t, begin, o_t, lse, o_slots, acc, top, total, stage, sems,
):
    i = pl.program_id(0)
    block_len = q_t.shape[1]
    per_group = q_heads // kv_heads
    acc[...] = jnp.zeros_like(acc)
    top[...] = jnp.full_like(top, masked_score)
    total[...] = jnp.zeros_like(total)
    begin_row = begin[...]

    def visit(j, carry):
        bias = block_bias(i, j, begin_row, block_len)
        at = pl.ds(pl.multiple_of(j * block_len, block_len), block_len)
        for h in range(q_heads):
            g = h // per_group
            span = slice(h * HD, (h + 1) * HD)
            scores = dot_nn(k_rows[g, at, :], q_t[span, :]) + bias
            old = top[h : h + 1, :]
            new = jnp.maximum(old, jnp.max(scores, axis=0, keepdims=True))
            weights = jnp.exp(scores - new)
            fade = jnp.exp(old - new)
            total[h : h + 1, :] = total[h : h + 1, :] * fade + jnp.sum(
                weights, axis=0, keepdims=True
            )
            top[h : h + 1, :] = new
            acc[span, :] = acc[span, :] * fade + dot_nn(
                v_t[g * HD : (g + 1) * HD, at], weights.astype(bf16)
            )
        return carry

    lax.fori_loop(first_block[i], i + 1, visit, 0)
    lse[...] = top[...] + jnp.log(total[...])
    scaled = [
        acc[h * HD : (h + 1) * HD, :] / total[h : h + 1, :] for h in range(q_heads)
    ]
    mixed = jnp.concatenate(scaled, axis=0)
    o_t[...] = mixed.astype(bf16)
    pages = block_len // page_rows
    stage[...] = mixed.T.astype(bf16).reshape(pages, page_rows, q_heads * HD)
    copies = [
        pltpu.make_async_copy(stage.at[a], o_slots.at[perm[i * pages + a]], sems.at[a])
        for a in range(pages)
    ]
    for copy in copies:
        copy.start()
    for copy in copies:
        copy.wait()


def attend_forward(q_t, k_rows, v_t, begin, first_block, perm, page_rows, block_len):
    total_rows = q_t.shape[1]
    kv_heads = k_rows.shape[0]
    q_heads = q_t.shape[0] // HD
    pages = block_len // page_rows
    return pl.pallas_call(
        functools.partial(forward_kernel, q_heads, kv_heads, page_rows),
        grid_spec=pltpu.PrefetchScalarGridSpec(
            num_scalar_prefetch=2,
            grid=(total_rows // block_len,),
            in_specs=[
                pl.BlockSpec((q_heads * HD, block_len), lambda i, *_: (0, i)),
                pl.BlockSpec((kv_heads, total_rows, HD), lambda i, *_: (0, 0, 0)),
                pl.BlockSpec((kv_heads * HD, total_rows), lambda i, *_: (0, 0)),
                pl.BlockSpec((1, block_len), lambda i, *_: (0, i)),
            ],
            out_specs=[
                pl.BlockSpec((q_heads * HD, block_len), lambda i, *_: (0, i)),
                pl.BlockSpec((q_heads, block_len), lambda i, *_: (0, i)),
                pl.BlockSpec(memory_space=pl.ANY),
            ],
            scratch_shapes=[
                pltpu.VMEM((q_heads * HD, block_len), f32),
                pltpu.VMEM((q_heads, block_len), f32),
                pltpu.VMEM((q_heads, block_len), f32),
                pltpu.VMEM((pages, page_rows, q_heads * HD), bf16),
                pltpu.SemaphoreType.DMA((pages,)),
            ],
        ),
        out_shape=[
            jax.ShapeDtypeStruct((q_heads * HD, total_rows), bf16),
            jax.ShapeDtypeStruct((q_heads, total_rows), f32),
            jax.ShapeDtypeStruct((total_rows // page_rows, page_rows, q_heads * HD), bf16),
        ],
        cost_estimate=pl.CostEstimate(
            flops=q_heads * total_rows * total_rows * HD,
            bytes_accessed=8 * q_t.size,
            transcendentals=q_heads * total_rows * total_rows // 4,
        ),
        name="attend_forward",
    )(first_block, perm, q_t, k_rows, v_t, begin)


def backward_kernel(
    q_heads, kv_heads, page_rows, pages, first_block, perm, *refs
):
    grad_pages = refs[:pages]
    (
        q_t, k_rows, k_t, v_rows, o_t, lse, begin, cos_ref, sin_ref, cos_all, sin_all,
        out, grad_q, grad_k, grad_v, stage, kv_stage, sems, kv_sems,
    ) = refs[pages:]
    i = pl.program_id(0)
    steps = pl.num_programs(0)
    block_len = q_t.shape[1]
    per_group = q_heads // kv_heads
    q_cols = q_heads * HD
    kv_cols = kv_heads * HD

    @pl.when(i == 0)
    def _():
        grad_k[...] = jnp.zeros_like(grad_k)
        grad_v[...] = jnp.zeros_like(grad_v)

    grad_rows = jnp.concatenate([r[0].astype(f32) for r in grad_pages], axis=0)
    grad_t = grad_rows.T
    grad_low = grad_t.astype(bf16)
    inner = [
        jnp.sum(
            grad_t[h * HD : (h + 1) * HD] * o_t[h * HD : (h + 1) * HD, :].astype(f32),
            axis=0,
            keepdims=True,
        )
        for h in range(q_heads)
    ]
    grad_q[...] = jnp.zeros_like(grad_q)
    begin_row = begin[...]

    def visit(j, carry):
        bias = block_bias(i, j, begin_row, block_len)
        at = pl.ds(pl.multiple_of(j * block_len, block_len), block_len)
        for g in range(kv_heads):
            kv_span = slice(g * HD, (g + 1) * HD)
            keys, vals, keys_t = k_rows[g, at, :], v_rows[g, at, :], k_t[kv_span, at]
            add_k = jnp.zeros((HD, block_len), f32)
            add_v = jnp.zeros((HD, block_len), f32)
            for h in range(g * per_group, (g + 1) * per_group):
                span = slice(h * HD, (h + 1) * HD)
                queries = q_t[span, :]
                probs = jnp.exp(dot_nn(keys, queries) + bias - lse[h : h + 1, :])
                grad_h = grad_low[span]
                grad_probs = dot_nn(vals, grad_h)
                grad_scores = (probs * (grad_probs - inner[h])).astype(bf16)
                add_v = add_v + dot_nt(grad_h, probs.astype(bf16))
                add_k = add_k + dot_nt(queries, grad_scores)
                grad_q[span, :] = grad_q[span, :] + dot_nn(keys_t, grad_scores)
            grad_k[kv_span, at] = grad_k[kv_span, at] + add_k
            grad_v[kv_span, at] = grad_v[kv_span, at] + add_v
        return carry

    lax.fori_loop(first_block[i], i + 1, visit, 0)

    def unrope(value, cos, sin):
        first, second = value[:HALF], value[HALF:]
        return jnp.concatenate([first * cos + second * sin, second * cos - first * sin], axis=0)

    cos, sin = cos_ref[...], sin_ref[...]
    parts = [
        unrope(grad_q[h * HD : (h + 1) * HD, :] * score_scale, cos, sin) for h in range(q_heads)
    ]
    stage[...] = jnp.concatenate(parts, axis=0).T.astype(bf16).reshape(pages, page_rows, q_cols)
    copies = [
        pltpu.make_async_copy(
            stage.at[a], out.at[perm[i * pages + a], :, pl.ds(0, q_cols)], sems.at[a]
        )
        for a in range(pages)
    ]
    for copy in copies:
        copy.start()
    for copy in copies:
        copy.wait()

    @pl.when(i == steps - 1)
    def _():
        all_pages = kv_stage.shape[0]
        cos, sin = cos_all[...], sin_all[...]
        parts = [unrope(grad_k[g * HD : (g + 1) * HD, :], cos, sin) for g in range(kv_heads)]
        both = jnp.concatenate(parts + [grad_v[...]], axis=0)
        kv_stage[...] = both.T.astype(bf16).reshape(all_pages, page_rows, 2 * kv_cols)
        copies = [
            pltpu.make_async_copy(
                kv_stage.at[a], out.at[perm[a], :, pl.ds(q_cols, 2 * kv_cols)], kv_sems.at[a]
            )
            for a in range(all_pages)
        ]
        for copy in copies:
            copy.start()
        for copy in copies:
            copy.wait()


def attend_backward(
    grad_slots, q_t, k_rows, k_t, v_rows, o_t, lse, begin, cos_t, sin_t, first_block, perm,
    page_rows, block_len,
):
    total_rows = q_t.shape[1]
    kv_heads = k_rows.shape[0]
    q_heads = q_t.shape[0] // HD
    pages = block_len // page_rows
    all_pages = total_rows // page_rows
    q_cols = q_heads * HD
    kv_cols = kv_heads * HD

    def page_spec(a):
        return pl.BlockSpec(
            (1, page_rows, q_cols),
            lambda i, first_ref, perm_ref, a=a: (perm_ref[i * pages + a], 0, 0),
        )

    def whole(shape):
        return pl.BlockSpec(shape, lambda i, *_: (0,) * len(shape))

    def column(rows):
        return pl.BlockSpec((rows, block_len), lambda i, *_: (0, i))

    return pl.pallas_call(
        functools.partial(backward_kernel, q_heads, kv_heads, page_rows, pages),
        grid_spec=pltpu.PrefetchScalarGridSpec(
            num_scalar_prefetch=2,
            grid=(total_rows // block_len,),
            in_specs=[page_spec(a) for a in range(pages)]
            + [
                column(q_cols),
                whole((kv_heads, total_rows, HD)),
                whole((kv_cols, total_rows)),
                whole((kv_heads, total_rows, HD)),
                column(q_cols),
                column(q_heads),
                column(1),
                column(HALF),
                column(HALF),
                whole((HALF, total_rows)),
                whole((HALF, total_rows)),
            ],
            out_specs=pl.BlockSpec(memory_space=pl.ANY),
            scratch_shapes=[
                pltpu.VMEM((q_cols, block_len), f32),
                pltpu.VMEM((kv_cols, total_rows), f32),
                pltpu.VMEM((kv_cols, total_rows), f32),
                pltpu.VMEM((pages, page_rows, q_cols), bf16),
                pltpu.VMEM((all_pages, page_rows, 2 * kv_cols), bf16),
                pltpu.SemaphoreType.DMA((pages,)),
                pltpu.SemaphoreType.DMA((all_pages,)),
            ],
        ),
        out_shape=jax.ShapeDtypeStruct((all_pages, page_rows, q_cols + 2 * kv_cols), bf16),
        cost_estimate=pl.CostEstimate(
            flops=3 * q_heads * total_rows * total_rows * HD,
            bytes_accessed=12 * q_t.size,
            transcendentals=q_heads * total_rows * total_rows // 4,
        ),
        name="attend_backward",
    )(
        first_block, perm, *([grad_slots] * pages), q_t, k_rows, k_t, v_rows, o_t, lse, begin,
        cos_t, sin_t, cos_t, sin_t,
    )


def feed_kernel(
    ring, tile, own_rows, *refs
):
    grad_rows = refs[:ring]
    (
        weights, grad_all, rows_all, act_all, grads_all, mixed_all, grad_own,
    held, grads_held, acc_n, acc_m, first_part, arrived, outgoing, mixed_stage, final_stage,
    load_sem, keep_sem, grad_sem, mixed_sem, final_sem,
    row_send, row_recv, sum_send, sum_recv, all_sem,
    ) = refs[ring:]
    me = lax.axis_index("tensor")
    right = lax.rem(me + 1, ring)
    left = lax.rem(me + ring - 1, ring)
    hidden = weights.shape[1] // 3
    tiles = hidden // tile

    barrier = pltpu.get_barrier_semaphore()
    for neighbour in (left, right):
        pl.semaphore_signal(barrier, inc=1, device_id={"tensor": neighbour}, device_id_type=MESH)
    pl.semaphore_wait(barrier, 2)

    load = pltpu.make_async_copy(own_rows, held.at[0], load_sem)
    load.start()

    def grad_load(s):
        return pltpu.make_async_copy(grad_rows[s], grads_held.at[s % 2], grad_sem.at[s % 2])

    def grad_keep(s):
        return pltpu.make_async_copy(
            grads_held.at[lax.rem(s, 2)], grad_all.at[s], all_sem.at[lax.rem(s, 2)]
        )

    grad_load(0).start()
    load.wait()

    def pass_rows(s):
        return pltpu.make_async_remote_copy(
            src_ref=held.at[s],
            dst_ref=held.at[s + 1],
            send_sem=row_send.at[s],
            recv_sem=row_recv.at[s],
            device_id={"tensor": right},
            device_id_type=MESH,
        )

    def pass_sum(s):
        return pltpu.make_async_remote_copy(
            src_ref=outgoing.at[s - 1],
            dst_ref=arrived.at[s - 1],
            send_sem=sum_send.at[s - 1],
            recv_sem=sum_recv.at[s - 1],
            device_id={"tensor": right},
            device_id_type=MESH,
        )

    def keep(s):
        return pltpu.make_async_copy(held.at[s], rows_all.at[s], keep_sem.at[s])

    def mixed_store(s):
        return pltpu.make_async_copy(mixed_stage, mixed_all.at[s], mixed_sem)

    def chunk(s, carry):
        @pl.when(s > 0)
        def _():
            pass_rows(s - 1).wait_recv()

        @pl.when(s < ring - 1)
        def _():
            pass_rows(s).start()

        keep(s).start()

        @pl.when(s > 0)
        def _():
            grad_keep(s - 1).wait()

        for k in range(ring):

            @pl.when(s == k)
            def _(k=k):
                grad_load(k).wait()
                if k < ring - 1:
                    grad_load(k + 1).start()

        grad_keep(s).start()
        slot = lax.rem(s, 2)
        acc_n[...] = jnp.zeros_like(acc_n)
        acc_m[...] = jnp.zeros_like(acc_m)

        def body(w_gate, w_up, w_down, act, grad_gate, grad_up):
            rows = held[s]
            gate = dot_nn(rows, w_gate[...])
            up = dot_nn(rows, w_up[...])
            grad_act = dot_nn(grads_held[slot], w_down[...])
            sig = 1.0 / (1.0 + jnp.exp(-gate))
            silu = gate * sig
            low_act = (silu * up).astype(bf16)
            low_up = (grad_act * silu).astype(bf16)
            low_gate = (grad_act * up * sig * (1.0 + gate * (1.0 - sig))).astype(bf16)
            act[...] = low_act
            grad_gate[...] = low_gate
            grad_up[...] = low_up
            acc_m[...] += dot_nt(low_act, w_down[...])
            acc_n[...] += dot_nt(low_gate, w_gate[...]) + dot_nt(low_up, w_up[...])

        width, count = own_rows.shape[1], own_rows.shape[0]
        pltpu.emit_pipeline(
            body,
            grid=(tiles,),
            in_specs=[
                pl.BlockSpec((width, tile), lambda k: (0, k)),
                pl.BlockSpec((width, tile), lambda k: (0, k + tiles)),
                pl.BlockSpec((width, tile), lambda k: (0, k + 2 * tiles)),
            ],
            out_specs=[
                pl.BlockSpec((count, tile), lambda k: (0, k)),
                pl.BlockSpec((count, tile), lambda k: (0, k)),
                pl.BlockSpec((count, tile), lambda k: (0, k + tiles)),
            ],
        )(weights, weights, weights, act_all.at[s], grads_all.at[s], grads_all.at[s])

        @pl.when(s > 0)
        def _():
            mixed_store(s - 1).wait()

        mixed_stage[...] = acc_m[...].astype(bf16)
        mixed_store(s).start()

        @pl.when(s == 0)
        def _():
            first_part[...] = acc_n[...]

        @pl.when(s == 1)
        def _():
            outgoing[0] = acc_n[...].astype(bf16)

        @pl.when(s > 1)
        def _():
            pass_sum(s - 1).wait_recv()
            outgoing[s - 1] = (acc_n[...] + arrived[s - 2].astype(f32)).astype(bf16)

        @pl.when(s > 0)
        def _():
            pass_sum(s).start()

        return carry

    lax.fori_loop(0, ring, chunk, 0)
    mixed_store(ring - 1).wait()
    pass_sum(ring - 1).wait_recv()
    final_stage[...] = (first_part[...] + arrived[ring - 2].astype(f32)).astype(bf16)
    final = pltpu.make_async_copy(final_stage, grad_own, final_sem)
    final.start()

    def settle(s, carry):
        keep(s).wait()

        @pl.when(s < ring - 1)
        def _():
            pass_rows(s).wait_send()

        @pl.when(s > 0)
        def _():
            pass_sum(s).wait_send()

        return carry

    lax.fori_loop(0, ring, settle, 0)
    grad_keep(ring - 1).wait()
    final.wait()


def feed(own_rows, grad_rows, weights, ring, tile=256, collective_id=7):
    count, width = own_rows.shape
    hidden = weights.shape[1] // 3
    any_spec = pl.BlockSpec(memory_space=pl.ANY)
    dma = pltpu.SemaphoreType.DMA
    return pl.pallas_call(
        functools.partial(feed_kernel, ring, min(tile, hidden)),
        out_shape=[
            jax.ShapeDtypeStruct((ring, count, width), bf16),
            jax.ShapeDtypeStruct((ring, count, width), bf16),
            jax.ShapeDtypeStruct((ring, count, hidden), bf16),
            jax.ShapeDtypeStruct((ring, count, 2 * hidden), bf16),
            jax.ShapeDtypeStruct((ring, count, width), bf16),
            jax.ShapeDtypeStruct((count, width), bf16),
        ],
        in_specs=[any_spec] * (2 + ring),
        out_specs=[any_spec] * 6,
        scratch_shapes=[
            pltpu.VMEM((ring, count, width), bf16),
            pltpu.VMEM((2, count, width), bf16),
            pltpu.VMEM((count, width), f32),
            pltpu.VMEM((count, width), f32),
            pltpu.VMEM((count, width), f32),
            pltpu.VMEM((ring - 1, count, width), bf16),
            pltpu.VMEM((ring - 1, count, width), bf16),
            pltpu.VMEM((count, width), bf16),
            pltpu.VMEM((count, width), bf16),
            dma,
            dma((ring,)),
            dma((2,)),
            dma,
            dma,
            dma((ring - 1,)),
            dma((ring - 1,)),
            dma((ring - 1,)),
            dma((ring - 1,)),
            dma((2,)),
        ],
        compiler_params=pltpu.CompilerParams(
            collective_id=collective_id, has_side_effects=True, vmem_limit_bytes=64 * 1024 * 1024 - 65536,
        ),
        cost_estimate=pl.CostEstimate(
            flops=12 * ring * count * width * hidden,
            bytes_accessed=8 * ring * count * width,
            transcendentals=ring * count * hidden,
        ),
        name="feed_forward",
    )(own_rows, *grad_rows, weights)


def flip(index, bit):
    return index + bit - 2 * bit * lax.rem(lax.div(index, bit), 2)


def collect_kernel(
    tp_count, dp_count, shard, gains, chunk, out, gains_out, chunk_out,
    own_sem, ring_send, ring_recv, send, recv, gain_send, gain_recv, chunk_send, chunk_recv,
):
    my_dp = lax.axis_index("dp")
    my_tp = lax.axis_index("tensor")
    rows = shard.shape[0]
    half = rows // 2
    bits = [1 << b for b in reversed(range(dp_count.bit_length() - 1))]
    orders = [bits, bits[:-1][::-1] + bits[-1:]]
    steps = len(bits)

    barrier = pltpu.get_barrier_semaphore()
    for j in range(1, tp_count):
        pl.semaphore_signal(
            barrier, inc=1, device_id={"tensor": lax.rem(my_tp + j, tp_count)}, device_id_type=MESH
        )
    for j in range(1, dp_count):
        pl.semaphore_signal(
            barrier, inc=1, device_id={"dp": lax.rem(my_dp + j, dp_count)}, device_id_type=MESH
        )
    pl.semaphore_wait(barrier, tp_count + dp_count - 2)

    home = out.at[my_tp, pl.ds(my_dp * rows, rows), :]
    own = pltpu.make_async_copy(shard, home, own_sem.at[0])
    own.start()
    own_gain = pltpu.make_async_copy(gains, gains_out.at[my_dp], own_sem.at[1])
    own_gain.start()

    def across(j):
        return pltpu.make_async_remote_copy(
            src_ref=shard,
            dst_ref=home,
            send_sem=ring_send.at[j],
            recv_sem=ring_recv.at[j],
            device_id={"tensor": lax.rem(my_tp + j, tp_count)},
            device_id_type=MESH,
        )

    def gain_copy(j):
        return pltpu.make_async_remote_copy(
            src_ref=gains,
            dst_ref=gains_out.at[my_dp],
            send_sem=gain_send.at[j],
            recv_sem=gain_recv.at[j],
            device_id={"dp": lax.rem(my_dp + j, dp_count)},
            device_id_type=MESH,
        )

    onward = pltpu.make_async_remote_copy(
        src_ref=chunk,
        dst_ref=chunk_out,
        send_sem=chunk_send,
        recv_sem=chunk_recv,
        device_id={"tensor": lax.rem(my_tp + 1, tp_count)},
        device_id_type=MESH,
    )

    def within(j, s, k, m):
        order = orders[s]
        owner = my_dp
        for b in range(k):
            if m >> b & 1:
                owner = flip(owner, order[b])
        block = out.at[
            lax.rem(my_tp - j + tp_count, tp_count), pl.ds(owner * rows + s * half, half), :
        ]
        at = (1 << k) - 1 + m
        return pltpu.make_async_remote_copy(
            src_ref=block,
            dst_ref=block,
            send_sem=send.at[j, s, at],
            recv_sem=recv.at[j, s, at],
            device_id={"dp": flip(my_dp, order[k])},
            device_id_type=MESH,
        )

    for j in range(1, tp_count):
        across(j).start()
    for j in range(1, dp_count):
        gain_copy(j).start()
    onward.start()
    own.wait()
    for phase in range(tp_count + steps):
        for k in reversed(range(steps + 1)):
            j = phase - k
            if not 0 <= j < tp_count:
                continue
            if k == 0:
                if j > 0:
                    across(j).wait_recv()
            else:
                for s in range(2):
                    for m in range(1 << (k - 1)):
                        within(j, s, k - 1, m).wait_recv()
            if k < steps:
                for s in range(2):
                    for m in range(1 << k):
                        within(j, s, k, m).start()
    for j in range(tp_count):
        if j > 0:
            across(j).wait_send()
        for s in range(2):
            for k in range(steps):
                for m in range(1 << k):
                    within(j, s, k, m).wait_send()
    own_gain.wait()
    for j in range(1, dp_count):
        gain_copy(j).wait()
    onward.wait()


def collect(shard, gains, chunk, tp_count, dp_count, collective_id):
    rows, cols = shard.shape
    dma = pltpu.SemaphoreType.DMA
    vmem_spec = pl.BlockSpec(memory_space=pltpu.VMEM)
    any_spec = pl.BlockSpec(memory_space=pl.ANY)
    return pl.pallas_call(
        functools.partial(collect_kernel, tp_count, dp_count),
        out_shape=[
            jax.ShapeDtypeStruct((tp_count, dp_count * rows, cols), shard.dtype),
            jax.ShapeDtypeStruct((dp_count,) + gains.shape, gains.dtype),
            jax.ShapeDtypeStruct(chunk.shape, chunk.dtype),
        ],
        in_specs=[vmem_spec, vmem_spec, any_spec],
        out_specs=[any_spec] * 3,
        scratch_shapes=[
            dma((2,)),
            dma((tp_count,)),
            dma((tp_count,)),
            dma((tp_count, 2, dp_count - 1)),
            dma((tp_count, 2, dp_count - 1)),
            dma((dp_count,)),
            dma((dp_count,)),
            dma,
            dma,
        ],
        compiler_params=pltpu.CompilerParams(collective_id=collective_id, has_side_effects=True),
        cost_estimate=pl.CostEstimate(
            flops=0, bytes_accessed=16 * tp_count * dp_count * shard.size, transcendentals=0
        ),
        name="collect",
    )(shard, gains, chunk)


def spread_kernel(rows, weight, out):
    out[0] = dot_nn(rows[...], weight[0]).astype(out.dtype)


def spread(rows, weights, part, cols):
    shards, width, _ = weights.shape
    count = rows.shape[0]
    return pl.pallas_call(
        spread_kernel,
        grid=(shards,),
        in_specs=[
            pl.BlockSpec((count, width), lambda t: (0, 0)),
            pl.BlockSpec((1, width, cols), lambda t: (t, 0, part)),
        ],
        out_specs=pl.BlockSpec((1, count, cols), lambda t: (t, 0, 0)),
        out_shape=jax.ShapeDtypeStruct((shards, count, cols), bf16),
        cost_estimate=pl.CostEstimate(
            flops=2 * shards * count * width * cols,
            bytes_accessed=2 * shards * width * cols,
            transcendentals=0,
        ),
        name="spread",
    )(rows, weights)


def gather_kernel(part, weight, begin, out):
    @pl.when(pl.program_id(0) == 0)
    def _():
        out[...] = begin[...]

    out[...] += dot_nt(part[0], weight[0])


def gather_sum(parts, weights, part, begin):
    shards, count, cols = parts.shape
    width = weights.shape[1]
    return pl.pallas_call(
        gather_kernel,
        grid=(shards,),
        in_specs=[
            pl.BlockSpec((1, count, cols), lambda t: (t, 0, 0)),
            pl.BlockSpec((1, width, cols), lambda t: (t, 0, part)),
            pl.BlockSpec((count, width), lambda t: (0, 0)),
        ],
        out_specs=pl.BlockSpec((count, width), lambda t: (0, 0)),
        out_shape=jax.ShapeDtypeStruct((count, width), f32),
        cost_estimate=pl.CostEstimate(
            flops=2 * shards * count * width * cols,
            bytes_accessed=2 * shards * width * cols,
            transcendentals=0,
        ),
        name="gather_sum",
    )(parts, weights, begin)


def outer_kernel(rows, part, out, turned):
    @pl.when(pl.program_id(0) == 0)
    def _():
        turned[...] = rows[...].T

    out[...] = dot_nn(turned[...], part[0]).astype(out.dtype)


def outer(rows, parts):
    shards, count, cols = parts.shape
    width = rows.shape[1]
    return pl.pallas_call(
        outer_kernel,
        grid=(shards,),
        in_specs=[
            pl.BlockSpec((count, width), lambda t: (0, 0)),
            pl.BlockSpec((1, count, cols), lambda t: (t, 0, 0)),
        ],
        out_specs=pl.BlockSpec((width, cols), lambda t: (0, t)),
        out_shape=jax.ShapeDtypeStruct((width, shards * cols), bf16),
        scratch_shapes=[pltpu.VMEM((width, count), bf16)],
        cost_estimate=pl.CostEstimate(
            flops=2 * shards * count * width * cols,
            bytes_accessed=2 * shards * width * cols,
            transcendentals=0,
        ),
        name="outer",
    )(rows, parts)


def rms_scale(hidden):
    return lax.rsqrt(jnp.mean(hidden * hidden, axis=1, keepdims=True) + epsilon)


def norm_back(grad_norm, hidden, scale_rows, gain):
    normed = hidden * scale_rows
    gain_part = jnp.sum(grad_norm * normed, axis=0)
    inner = grad_norm * gain
    grad_hidden = scale_rows * (inner - normed * jnp.mean(inner * normed, axis=1, keepdims=True))
    return (grad_hidden, gain_part)


def after(value, other):
    return lax.optimization_barrier((value, other))[0]


def local(
    tokens,
    upstream,
    lengths,
    positions,
    pages,
    attn_gain,
    w_query,
    w_key,
    w_value,
    w_out,
    mlp_gain,
    w_gate,
    w_up,
    w_down,
):
    dp_count = lax.axis_size("dp")
    tp_count = lax.axis_size("tensor")
    dp_index = lax.axis_index("dp")
    tp_index = lax.axis_index("tensor")
    tok_dev, width = tokens.shape
    tok_group = tok_dev * tp_count
    page_rows = tok_dev // dp_count
    group_pages = tp_count * dp_count
    page_count = pages.shape[0]
    device = dp_index * tp_count + tp_index
    everyone = ("tensor", "dp")

    local_ids = jnp.arange(dp_count, dtype=jnp.int32)
    inverse = (
        jnp.zeros((page_count,), jnp.int32).at[pages].set(jnp.arange(page_count, dtype=jnp.int32))
    )
    dealt = lax.dynamic_slice_in_dim(inverse, device * dp_count, dp_count)
    dest_group = dealt // group_pages
    send_order = jnp.zeros((dp_count,), jnp.int32).at[dest_group].set(local_ids)
    group_sources = lax.dynamic_slice_in_dim(pages, dp_index * group_pages, group_pages)
    perm = (
        (jnp.arange(group_pages, dtype=jnp.int32) // dp_count) * dp_count
        + group_sources // group_pages
    ).astype(jnp.int32)

    def reorder(rows, order):
        blocks = rows.reshape(dp_count, page_rows, rows.shape[1])
        return jnp.take(blocks, order, axis=0).reshape(rows.shape)

    hidden_in = reorder(tokens, send_order).astype(f32)
    grad_top = reorder(upstream, send_order).astype(f32)
    seq_lens = lengths[0]
    seq_ends = jnp.cumsum(seq_lens)
    place = (jnp.take(dealt, send_order) % group_pages) * page_rows
    place_rows = (place[:, None] + jnp.arange(page_rows, dtype=jnp.int32)[None, :]).reshape(-1)
    valid_rows = (place_rows < seq_ends[-1]).astype(f32)[:, None]

    row_ids = jnp.arange(tok_group, dtype=jnp.int32)
    begin = jnp.max(
        jnp.where(row_ids[:, None] >= seq_ends[None, :], seq_ends[None, :], 0), axis=1
    ).astype(jnp.int32)
    block_len = min(block_rows, tok_group)
    first_block = begin[::block_len] // block_len
    begin = begin[None, :]
    inverse_freq = theta_base ** (-(jnp.arange(HALF, dtype=f32) * 2.0) / HD)
    angles = inverse_freq[:, None] * positions.astype(f32)
    cos_t, sin_t = jnp.cos(angles), jnp.sin(angles)

    q_cols, kv_cols = w_query.shape[1], w_key.shape[1]
    kv_heads = kv_cols // HD
    per_group = q_cols // kv_cols
    group_q = per_group * HD
    groups = range(kv_heads)
    qkv_shard = jnp.concatenate(
        [
            part
            for g in groups
            for part in (
                w_query[:, g * group_q : (g + 1) * group_q],
                w_key[:, g * HD : (g + 1) * HD],
                w_value[:, g * HD : (g + 1) * HD],
            )
        ],
        axis=1,
    )

    def gather_all(shard):
        full = lax.all_gather(shard, everyone, axis=0, tiled=False)
        return full.reshape(tp_count, dp_count * shard.shape[0], shard.shape[1])

    def trade(value):
        blocks = value.reshape(group_pages, page_rows, value.shape[-1])
        return lax.all_to_all(blocks, everyone, split_axis=0, concat_axis=0, tiled=True)

    def trade_back(value):
        return trade(value).reshape(tp_count, tok_dev, value.shape[-1])

    ring_next = [(t, (t + 1) % tp_count) for t in range(tp_count)]

    def pass_on(value):
        return lax.ppermute(value, "tensor", ring_next)

    grad_out = grad_top * valid_rows
    grad_chunks = [grad_out.astype(bf16)]
    mlp_shard = jnp.concatenate([w_gate, w_up, w_down.T], axis=1)
    w_mlp = lax.all_gather(mlp_shard, "dp", axis=0, tiled=True)
    w_qkv, gains, grad_chunk = collect(
        qkv_shard, jnp.stack([attn_gain, mlp_gain]), grad_chunks[0], tp_count, dp_count, 1
    )
    grad_chunks.append(grad_chunk)
    for _ in range(tp_count - 2):
        grad_chunks.append(pass_on(grad_chunks[-1]))
    gains = gains.transpose(1, 0, 2).reshape(2, -1).astype(f32)
    gain_one, gain_two = gains[0], gains[1]

    scale_one = rms_scale(hidden_in)
    normed_one = (hidden_in * scale_one * gain_one).astype(bf16)
    qkv, slots = [], []
    for g in groups:
        qkv.append(spread(normed_one, w_qkv, g, group_q + 2 * HD))
        slots.append(trade(qkv[g]))
    out_shard = with_layout_constraint(w_out.T, Layout(major_to_minor=(0, 1)))
    w_out_t = gather_all(after(out_shard, w_qkv))
    saved, mixed = [], []
    last = qkv[-1]
    for g in groups:
        last = (last, grad_chunks[min(g + 1, tp_count - 1)])
        if g == len(groups) - 1:
            last = (last, w_mlp)
        q_t, k_t, k_rows, v_t, v_rows = prepare(
            after(slots[g], last), perm, cos_t, sin_t, per_group, 1
        )
        o_t, lse, last = attend_forward(
            q_t, k_rows, v_t, begin, first_block, perm, page_rows, block_len
        )
        saved.append((q_t, k_rows, k_t, v_rows, o_t, lse))
        mixed.append(trade_back(last))
    hidden_mid = hidden_in
    for g in groups:
        hidden_mid = gather_sum(mixed[g], w_out_t, g, hidden_mid)

    scale_two = rms_scale(hidden_mid)
    normed_two = (hidden_mid * scale_two * gain_two).astype(bf16)
    grad_mlp, mlp_rows, inner_act, grad_gate_up, partial_two, grad_normed_two = feed(
        normed_two, grad_chunks, w_mlp, tp_count
    )
    grad_normed_two = grad_normed_two.astype(f32)
    grad_mid_norm, gain_two_part = norm_back(grad_normed_two, hidden_mid, scale_two, gain_two)
    grad_mid = grad_out + grad_mid_norm

    def add_on(arrived, s):
        return (arrived.astype(f32) + partial_two[s].astype(f32)).astype(bf16)

    branch_two = pass_on(partial_two[1])

    def reduce_dp(grad):
        return lax.psum_scatter(grad.astype(bf16), "dp", scatter_dimension=0, tiled=True)

    def reduce_tensor(value):
        cols = value.shape[1] // tp_count
        total = lax.dynamic_slice_in_dim(value, tp_index * cols, cols, 1).astype(f32)
        for s in range(1, tp_count):
            target = lax.rem(tp_index + s, tp_count)
            block = lax.dynamic_slice_in_dim(value, target * cols, cols, 1)
            pairs = [(t, (t + s) % tp_count) for t in range(tp_count)]
            total = total + lax.ppermute(block, "tensor", pairs).astype(f32)
        return total

    def flat(value):
        return value.reshape(tok_group, value.shape[-1])

    grad_down_t = dot_tn(flat(grad_mlp), flat(inner_act)).astype(bf16)
    sum_down = reduce_dp(grad_down_t)
    grad_gate_up = dot_tn(flat(mlp_rows), flat(after(grad_gate_up, grad_down_t))).astype(bf16)
    sum_gate_up = reduce_dp(grad_gate_up)
    grad_z = after(grad_mid.astype(bf16), (grad_gate_up, branch_two))
    grad_slots = [trade(spread(grad_z, w_out_t, g, group_q)) for g in groups]
    grad_qkv = []
    last = grad_z
    for g in groups:
        q_t, k_rows, k_t, v_rows, o_t, lse = saved[g]
        back = attend_backward(
            after(grad_slots[g], last), q_t, k_rows, k_t, v_rows, o_t, lse, begin, cos_t, sin_t,
            first_block, perm, page_rows, block_len,
        )
        grad_qkv.append(trade_back(back))
        last = (back, sum_down)
    for s in range(2, tp_count - 1):
        branch_two = pass_on(add_on(after(branch_two, grad_slots[-1]), s))
    grad_wout = outer(after(grad_z, (back, branch_two)), jnp.concatenate(mixed, axis=2))
    branch_two = pass_on(add_on(after(branch_two, grad_qkv[-1]), tp_count - 1))
    sum_out = reduce_dp(grad_wout)
    normed_late = after(normed_one, (sum_gate_up, grad_wout))
    hidden = sum_gate_up.shape[1] // 2
    grad_wqkv = outer(normed_late, jnp.concatenate(grad_qkv, axis=2))
    sum_qkv = reduce_tensor(reduce_dp(grad_wqkv))
    grad_normed_one = jnp.zeros((tok_dev, width), f32)
    for g in groups:
        grad_normed_one = gather_sum(grad_qkv[g], w_qkv, g, grad_normed_one)
    sum_out = reduce_tensor(sum_out)
    each = group_q + 2 * HD
    sum_qkv = [sum_qkv[:, g * each : (g + 1) * each] for g in groups]
    result = (
        (after(hidden_mid, back) + branch_two.astype(f32) + partial_two[0].astype(f32)) * valid_rows
    ).astype(bf16)
    grad_in_norm, gain_one_part = norm_back(grad_normed_one, hidden_in, scale_one, gain_one)
    grad_in = (grad_mid + grad_in_norm).astype(bf16)

    gain_parts = jnp.stack([gain_one_part, gain_two_part]).reshape(2, dp_count, -1)
    gain_parts = jnp.broadcast_to(
        gain_parts.transpose(1, 0, 2)[None], (tp_count, dp_count, 2, gain_parts.shape[2])
    ).reshape(group_pages, 2, -1)
    gain_sums = jnp.sum(
        lax.all_to_all(gain_parts, everyone, split_axis=0, concat_axis=0, tiled=True), axis=0
    )
    return (
        reorder(result, dest_group),
        reorder(grad_in, dest_group),
        gain_sums[0],
        jnp.concatenate([part[:, :group_q] for part in sum_qkv], axis=1),
        jnp.concatenate([part[:, group_q : group_q + HD] for part in sum_qkv], axis=1),
        jnp.concatenate([part[:, group_q + HD :] for part in sum_qkv], axis=1),
        sum_out.T,
        gain_sums[1],
        sum_gate_up[:, :hidden].astype(f32),
        sum_gate_up[:, hidden:].astype(f32),
        sum_down.astype(f32).T,
    )


def solution(mesh):
    rows = P(("dp", "tensor"), None)
    weight = P("dp", "tensor")
    weight_t = P("tensor", "dp")
    return jax.shard_map(
        local,
        mesh=mesh,
        in_specs=(
            rows,
            rows,
            P("dp", None),
            P("dp", None),
            P(),
            P("dp"),
            weight,
            weight,
            weight,
            weight_t,
            P("dp"),
            weight,
            weight,
            weight_t,
        ),
        out_specs=(
            rows,
            rows,
            P("dp"),
            weight,
            weight,
            weight,
            weight_t,
            P("dp"),
            weight,
            weight,
            weight_t,
        ),
        check_vma=False,
    )
```

```python
import functools

import jax
import jax.numpy as jnp
from jax import lax
from jax.experimental import pallas as pl
from jax.experimental.layout import Layout, with_layout_constraint
from jax.experimental.pallas import tpu as pltpu
from jax.sharding import PartitionSpec as P

HD = 64
HALF = HD // 2

epsilon = 1e-05
theta_base = 500000.0
masked_score = -1e30
score_scale = HD**-0.5
block_rows = 256
MESH = pl.DeviceIdType.MESH
f32 = jnp.float32
bf16 = jnp.bfloat16


def dot_nn(left, right):
    return lax.dot_general(left, right, (((1,), (0,)), ((), ())), preferred_element_type=f32)


def dot_nt(left, right):
    return lax.dot_general(left, right, (((1,), (1,)), ((), ())), preferred_element_type=f32)


def dot_tn(left, right):
    return lax.dot_general(left, right, (((0,), (0,)), ((), ())), preferred_element_type=f32)


def prep_kernel(pages_per, q_heads, kv_heads, perm, *refs):
    page_refs = refs[:pages_per]
    cos_ref, sin_ref, q_t, k_t, k_rows, v_t, v_rows = refs[pages_per:]
    rows = jnp.concatenate([r[0].astype(f32) for r in page_refs], axis=0)
    turned = rows.T
    cos, sin = cos_ref[...], sin_ref[...]

    def rope(base):
        first, second = turned[base : base + HALF], turned[base + HALF : base + HD]
        return jnp.concatenate([first * cos - second * sin, second * cos + first * sin], axis=0)

    for h in range(q_heads):
        roped = rope(h * HD).astype(bf16)
        q_t[h * HD : (h + 1) * HD, :] = (roped.astype(f32) * score_scale).astype(bf16)
    k_base = q_heads * HD
    v_base = k_base + kv_heads * HD
    for g in range(kv_heads):
        roped = rope(k_base + g * HD)
        k_t[g * HD : (g + 1) * HD, :] = roped.astype(bf16)
        k_rows[g] = roped.T.astype(bf16)
        v_t[g * HD : (g + 1) * HD, :] = turned[v_base + g * HD : v_base + (g + 1) * HD].astype(bf16)
        v_rows[g] = rows[:, v_base + g * HD : v_base + (g + 1) * HD].astype(bf16)


def prepare(slots, perm, cos_t, sin_t, q_heads, kv_heads):
    page_rows, cols = slots.shape[1:]
    total_rows = slots.shape[0] * page_rows
    lanes = 128
    pages_per = lanes // page_rows

    def page_spec(a):
        return pl.BlockSpec(
            (1, page_rows, cols), lambda i, perm_ref, a=a: (perm_ref[i * pages_per + a], 0, 0)
        )

    table = pl.BlockSpec((HALF, lanes), lambda i, perm_ref: (0, i))
    return pl.pallas_call(
        functools.partial(prep_kernel, pages_per, q_heads, kv_heads),
        grid_spec=pltpu.PrefetchScalarGridSpec(
            num_scalar_prefetch=1,
            grid=(total_rows // lanes,),
            in_specs=[page_spec(a) for a in range(pages_per)] + [table, table],
            out_specs=[
                pl.BlockSpec((q_heads * HD, lanes), lambda i, perm_ref: (0, i)),
                pl.BlockSpec((kv_heads * HD, lanes), lambda i, perm_ref: (0, i)),
                pl.BlockSpec((kv_heads, lanes, HD), lambda i, perm_ref: (0, i, 0)),
                pl.BlockSpec((kv_heads * HD, lanes), lambda i, perm_ref: (0, i)),
                pl.BlockSpec((kv_heads, lanes, HD), lambda i, perm_ref: (0, i, 0)),
            ],
        ),
        out_shape=[
            jax.ShapeDtypeStruct((q_heads * HD, total_rows), bf16),
            jax.ShapeDtypeStruct((kv_heads * HD, total_rows), bf16),
            jax.ShapeDtypeStruct((kv_heads, total_rows, HD), bf16),
            jax.ShapeDtypeStruct((kv_heads * HD, total_rows), bf16),
            jax.ShapeDtypeStruct((kv_heads, total_rows, HD), bf16),
        ],
        cost_estimate=pl.CostEstimate(
            flops=8 * slots.size, bytes_accessed=6 * slots.size, transcendentals=0
        ),
        name="prepare",
    )(perm, *([slots] * pages_per), cos_t, sin_t)


def block_bias(i, j, begin_row, block_len):
    keys = j * block_len + lax.broadcasted_iota(jnp.int32, (block_len, block_len), 0)
    queries = i * block_len + lax.broadcasted_iota(jnp.int32, (block_len, block_len), 1)
    allowed = (keys >= begin_row) & (keys <= queries)
    return jnp.where(allowed, 0.0, masked_score)


def forward_kernel(
    q_heads, kv_heads, page_rows, first_block, perm,
    q_t, k_rows, v_t, begin, o_t, lse, o_slots, acc, top, total, stage, sems,
):
    i = pl.program_id(0)
    block_len = q_t.shape[1]
    per_group = q_heads // kv_heads
    acc[...] = jnp.zeros_like(acc)
    top[...] = jnp.full_like(top, masked_score)
    total[...] = jnp.zeros_like(total)
    begin_row = begin[...]

    def visit(j, carry):
        bias = block_bias(i, j, begin_row, block_len)
        at = pl.ds(pl.multiple_of(j * block_len, block_len), block_len)
        for h in range(q_heads):
            g = h // per_group
            span = slice(h * HD, (h + 1) * HD)
            scores = dot_nn(k_rows[g, at, :], q_t[span, :]) + bias
            old = top[h : h + 1, :]
            new = jnp.maximum(old, jnp.max(scores, axis=0, keepdims=True))
            weights = jnp.exp(scores - new)
            fade = jnp.exp(old - new)
            total[h : h + 1, :] = total[h : h + 1, :] * fade + jnp.sum(
                weights, axis=0, keepdims=True
            )
            top[h : h + 1, :] = new
            acc[span, :] = acc[span, :] * fade + dot_nn(
                v_t[g * HD : (g + 1) * HD, at], weights.astype(bf16)
            )
        return carry

    lax.fori_loop(first_block[i], i + 1, visit, 0)
    lse[...] = top[...] + jnp.log(total[...])
    scaled = [
        acc[h * HD : (h + 1) * HD, :] / total[h : h + 1, :] for h in range(q_heads)
    ]
    mixed = jnp.concatenate(scaled, axis=0)
    o_t[...] = mixed.astype(bf16)
    pages = block_len // page_rows
    stage[...] = mixed.T.astype(bf16).reshape(pages, page_rows, q_heads * HD)
    copies = [
        pltpu.make_async_copy(stage.at[a], o_slots.at[perm[i * pages + a]], sems.at[a])
        for a in range(pages)
    ]
    for copy in copies:
        copy.start()
    for copy in copies:
        copy.wait()


def attend_forward(q_t, k_rows, v_t, begin, first_block, perm, page_rows, block_len):
    total_rows = q_t.shape[1]
    kv_heads = k_rows.shape[0]
    q_heads = q_t.shape[0] // HD
    pages = block_len // page_rows
    return pl.pallas_call(
        functools.partial(forward_kernel, q_heads, kv_heads, page_rows),
        grid_spec=pltpu.PrefetchScalarGridSpec(
            num_scalar_prefetch=2,
            grid=(total_rows // block_len,),
            in_specs=[
                pl.BlockSpec((q_heads * HD, block_len), lambda i, *_: (0, i)),
                pl.BlockSpec((kv_heads, total_rows, HD), lambda i, *_: (0, 0, 0)),
                pl.BlockSpec((kv_heads * HD, total_rows), lambda i, *_: (0, 0)),
                pl.BlockSpec((1, block_len), lambda i, *_: (0, i)),
            ],
            out_specs=[
                pl.BlockSpec((q_heads * HD, block_len), lambda i, *_: (0, i)),
                pl.BlockSpec((q_heads, block_len), lambda i, *_: (0, i)),
                pl.BlockSpec(memory_space=pl.ANY),
            ],
            scratch_shapes=[
                pltpu.VMEM((q_heads * HD, block_len), f32),
                pltpu.VMEM((q_heads, block_len), f32),
                pltpu.VMEM((q_heads, block_len), f32),
                pltpu.VMEM((pages, page_rows, q_heads * HD), bf16),
                pltpu.SemaphoreType.DMA((pages,)),
            ],
        ),
        out_shape=[
            jax.ShapeDtypeStruct((q_heads * HD, total_rows), bf16),
            jax.ShapeDtypeStruct((q_heads, total_rows), f32),
            jax.ShapeDtypeStruct((total_rows // page_rows, page_rows, q_heads * HD), bf16),
        ],
        cost_estimate=pl.CostEstimate(
            flops=q_heads * total_rows * total_rows * HD,
            bytes_accessed=8 * q_t.size,
            transcendentals=q_heads * total_rows * total_rows // 4,
        ),
        name="attend_forward",
    )(first_block, perm, q_t, k_rows, v_t, begin)


def backward_kernel(
    q_heads, kv_heads, page_rows, pages, first_block, perm, *refs
):
    grad_pages = refs[:pages]
    (
        q_t, k_rows, k_t, v_rows, o_t, lse, begin, cos_ref, sin_ref, cos_all, sin_all,
        out, grad_q, grad_k, grad_v, stage, kv_stage, sems, kv_sems,
    ) = refs[pages:]
    i = pl.program_id(0)
    steps = pl.num_programs(0)
    block_len = q_t.shape[1]
    per_group = q_heads // kv_heads
    q_cols = q_heads * HD
    kv_cols = kv_heads * HD

    @pl.when(i == 0)
    def _():
        grad_k[...] = jnp.zeros_like(grad_k)
        grad_v[...] = jnp.zeros_like(grad_v)

    grad_rows = jnp.concatenate([r[0].astype(f32) for r in grad_pages], axis=0)
    grad_t = grad_rows.T
    grad_low = grad_t.astype(bf16)
    inner = [
        jnp.sum(
            grad_t[h * HD : (h + 1) * HD] * o_t[h * HD : (h + 1) * HD, :].astype(f32),
            axis=0,
            keepdims=True,
        )
        for h in range(q_heads)
    ]
    grad_q[...] = jnp.zeros_like(grad_q)
    begin_row = begin[...]

    def visit(j, carry):
        bias = block_bias(i, j, begin_row, block_len)
        at = pl.ds(pl.multiple_of(j * block_len, block_len), block_len)
        for g in range(kv_heads):
            kv_span = slice(g * HD, (g + 1) * HD)
            keys, vals, keys_t = k_rows[g, at, :], v_rows[g, at, :], k_t[kv_span, at]
            add_k = jnp.zeros((HD, block_len), f32)
            add_v = jnp.zeros((HD, block_len), f32)
            for h in range(g * per_group, (g + 1) * per_group):
                span = slice(h * HD, (h + 1) * HD)
                queries = q_t[span, :]
                probs = jnp.exp(dot_nn(keys, queries) + bias - lse[h : h + 1, :])
                grad_h = grad_low[span]
                grad_probs = dot_nn(vals, grad_h)
                grad_scores = (probs * (grad_probs - inner[h])).astype(bf16)
                add_v = add_v + dot_nt(grad_h, probs.astype(bf16))
                add_k = add_k + dot_nt(queries, grad_scores)
                grad_q[span, :] = grad_q[span, :] + dot_nn(keys_t, grad_scores)
            grad_k[kv_span, at] = grad_k[kv_span, at] + add_k
            grad_v[kv_span, at] = grad_v[kv_span, at] + add_v
        return carry

    lax.fori_loop(first_block[i], i + 1, visit, 0)

    def unrope(value, cos, sin):
        first, second = value[:HALF], value[HALF:]
        return jnp.concatenate([first * cos + second * sin, second * cos - first * sin], axis=0)

    cos, sin = cos_ref[...], sin_ref[...]
    parts = [
        unrope(grad_q[h * HD : (h + 1) * HD, :] * score_scale, cos, sin) for h in range(q_heads)
    ]
    stage[...] = jnp.concatenate(parts, axis=0).T.astype(bf16).reshape(pages, page_rows, q_cols)
    copies = [
        pltpu.make_async_copy(
            stage.at[a], out.at[perm[i * pages + a], :, pl.ds(0, q_cols)], sems.at[a]
        )
        for a in range(pages)
    ]
    for copy in copies:
        copy.start()
    for copy in copies:
        copy.wait()

    @pl.when(i == steps - 1)
    def _():
        all_pages = kv_stage.shape[0]
        cos, sin = cos_all[...], sin_all[...]
        parts = [unrope(grad_k[g * HD : (g + 1) * HD, :], cos, sin) for g in range(kv_heads)]
        both = jnp.concatenate(parts + [grad_v[...]], axis=0)
        kv_stage[...] = both.T.astype(bf16).reshape(all_pages, page_rows, 2 * kv_cols)
        copies = [
            pltpu.make_async_copy(
                kv_stage.at[a], out.at[perm[a], :, pl.ds(q_cols, 2 * kv_cols)], kv_sems.at[a]
            )
            for a in range(all_pages)
        ]
        for copy in copies:
            copy.start()
        for copy in copies:
            copy.wait()


def attend_backward(
    grad_slots, q_t, k_rows, k_t, v_rows, o_t, lse, begin, cos_t, sin_t, first_block, perm,
    page_rows, block_len,
):
    total_rows = q_t.shape[1]
    kv_heads = k_rows.shape[0]
    q_heads = q_t.shape[0] // HD
    pages = block_len // page_rows
    all_pages = total_rows // page_rows
    q_cols = q_heads * HD
    kv_cols = kv_heads * HD

    def page_spec(a):
        return pl.BlockSpec(
            (1, page_rows, q_cols),
            lambda i, first_ref, perm_ref, a=a: (perm_ref[i * pages + a], 0, 0),
        )

    def whole(shape):
        return pl.BlockSpec(shape, lambda i, *_: (0,) * len(shape))

    def column(rows):
        return pl.BlockSpec((rows, block_len), lambda i, *_: (0, i))

    return pl.pallas_call(
        functools.partial(backward_kernel, q_heads, kv_heads, page_rows, pages),
        grid_spec=pltpu.PrefetchScalarGridSpec(
            num_scalar_prefetch=2,
            grid=(total_rows // block_len,),
            in_specs=[page_spec(a) for a in range(pages)]
            + [
                column(q_cols),
                whole((kv_heads, total_rows, HD)),
                whole((kv_cols, total_rows)),
                whole((kv_heads, total_rows, HD)),
                column(q_cols),
                column(q_heads),
                column(1),
                column(HALF),
                column(HALF),
                whole((HALF, total_rows)),
                whole((HALF, total_rows)),
            ],
            out_specs=pl.BlockSpec(memory_space=pl.ANY),
            scratch_shapes=[
                pltpu.VMEM((q_cols, block_len), f32),
                pltpu.VMEM((kv_cols, total_rows), f32),
                pltpu.VMEM((kv_cols, total_rows), f32),
                pltpu.VMEM((pages, page_rows, q_cols), bf16),
                pltpu.VMEM((all_pages, page_rows, 2 * kv_cols), bf16),
                pltpu.SemaphoreType.DMA((pages,)),
                pltpu.SemaphoreType.DMA((all_pages,)),
            ],
        ),
        out_shape=jax.ShapeDtypeStruct((all_pages, page_rows, q_cols + 2 * kv_cols), bf16),
        cost_estimate=pl.CostEstimate(
            flops=3 * q_heads * total_rows * total_rows * HD,
            bytes_accessed=12 * q_t.size,
            transcendentals=q_heads * total_rows * total_rows // 4,
        ),
        name="attend_backward",
    )(
        first_block, perm, *([grad_slots] * pages), q_t, k_rows, k_t, v_rows, o_t, lse, begin,
        cos_t, sin_t, cos_t, sin_t,
    )


def feed_kernel(
    ring, tile, own_rows, *refs
):
    grad_rows = refs[:ring]
    (
        weights, grad_all, rows_all, act_all, grads_all, mixed_all, grad_own,
    held, grads_held, acc_n, acc_m, first_part, arrived, outgoing, mixed_stage, final_stage,
    load_sem, keep_sem, grad_sem, mixed_sem, final_sem,
    row_send, row_recv, sum_send, sum_recv, all_sem,
    ) = refs[ring:]
    me = lax.axis_index("tensor")
    right = lax.rem(me + 1, ring)
    left = lax.rem(me + ring - 1, ring)
    hidden = weights.shape[1] // 3
    tiles = hidden // tile

    barrier = pltpu.get_barrier_semaphore()
    for neighbour in (left, right):
        pl.semaphore_signal(barrier, inc=1, device_id={"tensor": neighbour}, device_id_type=MESH)
    pl.semaphore_wait(barrier, 2)

    load = pltpu.make_async_copy(own_rows, held.at[0], load_sem)
    load.start()

    def grad_load(s):
        return pltpu.make_async_copy(grad_rows[s], grads_held.at[s % 2], grad_sem.at[s % 2])

    def grad_keep(s):
        return pltpu.make_async_copy(
            grads_held.at[lax.rem(s, 2)], grad_all.at[s], all_sem.at[lax.rem(s, 2)]
        )

    grad_load(0).start()
    load.wait()

    def pass_rows(s):
        return pltpu.make_async_remote_copy(
            src_ref=held.at[s],
            dst_ref=held.at[s + 1],
            send_sem=row_send.at[s],
            recv_sem=row_recv.at[s],
            device_id={"tensor": right},
            device_id_type=MESH,
        )

    def pass_sum(s):
        return pltpu.make_async_remote_copy(
            src_ref=outgoing.at[s - 1],
            dst_ref=arrived.at[s - 1],
            send_sem=sum_send.at[s - 1],
            recv_sem=sum_recv.at[s - 1],
            device_id={"tensor": right},
            device_id_type=MESH,
        )

    def keep(s):
        return pltpu.make_async_copy(held.at[s], rows_all.at[s], keep_sem.at[s])

    def mixed_store(s):
        return pltpu.make_async_copy(mixed_stage, mixed_all.at[s], mixed_sem)

    def chunk(s, carry):
        @pl.when(s > 0)
        def _():
            pass_rows(s - 1).wait_recv()

        @pl.when(s < ring - 1)
        def _():
            pass_rows(s).start()

        keep(s).start()

        @pl.when(s > 0)
        def _():
            grad_keep(s - 1).wait()

        for k in range(ring):

            @pl.when(s == k)
            def _(k=k):
                grad_load(k).wait()
                if k < ring - 1:
                    grad_load(k + 1).start()

        grad_keep(s).start()
        slot = lax.rem(s, 2)
        acc_n[...] = jnp.zeros_like(acc_n)
        acc_m[...] = jnp.zeros_like(acc_m)

        def body(w_gate, w_up, w_down, act, grad_gate, grad_up):
            rows = held[s]
            gate = dot_nn(rows, w_gate[...])
            up = dot_nn(rows, w_up[...])
            grad_act = dot_nn(grads_held[slot], w_down[...])
            sig = 1.0 / (1.0 + jnp.exp(-gate))
            silu = gate * sig
            low_act = (silu * up).astype(bf16)
            low_up = (grad_act * silu).astype(bf16)
            low_gate = (grad_act * up * sig * (1.0 + gate * (1.0 - sig))).astype(bf16)
            act[...] = low_act
            grad_gate[...] = low_gate
            grad_up[...] = low_up
            acc_m[...] += dot_nt(low_act, w_down[...])
            acc_n[...] += dot_nt(low_gate, w_gate[...]) + dot_nt(low_up, w_up[...])

        width, count = own_rows.shape[1], own_rows.shape[0]
        pltpu.emit_pipeline(
            body,
            grid=(tiles,),
            in_specs=[
                pl.BlockSpec((width, tile), lambda k: (0, k)),
                pl.BlockSpec((width, tile), lambda k: (0, k + tiles)),
                pl.BlockSpec((width, tile), lambda k: (0, k + 2 * tiles)),
            ],
            out_specs=[
                pl.BlockSpec((count, tile), lambda k: (0, k)),
                pl.BlockSpec((count, tile), lambda k: (0, k)),
                pl.BlockSpec((count, tile), lambda k: (0, k + tiles)),
            ],
        )(weights, weights, weights, act_all.at[s], grads_all.at[s], grads_all.at[s])

        @pl.when(s > 0)
        def _():
            mixed_store(s - 1).wait()

        mixed_stage[...] = acc_m[...].astype(bf16)
        mixed_store(s).start()

        @pl.when(s == 0)
        def _():
            first_part[...] = acc_n[...]

        @pl.when(s == 1)
        def _():
            outgoing[0] = acc_n[...].astype(bf16)

        @pl.when(s > 1)
        def _():
            pass_sum(s - 1).wait_recv()
            outgoing[s - 1] = (acc_n[...] + arrived[s - 2].astype(f32)).astype(bf16)

        @pl.when(s > 0)
        def _():
            pass_sum(s).start()

        return carry

    lax.fori_loop(0, ring, chunk, 0)
    mixed_store(ring - 1).wait()
    pass_sum(ring - 1).wait_recv()
    final_stage[...] = (first_part[...] + arrived[ring - 2].astype(f32)).astype(bf16)
    final = pltpu.make_async_copy(final_stage, grad_own, final_sem)
    final.start()

    def settle(s, carry):
        keep(s).wait()

        @pl.when(s < ring - 1)
        def _():
            pass_rows(s).wait_send()

        @pl.when(s > 0)
        def _():
            pass_sum(s).wait_send()

        return carry

    lax.fori_loop(0, ring, settle, 0)
    grad_keep(ring - 1).wait()
    final.wait()


def feed(own_rows, grad_rows, weights, ring, tile=256, collective_id=7):
    count, width = own_rows.shape
    hidden = weights.shape[1] // 3
    any_spec = pl.BlockSpec(memory_space=pl.ANY)
    dma = pltpu.SemaphoreType.DMA
    return pl.pallas_call(
        functools.partial(feed_kernel, ring, min(tile, hidden)),
        out_shape=[
            jax.ShapeDtypeStruct((ring, count, width), bf16),
            jax.ShapeDtypeStruct((ring, count, width), bf16),
            jax.ShapeDtypeStruct((ring, count, hidden), bf16),
            jax.ShapeDtypeStruct((ring, count, 2 * hidden), bf16),
            jax.ShapeDtypeStruct((ring, count, width), bf16),
            jax.ShapeDtypeStruct((count, width), bf16),
        ],
        in_specs=[any_spec] * (2 + ring),
        out_specs=[any_spec] * 6,
        scratch_shapes=[
            pltpu.VMEM((ring, count, width), bf16),
            pltpu.VMEM((2, count, width), bf16),
            pltpu.VMEM((count, width), f32),
            pltpu.VMEM((count, width), f32),
            pltpu.VMEM((count, width), f32),
            pltpu.VMEM((ring - 1, count, width), bf16),
            pltpu.VMEM((ring - 1, count, width), bf16),
            pltpu.VMEM((count, width), bf16),
            pltpu.VMEM((count, width), bf16),
            dma,
            dma((ring,)),
            dma((2,)),
            dma,
            dma,
            dma((ring - 1,)),
            dma((ring - 1,)),
            dma((ring - 1,)),
            dma((ring - 1,)),
            dma((2,)),
        ],
        compiler_params=pltpu.CompilerParams(
            collective_id=collective_id, has_side_effects=True, vmem_limit_bytes=64 * 1024 * 1024 - 65536,
        ),
        cost_estimate=pl.CostEstimate(
            flops=12 * ring * count * width * hidden,
            bytes_accessed=8 * ring * count * width,
            transcendentals=ring * count * hidden,
        ),
        name="feed_forward",
    )(own_rows, *grad_rows, weights)


def flip(index, bit):
    return index + bit - 2 * bit * lax.rem(lax.div(index, bit), 2)


def collect_kernel(
    tp_count, dp_count, hops, shard, gains, chunk, out, gains_out, chunks_out,
    own_sem, ring_send, ring_recv, send, recv, gain_send, gain_recv, chunk_send, chunk_recv,
):
    my_dp = lax.axis_index("dp")
    my_tp = lax.axis_index("tensor")
    rows = shard.shape[0]
    half = rows // 2
    bits = [1 << b for b in reversed(range(dp_count.bit_length() - 1))]
    orders = [bits, bits[:-1][::-1] + bits[-1:]]
    steps = len(bits)

    barrier = pltpu.get_barrier_semaphore()
    for j in range(1, tp_count):
        pl.semaphore_signal(
            barrier, inc=1, device_id={"tensor": lax.rem(my_tp + j, tp_count)}, device_id_type=MESH
        )
    for j in range(1, dp_count):
        pl.semaphore_signal(
            barrier, inc=1, device_id={"dp": lax.rem(my_dp + j, dp_count)}, device_id_type=MESH
        )
    pl.semaphore_wait(barrier, tp_count + dp_count - 2)

    home = out.at[my_tp, pl.ds(my_dp * rows, rows), :]
    own = pltpu.make_async_copy(shard, home, own_sem.at[0])
    own.start()
    own_gain = pltpu.make_async_copy(gains, gains_out.at[my_dp], own_sem.at[1])
    own_gain.start()

    def across(j):
        return pltpu.make_async_remote_copy(
            src_ref=shard,
            dst_ref=home,
            send_sem=ring_send.at[j],
            recv_sem=ring_recv.at[j],
            device_id={"tensor": lax.rem(my_tp + j, tp_count)},
            device_id_type=MESH,
        )

    def gain_copy(j):
        return pltpu.make_async_remote_copy(
            src_ref=gains,
            dst_ref=gains_out.at[my_dp],
            send_sem=gain_send.at[j],
            recv_sem=gain_recv.at[j],
            device_id={"dp": lax.rem(my_dp + j, dp_count)},
            device_id_type=MESH,
        )

    def onward(hop):
        return pltpu.make_async_remote_copy(
            src_ref=chunk if hop == 0 else chunks_out.at[hop - 1],
            dst_ref=chunks_out.at[hop],
            send_sem=chunk_send.at[hop],
            recv_sem=chunk_recv.at[hop],
            device_id={"tensor": lax.rem(my_tp + 1, tp_count)},
            device_id_type=MESH,
        )

    def within(j, s, k, m):
        order = orders[s]
        owner = my_dp
        for b in range(k):
            if m >> b & 1:
                owner = flip(owner, order[b])
        block = out.at[
            lax.rem(my_tp - j + tp_count, tp_count), pl.ds(owner * rows + s * half, half), :
        ]
        at = (1 << k) - 1 + m
        return pltpu.make_async_remote_copy(
            src_ref=block,
            dst_ref=block,
            send_sem=send.at[j, s, at],
            recv_sem=recv.at[j, s, at],
            device_id={"dp": flip(my_dp, order[k])},
            device_id_type=MESH,
        )

    for j in range(1, tp_count):
        across(j).start()
    for j in range(1, dp_count):
        gain_copy(j).start()
    onward(0).start()
    own.wait()
    for phase in range(tp_count + steps):
        for k in reversed(range(steps + 1)):
            j = phase - k
            if not 0 <= j < tp_count:
                continue
            if k == 0:
                if j > 0:
                    across(j).wait_recv()
            else:
                for s in range(2):
                    for m in range(1 << (k - 1)):
                        within(j, s, k - 1, m).wait_recv()
            if k < steps:
                for s in range(2):
                    for m in range(1 << k):
                        within(j, s, k, m).start()
        if tp_count <= phase < tp_count + hops - 1:
            onward(phase - tp_count).wait_recv()
            onward(phase - tp_count + 1).start()
    for j in range(tp_count):
        if j > 0:
            across(j).wait_send()
        for s in range(2):
            for k in range(steps):
                for m in range(1 << k):
                    within(j, s, k, m).wait_send()
    own_gain.wait()
    for j in range(1, dp_count):
        gain_copy(j).wait()
    for hop in range(hops):
        if hop == hops - 1:
            onward(hop).wait_recv()
        onward(hop).wait_send()


def collect(shard, gains, chunk, tp_count, dp_count, hops, collective_id):
    rows, cols = shard.shape
    dma = pltpu.SemaphoreType.DMA
    vmem_spec = pl.BlockSpec(memory_space=pltpu.VMEM)
    any_spec = pl.BlockSpec(memory_space=pl.ANY)
    return pl.pallas_call(
        functools.partial(collect_kernel, tp_count, dp_count, hops),
        out_shape=[
            jax.ShapeDtypeStruct((tp_count, dp_count * rows, cols), shard.dtype),
            jax.ShapeDtypeStruct((dp_count,) + gains.shape, gains.dtype),
            jax.ShapeDtypeStruct((hops,) + chunk.shape, chunk.dtype),
        ],
        in_specs=[vmem_spec, vmem_spec, any_spec],
        out_specs=[any_spec] * 3,
        scratch_shapes=[
            dma((2,)),
            dma((tp_count,)),
            dma((tp_count,)),
            dma((tp_count, 2, dp_count - 1)),
            dma((tp_count, 2, dp_count - 1)),
            dma((dp_count,)),
            dma((dp_count,)),
            dma((hops,)),
            dma((hops,)),
        ],
        compiler_params=pltpu.CompilerParams(collective_id=collective_id, has_side_effects=True),
        cost_estimate=pl.CostEstimate(
            flops=0, bytes_accessed=16 * tp_count * dp_count * shard.size, transcendentals=0
        ),
        name="collect",
    )(shard, gains, chunk)


def spread_kernel(rows, weight, out):
    out[0] = dot_nn(rows[...], weight[0]).astype(out.dtype)


def spread(rows, weights, part, cols):
    shards, width, _ = weights.shape
    count = rows.shape[0]
    return pl.pallas_call(
        spread_kernel,
        grid=(shards,),
        in_specs=[
            pl.BlockSpec((count, width), lambda t: (0, 0)),
            pl.BlockSpec((1, width, cols), lambda t: (t, 0, part)),
        ],
        out_specs=pl.BlockSpec((1, count, cols), lambda t: (t, 0, 0)),
        out_shape=jax.ShapeDtypeStruct((shards, count, cols), bf16),
        cost_estimate=pl.CostEstimate(
            flops=2 * shards * count * width * cols,
            bytes_accessed=2 * shards * width * cols,
            transcendentals=0,
        ),
        name="spread",
    )(rows, weights)


def gather_kernel(part, weight, begin, out):
    @pl.when(pl.program_id(0) == 0)
    def _():
        out[...] = begin[...]

    out[...] += dot_nt(part[0], weight[0])


def gather_sum(parts, weights, part, begin):
    shards, count, cols = parts.shape
    width = weights.shape[1]
    return pl.pallas_call(
        gather_kernel,
        grid=(shards,),
        in_specs=[
            pl.BlockSpec((1, count, cols), lambda t: (t, 0, 0)),
            pl.BlockSpec((1, width, cols), lambda t: (t, 0, part)),
            pl.BlockSpec((count, width), lambda t: (0, 0)),
        ],
        out_specs=pl.BlockSpec((count, width), lambda t: (0, 0)),
        out_shape=jax.ShapeDtypeStruct((count, width), f32),
        cost_estimate=pl.CostEstimate(
            flops=2 * shards * count * width * cols,
            bytes_accessed=2 * shards * width * cols,
            transcendentals=0,
        ),
        name="gather_sum",
    )(parts, weights, begin)


def outer_kernel(rows, part, out, turned):
    @pl.when(pl.program_id(0) == 0)
    def _():
        turned[...] = rows[...].T

    out[...] = dot_nn(turned[...], part[0]).astype(out.dtype)


def outer(rows, parts):
    shards, count, cols = parts.shape
    width = rows.shape[1]
    return pl.pallas_call(
        outer_kernel,
        grid=(shards,),
        in_specs=[
            pl.BlockSpec((count, width), lambda t: (0, 0)),
            pl.BlockSpec((1, count, cols), lambda t: (t, 0, 0)),
        ],
        out_specs=pl.BlockSpec((width, cols), lambda t: (0, t)),
        out_shape=jax.ShapeDtypeStruct((width, shards * cols), bf16),
        scratch_shapes=[pltpu.VMEM((width, count), bf16)],
        cost_estimate=pl.CostEstimate(
            flops=2 * shards * count * width * cols,
            bytes_accessed=2 * shards * width * cols,
            transcendentals=0,
        ),
        name="outer",
    )(rows, parts)


def rms_scale(hidden):
    return lax.rsqrt(jnp.mean(hidden * hidden, axis=1, keepdims=True) + epsilon)


def norm_back(grad_norm, hidden, scale_rows, gain):
    normed = hidden * scale_rows
    gain_part = jnp.sum(grad_norm * normed, axis=0)
    inner = grad_norm * gain
    grad_hidden = scale_rows * (inner - normed * jnp.mean(inner * normed, axis=1, keepdims=True))
    return (grad_hidden, gain_part)


def after(value, other):
    return lax.optimization_barrier((value, other))[0]


def local(
    tokens,
    upstream,
    lengths,
    positions,
    pages,
    attn_gain,
    w_query,
    w_key,
    w_value,
    w_out,
    mlp_gain,
    w_gate,
    w_up,
    w_down,
):
    dp_count = lax.axis_size("dp")
    tp_count = lax.axis_size("tensor")
    dp_index = lax.axis_index("dp")
    tp_index = lax.axis_index("tensor")
    tok_dev, width = tokens.shape
    tok_group = tok_dev * tp_count
    page_rows = tok_dev // dp_count
    group_pages = tp_count * dp_count
    page_count = pages.shape[0]
    device = dp_index * tp_count + tp_index
    everyone = ("tensor", "dp")

    local_ids = jnp.arange(dp_count, dtype=jnp.int32)
    inverse = (
        jnp.zeros((page_count,), jnp.int32).at[pages].set(jnp.arange(page_count, dtype=jnp.int32))
    )
    dealt = lax.dynamic_slice_in_dim(inverse, device * dp_count, dp_count)
    dest_group = dealt // group_pages
    send_order = jnp.zeros((dp_count,), jnp.int32).at[dest_group].set(local_ids)
    group_sources = lax.dynamic_slice_in_dim(pages, dp_index * group_pages, group_pages)
    perm = (
        (jnp.arange(group_pages, dtype=jnp.int32) // dp_count) * dp_count
        + group_sources // group_pages
    ).astype(jnp.int32)

    def reorder(rows, order):
        blocks = rows.reshape(dp_count, page_rows, rows.shape[1])
        return jnp.take(blocks, order, axis=0).reshape(rows.shape)

    hidden_in = reorder(tokens, send_order).astype(f32)
    grad_top = reorder(upstream, send_order).astype(f32)
    seq_lens = lengths[0]
    seq_ends = jnp.cumsum(seq_lens)
    place = (jnp.take(dealt, send_order) % group_pages) * page_rows
    place_rows = (place[:, None] + jnp.arange(page_rows, dtype=jnp.int32)[None, :]).reshape(-1)
    valid_rows = (place_rows < seq_ends[-1]).astype(f32)[:, None]

    row_ids = jnp.arange(tok_group, dtype=jnp.int32)
    begin = jnp.max(
        jnp.where(row_ids[:, None] >= seq_ends[None, :], seq_ends[None, :], 0), axis=1
    ).astype(jnp.int32)
    block_len = min(block_rows, tok_group)
    first_block = begin[::block_len] // block_len
    begin = begin[None, :]
    inverse_freq = theta_base ** (-(jnp.arange(HALF, dtype=f32) * 2.0) / HD)
    angles = inverse_freq[:, None] * positions.astype(f32)
    cos_t, sin_t = jnp.cos(angles), jnp.sin(angles)

    q_cols, kv_cols = w_query.shape[1], w_key.shape[1]
    kv_heads = kv_cols // HD
    per_group = q_cols // kv_cols
    group_q = per_group * HD
    groups = range(kv_heads)
    qkv_shard = jnp.concatenate(
        [
            part
            for g in groups
            for part in (
                w_query[:, g * group_q : (g + 1) * group_q],
                w_key[:, g * HD : (g + 1) * HD],
                w_value[:, g * HD : (g + 1) * HD],
            )
        ],
        axis=1,
    )

    def gather_all(shard):
        full = lax.all_gather(shard, everyone, axis=0, tiled=False)
        return full.reshape(tp_count, dp_count * shard.shape[0], shard.shape[1])

    def trade(value):
        blocks = value.reshape(group_pages, page_rows, value.shape[-1])
        return lax.all_to_all(blocks, everyone, split_axis=0, concat_axis=0, tiled=True)

    def trade_back(value):
        return trade(value).reshape(tp_count, tok_dev, value.shape[-1])

    ring_next = [(t, (t + 1) % tp_count) for t in range(tp_count)]

    def pass_on(value):
        return lax.ppermute(value, "tensor", ring_next)

    grad_out = grad_top * valid_rows
    grad_chunks = [grad_out.astype(bf16)]
    mlp_shard = jnp.concatenate([w_gate, w_up, w_down.T], axis=1)
    w_mlp = lax.all_gather(mlp_shard, "dp", axis=0, tiled=True)
    hops = min(2, tp_count - 1)
    w_qkv, gains, got_chunks = collect(
        qkv_shard, jnp.stack([attn_gain, mlp_gain]), grad_chunks[0], tp_count, dp_count, hops, 1
    )
    grad_chunks += [got_chunks[hop] for hop in range(hops)]
    gains = gains.transpose(1, 0, 2).reshape(2, -1).astype(f32)
    gain_one, gain_two = gains[0], gains[1]

    scale_one = rms_scale(hidden_in)
    normed_one = (hidden_in * scale_one * gain_one).astype(bf16)
    qkv, slots = [], []
    for g in groups:
        qkv.append(spread(normed_one, w_qkv, g, group_q + 2 * HD))
        slots.append(trade(qkv[g]))
    out_shard = with_layout_constraint(w_out.T, Layout(major_to_minor=(0, 1)))
    w_out_t = gather_all(after(out_shard, w_qkv))
    saved, mixed = [], []
    last = qkv[-1]
    for hop in range(hops + 1, tp_count):
        grad_chunks.append(pass_on(after(grad_chunks[-1], slots[-1])))
    for g in groups:
        if g == len(groups) - 1:
            last = (last, w_mlp)
        q_t, k_t, k_rows, v_t, v_rows = prepare(
            after(slots[g], last), perm, cos_t, sin_t, per_group, 1
        )
        o_t, lse, last = attend_forward(
            q_t, k_rows, v_t, begin, first_block, perm, page_rows, block_len
        )
        saved.append((q_t, k_rows, k_t, v_rows, o_t, lse))
        mixed.append(trade_back(last))
    hidden_mid = hidden_in
    for g in groups:
        hidden_mid = gather_sum(mixed[g], w_out_t, g, hidden_mid)

    scale_two = rms_scale(hidden_mid)
    normed_two = (hidden_mid * scale_two * gain_two).astype(bf16)
    grad_mlp, mlp_rows, inner_act, grad_gate_up, partial_two, grad_normed_two = feed(
        normed_two, grad_chunks, w_mlp, tp_count
    )
    grad_normed_two = grad_normed_two.astype(f32)
    grad_mid_norm, gain_two_part = norm_back(grad_normed_two, hidden_mid, scale_two, gain_two)
    grad_mid = grad_out + grad_mid_norm

    def add_on(arrived, s):
        return (arrived.astype(f32) + partial_two[s].astype(f32)).astype(bf16)

    def reduce_dp(grad):
        return lax.psum_scatter(grad.astype(bf16), "dp", scatter_dimension=0, tiled=True)

    def reduce_tensor(value):
        cols = value.shape[1] // tp_count
        total = lax.dynamic_slice_in_dim(value, tp_index * cols, cols, 1).astype(f32)
        for s in range(1, tp_count):
            target = lax.rem(tp_index + s, tp_count)
            block = lax.dynamic_slice_in_dim(value, target * cols, cols, 1)
            pairs = [(t, (t + s) % tp_count) for t in range(tp_count)]
            total = total + lax.ppermute(block, "tensor", pairs).astype(f32)
        return total

    def flat(value):
        return value.reshape(tok_group, value.shape[-1])

    grad_down_t = dot_tn(flat(grad_mlp), flat(inner_act)).astype(bf16)
    sum_down = reduce_dp(grad_down_t)
    grad_gate_up = dot_tn(flat(mlp_rows), flat(after(grad_gate_up, grad_down_t))).astype(bf16)
    sum_gate_up = reduce_dp(grad_gate_up)
    grad_z = after(grad_mid.astype(bf16), grad_gate_up)
    grad_slots = [trade(spread(grad_z, w_out_t, g, group_q)) for g in groups]
    grad_qkv = []
    last = grad_z
    for g in groups:
        q_t, k_rows, k_t, v_rows, o_t, lse = saved[g]
        back = attend_backward(
            after(grad_slots[g], last), q_t, k_rows, k_t, v_rows, o_t, lse, begin, cos_t, sin_t,
            first_block, perm, page_rows, block_len,
        )
        grad_qkv.append(trade_back(back))
        last = (back, sum_down)
    branch_two = pass_on(after(partial_two[1], grad_slots[-1]))
    grad_wout = outer(after(grad_z, (back, branch_two)), jnp.concatenate(mixed, axis=2))
    for s in range(2, tp_count):
        branch_two = pass_on(add_on(after(branch_two, grad_qkv[-1]), s))
    sum_out = reduce_dp(grad_wout)
    normed_late = after(normed_one, (sum_gate_up, grad_wout))
    hidden = sum_gate_up.shape[1] // 2
    grad_wqkv = outer(normed_late, jnp.concatenate(grad_qkv, axis=2))
    sum_qkv = reduce_tensor(reduce_dp(grad_wqkv))
    grad_normed_one = jnp.zeros((tok_dev, width), f32)
    for g in groups:
        grad_normed_one = gather_sum(grad_qkv[g], w_qkv, g, grad_normed_one)
    sum_out = reduce_tensor(sum_out)
    each = group_q + 2 * HD
    sum_qkv = [sum_qkv[:, g * each : (g + 1) * each] for g in groups]
    result = (
        (after(hidden_mid, back) + branch_two.astype(f32) + partial_two[0].astype(f32)) * valid_rows
    ).astype(bf16)
    grad_in_norm, gain_one_part = norm_back(grad_normed_one, hidden_in, scale_one, gain_one)
    grad_in = (grad_mid + grad_in_norm).astype(bf16)

    gain_parts = jnp.stack([gain_one_part, gain_two_part]).reshape(2, dp_count, -1)
    gain_parts = jnp.broadcast_to(
        gain_parts.transpose(1, 0, 2)[None], (tp_count, dp_count, 2, gain_parts.shape[2])
    ).reshape(group_pages, 2, -1)
    gain_sums = jnp.sum(
        lax.all_to_all(gain_parts, everyone, split_axis=0, concat_axis=0, tiled=True), axis=0
    )
    return (
        reorder(result, dest_group),
        reorder(grad_in, dest_group),
        gain_sums[0],
        jnp.concatenate([part[:, :group_q] for part in sum_qkv], axis=1),
        jnp.concatenate([part[:, group_q : group_q + HD] for part in sum_qkv], axis=1),
        jnp.concatenate([part[:, group_q + HD :] for part in sum_qkv], axis=1),
        sum_out.T,
        gain_sums[1],
        sum_gate_up[:, :hidden].astype(f32),
        sum_gate_up[:, hidden:].astype(f32),
        sum_down.astype(f32).T,
    )


def solution(mesh):
    rows = P(("dp", "tensor"), None)
    weight = P("dp", "tensor")
    weight_t = P("tensor", "dp")
    return jax.shard_map(
        local,
        mesh=mesh,
        in_specs=(
            rows,
            rows,
            P("dp", None),
            P("dp", None),
            P(),
            P("dp"),
            weight,
            weight,
            weight,
            weight_t,
            P("dp"),
            weight,
            weight,
            weight_t,
        ),
        out_specs=(
            rows,
            rows,
            P("dp"),
            weight,
            weight,
            weight,
            weight_t,
            P("dp"),
            weight,
            weight,
            weight_t,
        ),
        check_vma=False,
    )
```

```python
import functools

import jax
import jax.numpy as jnp
from jax import lax
from jax.experimental import pallas as pl
from jax.experimental.layout import Layout, with_layout_constraint
from jax.experimental.pallas import tpu as pltpu
from jax.sharding import PartitionSpec as P

HD = 64
HALF = HD // 2

epsilon = 1e-05
theta_base = 500000.0
masked_score = -1e30
score_scale = HD**-0.5
block_rows = 256
MESH = pl.DeviceIdType.MESH
f32 = jnp.float32
bf16 = jnp.bfloat16


def dot_nn(left, right):
    return lax.dot_general(left, right, (((1,), (0,)), ((), ())), preferred_element_type=f32)


def dot_nt(left, right):
    return lax.dot_general(left, right, (((1,), (1,)), ((), ())), preferred_element_type=f32)


def dot_tn(left, right):
    return lax.dot_general(left, right, (((0,), (0,)), ((), ())), preferred_element_type=f32)


def prep_kernel(pages_per, q_heads, kv_heads, perm, *refs):
    page_refs = refs[:pages_per]
    cos_ref, sin_ref, q_t, k_t, k_rows, v_t, v_rows = refs[pages_per:]
    rows = jnp.concatenate([r[0].astype(f32) for r in page_refs], axis=0)
    turned = rows.T
    cos, sin = cos_ref[...], sin_ref[...]

    def rope(base):
        first, second = turned[base : base + HALF], turned[base + HALF : base + HD]
        return jnp.concatenate([first * cos - second * sin, second * cos + first * sin], axis=0)

    for h in range(q_heads):
        roped = rope(h * HD).astype(bf16)
        q_t[h * HD : (h + 1) * HD, :] = (roped.astype(f32) * score_scale).astype(bf16)
    k_base = q_heads * HD
    v_base = k_base + kv_heads * HD
    for g in range(kv_heads):
        roped = rope(k_base + g * HD)
        k_t[g * HD : (g + 1) * HD, :] = roped.astype(bf16)
        k_rows[g] = roped.T.astype(bf16)
        v_t[g * HD : (g + 1) * HD, :] = turned[v_base + g * HD : v_base + (g + 1) * HD].astype(bf16)
        v_rows[g] = rows[:, v_base + g * HD : v_base + (g + 1) * HD].astype(bf16)


def prepare(slots, perm, cos_t, sin_t, q_heads, kv_heads):
    page_rows, cols = slots.shape[1:]
    total_rows = slots.shape[0] * page_rows
    lanes = 128
    pages_per = lanes // page_rows

    def page_spec(a):
        return pl.BlockSpec(
            (1, page_rows, cols), lambda i, perm_ref, a=a: (perm_ref[i * pages_per + a], 0, 0)
        )

    table = pl.BlockSpec((HALF, lanes), lambda i, perm_ref: (0, i))
    return pl.pallas_call(
        functools.partial(prep_kernel, pages_per, q_heads, kv_heads),
        grid_spec=pltpu.PrefetchScalarGridSpec(
            num_scalar_prefetch=1,
            grid=(total_rows // lanes,),
            in_specs=[page_spec(a) for a in range(pages_per)] + [table, table],
            out_specs=[
                pl.BlockSpec((q_heads * HD, lanes), lambda i, perm_ref: (0, i)),
                pl.BlockSpec((kv_heads * HD, lanes), lambda i, perm_ref: (0, i)),
                pl.BlockSpec((kv_heads, lanes, HD), lambda i, perm_ref: (0, i, 0)),
                pl.BlockSpec((kv_heads * HD, lanes), lambda i, perm_ref: (0, i)),
                pl.BlockSpec((kv_heads, lanes, HD), lambda i, perm_ref: (0, i, 0)),
            ],
        ),
        out_shape=[
            jax.ShapeDtypeStruct((q_heads * HD, total_rows), bf16),
            jax.ShapeDtypeStruct((kv_heads * HD, total_rows), bf16),
            jax.ShapeDtypeStruct((kv_heads, total_rows, HD), bf16),
            jax.ShapeDtypeStruct((kv_heads * HD, total_rows), bf16),
            jax.ShapeDtypeStruct((kv_heads, total_rows, HD), bf16),
        ],
        cost_estimate=pl.CostEstimate(
            flops=8 * slots.size, bytes_accessed=6 * slots.size, transcendentals=0
        ),
        name="prepare",
    )(perm, *([slots] * pages_per), cos_t, sin_t)


def block_bias(i, j, begin_row, block_len):
    keys = j * block_len + lax.broadcasted_iota(jnp.int32, (block_len, block_len), 0)
    queries = i * block_len + lax.broadcasted_iota(jnp.int32, (block_len, block_len), 1)
    allowed = (keys >= begin_row) & (keys <= queries)
    return jnp.where(allowed, 0.0, masked_score)


def forward_kernel(
    q_heads, kv_heads, page_rows, first_block, perm,
    q_t, k_rows, v_t, begin, o_t, lse, o_slots, acc, top, total, stage, sems,
):
    i = pl.program_id(0)
    block_len = q_t.shape[1]
    per_group = q_heads // kv_heads
    acc[...] = jnp.zeros_like(acc)
    top[...] = jnp.full_like(top, masked_score)
    total[...] = jnp.zeros_like(total)
    begin_row = begin[...]

    def visit(j, carry):
        bias = block_bias(i, j, begin_row, block_len)
        at = pl.ds(pl.multiple_of(j * block_len, block_len), block_len)
        for h in range(q_heads):
            g = h // per_group
            span = slice(h * HD, (h + 1) * HD)
            scores = dot_nn(k_rows[g, at, :], q_t[span, :]) + bias
            old = top[h : h + 1, :]
            new = jnp.maximum(old, jnp.max(scores, axis=0, keepdims=True))
            weights = jnp.exp(scores - new)
            fade = jnp.exp(old - new)
            total[h : h + 1, :] = total[h : h + 1, :] * fade + jnp.sum(
                weights, axis=0, keepdims=True
            )
            top[h : h + 1, :] = new
            acc[span, :] = acc[span, :] * fade + dot_nn(
                v_t[g * HD : (g + 1) * HD, at], weights.astype(bf16)
            )
        return carry

    lax.fori_loop(first_block[i], i + 1, visit, 0)
    lse[...] = top[...] + jnp.log(total[...])
    scaled = [
        acc[h * HD : (h + 1) * HD, :] / total[h : h + 1, :] for h in range(q_heads)
    ]
    mixed = jnp.concatenate(scaled, axis=0)
    o_t[...] = mixed.astype(bf16)
    pages = block_len // page_rows
    stage[...] = mixed.T.astype(bf16).reshape(pages, page_rows, q_heads * HD)
    copies = [
        pltpu.make_async_copy(stage.at[a], o_slots.at[perm[i * pages + a]], sems.at[a])
        for a in range(pages)
    ]
    for copy in copies:
        copy.start()
    for copy in copies:
        copy.wait()


def attend_forward(q_t, k_rows, v_t, begin, first_block, perm, page_rows, block_len):
    total_rows = q_t.shape[1]
    kv_heads = k_rows.shape[0]
    q_heads = q_t.shape[0] // HD
    pages = block_len // page_rows
    return pl.pallas_call(
        functools.partial(forward_kernel, q_heads, kv_heads, page_rows),
        grid_spec=pltpu.PrefetchScalarGridSpec(
            num_scalar_prefetch=2,
            grid=(total_rows // block_len,),
            in_specs=[
                pl.BlockSpec((q_heads * HD, block_len), lambda i, *_: (0, i)),
                pl.BlockSpec((kv_heads, total_rows, HD), lambda i, *_: (0, 0, 0)),
                pl.BlockSpec((kv_heads * HD, total_rows), lambda i, *_: (0, 0)),
                pl.BlockSpec((1, block_len), lambda i, *_: (0, i)),
            ],
            out_specs=[
                pl.BlockSpec((q_heads * HD, block_len), lambda i, *_: (0, i)),
                pl.BlockSpec((q_heads, block_len), lambda i, *_: (0, i)),
                pl.BlockSpec(memory_space=pl.ANY),
            ],
            scratch_shapes=[
                pltpu.VMEM((q_heads * HD, block_len), f32),
                pltpu.VMEM((q_heads, block_len), f32),
                pltpu.VMEM((q_heads, block_len), f32),
                pltpu.VMEM((pages, page_rows, q_heads * HD), bf16),
                pltpu.SemaphoreType.DMA((pages,)),
            ],
        ),
        out_shape=[
            jax.ShapeDtypeStruct((q_heads * HD, total_rows), bf16),
            jax.ShapeDtypeStruct((q_heads, total_rows), f32),
            jax.ShapeDtypeStruct((total_rows // page_rows, page_rows, q_heads * HD), bf16),
        ],
        cost_estimate=pl.CostEstimate(
            flops=q_heads * total_rows * total_rows * HD,
            bytes_accessed=8 * q_t.size,
            transcendentals=q_heads * total_rows * total_rows // 4,
        ),
        name="attend_forward",
    )(first_block, perm, q_t, k_rows, v_t, begin)


def backward_kernel(
    q_heads, kv_heads, page_rows, pages, first_block, perm, *refs
):
    grad_pages = refs[:pages]
    (
        q_t, k_rows, k_t, v_rows, o_t, lse, begin, cos_ref, sin_ref, cos_all, sin_all,
        out, grad_q, grad_k, grad_v, stage, kv_stage, sems, kv_sems,
    ) = refs[pages:]
    i = pl.program_id(0)
    steps = pl.num_programs(0)
    block_len = q_t.shape[1]
    per_group = q_heads // kv_heads
    q_cols = q_heads * HD
    kv_cols = kv_heads * HD

    @pl.when(i == 0)
    def _():
        grad_k[...] = jnp.zeros_like(grad_k)
        grad_v[...] = jnp.zeros_like(grad_v)

    grad_rows = jnp.concatenate([r[0].astype(f32) for r in grad_pages], axis=0)
    grad_t = grad_rows.T
    grad_low = grad_t.astype(bf16)
    inner = [
        jnp.sum(
            grad_t[h * HD : (h + 1) * HD] * o_t[h * HD : (h + 1) * HD, :].astype(f32),
            axis=0,
            keepdims=True,
        )
        for h in range(q_heads)
    ]
    grad_q[...] = jnp.zeros_like(grad_q)
    begin_row = begin[...]

    def visit(j, carry):
        bias = block_bias(i, j, begin_row, block_len)
        at = pl.ds(pl.multiple_of(j * block_len, block_len), block_len)
        for g in range(kv_heads):
            kv_span = slice(g * HD, (g + 1) * HD)
            keys, vals, keys_t = k_rows[g, at, :], v_rows[g, at, :], k_t[kv_span, at]
            add_k = jnp.zeros((HD, block_len), f32)
            add_v = jnp.zeros((HD, block_len), f32)
            for h in range(g * per_group, (g + 1) * per_group):
                span = slice(h * HD, (h + 1) * HD)
                queries = q_t[span, :]
                probs = jnp.exp(dot_nn(keys, queries) + bias - lse[h : h + 1, :])
                grad_h = grad_low[span]
                grad_probs = dot_nn(vals, grad_h)
                grad_scores = (probs * (grad_probs - inner[h])).astype(bf16)
                add_v = add_v + dot_nt(grad_h, probs.astype(bf16))
                add_k = add_k + dot_nt(queries, grad_scores)
                grad_q[span, :] = grad_q[span, :] + dot_nn(keys_t, grad_scores)
            grad_k[kv_span, at] = grad_k[kv_span, at] + add_k
            grad_v[kv_span, at] = grad_v[kv_span, at] + add_v
        return carry

    lax.fori_loop(first_block[i], i + 1, visit, 0)

    def unrope(value, cos, sin):
        first, second = value[:HALF], value[HALF:]
        return jnp.concatenate([first * cos + second * sin, second * cos - first * sin], axis=0)

    cos, sin = cos_ref[...], sin_ref[...]
    parts = [
        unrope(grad_q[h * HD : (h + 1) * HD, :] * score_scale, cos, sin) for h in range(q_heads)
    ]
    stage[...] = jnp.concatenate(parts, axis=0).T.astype(bf16).reshape(pages, page_rows, q_cols)
    copies = [
        pltpu.make_async_copy(
            stage.at[a], out.at[perm[i * pages + a], :, pl.ds(0, q_cols)], sems.at[a]
        )
        for a in range(pages)
    ]
    for copy in copies:
        copy.start()
    for copy in copies:
        copy.wait()

    @pl.when(i == steps - 1)
    def _():
        all_pages = kv_stage.shape[0]
        cos, sin = cos_all[...], sin_all[...]
        parts = [unrope(grad_k[g * HD : (g + 1) * HD, :], cos, sin) for g in range(kv_heads)]
        both = jnp.concatenate(parts + [grad_v[...]], axis=0)
        kv_stage[...] = both.T.astype(bf16).reshape(all_pages, page_rows, 2 * kv_cols)
        copies = [
            pltpu.make_async_copy(
                kv_stage.at[a], out.at[perm[a], :, pl.ds(q_cols, 2 * kv_cols)], kv_sems.at[a]
            )
            for a in range(all_pages)
        ]
        for copy in copies:
            copy.start()
        for copy in copies:
            copy.wait()


def attend_backward(
    grad_slots, part, q_t, k_rows, k_t, v_rows, o_t, lse, begin, cos_t, sin_t, first_block, perm,
    page_rows, block_len,
):
    total_rows = q_t.shape[1]
    kv_heads = k_rows.shape[0]
    q_heads = q_t.shape[0] // HD
    pages = block_len // page_rows
    all_pages = total_rows // page_rows
    q_cols = q_heads * HD
    kv_cols = kv_heads * HD

    def page_spec(a):
        return pl.BlockSpec(
            (1, page_rows, q_cols),
            lambda i, first_ref, perm_ref, a=a: (perm_ref[i * pages + a], 0, part),
        )

    def whole(shape):
        return pl.BlockSpec(shape, lambda i, *_: (0,) * len(shape))

    def column(rows):
        return pl.BlockSpec((rows, block_len), lambda i, *_: (0, i))

    return pl.pallas_call(
        functools.partial(backward_kernel, q_heads, kv_heads, page_rows, pages),
        grid_spec=pltpu.PrefetchScalarGridSpec(
            num_scalar_prefetch=2,
            grid=(total_rows // block_len,),
            in_specs=[page_spec(a) for a in range(pages)]
            + [
                column(q_cols),
                whole((kv_heads, total_rows, HD)),
                whole((kv_cols, total_rows)),
                whole((kv_heads, total_rows, HD)),
                column(q_cols),
                column(q_heads),
                column(1),
                column(HALF),
                column(HALF),
                whole((HALF, total_rows)),
                whole((HALF, total_rows)),
            ],
            out_specs=pl.BlockSpec(memory_space=pl.ANY),
            scratch_shapes=[
                pltpu.VMEM((q_cols, block_len), f32),
                pltpu.VMEM((kv_cols, total_rows), f32),
                pltpu.VMEM((kv_cols, total_rows), f32),
                pltpu.VMEM((pages, page_rows, q_cols), bf16),
                pltpu.VMEM((all_pages, page_rows, 2 * kv_cols), bf16),
                pltpu.SemaphoreType.DMA((pages,)),
                pltpu.SemaphoreType.DMA((all_pages,)),
            ],
        ),
        out_shape=jax.ShapeDtypeStruct((all_pages, page_rows, q_cols + 2 * kv_cols), bf16),
        cost_estimate=pl.CostEstimate(
            flops=3 * q_heads * total_rows * total_rows * HD,
            bytes_accessed=12 * q_t.size,
            transcendentals=q_heads * total_rows * total_rows // 4,
        ),
        name="attend_backward",
    )(
        first_block, perm, *([grad_slots] * pages), q_t, k_rows, k_t, v_rows, o_t, lse, begin,
        cos_t, sin_t, cos_t, sin_t,
    )


def feed_kernel(
    ring, tile, own_rows, *refs
):
    grad_rows = refs[:ring]
    (
        weights, grads_t, rows_t, act_all, grads_all, mixed_all, grad_own,
    held, grads_held, acc_n, acc_m, first_part, arrived, outgoing, mixed_stage, final_stage,
    turned, load_sem, keep_sem, grad_sem, mixed_sem, final_sem,
    row_send, row_recv, sum_send, sum_recv, all_sem,
    ) = refs[ring:]
    me = lax.axis_index("tensor")
    right = lax.rem(me + 1, ring)
    left = lax.rem(me + ring - 1, ring)
    hidden = weights.shape[1] // 3
    tiles = hidden // tile

    barrier = pltpu.get_barrier_semaphore()
    for neighbour in (left, right):
        pl.semaphore_signal(barrier, inc=1, device_id={"tensor": neighbour}, device_id_type=MESH)
    pl.semaphore_wait(barrier, 2)

    load = pltpu.make_async_copy(own_rows, held.at[0], load_sem)
    load.start()

    def grad_load(s):
        return pltpu.make_async_copy(grad_rows[s], grads_held.at[s % 2], grad_sem.at[s % 2])

    def part_of(array, s):
        count = own_rows.shape[0]
        return array.at[:, pl.ds(pl.multiple_of(s * count, 128), count)]

    def grad_keep(s):
        return pltpu.make_async_copy(turned.at[1], part_of(grads_t, s), all_sem)

    grad_load(0).start()
    load.wait()

    def pass_rows(s):
        return pltpu.make_async_remote_copy(
            src_ref=held.at[s],
            dst_ref=held.at[s + 1],
            send_sem=row_send.at[s],
            recv_sem=row_recv.at[s],
            device_id={"tensor": right},
            device_id_type=MESH,
        )

    def pass_sum(s):
        return pltpu.make_async_remote_copy(
            src_ref=outgoing.at[s - 1],
            dst_ref=arrived.at[s - 1],
            send_sem=sum_send.at[s - 1],
            recv_sem=sum_recv.at[s - 1],
            device_id={"tensor": right},
            device_id_type=MESH,
        )

    def keep(s):
        return pltpu.make_async_copy(turned.at[0], part_of(rows_t, s), keep_sem)

    def mixed_store(s):
        return pltpu.make_async_copy(mixed_stage, mixed_all.at[s], mixed_sem)

    def chunk(s, carry):
        @pl.when(s > 0)
        def _():
            pass_rows(s - 1).wait_recv()

        @pl.when(s < ring - 1)
        def _():
            pass_rows(s).start()

        @pl.when(s > 0)
        def _():
            keep(s - 1).wait()
            grad_keep(s - 1).wait()

        turned[0] = held[s].T
        keep(s).start()
        for k in range(ring):

            @pl.when(s == k)
            def _(k=k):
                grad_load(k).wait()
                if k < ring - 1:
                    grad_load(k + 1).start()

        slot = lax.rem(s, 2)
        turned[1] = grads_held[slot].T
        grad_keep(s).start()
        acc_n[...] = jnp.zeros_like(acc_n)
        acc_m[...] = jnp.zeros_like(acc_m)

        def body(w_gate, w_up, w_down, act, grad_gate, grad_up):
            rows = held[s]
            gate = dot_nn(rows, w_gate[...])
            up = dot_nn(rows, w_up[...])
            grad_act = dot_nn(grads_held[slot], w_down[...])
            sig = 1.0 / (1.0 + jnp.exp(-gate))
            silu = gate * sig
            low_act = (silu * up).astype(bf16)
            low_up = (grad_act * silu).astype(bf16)
            low_gate = (grad_act * up * sig * (1.0 + gate * (1.0 - sig))).astype(bf16)
            act[...] = low_act
            grad_gate[...] = low_gate
            grad_up[...] = low_up
            acc_m[...] += dot_nt(low_act, w_down[...])
            acc_n[...] += dot_nt(low_gate, w_gate[...]) + dot_nt(low_up, w_up[...])

        width, count = own_rows.shape[1], own_rows.shape[0]
        pltpu.emit_pipeline(
            body,
            grid=(tiles,),
            in_specs=[
                pl.BlockSpec((width, tile), lambda k: (0, k)),
                pl.BlockSpec((width, tile), lambda k: (0, k + tiles)),
                pl.BlockSpec((width, tile), lambda k: (0, k + 2 * tiles)),
            ],
            out_specs=[
                pl.BlockSpec((count, tile), lambda k: (0, k)),
                pl.BlockSpec((count, tile), lambda k: (0, k)),
                pl.BlockSpec((count, tile), lambda k: (0, k + tiles)),
            ],
        )(weights, weights, weights, act_all.at[s], grads_all.at[s], grads_all.at[s])

        @pl.when(s > 0)
        def _():
            mixed_store(s - 1).wait()

        mixed_stage[...] = acc_m[...].astype(bf16)
        mixed_store(s).start()

        @pl.when(s == 0)
        def _():
            first_part[...] = acc_n[...]

        @pl.when(s == 1)
        def _():
            outgoing[0] = acc_n[...].astype(bf16)

        @pl.when(s > 1)
        def _():
            pass_sum(s - 1).wait_recv()
            outgoing[s - 1] = (acc_n[...] + arrived[s - 2].astype(f32)).astype(bf16)

        @pl.when(s > 0)
        def _():
            pass_sum(s).start()

        return carry

    lax.fori_loop(0, ring, chunk, 0)
    mixed_store(ring - 1).wait()
    pass_sum(ring - 1).wait_recv()
    final_stage[...] = (first_part[...] + arrived[ring - 2].astype(f32)).astype(bf16)
    final = pltpu.make_async_copy(final_stage, grad_own, final_sem)
    final.start()

    def settle(s, carry):
        @pl.when(s < ring - 1)
        def _():
            pass_rows(s).wait_send()

        @pl.when(s > 0)
        def _():
            pass_sum(s).wait_send()

        return carry

    lax.fori_loop(0, ring, settle, 0)
    keep(ring - 1).wait()
    grad_keep(ring - 1).wait()
    final.wait()


def feed(own_rows, grad_rows, weights, ring, tile=256, collective_id=7):
    count, width = own_rows.shape
    hidden = weights.shape[1] // 3
    any_spec = pl.BlockSpec(memory_space=pl.ANY)
    dma = pltpu.SemaphoreType.DMA
    return pl.pallas_call(
        functools.partial(feed_kernel, ring, min(tile, hidden)),
        out_shape=[
            jax.ShapeDtypeStruct((width, ring * count), bf16),
            jax.ShapeDtypeStruct((width, ring * count), bf16),
            jax.ShapeDtypeStruct((ring, count, hidden), bf16),
            jax.ShapeDtypeStruct((ring, count, 2 * hidden), bf16),
            jax.ShapeDtypeStruct((ring, count, width), bf16),
            jax.ShapeDtypeStruct((count, width), bf16),
        ],
        in_specs=[any_spec] * (2 + ring),
        out_specs=[any_spec] * 6,
        scratch_shapes=[
            pltpu.VMEM((ring, count, width), bf16),
            pltpu.VMEM((2, count, width), bf16),
            pltpu.VMEM((count, width), f32),
            pltpu.VMEM((count, width), f32),
            pltpu.VMEM((count, width), f32),
            pltpu.VMEM((ring - 1, count, width), bf16),
            pltpu.VMEM((ring - 1, count, width), bf16),
            pltpu.VMEM((count, width), bf16),
            pltpu.VMEM((count, width), bf16),
            pltpu.VMEM((2, width, count), bf16),
            dma,
            dma,
            dma((2,)),
            dma,
            dma,
            dma((ring - 1,)),
            dma((ring - 1,)),
            dma((ring - 1,)),
            dma((ring - 1,)),
            dma,
        ],
        compiler_params=pltpu.CompilerParams(
            collective_id=collective_id, has_side_effects=True, vmem_limit_bytes=64 * 1024 * 1024 - 65536,
        ),
        cost_estimate=pl.CostEstimate(
            flops=12 * ring * count * width * hidden,
            bytes_accessed=8 * ring * count * width,
            transcendentals=ring * count * hidden,
        ),
        name="feed_forward",
    )(own_rows, *grad_rows, weights)


def weigh_kernel(
    tp_count, dp_count, tile, grads, rows_t, grads_t, gate_up, act, slots, out,
    left, left_sem, own_sem, send, recv,
):
    count = dp_count * tp_count
    my_dp = lax.axis_index("dp")
    my_tp = lax.axis_index("tensor")
    me = my_dp * tp_count + my_tp
    page_rows = slots.shape[1]

    loads = [
        pltpu.make_async_copy(source, left.at[k], left_sem.at[k])
        for k, source in enumerate((rows_t, grads_t))
    ]
    for load in loads:
        load.start()

    barrier = pltpu.get_barrier_semaphore()

    def place(peer):
        return {"dp": lax.div(peer, tp_count), "tensor": lax.rem(peer, tp_count)}

    def greet(j, carry):
        peer = lax.rem(me + j, count)
        pl.semaphore_signal(barrier, inc=1, device_id=place(peer), device_id_type=MESH)
        return carry

    lax.fori_loop(1, count, greet, 0)
    pl.semaphore_wait(barrier, count - 1)

    home = slots.at[my_tp * dp_count + my_dp]

    def block(p_dp, p_tp):
        return grads.at[p_tp, pl.ds(p_dp * page_rows, page_rows), :]

    own = pltpu.make_async_copy(block(my_dp, my_tp), home, own_sem)
    own.start()

    def copy_to(j):
        peer = lax.rem(me + j, count)
        return pltpu.make_async_remote_copy(
            src_ref=block(lax.div(peer, tp_count), lax.rem(peer, tp_count)),
            dst_ref=home,
            send_sem=send.at[j],
            recv_sem=recv.at[j],
            device_id=place(peer),
            device_id_type=MESH,
        )

    def start(j, carry):
        copy_to(j).start()
        return carry

    def finish(j, carry):
        copy_to(j).wait()
        return carry

    lax.fori_loop(1, count, start, 0)

    width = rows_t.shape[0]
    step = min(512, width)

    def multiply(k, right, first):
        ring, rows, cols = right.shape

        def body(part, result):
            values = part[...].reshape(ring * rows, tile)
            for m in range(0, width, step):
                result[m : m + step, :] = dot_nn(left[k, m : m + step, :], values).astype(bf16)

        pltpu.emit_pipeline(
            body,
            grid=(cols // tile,),
            in_specs=[pl.BlockSpec((ring, rows, tile), lambda n: (0, 0, n))],
            out_specs=[pl.BlockSpec((width, tile), lambda n: (0, n + first))],
        )(right, out)

    loads[0].wait()
    multiply(0, gate_up, 0)
    loads[1].wait()
    multiply(1, act, gate_up.shape[2] // tile)
    own.wait()
    lax.fori_loop(1, count, finish, 0)


def weigh(grads, rows_t, grads_t, gate_up, act, tp_count, dp_count, collective_id):
    count = tp_count * dp_count
    cols = grads.shape[2]
    page_rows = grads.shape[1] // dp_count
    width, rows = rows_t.shape
    hidden = act.shape[2]
    any_spec = pl.BlockSpec(memory_space=pl.ANY)
    dma = pltpu.SemaphoreType.DMA
    return pl.pallas_call(
        functools.partial(weigh_kernel, tp_count, dp_count, min(512, hidden)),
        out_shape=[
            jax.ShapeDtypeStruct((count, page_rows, cols), bf16),
            jax.ShapeDtypeStruct((width, 3 * hidden), bf16),
        ],
        in_specs=[any_spec] * 5,
        out_specs=[any_spec] * 2,
        scratch_shapes=[
            pltpu.VMEM((2, width, rows), bf16),
            dma((2,)),
            dma,
            dma((count,)),
            dma((count,)),
        ],
        compiler_params=pltpu.CompilerParams(
            collective_id=collective_id, has_side_effects=True, vmem_limit_bytes=48 * 1024 * 1024
        ),
        cost_estimate=pl.CostEstimate(
            flops=6 * rows * width * hidden,
            bytes_accessed=2 * width * (2 * rows + 3 * hidden),
            transcendentals=0,
        ),
        name="weigh",
    )(grads, rows_t, grads_t, gate_up, act)


def flip(index, bit):
    return index + bit - 2 * bit * lax.rem(lax.div(index, bit), 2)


def collect_kernel(
    tp_count, dp_count, hops, shard, gains, chunk, out, gains_out, chunks_out,
    own_sem, ring_send, ring_recv, send, recv, gain_send, gain_recv, chunk_send, chunk_recv,
):
    my_dp = lax.axis_index("dp")
    my_tp = lax.axis_index("tensor")
    rows = shard.shape[0]
    half = rows // 2
    bits = [1 << b for b in reversed(range(dp_count.bit_length() - 1))]
    orders = [bits, bits[:-1][::-1] + bits[-1:]]
    steps = len(bits)

    barrier = pltpu.get_barrier_semaphore()
    for j in range(1, tp_count):
        pl.semaphore_signal(
            barrier, inc=1, device_id={"tensor": lax.rem(my_tp + j, tp_count)}, device_id_type=MESH
        )
    for j in range(1, dp_count):
        pl.semaphore_signal(
            barrier, inc=1, device_id={"dp": lax.rem(my_dp + j, dp_count)}, device_id_type=MESH
        )
    pl.semaphore_wait(barrier, tp_count + dp_count - 2)

    home = out.at[my_tp, pl.ds(my_dp * rows, rows), :]
    own = pltpu.make_async_copy(shard, home, own_sem.at[0])
    own.start()
    own_gain = pltpu.make_async_copy(gains, gains_out.at[my_dp], own_sem.at[1])
    own_gain.start()

    def across(j):
        return pltpu.make_async_remote_copy(
            src_ref=shard,
            dst_ref=home,
            send_sem=ring_send.at[j],
            recv_sem=ring_recv.at[j],
            device_id={"tensor": lax.rem(my_tp + j, tp_count)},
            device_id_type=MESH,
        )

    def gain_copy(j):
        return pltpu.make_async_remote_copy(
            src_ref=gains,
            dst_ref=gains_out.at[my_dp],
            send_sem=gain_send.at[j],
            recv_sem=gain_recv.at[j],
            device_id={"dp": lax.rem(my_dp + j, dp_count)},
            device_id_type=MESH,
        )

    def onward(hop):
        return pltpu.make_async_remote_copy(
            src_ref=chunk if hop == 0 else chunks_out.at[hop - 1],
            dst_ref=chunks_out.at[hop],
            send_sem=chunk_send.at[hop],
            recv_sem=chunk_recv.at[hop],
            device_id={"tensor": lax.rem(my_tp + 1, tp_count)},
            device_id_type=MESH,
        )

    def within(j, s, k, m):
        order = orders[s]
        owner = my_dp
        for b in range(k):
            if m >> b & 1:
                owner = flip(owner, order[b])
        block = out.at[
            lax.rem(my_tp - j + tp_count, tp_count), pl.ds(owner * rows + s * half, half), :
        ]
        at = (1 << k) - 1 + m
        return pltpu.make_async_remote_copy(
            src_ref=block,
            dst_ref=block,
            send_sem=send.at[j, s, at],
            recv_sem=recv.at[j, s, at],
            device_id={"dp": flip(my_dp, order[k])},
            device_id_type=MESH,
        )

    for j in range(1, tp_count):
        across(j).start()
    for j in range(1, dp_count):
        gain_copy(j).start()
    onward(0).start()
    own.wait()
    for phase in range(tp_count + steps):
        for k in reversed(range(steps + 1)):
            j = phase - k
            if not 0 <= j < tp_count:
                continue
            if k == 0:
                if j > 0:
                    across(j).wait_recv()
            else:
                for s in range(2):
                    for m in range(1 << (k - 1)):
                        within(j, s, k - 1, m).wait_recv()
            if k < steps:
                for s in range(2):
                    for m in range(1 << k):
                        within(j, s, k, m).start()
        if tp_count <= phase < tp_count + hops - 1:
            onward(phase - tp_count).wait_recv()
            onward(phase - tp_count + 1).start()
    for j in range(tp_count):
        if j > 0:
            across(j).wait_send()
        for s in range(2):
            for k in range(steps):
                for m in range(1 << k):
                    within(j, s, k, m).wait_send()
    own_gain.wait()
    for j in range(1, dp_count):
        gain_copy(j).wait()
    for hop in range(hops):
        if hop == hops - 1:
            onward(hop).wait_recv()
        onward(hop).wait_send()


def collect(shard, gains, chunk, tp_count, dp_count, hops, collective_id):
    rows, cols = shard.shape
    dma = pltpu.SemaphoreType.DMA
    vmem_spec = pl.BlockSpec(memory_space=pltpu.VMEM)
    any_spec = pl.BlockSpec(memory_space=pl.ANY)
    return pl.pallas_call(
        functools.partial(collect_kernel, tp_count, dp_count, hops),
        out_shape=[
            jax.ShapeDtypeStruct((tp_count, dp_count * rows, cols), shard.dtype),
            jax.ShapeDtypeStruct((dp_count,) + gains.shape, gains.dtype),
            jax.ShapeDtypeStruct((hops,) + chunk.shape, chunk.dtype),
        ],
        in_specs=[vmem_spec, vmem_spec, any_spec],
        out_specs=[any_spec] * 3,
        scratch_shapes=[
            dma((2,)),
            dma((tp_count,)),
            dma((tp_count,)),
            dma((tp_count, 2, dp_count - 1)),
            dma((tp_count, 2, dp_count - 1)),
            dma((dp_count,)),
            dma((dp_count,)),
            dma((hops,)),
            dma((hops,)),
        ],
        compiler_params=pltpu.CompilerParams(collective_id=collective_id, has_side_effects=True),
        cost_estimate=pl.CostEstimate(
            flops=0, bytes_accessed=16 * tp_count * dp_count * shard.size, transcendentals=0
        ),
        name="collect",
    )(shard, gains, chunk)


def spread_kernel(rows, weight, out):
    out[0] = dot_nn(rows[...], weight[0]).astype(out.dtype)


def spread(rows, weights, part, cols):
    shards, width, _ = weights.shape
    count = rows.shape[0]
    return pl.pallas_call(
        spread_kernel,
        grid=(shards,),
        in_specs=[
            pl.BlockSpec((count, width), lambda t: (0, 0)),
            pl.BlockSpec((1, width, cols), lambda t: (t, 0, part)),
        ],
        out_specs=pl.BlockSpec((1, count, cols), lambda t: (t, 0, 0)),
        out_shape=jax.ShapeDtypeStruct((shards, count, cols), bf16),
        cost_estimate=pl.CostEstimate(
            flops=2 * shards * count * width * cols,
            bytes_accessed=2 * shards * width * cols,
            transcendentals=0,
        ),
        name="spread",
    )(rows, weights)


def gather_kernel(part, weight, begin, out):
    @pl.when(pl.program_id(0) == 0)
    def _():
        out[...] = begin[...]

    out[...] += dot_nt(part[0], weight[0])


def gather_sum(parts, weights, part, begin):
    shards, count, cols = parts.shape
    width = weights.shape[1]
    return pl.pallas_call(
        gather_kernel,
        grid=(shards,),
        in_specs=[
            pl.BlockSpec((1, count, cols), lambda t: (t, 0, 0)),
            pl.BlockSpec((1, width, cols), lambda t: (t, 0, part)),
            pl.BlockSpec((count, width), lambda t: (0, 0)),
        ],
        out_specs=pl.BlockSpec((count, width), lambda t: (0, 0)),
        out_shape=jax.ShapeDtypeStruct((count, width), f32),
        cost_estimate=pl.CostEstimate(
            flops=2 * shards * count * width * cols,
            bytes_accessed=2 * shards * width * cols,
            transcendentals=0,
        ),
        name="gather_sum",
    )(parts, weights, begin)


def outer_kernel(rows, part, out, turned):
    @pl.when(pl.program_id(0) == 0)
    def _():
        turned[...] = rows[...].T

    out[...] = dot_nn(turned[...], part[0]).astype(out.dtype)


def outer(rows, parts):
    shards, count, cols = parts.shape
    width = rows.shape[1]
    return pl.pallas_call(
        outer_kernel,
        grid=(shards,),
        in_specs=[
            pl.BlockSpec((count, width), lambda t: (0, 0)),
            pl.BlockSpec((1, count, cols), lambda t: (t, 0, 0)),
        ],
        out_specs=pl.BlockSpec((width, cols), lambda t: (0, t)),
        out_shape=jax.ShapeDtypeStruct((width, shards * cols), bf16),
        scratch_shapes=[pltpu.VMEM((width, count), bf16)],
        cost_estimate=pl.CostEstimate(
            flops=2 * shards * count * width * cols,
            bytes_accessed=2 * shards * width * cols,
            transcendentals=0,
        ),
        name="outer",
    )(rows, parts)


def rms_scale(hidden):
    return lax.rsqrt(jnp.mean(hidden * hidden, axis=1, keepdims=True) + epsilon)


def norm_back(grad_norm, hidden, scale_rows, gain):
    normed = hidden * scale_rows
    gain_part = jnp.sum(grad_norm * normed, axis=0)
    inner = grad_norm * gain
    grad_hidden = scale_rows * (inner - normed * jnp.mean(inner * normed, axis=1, keepdims=True))
    return (grad_hidden, gain_part)


def after(value, other):
    return lax.optimization_barrier((value, other))[0]


def local(
    tokens,
    upstream,
    lengths,
    positions,
    pages,
    attn_gain,
    w_query,
    w_key,
    w_value,
    w_out,
    mlp_gain,
    w_gate,
    w_up,
    w_down,
):
    dp_count = lax.axis_size("dp")
    tp_count = lax.axis_size("tensor")
    dp_index = lax.axis_index("dp")
    tp_index = lax.axis_index("tensor")
    tok_dev, width = tokens.shape
    tok_group = tok_dev * tp_count
    page_rows = tok_dev // dp_count
    group_pages = tp_count * dp_count
    page_count = pages.shape[0]
    device = dp_index * tp_count + tp_index
    everyone = ("tensor", "dp")

    local_ids = jnp.arange(dp_count, dtype=jnp.int32)
    inverse = (
        jnp.zeros((page_count,), jnp.int32).at[pages].set(jnp.arange(page_count, dtype=jnp.int32))
    )
    dealt = lax.dynamic_slice_in_dim(inverse, device * dp_count, dp_count)
    dest_group = dealt // group_pages
    send_order = jnp.zeros((dp_count,), jnp.int32).at[dest_group].set(local_ids)
    group_sources = lax.dynamic_slice_in_dim(pages, dp_index * group_pages, group_pages)
    perm = (
        (jnp.arange(group_pages, dtype=jnp.int32) // dp_count) * dp_count
        + group_sources // group_pages
    ).astype(jnp.int32)

    def reorder(rows, order):
        blocks = rows.reshape(dp_count, page_rows, rows.shape[1])
        return jnp.take(blocks, order, axis=0).reshape(rows.shape)

    hidden_in = reorder(tokens, send_order).astype(f32)
    grad_top = reorder(upstream, send_order).astype(f32)
    seq_lens = lengths[0]
    seq_ends = jnp.cumsum(seq_lens)
    place = (jnp.take(dealt, send_order) % group_pages) * page_rows
    place_rows = (place[:, None] + jnp.arange(page_rows, dtype=jnp.int32)[None, :]).reshape(-1)
    valid_rows = (place_rows < seq_ends[-1]).astype(f32)[:, None]

    row_ids = jnp.arange(tok_group, dtype=jnp.int32)
    begin = jnp.max(
        jnp.where(row_ids[:, None] >= seq_ends[None, :], seq_ends[None, :], 0), axis=1
    ).astype(jnp.int32)
    block_len = min(block_rows, tok_group)
    first_block = begin[::block_len] // block_len
    begin = begin[None, :]
    inverse_freq = theta_base ** (-(jnp.arange(HALF, dtype=f32) * 2.0) / HD)
    angles = inverse_freq[:, None] * positions.astype(f32)
    cos_t, sin_t = jnp.cos(angles), jnp.sin(angles)

    q_cols, kv_cols = w_query.shape[1], w_key.shape[1]
    kv_heads = kv_cols // HD
    per_group = q_cols // kv_cols
    group_q = per_group * HD
    groups = range(kv_heads)
    qkv_shard = jnp.concatenate(
        [
            part
            for g in groups
            for part in (
                w_query[:, g * group_q : (g + 1) * group_q],
                w_key[:, g * HD : (g + 1) * HD],
                w_value[:, g * HD : (g + 1) * HD],
            )
        ],
        axis=1,
    )

    def gather_all(shard):
        full = lax.all_gather(shard, everyone, axis=0, tiled=False)
        return full.reshape(tp_count, dp_count * shard.shape[0], shard.shape[1])

    def trade(value):
        blocks = value.reshape(group_pages, page_rows, value.shape[-1])
        return lax.all_to_all(blocks, everyone, split_axis=0, concat_axis=0, tiled=True)

    def trade_back(value):
        return trade(value).reshape(tp_count, tok_dev, value.shape[-1])

    ring_next = [(t, (t + 1) % tp_count) for t in range(tp_count)]

    def pass_on(value):
        return lax.ppermute(value, "tensor", ring_next)

    grad_out = grad_top * valid_rows
    grad_chunks = [grad_out.astype(bf16)]
    mlp_shard = jnp.concatenate([w_gate, w_up, w_down.T], axis=1)
    w_mlp = lax.all_gather(mlp_shard, "dp", axis=0, tiled=True)
    hops = min(2, tp_count - 1)
    w_qkv, gains, got_chunks = collect(
        qkv_shard, jnp.stack([attn_gain, mlp_gain]), grad_chunks[0], tp_count, dp_count, hops, 1
    )
    grad_chunks += [got_chunks[hop] for hop in range(hops)]
    gains = gains.transpose(1, 0, 2).reshape(2, -1).astype(f32)
    gain_one, gain_two = gains[0], gains[1]

    scale_one = rms_scale(hidden_in)
    normed_one = (hidden_in * scale_one * gain_one).astype(bf16)
    qkv, slots = [], []
    for g in groups:
        qkv.append(spread(normed_one, w_qkv, g, group_q + 2 * HD))
        slots.append(trade(qkv[g]))
    out_shard = with_layout_constraint(w_out.T, Layout(major_to_minor=(0, 1)))
    w_out_t = gather_all(after(out_shard, w_qkv))
    saved, mixed = [], []
    last = qkv[-1]
    for hop in range(hops + 1, tp_count):
        grad_chunks.append(pass_on(after(grad_chunks[-1], slots[0])))
    for g in groups:
        if g == len(groups) - 1:
            last = (last, w_mlp, grad_chunks[-1])
        q_t, k_t, k_rows, v_t, v_rows = prepare(
            after(slots[g], last), perm, cos_t, sin_t, per_group, 1
        )
        o_t, lse, last = attend_forward(
            q_t, k_rows, v_t, begin, first_block, perm, page_rows, block_len
        )
        saved.append((q_t, k_rows, k_t, v_rows, o_t, lse))
        mixed.append(trade_back(last))
    hidden_mid = hidden_in
    for g in groups:
        hidden_mid = gather_sum(mixed[g], w_out_t, g, hidden_mid)

    scale_two = rms_scale(hidden_mid)
    normed_two = (hidden_mid * scale_two * gain_two).astype(bf16)
    grads_t, rows_t, inner_act, grad_gate_up, partial_two, grad_normed_two = feed(
        normed_two, grad_chunks, w_mlp, tp_count
    )
    grad_normed_two = grad_normed_two.astype(f32)
    grad_mid_norm, gain_two_part = norm_back(grad_normed_two, hidden_mid, scale_two, gain_two)
    grad_mid = grad_out + grad_mid_norm

    def add_on(arrived, s):
        return (arrived.astype(f32) + partial_two[s].astype(f32)).astype(bf16)

    def reduce_dp(grad):
        return lax.psum_scatter(grad.astype(bf16), "dp", scatter_dimension=0, tiled=True)

    def reduce_tensor(value):
        cols = value.shape[1] // tp_count
        total = lax.dynamic_slice_in_dim(value, tp_index * cols, cols, 1).astype(f32)
        for s in range(1, tp_count):
            target = lax.rem(tp_index + s, tp_count)
            block = lax.dynamic_slice_in_dim(value, target * cols, cols, 1)
            pairs = [(t, (t + s) % tp_count) for t in range(tp_count)]
            total = total + lax.ppermute(block, "tensor", pairs).astype(f32)
        return total

    grad_z = grad_mid.astype(bf16)
    grad_wout = outer(grad_z, jnp.concatenate(mixed, axis=2))
    sum_out = reduce_dp(grad_wout)
    grad_slots, grad_wmlp = weigh(
        spread(after(grad_z, grad_wout), w_out_t, 0, q_cols),
        rows_t, grads_t, grad_gate_up, inner_act, tp_count, dp_count, 2,
    )
    sum_mlp = reduce_dp(grad_wmlp)
    branch_two = pass_on(after(partial_two[1], grad_slots))
    grad_qkv = []
    for g in groups:
        q_t, k_rows, k_t, v_rows, o_t, lse = saved[g]
        back = attend_backward(
            grad_slots if g == 0 else after(grad_slots, (back, sum_out)), g, q_t, k_rows, k_t,
            v_rows, o_t, lse, begin, cos_t, sin_t, first_block, perm, page_rows, block_len,
        )
        grad_qkv.append(trade_back(after(back, branch_two) if g == len(groups) - 1 else back))
    hidden = sum_mlp.shape[1] // 3
    grad_wqkv = outer(after(normed_one, sum_mlp), jnp.concatenate(grad_qkv, axis=2))
    sum_qkv = reduce_tensor(reduce_dp(grad_wqkv))
    each = group_q + 2 * HD
    sum_qkv = [sum_qkv[:, g * each : (g + 1) * each] for g in groups]
    branch_two = add_on(after(branch_two, grad_qkv[-1]), 2)
    grad_normed_one = jnp.zeros((tok_dev, width), f32)
    for g in groups:
        grad_normed_one = gather_sum(after(grad_qkv[g], grad_wqkv), w_qkv, g, grad_normed_one)
    for s in range(3, tp_count):
        branch_two = add_on(after(pass_on(branch_two), grad_normed_one), s)
    branch_two = pass_on(branch_two)
    sum_out = reduce_tensor(sum_out)
    result = (
        (after(hidden_mid, back) + branch_two.astype(f32) + partial_two[0].astype(f32)) * valid_rows
    ).astype(bf16)
    grad_in_norm, gain_one_part = norm_back(grad_normed_one, hidden_in, scale_one, gain_one)
    grad_in = (grad_mid + grad_in_norm).astype(bf16)

    gain_parts = jnp.stack([gain_one_part, gain_two_part]).reshape(2, dp_count, -1)
    gain_parts = jnp.broadcast_to(
        gain_parts.transpose(1, 0, 2)[None], (tp_count, dp_count, 2, gain_parts.shape[2])
    ).reshape(group_pages, 2, -1)
    gain_sums = jnp.sum(
        lax.all_to_all(gain_parts, everyone, split_axis=0, concat_axis=0, tiled=True), axis=0
    )
    return (
        reorder(result, dest_group),
        reorder(grad_in, dest_group),
        gain_sums[0],
        jnp.concatenate([part[:, :group_q] for part in sum_qkv], axis=1),
        jnp.concatenate([part[:, group_q : group_q + HD] for part in sum_qkv], axis=1),
        jnp.concatenate([part[:, group_q + HD :] for part in sum_qkv], axis=1),
        sum_out.T,
        gain_sums[1],
        sum_mlp[:, :hidden].astype(f32),
        sum_mlp[:, hidden : 2 * hidden].astype(f32),
        sum_mlp[:, 2 * hidden :].astype(f32).T,
    )


def solution(mesh):
    rows = P(("dp", "tensor"), None)
    weight = P("dp", "tensor")
    weight_t = P("tensor", "dp")
    return jax.shard_map(
        local,
        mesh=mesh,
        in_specs=(
            rows,
            rows,
            P("dp", None),
            P("dp", None),
            P(),
            P("dp"),
            weight,
            weight,
            weight,
            weight_t,
            P("dp"),
            weight,
            weight,
            weight_t,
        ),
        out_specs=(
            rows,
            rows,
            P("dp"),
            weight,
            weight,
            weight,
            weight_t,
            P("dp"),
            weight,
            weight,
            weight_t,
        ),
        check_vma=False,
    )
```

```python
import functools

import jax
import jax.numpy as jnp
from jax import lax
from jax.experimental import pallas as pl
from jax.experimental.pallas import tpu as pltpu
from jax.sharding import PartitionSpec as P

HD = 64
HALF = HD // 2

epsilon = 1e-05
theta_base = 500000.0
masked_score = -1e30
score_scale = HD**-0.5
block_rows = 256
MESH = pl.DeviceIdType.MESH
f32 = jnp.float32
bf16 = jnp.bfloat16


def dot_nn(left, right):
    return lax.dot_general(left, right, (((1,), (0,)), ((), ())), preferred_element_type=f32)


def dot_nt(left, right):
    return lax.dot_general(left, right, (((1,), (1,)), ((), ())), preferred_element_type=f32)


def dot_tn(left, right):
    return lax.dot_general(left, right, (((0,), (0,)), ((), ())), preferred_element_type=f32)


def prep_kernel(pages_per, q_heads, kv_heads, perm, *refs):
    page_refs = refs[:pages_per]
    cos_ref, sin_ref, q_t, k_t, k_rows, v_t, v_rows = refs[pages_per:]
    rows = jnp.concatenate([r[0].astype(f32) for r in page_refs], axis=0)
    turned = rows.T
    cos, sin = cos_ref[...], sin_ref[...]

    def rope(base):
        first, second = turned[base : base + HALF], turned[base + HALF : base + HD]
        return jnp.concatenate([first * cos - second * sin, second * cos + first * sin], axis=0)

    for h in range(q_heads):
        roped = rope(h * HD).astype(bf16)
        q_t[h * HD : (h + 1) * HD, :] = (roped.astype(f32) * score_scale).astype(bf16)
    k_base = q_heads * HD
    v_base = k_base + kv_heads * HD
    for g in range(kv_heads):
        roped = rope(k_base + g * HD)
        k_t[g * HD : (g + 1) * HD, :] = roped.astype(bf16)
        k_rows[g] = roped.T.astype(bf16)
        v_t[g * HD : (g + 1) * HD, :] = turned[v_base + g * HD : v_base + (g + 1) * HD].astype(bf16)
        v_rows[g] = rows[:, v_base + g * HD : v_base + (g + 1) * HD].astype(bf16)


def prepare(slots, perm, cos_t, sin_t, q_heads, kv_heads):
    page_rows, cols = slots.shape[1:]
    total_rows = slots.shape[0] * page_rows
    lanes = min(256, total_rows)
    pages_per = lanes // page_rows

    def page_spec(a):
        return pl.BlockSpec(
            (1, page_rows, cols), lambda i, perm_ref, a=a: (perm_ref[i * pages_per + a], 0, 0)
        )

    table = pl.BlockSpec((HALF, lanes), lambda i, perm_ref: (0, i))
    return pl.pallas_call(
        functools.partial(prep_kernel, pages_per, q_heads, kv_heads),
        grid_spec=pltpu.PrefetchScalarGridSpec(
            num_scalar_prefetch=1,
            grid=(total_rows // lanes,),
            in_specs=[page_spec(a) for a in range(pages_per)] + [table, table],
            out_specs=[
                pl.BlockSpec((q_heads * HD, lanes), lambda i, perm_ref: (0, i)),
                pl.BlockSpec((kv_heads * HD, lanes), lambda i, perm_ref: (0, i)),
                pl.BlockSpec((kv_heads, lanes, HD), lambda i, perm_ref: (0, i, 0)),
                pl.BlockSpec((kv_heads * HD, lanes), lambda i, perm_ref: (0, i)),
                pl.BlockSpec((kv_heads, lanes, HD), lambda i, perm_ref: (0, i, 0)),
            ],
        ),
        out_shape=[
            jax.ShapeDtypeStruct((q_heads * HD, total_rows), bf16),
            jax.ShapeDtypeStruct((kv_heads * HD, total_rows), bf16),
            jax.ShapeDtypeStruct((kv_heads, total_rows, HD), bf16),
            jax.ShapeDtypeStruct((kv_heads * HD, total_rows), bf16),
            jax.ShapeDtypeStruct((kv_heads, total_rows, HD), bf16),
        ],
        cost_estimate=pl.CostEstimate(
            flops=8 * slots.size, bytes_accessed=6 * slots.size, transcendentals=0
        ),
        name="prepare",
    )(perm, *([slots] * pages_per), cos_t, sin_t)


def block_bias(i, j, begin_row, block_len):
    keys = j * block_len + lax.broadcasted_iota(jnp.int32, (block_len, block_len), 0)
    queries = i * block_len + lax.broadcasted_iota(jnp.int32, (block_len, block_len), 1)
    allowed = (keys >= begin_row) & (keys <= queries)
    return jnp.where(allowed, 0.0, masked_score)


def forward_kernel(
    q_heads, kv_heads, page_rows, first_block, perm,
    q_t, k_rows, v_t, begin, o_t, lse, o_slots, acc, top, total, stage, sems,
):
    i = pl.program_id(0)
    block_len = q_t.shape[1]
    per_group = q_heads // kv_heads
    acc[...] = jnp.zeros_like(acc)
    top[...] = jnp.full_like(top, masked_score)
    total[...] = jnp.zeros_like(total)
    begin_row = begin[...]

    def visit(j, carry):
        bias = block_bias(i, j, begin_row, block_len)
        at = pl.ds(pl.multiple_of(j * block_len, block_len), block_len)
        for h in range(q_heads):
            g = h // per_group
            span = slice(h * HD, (h + 1) * HD)
            scores = dot_nn(k_rows[g, at, :], q_t[span, :]) + bias
            old = top[h : h + 1, :]
            new = jnp.maximum(old, jnp.max(scores, axis=0, keepdims=True))
            weights = jnp.exp(scores - new)
            fade = jnp.exp(old - new)
            total[h : h + 1, :] = total[h : h + 1, :] * fade + jnp.sum(
                weights, axis=0, keepdims=True
            )
            top[h : h + 1, :] = new
            acc[span, :] = acc[span, :] * fade + dot_nn(
                v_t[g * HD : (g + 1) * HD, at], weights.astype(bf16)
            )
        return carry

    lax.fori_loop(first_block[i], i + 1, visit, 0)
    lse[...] = top[...] + jnp.log(total[...])
    scaled = [
        acc[h * HD : (h + 1) * HD, :] / total[h : h + 1, :] for h in range(q_heads)
    ]
    mixed = jnp.concatenate(scaled, axis=0)
    o_t[...] = mixed.astype(bf16)
    pages = block_len // page_rows
    stage[...] = mixed.T.astype(bf16).reshape(pages, page_rows, q_heads * HD)
    copies = [
        pltpu.make_async_copy(stage.at[a], o_slots.at[perm[i * pages + a]], sems.at[a])
        for a in range(pages)
    ]
    for copy in copies:
        copy.start()
    for copy in copies:
        copy.wait()


def attend_forward(q_t, k_rows, v_t, begin, first_block, perm, page_rows, block_len):
    total_rows = q_t.shape[1]
    kv_heads = k_rows.shape[0]
    q_heads = q_t.shape[0] // HD
    pages = block_len // page_rows
    return pl.pallas_call(
        functools.partial(forward_kernel, q_heads, kv_heads, page_rows),
        grid_spec=pltpu.PrefetchScalarGridSpec(
            num_scalar_prefetch=2,
            grid=(total_rows // block_len,),
            in_specs=[
                pl.BlockSpec((q_heads * HD, block_len), lambda i, *_: (0, i)),
                pl.BlockSpec((kv_heads, total_rows, HD), lambda i, *_: (0, 0, 0)),
                pl.BlockSpec((kv_heads * HD, total_rows), lambda i, *_: (0, 0)),
                pl.BlockSpec((1, block_len), lambda i, *_: (0, i)),
            ],
            out_specs=[
                pl.BlockSpec((q_heads * HD, block_len), lambda i, *_: (0, i)),
                pl.BlockSpec((q_heads, block_len), lambda i, *_: (0, i)),
                pl.BlockSpec(memory_space=pl.ANY),
            ],
            scratch_shapes=[
                pltpu.VMEM((q_heads * HD, block_len), f32),
                pltpu.VMEM((q_heads, block_len), f32),
                pltpu.VMEM((q_heads, block_len), f32),
                pltpu.VMEM((pages, page_rows, q_heads * HD), bf16),
                pltpu.SemaphoreType.DMA((pages,)),
            ],
        ),
        out_shape=[
            jax.ShapeDtypeStruct((q_heads * HD, total_rows), bf16),
            jax.ShapeDtypeStruct((q_heads, total_rows), f32),
            jax.ShapeDtypeStruct((total_rows // page_rows, page_rows, q_heads * HD), bf16),
        ],
        cost_estimate=pl.CostEstimate(
            flops=q_heads * total_rows * total_rows * HD,
            bytes_accessed=8 * q_t.size,
            transcendentals=q_heads * total_rows * total_rows // 4,
        ),
        name="attend_forward",
    )(first_block, perm, q_t, k_rows, v_t, begin)


def backward_kernel(
    q_heads, kv_heads, page_rows, pages, first_block, perm, *refs
):
    grad_pages = refs[:pages]
    (
        q_t, k_rows, k_t, v_rows, o_t, lse, begin, cos_ref, sin_ref, cos_all, sin_all,
        out, grad_q, grad_k, grad_v, stage, kv_stage, sems, kv_sems,
    ) = refs[pages:]
    i = pl.program_id(0)
    steps = pl.num_programs(0)
    block_len = q_t.shape[1]
    per_group = q_heads // kv_heads
    q_cols = q_heads * HD
    kv_cols = kv_heads * HD

    @pl.when(i == 0)
    def _():
        grad_k[...] = jnp.zeros_like(grad_k)
        grad_v[...] = jnp.zeros_like(grad_v)

    grad_rows = jnp.concatenate([r[0].astype(f32) for r in grad_pages], axis=0)
    grad_t = grad_rows.T
    grad_low = grad_t.astype(bf16)
    inner = [
        jnp.sum(
            grad_t[h * HD : (h + 1) * HD] * o_t[h * HD : (h + 1) * HD, :].astype(f32),
            axis=0,
            keepdims=True,
        )
        for h in range(q_heads)
    ]
    grad_q[...] = jnp.zeros_like(grad_q)
    begin_row = begin[...]

    def visit(j, carry):
        bias = block_bias(i, j, begin_row, block_len)
        at = pl.ds(pl.multiple_of(j * block_len, block_len), block_len)
        for g in range(kv_heads):
            kv_span = slice(g * HD, (g + 1) * HD)
            keys, vals, keys_t = k_rows[g, at, :], v_rows[g, at, :], k_t[kv_span, at]
            add_k = jnp.zeros((HD, block_len), f32)
            add_v = jnp.zeros((HD, block_len), f32)
            for h in range(g * per_group, (g + 1) * per_group):
                span = slice(h * HD, (h + 1) * HD)
                queries = q_t[span, :]
                probs = jnp.exp(dot_nn(keys, queries) + bias - lse[h : h + 1, :])
                grad_h = grad_low[span]
                grad_probs = dot_nn(vals, grad_h)
                grad_scores = (probs * (grad_probs - inner[h])).astype(bf16)
                add_v = add_v + dot_nt(grad_h, probs.astype(bf16))
                add_k = add_k + dot_nt(queries, grad_scores)
                grad_q[span, :] = grad_q[span, :] + dot_nn(keys_t, grad_scores)
            grad_k[kv_span, at] = grad_k[kv_span, at] + add_k
            grad_v[kv_span, at] = grad_v[kv_span, at] + add_v
        return carry

    lax.fori_loop(first_block[i], i + 1, visit, 0)

    def unrope(value, cos, sin):
        first, second = value[:HALF], value[HALF:]
        return jnp.concatenate([first * cos + second * sin, second * cos - first * sin], axis=0)

    cos, sin = cos_ref[...], sin_ref[...]
    parts = [
        unrope(grad_q[h * HD : (h + 1) * HD, :] * score_scale, cos, sin) for h in range(q_heads)
    ]
    stage[...] = jnp.concatenate(parts, axis=0).T.astype(bf16).reshape(pages, page_rows, q_cols)
    copies = [
        pltpu.make_async_copy(
            stage.at[a], out.at[perm[i * pages + a], :, pl.ds(0, q_cols)], sems.at[a]
        )
        for a in range(pages)
    ]
    for copy in copies:
        copy.start()
    for copy in copies:
        copy.wait()

    @pl.when(i == steps - 1)
    def _():
        all_pages = kv_stage.shape[0]
        cos, sin = cos_all[...], sin_all[...]
        parts = [unrope(grad_k[g * HD : (g + 1) * HD, :], cos, sin) for g in range(kv_heads)]
        both = jnp.concatenate(parts + [grad_v[...]], axis=0)
        kv_stage[...] = both.T.astype(bf16).reshape(all_pages, page_rows, 2 * kv_cols)
        copies = [
            pltpu.make_async_copy(
                kv_stage.at[a], out.at[perm[a], :, pl.ds(q_cols, 2 * kv_cols)], kv_sems.at[a]
            )
            for a in range(all_pages)
        ]
        for copy in copies:
            copy.start()
        for copy in copies:
            copy.wait()


def attend_backward(
    grad_slots, part, q_t, k_rows, k_t, v_rows, o_t, lse, begin, cos_t, sin_t, first_block, perm,
    page_rows, block_len,
):
    total_rows = q_t.shape[1]
    kv_heads = k_rows.shape[0]
    q_heads = q_t.shape[0] // HD
    pages = block_len // page_rows
    all_pages = total_rows // page_rows
    q_cols = q_heads * HD
    kv_cols = kv_heads * HD

    def page_spec(a):
        return pl.BlockSpec(
            (1, page_rows, q_cols),
            lambda i, first_ref, perm_ref, a=a: (perm_ref[i * pages + a], 0, part),
        )

    def whole(shape):
        return pl.BlockSpec(shape, lambda i, *_: (0,) * len(shape))

    def column(rows):
        return pl.BlockSpec((rows, block_len), lambda i, *_: (0, i))

    return pl.pallas_call(
        functools.partial(backward_kernel, q_heads, kv_heads, page_rows, pages),
        grid_spec=pltpu.PrefetchScalarGridSpec(
            num_scalar_prefetch=2,
            grid=(total_rows // block_len,),
            in_specs=[page_spec(a) for a in range(pages)]
            + [
                column(q_cols),
                whole((kv_heads, total_rows, HD)),
                whole((kv_cols, total_rows)),
                whole((kv_heads, total_rows, HD)),
                column(q_cols),
                column(q_heads),
                column(1),
                column(HALF),
                column(HALF),
                whole((HALF, total_rows)),
                whole((HALF, total_rows)),
            ],
            out_specs=pl.BlockSpec(memory_space=pl.ANY),
            scratch_shapes=[
                pltpu.VMEM((q_cols, block_len), f32),
                pltpu.VMEM((kv_cols, total_rows), f32),
                pltpu.VMEM((kv_cols, total_rows), f32),
                pltpu.VMEM((pages, page_rows, q_cols), bf16),
                pltpu.VMEM((all_pages, page_rows, 2 * kv_cols), bf16),
                pltpu.SemaphoreType.DMA((pages,)),
                pltpu.SemaphoreType.DMA((all_pages,)),
            ],
        ),
        out_shape=jax.ShapeDtypeStruct((all_pages, page_rows, q_cols + 2 * kv_cols), bf16),
        cost_estimate=pl.CostEstimate(
            flops=3 * q_heads * total_rows * total_rows * HD,
            bytes_accessed=12 * q_t.size,
            transcendentals=q_heads * total_rows * total_rows // 4,
        ),
        name="attend_backward",
    )(
        first_block, perm, *([grad_slots] * pages), q_t, k_rows, k_t, v_rows, o_t, lse, begin,
        cos_t, sin_t, cos_t, sin_t,
    )


def feed_kernel(
    ring, tile, own_rows, *refs
):
    grad_rows = refs[:ring]
    (
        weights, grads_t, rows_t, act_all, grads_all, mixed_all, grad_own,
    held, grads_held, acc_n, acc_m, first_part, arrived, outgoing, mixed_stage, final_stage,
    turned, load_sem, keep_sem, grad_sem, mixed_sem, final_sem,
    row_send, row_recv, sum_send, sum_recv, all_sem,
    ) = refs[ring:]
    me = lax.axis_index("tensor")
    right = lax.rem(me + 1, ring)
    left = lax.rem(me + ring - 1, ring)
    hidden = weights.shape[1] // 3
    tiles = hidden // tile

    barrier = pltpu.get_barrier_semaphore()
    for neighbour in (left, right):
        pl.semaphore_signal(barrier, inc=1, device_id={"tensor": neighbour}, device_id_type=MESH)
    pl.semaphore_wait(barrier, 2)

    load = pltpu.make_async_copy(own_rows, held.at[0], load_sem)
    load.start()

    def grad_load(s):
        return pltpu.make_async_copy(grad_rows[s], grads_held.at[s % 2], grad_sem.at[s % 2])

    def part_of(array, s):
        count = own_rows.shape[0]
        return array.at[:, pl.ds(pl.multiple_of(s * count, 128), count)]

    def grad_keep(s):
        return pltpu.make_async_copy(turned.at[1], part_of(grads_t, s), all_sem)

    grad_load(0).start()
    load.wait()

    def pass_rows(s):
        return pltpu.make_async_remote_copy(
            src_ref=held.at[s],
            dst_ref=held.at[s + 1],
            send_sem=row_send.at[s],
            recv_sem=row_recv.at[s],
            device_id={"tensor": right},
            device_id_type=MESH,
        )

    def pass_sum(s):
        return pltpu.make_async_remote_copy(
            src_ref=outgoing.at[s - 1],
            dst_ref=arrived.at[s - 1],
            send_sem=sum_send.at[s - 1],
            recv_sem=sum_recv.at[s - 1],
            device_id={"tensor": right},
            device_id_type=MESH,
        )

    def keep(s):
        return pltpu.make_async_copy(turned.at[0], part_of(rows_t, s), keep_sem)

    def mixed_store(s):
        return pltpu.make_async_copy(mixed_stage, mixed_all.at[s], mixed_sem)

    def chunk(s, carry):
        @pl.when(s > 0)
        def _():
            pass_rows(s - 1).wait_recv()

        @pl.when(s < ring - 1)
        def _():
            pass_rows(s).start()

        @pl.when(s > 0)
        def _():
            keep(s - 1).wait()
            grad_keep(s - 1).wait()

        turned[0] = held[s].T
        keep(s).start()
        for k in range(ring):

            @pl.when(s == k)
            def _(k=k):
                grad_load(k).wait()
                if k < ring - 1:
                    grad_load(k + 1).start()

        slot = lax.rem(s, 2)
        turned[1] = grads_held[slot].T
        grad_keep(s).start()
        acc_n[...] = jnp.zeros_like(acc_n)
        acc_m[...] = jnp.zeros_like(acc_m)

        def body(w_gate, w_up, w_down, act, grad_gate, grad_up):
            rows = held[s]
            gate = dot_nn(rows, w_gate[...])
            up = dot_nn(rows, w_up[...])
            grad_act = dot_nn(grads_held[slot], w_down[...])
            sig = 1.0 / (1.0 + jnp.exp(-gate))
            silu = gate * sig
            low_act = (silu * up).astype(bf16)
            low_up = (grad_act * silu).astype(bf16)
            low_gate = (grad_act * up * sig * (1.0 + gate * (1.0 - sig))).astype(bf16)
            act[...] = low_act
            grad_gate[...] = low_gate
            grad_up[...] = low_up
            acc_m[...] += dot_nt(low_act, w_down[...])
            acc_n[...] += dot_nt(low_gate, w_gate[...]) + dot_nt(low_up, w_up[...])

        width, count = own_rows.shape[1], own_rows.shape[0]
        pltpu.emit_pipeline(
            body,
            grid=(tiles,),
            in_specs=[
                pl.BlockSpec((width, tile), lambda k: (0, k)),
                pl.BlockSpec((width, tile), lambda k: (0, k + tiles)),
                pl.BlockSpec((width, tile), lambda k: (0, k + 2 * tiles)),
            ],
            out_specs=[
                pl.BlockSpec((count, tile), lambda k: (0, k)),
                pl.BlockSpec((count, tile), lambda k: (0, k)),
                pl.BlockSpec((count, tile), lambda k: (0, k + tiles)),
            ],
        )(weights, weights, weights, act_all.at[s], grads_all.at[s], grads_all.at[s])

        @pl.when(s > 0)
        def _():
            mixed_store(s - 1).wait()

        mixed_stage[...] = acc_m[...].astype(bf16)
        mixed_store(s).start()

        @pl.when(s == 0)
        def _():
            first_part[...] = acc_n[...]

        @pl.when(s == 1)
        def _():
            outgoing[0] = acc_n[...].astype(bf16)

        @pl.when(s > 1)
        def _():
            pass_sum(s - 1).wait_recv()
            outgoing[s - 1] = (acc_n[...] + arrived[s - 2].astype(f32)).astype(bf16)

        @pl.when(s > 0)
        def _():
            pass_sum(s).start()

        return carry

    lax.fori_loop(0, ring, chunk, 0)
    mixed_store(ring - 1).wait()
    pass_sum(ring - 1).wait_recv()
    final_stage[...] = (first_part[...] + arrived[ring - 2].astype(f32)).astype(bf16)
    final = pltpu.make_async_copy(final_stage, grad_own, final_sem)
    final.start()

    def settle(s, carry):
        @pl.when(s < ring - 1)
        def _():
            pass_rows(s).wait_send()

        @pl.when(s > 0)
        def _():
            pass_sum(s).wait_send()

        return carry

    lax.fori_loop(0, ring, settle, 0)
    keep(ring - 1).wait()
    grad_keep(ring - 1).wait()
    final.wait()


def feed(own_rows, grad_rows, weights, ring, tile=256, collective_id=7):
    count, width = own_rows.shape
    hidden = weights.shape[1] // 3
    any_spec = pl.BlockSpec(memory_space=pl.ANY)
    dma = pltpu.SemaphoreType.DMA
    return pl.pallas_call(
        functools.partial(feed_kernel, ring, min(tile, hidden)),
        out_shape=[
            jax.ShapeDtypeStruct((width, ring * count), bf16),
            jax.ShapeDtypeStruct((width, ring * count), bf16),
            jax.ShapeDtypeStruct((ring, count, hidden), bf16),
            jax.ShapeDtypeStruct((ring, count, 2 * hidden), bf16),
            jax.ShapeDtypeStruct((ring, count, width), bf16),
            jax.ShapeDtypeStruct((count, width), bf16),
        ],
        in_specs=[any_spec] * (2 + ring),
        out_specs=[any_spec] * 6,
        scratch_shapes=[
            pltpu.VMEM((ring, count, width), bf16),
            pltpu.VMEM((2, count, width), bf16),
            pltpu.VMEM((count, width), f32),
            pltpu.VMEM((count, width), f32),
            pltpu.VMEM((count, width), f32),
            pltpu.VMEM((ring - 1, count, width), bf16),
            pltpu.VMEM((ring - 1, count, width), bf16),
            pltpu.VMEM((count, width), bf16),
            pltpu.VMEM((count, width), bf16),
            pltpu.VMEM((2, width, count), bf16),
            dma,
            dma,
            dma((2,)),
            dma,
            dma,
            dma((ring - 1,)),
            dma((ring - 1,)),
            dma((ring - 1,)),
            dma((ring - 1,)),
            dma,
        ],
        compiler_params=pltpu.CompilerParams(
            collective_id=collective_id, has_side_effects=True, vmem_limit_bytes=64 * 1024 * 1024 - 65536,
        ),
        cost_estimate=pl.CostEstimate(
            flops=12 * ring * count * width * hidden,
            bytes_accessed=8 * ring * count * width,
            transcendentals=ring * count * hidden,
        ),
        name="feed_forward",
    )(own_rows, *grad_rows, weights)


def weigh_kernel(
    tp_count, dp_count, tile, grads, rows_t, grads_t, gate_up, act, slots, out,
    left, left_sem, own_sem, send, recv,
):
    count = dp_count * tp_count
    my_dp = lax.axis_index("dp")
    my_tp = lax.axis_index("tensor")
    me = my_dp * tp_count + my_tp
    page_rows = slots.shape[1]

    loads = [
        pltpu.make_async_copy(source, left.at[k], left_sem.at[k])
        for k, source in enumerate((rows_t, grads_t))
    ]
    for load in loads:
        load.start()

    barrier = pltpu.get_barrier_semaphore()

    def place(peer):
        return {"dp": lax.div(peer, tp_count), "tensor": lax.rem(peer, tp_count)}

    def greet(j, carry):
        peer = lax.rem(me + j, count)
        pl.semaphore_signal(barrier, inc=1, device_id=place(peer), device_id_type=MESH)
        return carry

    lax.fori_loop(1, count, greet, 0)
    pl.semaphore_wait(barrier, count - 1)

    home = slots.at[my_tp * dp_count + my_dp]

    def block(p_dp, p_tp):
        return grads.at[p_tp, pl.ds(p_dp * page_rows, page_rows), :]

    own = pltpu.make_async_copy(block(my_dp, my_tp), home, own_sem)
    own.start()

    def copy_to(j):
        peer = lax.rem(me + j, count)
        return pltpu.make_async_remote_copy(
            src_ref=block(lax.div(peer, tp_count), lax.rem(peer, tp_count)),
            dst_ref=home,
            send_sem=send.at[j],
            recv_sem=recv.at[j],
            device_id=place(peer),
            device_id_type=MESH,
        )

    def start(j, carry):
        copy_to(j).start()
        return carry

    def finish(j, carry):
        copy_to(j).wait()
        return carry

    lax.fori_loop(1, count, start, 0)

    width = rows_t.shape[0]
    step = min(512, width)

    def multiply(k, right, first):
        ring, rows, cols = right.shape

        def body(part, result):
            values = part[...].reshape(ring * rows, tile)
            for m in range(0, width, step):
                result[m : m + step, :] = dot_nn(left[k, m : m + step, :], values).astype(bf16)

        pltpu.emit_pipeline(
            body,
            grid=(cols // tile,),
            in_specs=[pl.BlockSpec((ring, rows, tile), lambda n: (0, 0, n))],
            out_specs=[pl.BlockSpec((width, tile), lambda n: (0, n + first))],
        )(right, out)

    loads[0].wait()
    multiply(0, gate_up, 0)
    loads[1].wait()
    multiply(1, act, gate_up.shape[2] // tile)
    own.wait()
    lax.fori_loop(1, count, finish, 0)


def weigh(grads, rows_t, grads_t, gate_up, act, tp_count, dp_count, collective_id):
    count = tp_count * dp_count
    cols = grads.shape[2]
    page_rows = grads.shape[1] // dp_count
    width, rows = rows_t.shape
    hidden = act.shape[2]
    any_spec = pl.BlockSpec(memory_space=pl.ANY)
    dma = pltpu.SemaphoreType.DMA
    return pl.pallas_call(
        functools.partial(weigh_kernel, tp_count, dp_count, min(512, hidden)),
        out_shape=[
            jax.ShapeDtypeStruct((count, page_rows, cols), bf16),
            jax.ShapeDtypeStruct((width, 3 * hidden), bf16),
        ],
        in_specs=[any_spec] * 5,
        out_specs=[any_spec] * 2,
        scratch_shapes=[
            pltpu.VMEM((2, width, rows), bf16),
            dma((2,)),
            dma,
            dma((count,)),
            dma((count,)),
        ],
        compiler_params=pltpu.CompilerParams(
            collective_id=collective_id, has_side_effects=True, vmem_limit_bytes=48 * 1024 * 1024
        ),
        cost_estimate=pl.CostEstimate(
            flops=6 * rows * width * hidden,
            bytes_accessed=2 * width * (2 * rows + 3 * hidden),
            transcendentals=0,
        ),
        name="weigh",
    )(grads, rows_t, grads_t, gate_up, act)


def flip(index, bit):
    return index + bit - 2 * bit * lax.rem(lax.div(index, bit), 2)


def collect_kernel(
    tp_count, dp_count, hops, shard, second, gains, chunk, out, second_out, gains_out, chunks_out,
    second_send, second_recv, own_sem, ring_send, ring_recv, send, recv, gain_send, gain_recv, chunk_send, chunk_recv,
):
    my_dp = lax.axis_index("dp")
    my_tp = lax.axis_index("tensor")
    rows = shard.shape[0]
    half = rows // 2
    bits = [1 << b for b in reversed(range(dp_count.bit_length() - 1))]
    orders = [bits, bits[:-1][::-1] + bits[-1:]]
    steps = len(bits)

    barrier = pltpu.get_barrier_semaphore()
    for j in range(1, tp_count):
        pl.semaphore_signal(
            barrier, inc=1, device_id={"tensor": lax.rem(my_tp + j, tp_count)}, device_id_type=MESH
        )
    for j in range(1, dp_count):
        pl.semaphore_signal(
            barrier, inc=1, device_id={"dp": lax.rem(my_dp + j, dp_count)}, device_id_type=MESH
        )
    pl.semaphore_wait(barrier, tp_count + dp_count - 2)

    home = out.at[my_tp, pl.ds(my_dp * rows, rows), :]
    own = pltpu.make_async_copy(shard, home, own_sem.at[0])
    own.start()
    own_gain = pltpu.make_async_copy(gains, gains_out.at[my_dp], own_sem.at[1])
    own_gain.start()
    own_second = pltpu.make_async_copy(second, second_out.at[my_tp], own_sem.at[2])
    own_second.start()

    def second_copy(j):
        return pltpu.make_async_remote_copy(
            src_ref=second,
            dst_ref=second_out.at[my_tp],
            send_sem=second_send.at[j],
            recv_sem=second_recv.at[j],
            device_id={"tensor": lax.rem(my_tp + j, tp_count)},
            device_id_type=MESH,
        )

    def across(j):
        return pltpu.make_async_remote_copy(
            src_ref=shard,
            dst_ref=home,
            send_sem=ring_send.at[j],
            recv_sem=ring_recv.at[j],
            device_id={"tensor": lax.rem(my_tp + j, tp_count)},
            device_id_type=MESH,
        )

    def gain_copy(j):
        return pltpu.make_async_remote_copy(
            src_ref=gains,
            dst_ref=gains_out.at[my_dp],
            send_sem=gain_send.at[j],
            recv_sem=gain_recv.at[j],
            device_id={"dp": lax.rem(my_dp + j, dp_count)},
            device_id_type=MESH,
        )

    def onward(hop):
        return pltpu.make_async_remote_copy(
            src_ref=chunk if hop == 0 else chunks_out.at[hop - 1],
            dst_ref=chunks_out.at[hop],
            send_sem=chunk_send.at[hop],
            recv_sem=chunk_recv.at[hop],
            device_id={"tensor": lax.rem(my_tp + 1, tp_count)},
            device_id_type=MESH,
        )

    def within(j, s, k, m):
        order = orders[s]
        owner = my_dp
        for b in range(k):
            if m >> b & 1:
                owner = flip(owner, order[b])
        block = out.at[
            lax.rem(my_tp - j + tp_count, tp_count), pl.ds(owner * rows + s * half, half), :
        ]
        at = (1 << k) - 1 + m
        return pltpu.make_async_remote_copy(
            src_ref=block,
            dst_ref=block,
            send_sem=send.at[j, s, at],
            recv_sem=recv.at[j, s, at],
            device_id={"dp": flip(my_dp, order[k])},
            device_id_type=MESH,
        )

    for j in range(1, tp_count):
        across(j).start()
    for j in range(1, dp_count):
        gain_copy(j).start()
    onward(0).start()
    own.wait()
    for phase in range(tp_count + steps):
        for k in reversed(range(steps + 1)):
            j = phase - k
            if not 0 <= j < tp_count:
                continue
            if k == 0:
                if j > 0:
                    across(j).wait_recv()
            else:
                for s in range(2):
                    for m in range(1 << (k - 1)):
                        within(j, s, k - 1, m).wait_recv()
            if k < steps:
                for s in range(2):
                    for m in range(1 << k):
                        within(j, s, k, m).start()
        if phase == tp_count:
            for j in range(1, tp_count):
                second_copy(j).start()
        if tp_count <= phase < tp_count + hops - 1:
            onward(phase - tp_count).wait_recv()
            onward(phase - tp_count + 1).start()
    for j in range(tp_count):
        if j > 0:
            across(j).wait_send()
        for s in range(2):
            for k in range(steps):
                for m in range(1 << k):
                    within(j, s, k, m).wait_send()
    own_gain.wait()
    own_second.wait()
    for j in range(1, tp_count):
        second_copy(j).wait()
    for j in range(1, dp_count):
        gain_copy(j).wait()
    for hop in range(hops):
        if hop == hops - 1:
            onward(hop).wait_recv()
        onward(hop).wait_send()


def collect(shard, second, gains, chunk, tp_count, dp_count, hops, collective_id):
    rows, cols = shard.shape
    dma = pltpu.SemaphoreType.DMA
    vmem_spec = pl.BlockSpec(memory_space=pltpu.VMEM)
    any_spec = pl.BlockSpec(memory_space=pl.ANY)
    return pl.pallas_call(
        functools.partial(collect_kernel, tp_count, dp_count, hops),
        out_shape=[
            jax.ShapeDtypeStruct((tp_count, dp_count * rows, cols), shard.dtype),
            jax.ShapeDtypeStruct((tp_count,) + second.shape, second.dtype),
            jax.ShapeDtypeStruct((dp_count,) + gains.shape, gains.dtype),
            jax.ShapeDtypeStruct((hops,) + chunk.shape, chunk.dtype),
        ],
        in_specs=[vmem_spec, vmem_spec, vmem_spec, any_spec],
        out_specs=[any_spec] * 4,
        scratch_shapes=[
            dma((tp_count,)),
            dma((tp_count,)),
            dma((3,)),
            dma((tp_count,)),
            dma((tp_count,)),
            dma((tp_count, 2, dp_count - 1)),
            dma((tp_count, 2, dp_count - 1)),
            dma((dp_count,)),
            dma((dp_count,)),
            dma((hops,)),
            dma((hops,)),
        ],
        compiler_params=pltpu.CompilerParams(collective_id=collective_id, has_side_effects=True),
        cost_estimate=pl.CostEstimate(
            flops=0, bytes_accessed=16 * tp_count * dp_count * shard.size, transcendentals=0
        ),
        name="collect",
    )(shard, second, gains, chunk)


def spread_kernel(rows, weight, out):
    out[0] = dot_nn(rows[...], weight[0]).astype(out.dtype)


def spread(rows, weights, part, cols):
    shards, width, _ = weights.shape
    count = rows.shape[0]
    return pl.pallas_call(
        spread_kernel,
        grid=(shards,),
        in_specs=[
            pl.BlockSpec((count, width), lambda t: (0, 0)),
            pl.BlockSpec((1, width, cols), lambda t: (t, 0, part)),
        ],
        out_specs=pl.BlockSpec((1, count, cols), lambda t: (t, 0, 0)),
        out_shape=jax.ShapeDtypeStruct((shards, count, cols), bf16),
        cost_estimate=pl.CostEstimate(
            flops=2 * shards * count * width * cols,
            bytes_accessed=2 * shards * width * cols,
            transcendentals=0,
        ),
        name="spread",
    )(rows, weights)


def gather_kernel(has_begin, part, weight, *refs):
    out = refs[-1]

    @pl.when(pl.program_id(0) == 0)
    def _():
        out[...] = refs[0][...] if has_begin else jnp.zeros_like(out)

    out[...] += dot_nt(part[0], weight[0])


def gather_sum(parts, weights, part, begin):
    shards, count, cols = parts.shape
    width = weights.shape[1]
    whole = pl.BlockSpec((count, width), lambda t: (0, 0))
    begins = [] if begin is None else [begin]
    return pl.pallas_call(
        functools.partial(gather_kernel, begin is not None),
        grid=(shards,),
        in_specs=[
            pl.BlockSpec((1, count, cols), lambda t: (t, 0, 0)),
            pl.BlockSpec((1, width, cols), lambda t: (t, 0, part)),
        ]
        + [whole] * len(begins),
        out_specs=whole,
        out_shape=jax.ShapeDtypeStruct((count, width), f32),
        cost_estimate=pl.CostEstimate(
            flops=2 * shards * count * width * cols,
            bytes_accessed=2 * shards * width * cols,
            transcendentals=0,
        ),
        name="gather_sum",
    )(parts, weights, *begins)


def outer_kernel(rows, *refs):
    parts, out, turned = refs[:-2], refs[-2], refs[-1]

    @pl.when(pl.program_id(0) == 0)
    def _():
        turned[...] = rows[...].T

    at = 0
    for part in parts:
        cols = part.shape[2]
        out[:, at : at + cols] = dot_nn(turned[...], part[0]).astype(out.dtype)
        at += cols


def outer(rows, parts):
    shards, count, _ = parts[0].shape
    cols = sum(part.shape[2] for part in parts)
    width = rows.shape[1]
    return pl.pallas_call(
        outer_kernel,
        grid=(shards,),
        in_specs=[pl.BlockSpec((count, width), lambda t: (0, 0))]
        + [pl.BlockSpec((1, count, part.shape[2]), lambda t: (t, 0, 0)) for part in parts],
        out_specs=pl.BlockSpec((width, cols), lambda t: (0, t)),
        out_shape=jax.ShapeDtypeStruct((width, shards * cols), bf16),
        scratch_shapes=[pltpu.VMEM((width, count), bf16)],
        cost_estimate=pl.CostEstimate(
            flops=2 * shards * count * width * cols,
            bytes_accessed=2 * shards * width * cols,
            transcendentals=0,
        ),
        name="outer",
    )(rows, *parts)


def rms_scale(hidden):
    return lax.rsqrt(jnp.mean(hidden * hidden, axis=1, keepdims=True) + epsilon)


def norm_back(grad_norm, hidden, scale_rows, gain):
    normed = hidden * scale_rows
    gain_part = jnp.sum(grad_norm * normed, axis=0)
    inner = grad_norm * gain
    grad_hidden = scale_rows * (inner - normed * jnp.mean(inner * normed, axis=1, keepdims=True))
    return (grad_hidden, gain_part)


def after(value, other):
    return lax.optimization_barrier((value, other))[0]


def local(
    tokens,
    upstream,
    lengths,
    positions,
    pages,
    attn_gain,
    w_query,
    w_key,
    w_value,
    w_out,
    mlp_gain,
    w_gate,
    w_up,
    w_down,
):
    dp_count = lax.axis_size("dp")
    tp_count = lax.axis_size("tensor")
    dp_index = lax.axis_index("dp")
    tp_index = lax.axis_index("tensor")
    tok_dev, width = tokens.shape
    tok_group = tok_dev * tp_count
    page_rows = tok_dev // dp_count
    group_pages = tp_count * dp_count
    page_count = pages.shape[0]
    device = dp_index * tp_count + tp_index
    everyone = ("tensor", "dp")

    local_ids = jnp.arange(dp_count, dtype=jnp.int32)
    inverse = (
        jnp.zeros((page_count,), jnp.int32).at[pages].set(jnp.arange(page_count, dtype=jnp.int32))
    )
    dealt = lax.dynamic_slice_in_dim(inverse, device * dp_count, dp_count)
    dest_group = dealt // group_pages
    send_order = jnp.zeros((dp_count,), jnp.int32).at[dest_group].set(local_ids)
    group_sources = lax.dynamic_slice_in_dim(pages, dp_index * group_pages, group_pages)
    perm = (
        (jnp.arange(group_pages, dtype=jnp.int32) // dp_count) * dp_count
        + group_sources // group_pages
    ).astype(jnp.int32)

    def reorder(rows, order):
        blocks = rows.reshape(dp_count, page_rows, rows.shape[1])
        return jnp.take(blocks, order, axis=0, mode="clip").reshape(rows.shape)

    hidden_in = reorder(tokens, send_order).astype(f32)
    grad_top = reorder(upstream, send_order).astype(f32)
    seq_lens = lengths[0]
    seq_ends = jnp.cumsum(seq_lens)
    place = (jnp.take(dealt, send_order, mode="clip") % group_pages) * page_rows
    place_rows = (place[:, None] + jnp.arange(page_rows, dtype=jnp.int32)[None, :]).reshape(-1)
    valid_rows = (place_rows < seq_ends[-1]).astype(f32)[:, None]

    row_ids = jnp.arange(tok_group, dtype=jnp.int32)
    begin = jnp.max(
        jnp.where(row_ids[:, None] >= seq_ends[None, :], seq_ends[None, :], 0), axis=1
    ).astype(jnp.int32)
    block_len = min(block_rows, tok_group)
    first_block = begin[::block_len] // block_len
    begin = begin[None, :]
    inverse_freq = theta_base ** (-(jnp.arange(HALF, dtype=f32) * 2.0) / HD)
    angles = inverse_freq[:, None] * positions.astype(f32)
    cos_t, sin_t = jnp.cos(angles), jnp.sin(angles)

    q_cols, kv_cols = w_query.shape[1], w_key.shape[1]
    kv_heads = kv_cols // HD
    per_group = q_cols // kv_cols
    group_q = per_group * HD
    groups = range(kv_heads)
    qkv_shard = jnp.concatenate(
        [
            part
            for g in groups
            for part in (
                w_query[:, g * group_q : (g + 1) * group_q],
                w_key[:, g * HD : (g + 1) * HD],
                w_value[:, g * HD : (g + 1) * HD],
            )
        ],
        axis=1,
    )

    def trade(value):
        blocks = value.reshape(group_pages, page_rows, value.shape[-1])
        return lax.all_to_all(blocks, everyone, split_axis=0, concat_axis=0, tiled=True)

    def trade_back(value):
        return trade(value).reshape(tp_count, tok_dev, value.shape[-1])

    ring_next = [(t, (t + 1) % tp_count) for t in range(tp_count)]

    def pass_on(value):
        return lax.ppermute(value, "tensor", ring_next)

    grad_out = grad_top * valid_rows
    grad_chunks = [grad_out.astype(bf16)]
    mlp_shard = jnp.concatenate([w_gate, w_up, w_down.T], axis=1)
    w_mlp = lax.all_gather(mlp_shard, "dp", axis=0, tiled=True)
    hops = min(2, tp_count - 1)
    w_qkv, out_shards, gains, got_chunks = collect(
        qkv_shard, w_out.T, jnp.stack([attn_gain, mlp_gain]), grad_chunks[0], tp_count, dp_count,
        hops, 1,
    )
    w_out_t = lax.all_gather(out_shards, "dp", axis=1, tiled=True)
    grad_chunks += [got_chunks[hop] for hop in range(hops)]
    gains = gains.transpose(1, 0, 2).reshape(2, -1).astype(f32)
    gain_one, gain_two = gains[0], gains[1]

    scale_one = rms_scale(hidden_in)
    normed_one = (hidden_in * scale_one * gain_one).astype(bf16)
    qkv, slots = [], []
    for g in groups:
        qkv.append(spread(normed_one, w_qkv, g, group_q + 2 * HD))
        slots.append(trade(qkv[g]))
    saved, mixed = [], []
    last = qkv[-1]
    for hop in range(hops + 1, tp_count):
        grad_chunks.append(pass_on(after(grad_chunks[-1], slots[0])))
    for g in groups:
        if g == len(groups) - 1:
            last = (last, w_mlp, grad_chunks[-1])
        q_t, k_t, k_rows, v_t, v_rows = prepare(
            after(slots[g], last), perm, cos_t, sin_t, per_group, 1
        )
        o_t, lse, last = attend_forward(
            q_t, k_rows, v_t, begin, first_block, perm, page_rows, block_len
        )
        saved.append((q_t, k_rows, k_t, v_rows, o_t, lse))
        mixed.append(trade_back(last))
    hidden_mid = hidden_in
    for g in groups:
        hidden_mid = gather_sum(mixed[g], w_out_t, g, hidden_mid)

    scale_two = rms_scale(hidden_mid)
    normed_two = (hidden_mid * scale_two * gain_two).astype(bf16)
    grads_t, rows_t, inner_act, grad_gate_up, partial_two, grad_normed_two = feed(
        normed_two, grad_chunks, w_mlp, tp_count
    )
    grad_normed_two = grad_normed_two.astype(f32)
    grad_mid_norm, gain_two_part = norm_back(grad_normed_two, hidden_mid, scale_two, gain_two)
    grad_mid = grad_out + grad_mid_norm

    def add_on(arrived, s):
        return (arrived.astype(f32) + partial_two[s].astype(f32)).astype(bf16)

    def reduce_dp(grad):
        return lax.psum_scatter(grad.astype(bf16), "dp", scatter_dimension=0, tiled=True)

    def reduce_tensor(value):
        cols = value.shape[1] // tp_count
        total = lax.dynamic_slice_in_dim(value, tp_index * cols, cols, 1).astype(f32)
        for s in range(1, tp_count):
            target = lax.rem(tp_index + s, tp_count)
            block = lax.dynamic_slice_in_dim(value, target * cols, cols, 1)
            pairs = [(t, (t + s) % tp_count) for t in range(tp_count)]
            total = total + lax.ppermute(block, "tensor", pairs).astype(f32)
        return total

    grad_z = grad_mid.astype(bf16)
    grad_wout = outer(grad_z, mixed)
    sum_out = reduce_dp(grad_wout)
    grad_slots, grad_wmlp = weigh(
        spread(after(grad_z, grad_wout), w_out_t, 0, q_cols),
        rows_t, grads_t, grad_gate_up, inner_act, tp_count, dp_count, 2,
    )
    sum_mlp = reduce_dp(grad_wmlp)
    branch_two = pass_on(after(partial_two[1], grad_slots))
    grad_qkv = []
    for g in groups:
        q_t, k_rows, k_t, v_rows, o_t, lse = saved[g]
        back = attend_backward(
            grad_slots if g == 0 else after(grad_slots, (back, sum_out)), g, q_t,
            k_rows, k_t, v_rows, o_t, lse, begin, cos_t, sin_t, first_block, perm, page_rows,
            block_len,
        )
        grad_qkv.append(trade_back(after(back, (grad_qkv[-1], branch_two)) if grad_qkv else back))
    hidden = sum_mlp.shape[1] // 3
    sum_out = reduce_tensor(sum_out)
    for s in range(2, tp_count - 1):
        branch_two = pass_on(add_on(after(branch_two, tuple(grad_qkv)), s))
    grad_wqkv = outer(after(normed_one, (sum_mlp, sum_out)), grad_qkv)
    sum_qkv = reduce_tensor(reduce_dp(grad_wqkv))
    each = group_q + 2 * HD
    sum_qkv = [sum_qkv[:, g * each : (g + 1) * each] for g in groups]
    grad_normed_one = None
    for g in groups:
        grad_normed_one = gather_sum(after(grad_qkv[g], grad_wqkv), w_qkv, g, grad_normed_one)
    branch_two = pass_on(add_on(after(branch_two, grad_normed_one), tp_count - 1))
    result = (
        (after(hidden_mid, back) + branch_two.astype(f32) + partial_two[0].astype(f32)) * valid_rows
    ).astype(bf16)
    grad_in_norm, gain_one_part = norm_back(grad_normed_one, hidden_in, scale_one, gain_one)
    grad_in = (grad_mid + grad_in_norm).astype(bf16)

    gain_parts = jnp.stack([gain_one_part, gain_two_part]).reshape(2, dp_count, -1)
    gain_parts = jnp.broadcast_to(
        gain_parts.transpose(1, 0, 2)[None], (tp_count, dp_count, 2, gain_parts.shape[2])
    ).reshape(group_pages, 2, -1)
    gain_sums = jnp.sum(
        lax.all_to_all(gain_parts, everyone, split_axis=0, concat_axis=0, tiled=True), axis=0
    )
    return (
        reorder(result, dest_group),
        reorder(grad_in, dest_group),
        gain_sums[0],
        jnp.concatenate([part[:, :group_q] for part in sum_qkv], axis=1),
        jnp.concatenate([part[:, group_q : group_q + HD] for part in sum_qkv], axis=1),
        jnp.concatenate([part[:, group_q + HD :] for part in sum_qkv], axis=1),
        sum_out.T,
        gain_sums[1],
        sum_mlp[:, :hidden].astype(f32),
        sum_mlp[:, hidden : 2 * hidden].astype(f32),
        sum_mlp[:, 2 * hidden :].astype(f32).T,
    )


def solution(mesh):
    rows = P(("dp", "tensor"), None)
    weight = P("dp", "tensor")
    weight_t = P("tensor", "dp")
    return jax.shard_map(
        local,
        mesh=mesh,
        in_specs=(
            rows,
            rows,
            P("dp", None),
            P("dp", None),
            P(),
            P("dp"),
            weight,
            weight,
            weight,
            weight_t,
            P("dp"),
            weight,
            weight,
            weight_t,
        ),
        out_specs=(
            rows,
            rows,
            P("dp"),
            weight,
            weight,
            weight,
            weight_t,
            P("dp"),
            weight,
            weight,
            weight_t,
        ),
        check_vma=False,
    )
```

```python
import functools

import jax
import jax.numpy as jnp
from jax import lax
from jax.experimental import pallas as pl
from jax.experimental.pallas import tpu as pltpu
from jax.sharding import PartitionSpec as P

HD = 64
HALF = HD // 2

epsilon = 1e-05
theta_base = 500000.0
masked_score = -1e30
score_scale = HD**-0.5
block_rows = 512
key_rows = 256
MESH = pl.DeviceIdType.MESH
f32 = jnp.float32
bf16 = jnp.bfloat16


def dot_nn(left, right):
    return lax.dot_general(left, right, (((1,), (0,)), ((), ())), preferred_element_type=f32)


def dot_nt(left, right):
    return lax.dot_general(left, right, (((1,), (1,)), ((), ())), preferred_element_type=f32)


def dot_tn(left, right):
    return lax.dot_general(left, right, (((0,), (0,)), ((), ())), preferred_element_type=f32)


def prep_kernel(pages_per, q_heads, kv_heads, perm, *refs):
    page_refs = refs[:pages_per]
    cos_ref, sin_ref, q_t, k_t, k_rows, v_t, v_rows = refs[pages_per:]
    rows = jnp.concatenate([r[0].astype(f32) for r in page_refs], axis=0)
    turned = rows.T
    cos, sin = cos_ref[...], sin_ref[...]

    def rope(base):
        first, second = turned[base : base + HALF], turned[base + HALF : base + HD]
        return jnp.concatenate([first * cos - second * sin, second * cos + first * sin], axis=0)

    for h in range(q_heads):
        roped = rope(h * HD).astype(bf16)
        q_t[h * HD : (h + 1) * HD, :] = (roped.astype(f32) * score_scale).astype(bf16)
    k_base = q_heads * HD
    v_base = k_base + kv_heads * HD
    for g in range(kv_heads):
        roped = rope(k_base + g * HD)
        k_t[g * HD : (g + 1) * HD, :] = roped.astype(bf16)
        k_rows[g] = roped.T.astype(bf16)
        v_t[g * HD : (g + 1) * HD, :] = turned[v_base + g * HD : v_base + (g + 1) * HD].astype(bf16)
        v_rows[g] = rows[:, v_base + g * HD : v_base + (g + 1) * HD].astype(bf16)


def prepare(slots, part, perm, cos_t, sin_t, q_heads, kv_heads):
    page_rows = slots.shape[1]
    cols = (q_heads + 2 * kv_heads) * HD
    total_rows = slots.shape[0] * page_rows
    lanes = min(256, total_rows)
    pages_per = lanes // page_rows

    def page_spec(a):
        return pl.BlockSpec(
            (1, page_rows, cols), lambda i, perm_ref, a=a: (perm_ref[i * pages_per + a], 0, part)
        )

    table = pl.BlockSpec((HALF, lanes), lambda i, perm_ref: (0, i))
    return pl.pallas_call(
        functools.partial(prep_kernel, pages_per, q_heads, kv_heads),
        grid_spec=pltpu.PrefetchScalarGridSpec(
            num_scalar_prefetch=1,
            grid=(total_rows // lanes,),
            in_specs=[page_spec(a) for a in range(pages_per)] + [table, table],
            out_specs=[
                pl.BlockSpec((q_heads * HD, lanes), lambda i, perm_ref: (0, i)),
                pl.BlockSpec((kv_heads * HD, lanes), lambda i, perm_ref: (0, i)),
                pl.BlockSpec((kv_heads, lanes, HD), lambda i, perm_ref: (0, i, 0)),
                pl.BlockSpec((kv_heads * HD, lanes), lambda i, perm_ref: (0, i)),
                pl.BlockSpec((kv_heads, lanes, HD), lambda i, perm_ref: (0, i, 0)),
            ],
        ),
        out_shape=[
            jax.ShapeDtypeStruct((q_heads * HD, total_rows), bf16),
            jax.ShapeDtypeStruct((kv_heads * HD, total_rows), bf16),
            jax.ShapeDtypeStruct((kv_heads, total_rows, HD), bf16),
            jax.ShapeDtypeStruct((kv_heads * HD, total_rows), bf16),
            jax.ShapeDtypeStruct((kv_heads, total_rows, HD), bf16),
        ],
        cost_estimate=pl.CostEstimate(
            flops=8 * slots.size, bytes_accessed=6 * slots.size, transcendentals=0
        ),
        name="prepare",
    )(perm, *([slots] * pages_per), cos_t, sin_t)


def block_bias(i, j, begin_row, block_len, key_len):
    keys = j * key_len + lax.broadcasted_iota(jnp.int32, (key_len, block_len), 0)
    queries = i * block_len + lax.broadcasted_iota(jnp.int32, (key_len, block_len), 1)
    allowed = (keys >= begin_row) & (keys <= queries)
    return jnp.where(allowed, 0.0, masked_score)


def forward_kernel(
    q_heads, kv_heads, page_rows, first_block, perm,
    q_t, k_rows, v_t, begin, o_t, lse, o_slots, acc, stage, sems,
):
    i = pl.program_id(0)
    block_len = q_t.shape[1]
    key_len = min(key_rows, k_rows.shape[1])
    per_group = q_heads // kv_heads
    acc[...] = jnp.zeros_like(acc)
    begin_row = begin[...]

    def visit(j, carry):
        bias = block_bias(i, j, begin_row, block_len, key_len)
        at = pl.ds(pl.multiple_of(j * key_len, key_len), key_len)
        scores = [
            dot_nn(k_rows[h // per_group, at, :], q_t[h * HD : (h + 1) * HD, :]) + bias
            for h in range(q_heads)
        ]
        tops = [
            jnp.maximum(carry[h][0], jnp.max(scores[h], axis=0, keepdims=True))
            for h in range(q_heads)
        ]
        weights = [jnp.exp(scores[h] - tops[h]) for h in range(q_heads)]
        fades = [jnp.exp(carry[h][0] - tops[h]) for h in range(q_heads)]
        totals = [
            carry[h][1] * fades[h] + jnp.sum(weights[h], axis=0, keepdims=True)
            for h in range(q_heads)
        ]
        for h in range(q_heads):
            g = h // per_group
            span = slice(h * HD, (h + 1) * HD)
            acc[span, :] = acc[span, :] * fades[h] + dot_nn(
                v_t[g * HD : (g + 1) * HD, at], weights[h].astype(bf16)
            )
        return tuple(zip(tops, totals))

    start = tuple(
        (jnp.full((1, block_len), masked_score, f32), jnp.zeros((1, block_len), f32))
        for _ in range(q_heads)
    )
    stats = lax.fori_loop(
        first_block[i], lax.div((i + 1) * block_len - 1, key_len) + 1, visit, start
    )
    for h in range(q_heads):
        lse[h : h + 1, :] = stats[h][0] + jnp.log(stats[h][1])
    mixed = jnp.concatenate(
        [acc[h * HD : (h + 1) * HD, :] / stats[h][1] for h in range(q_heads)], axis=0
    )
    o_t[...] = mixed.astype(bf16)
    pages = block_len // page_rows
    stage[...] = mixed.T.astype(bf16).reshape(pages, page_rows, q_heads * HD)
    copies = [
        pltpu.make_async_copy(stage.at[a], o_slots.at[perm[i * pages + a]], sems.at[a])
        for a in range(pages)
    ]
    for copy in copies:
        copy.start()
    for copy in copies:
        copy.wait()


def attend_forward(q_t, k_rows, v_t, begin, first_block, perm, page_rows, block_len):
    total_rows = q_t.shape[1]
    kv_heads = k_rows.shape[0]
    q_heads = q_t.shape[0] // HD
    pages = block_len // page_rows
    return pl.pallas_call(
        functools.partial(forward_kernel, q_heads, kv_heads, page_rows),
        grid_spec=pltpu.PrefetchScalarGridSpec(
            num_scalar_prefetch=2,
            grid=(total_rows // block_len,),
            in_specs=[
                pl.BlockSpec((q_heads * HD, block_len), lambda i, *_: (0, i)),
                pl.BlockSpec((kv_heads, total_rows, HD), lambda i, *_: (0, 0, 0)),
                pl.BlockSpec((kv_heads * HD, total_rows), lambda i, *_: (0, 0)),
                pl.BlockSpec((1, block_len), lambda i, *_: (0, i)),
            ],
            out_specs=[
                pl.BlockSpec((q_heads * HD, block_len), lambda i, *_: (0, i)),
                pl.BlockSpec((q_heads, block_len), lambda i, *_: (0, i)),
                pl.BlockSpec(memory_space=pl.ANY),
            ],
            scratch_shapes=[
                pltpu.VMEM((q_heads * HD, block_len), f32),
                pltpu.VMEM((pages, page_rows, q_heads * HD), bf16),
                pltpu.SemaphoreType.DMA((pages,)),
            ],
        ),
        out_shape=[
            jax.ShapeDtypeStruct((q_heads * HD, total_rows), bf16),
            jax.ShapeDtypeStruct((q_heads, total_rows), f32),
            jax.ShapeDtypeStruct((total_rows // page_rows, page_rows, q_heads * HD), bf16),
        ],
        cost_estimate=pl.CostEstimate(
            flops=q_heads * total_rows * total_rows * HD,
            bytes_accessed=8 * q_t.size,
            transcendentals=q_heads * total_rows * total_rows // 4,
        ),
        name="attend_forward",
    )(first_block, perm, q_t, k_rows, v_t, begin)


def backward_kernel(
    q_heads, kv_heads, page_rows, pages, first_block, perm, *refs
):
    grad_pages = refs[:pages]
    (
        q_t, k_rows, k_t, v_rows, o_t, lse, begin, cos_ref, sin_ref, cos_all, sin_all,
        out, grad_q, grad_k, grad_v, stage, kv_stage, sems, kv_sems,
    ) = refs[pages:]
    i = pl.program_id(0)
    steps = pl.num_programs(0)
    block_len = q_t.shape[1]
    key_len = min(key_rows, k_rows.shape[1])
    per_group = q_heads // kv_heads
    q_cols = q_heads * HD
    kv_cols = kv_heads * HD

    @pl.when(i == 0)
    def _():
        grad_k[...] = jnp.zeros_like(grad_k)
        grad_v[...] = jnp.zeros_like(grad_v)

    grad_rows = jnp.concatenate([r[0].astype(f32) for r in grad_pages], axis=0)
    grad_t = grad_rows.T
    grad_low = grad_t.astype(bf16)
    inner = [
        jnp.sum(
            grad_t[h * HD : (h + 1) * HD] * o_t[h * HD : (h + 1) * HD, :].astype(f32),
            axis=0,
            keepdims=True,
        )
        for h in range(q_heads)
    ]
    grad_q[...] = jnp.zeros_like(grad_q)
    begin_row = begin[...]

    def visit(j, carry):
        bias = block_bias(i, j, begin_row, block_len, key_len)
        at = pl.ds(pl.multiple_of(j * key_len, key_len), key_len)
        for g in range(kv_heads):
            kv_span = slice(g * HD, (g + 1) * HD)
            keys, vals, keys_t = k_rows[g, at, :], v_rows[g, at, :], k_t[kv_span, at]
            heads = range(g * per_group, (g + 1) * per_group)
            spans = [slice(h * HD, (h + 1) * HD) for h in heads]
            scores = [dot_nn(keys, q_t[span, :]) + bias for span in spans]
            grad_probs = [dot_nn(vals, grad_low[span]) for span in spans]
            probs = [jnp.exp(s - lse[h : h + 1, :]) for s, h in zip(scores, heads)]
            grad_scores = [
                (p * (d - inner[h])).astype(bf16) for p, d, h in zip(probs, grad_probs, heads)
            ]
            low_probs = [p.astype(bf16) for p in probs]
            grad_v[kv_span, at] += sum(
                dot_nt(grad_low[span], p) for span, p in zip(spans, low_probs)
            )
            grad_k[kv_span, at] += sum(
                dot_nt(q_t[span, :], d) for span, d in zip(spans, grad_scores)
            )
            for span, d in zip(spans, grad_scores):
                grad_q[span, :] += dot_nn(keys_t, d)
        return carry

    lax.fori_loop(first_block[i], lax.div((i + 1) * block_len - 1, key_len) + 1, visit, 0)

    def unrope(value, cos, sin):
        first, second = value[:HALF], value[HALF:]
        return jnp.concatenate([first * cos + second * sin, second * cos - first * sin], axis=0)

    cos, sin = cos_ref[...], sin_ref[...]
    parts = [
        unrope(grad_q[h * HD : (h + 1) * HD, :] * score_scale, cos, sin) for h in range(q_heads)
    ]
    stage[...] = jnp.concatenate(parts, axis=0).T.astype(bf16).reshape(pages, page_rows, q_cols)
    copies = [
        pltpu.make_async_copy(
            stage.at[a], out.at[perm[i * pages + a], :, pl.ds(0, q_cols)], sems.at[a]
        )
        for a in range(pages)
    ]
    for copy in copies:
        copy.start()
    for copy in copies:
        copy.wait()

    @pl.when(i == steps - 1)
    def _():
        all_pages = kv_stage.shape[0]
        cos, sin = cos_all[...], sin_all[...]
        parts = [unrope(grad_k[g * HD : (g + 1) * HD, :], cos, sin) for g in range(kv_heads)]
        both = jnp.concatenate(parts + [grad_v[...]], axis=0)
        kv_stage[...] = both.T.astype(bf16).reshape(all_pages, page_rows, 2 * kv_cols)
        copies = [
            pltpu.make_async_copy(
                kv_stage.at[a], out.at[perm[a], :, pl.ds(q_cols, 2 * kv_cols)], kv_sems.at[a]
            )
            for a in range(all_pages)
        ]
        for copy in copies:
            copy.start()
        for copy in copies:
            copy.wait()


def attend_backward(
    grad_slots, part, q_t, k_rows, k_t, v_rows, o_t, lse, begin, cos_t, sin_t, first_block, perm,
    page_rows, block_len,
):
    total_rows = q_t.shape[1]
    kv_heads = k_rows.shape[0]
    q_heads = q_t.shape[0] // HD
    pages = block_len // page_rows
    all_pages = total_rows // page_rows
    q_cols = q_heads * HD
    kv_cols = kv_heads * HD

    def page_spec(a):
        return pl.BlockSpec(
            (1, page_rows, q_cols),
            lambda i, first_ref, perm_ref, a=a: (perm_ref[i * pages + a], 0, part),
        )

    def whole(shape):
        return pl.BlockSpec(shape, lambda i, *_: (0,) * len(shape))

    def column(rows):
        return pl.BlockSpec((rows, block_len), lambda i, *_: (0, i))

    return pl.pallas_call(
        functools.partial(backward_kernel, q_heads, kv_heads, page_rows, pages),
        grid_spec=pltpu.PrefetchScalarGridSpec(
            num_scalar_prefetch=2,
            grid=(total_rows // block_len,),
            in_specs=[page_spec(a) for a in range(pages)]
            + [
                column(q_cols),
                whole((kv_heads, total_rows, HD)),
                whole((kv_cols, total_rows)),
                whole((kv_heads, total_rows, HD)),
                column(q_cols),
                column(q_heads),
                column(1),
                column(HALF),
                column(HALF),
                whole((HALF, total_rows)),
                whole((HALF, total_rows)),
            ],
            out_specs=pl.BlockSpec(memory_space=pl.ANY),
            scratch_shapes=[
                pltpu.VMEM((q_cols, block_len), f32),
                pltpu.VMEM((kv_cols, total_rows), f32),
                pltpu.VMEM((kv_cols, total_rows), f32),
                pltpu.VMEM((pages, page_rows, q_cols), bf16),
                pltpu.VMEM((all_pages, page_rows, 2 * kv_cols), bf16),
                pltpu.SemaphoreType.DMA((pages,)),
                pltpu.SemaphoreType.DMA((all_pages,)),
            ],
        ),
        out_shape=jax.ShapeDtypeStruct((all_pages, page_rows, q_cols + 2 * kv_cols), bf16),
        cost_estimate=pl.CostEstimate(
            flops=3 * q_heads * total_rows * total_rows * HD,
            bytes_accessed=12 * q_t.size,
            transcendentals=q_heads * total_rows * total_rows // 4,
        ),
        name="attend_backward",
    )(
        first_block, perm, *([grad_slots] * pages), q_t, k_rows, k_t, v_rows, o_t, lse, begin,
        cos_t, sin_t, cos_t, sin_t,
    )


def project_kernel(
    tp_count, dp_count, rows, weights, slots, held, stage, load_sem, own_sem, send, recv
):
    count = dp_count * tp_count
    my_dp = lax.axis_index("dp")
    my_tp = lax.axis_index("tensor")
    me = my_dp * tp_count + my_tp
    page_rows = slots.shape[1]

    def load(j):
        shard = lax.rem(my_tp + 1 + j, tp_count)
        return pltpu.make_async_copy(weights.at[shard], held.at[j % 2], load_sem.at[j % 2])

    load(0).start()
    barrier = pltpu.get_barrier_semaphore()

    def greet(j, carry):
        peer = lax.rem(me + j, count)
        pl.semaphore_signal(
            barrier,
            inc=1,
            device_id={"dp": lax.div(peer, tp_count), "tensor": lax.rem(peer, tp_count)},
            device_id_type=MESH,
        )
        return carry

    lax.fori_loop(1, count, greet, 0)
    pl.semaphore_wait(barrier, count - 1)
    home = slots.at[my_tp * dp_count + my_dp]

    def copy_to(j, off):
        p_dp = lax.rem(my_dp + off, dp_count)
        return pltpu.make_async_remote_copy(
            src_ref=stage.at[j, pl.ds(p_dp * page_rows, page_rows), :],
            dst_ref=home,
            send_sem=send.at[j, off],
            recv_sem=recv.at[j, off],
            device_id={"dp": p_dp, "tensor": lax.rem(my_tp + 1 + j, tp_count)},
            device_id_type=MESH,
        )

    def each(j, act):
        def one(off, carry):
            act(copy_to(j, off))
            return carry

        lax.fori_loop(1 if j == tp_count - 1 else 0, dp_count, one, 0)

    for j in range(tp_count):
        load(j).wait()
        if j + 1 < tp_count:
            load(j + 1).start()
        stage[j] = dot_nn(rows[...], held[j % 2]).astype(bf16)
        if j > 0:
            each(j - 1, lambda copy: copy.start())
    each(tp_count - 1, lambda copy: copy.start())
    own = pltpu.make_async_copy(
        stage.at[tp_count - 1, pl.ds(my_dp * page_rows, page_rows), :], home, own_sem
    )
    own.start()
    own.wait()
    for j in range(tp_count):
        each(j, lambda copy: copy.wait())


def project(rows, weights, dp_count, collective_id):
    tp_count, width, cols = weights.shape
    total = rows.shape[0]
    page_rows = total // dp_count
    any_spec = pl.BlockSpec(memory_space=pl.ANY)
    dma = pltpu.SemaphoreType.DMA
    return pl.pallas_call(
        functools.partial(project_kernel, tp_count, dp_count),
        out_shape=jax.ShapeDtypeStruct((tp_count * dp_count, page_rows, cols), bf16),
        in_specs=[pl.BlockSpec(memory_space=pltpu.VMEM), any_spec],
        out_specs=any_spec,
        scratch_shapes=[
            pltpu.VMEM((2, width, cols), bf16),
            pltpu.VMEM((tp_count, total, cols), bf16),
            dma((2,)),
            dma,
            dma((tp_count, dp_count)),
            dma((tp_count, dp_count)),
        ],
        compiler_params=pltpu.CompilerParams(
            collective_id=collective_id, has_side_effects=True, vmem_limit_bytes=32 * 1024 * 1024
        ),
        cost_estimate=pl.CostEstimate(
            flops=2 * tp_count * total * width * cols,
            bytes_accessed=16 * tp_count * width * cols,
            transcendentals=0,
        ),
        name="project",
    )(rows, weights)


def feed_kernel(
    ring, tile, own_rows, *refs
):
    grad_rows = refs[:ring]
    (
        weights, grads_t, rows_t, act_all, grads_all, mixed_all, grad_own,
    held, grads_held, acc_n, acc_m, first_part, arrived, outgoing, mixed_stage, final_stage,
    turned, load_sem, keep_sem, grad_sem, mixed_sem, final_sem,
    row_send, row_recv, sum_send, sum_recv, all_sem,
    ) = refs[ring:]
    me = lax.axis_index("tensor")
    right = lax.rem(me + 1, ring)
    left = lax.rem(me + ring - 1, ring)
    hidden = weights.shape[1] // 3
    tiles = hidden // tile

    barrier = pltpu.get_barrier_semaphore()
    for neighbour in (left, right):
        pl.semaphore_signal(barrier, inc=1, device_id={"tensor": neighbour}, device_id_type=MESH)
    pl.semaphore_wait(barrier, 2)

    load = pltpu.make_async_copy(own_rows, held.at[0], load_sem)
    load.start()

    def grad_load(s):
        return pltpu.make_async_copy(grad_rows[s], grads_held.at[s % 2], grad_sem.at[s % 2])

    def part_of(array, s):
        count = own_rows.shape[0]
        return array.at[:, pl.ds(pl.multiple_of(s * count, 128), count)]

    def grad_keep(s):
        return pltpu.make_async_copy(turned.at[1], part_of(grads_t, s), all_sem)

    grad_load(0).start()
    load.wait()

    def pass_rows(s):
        return pltpu.make_async_remote_copy(
            src_ref=held.at[s],
            dst_ref=held.at[s + 1],
            send_sem=row_send.at[s],
            recv_sem=row_recv.at[s],
            device_id={"tensor": right},
            device_id_type=MESH,
        )

    def pass_sum(s):
        return pltpu.make_async_remote_copy(
            src_ref=outgoing.at[s - 1],
            dst_ref=arrived.at[s - 1],
            send_sem=sum_send.at[s - 1],
            recv_sem=sum_recv.at[s - 1],
            device_id={"tensor": right},
            device_id_type=MESH,
        )

    def keep(s):
        return pltpu.make_async_copy(turned.at[0], part_of(rows_t, s), keep_sem)

    def mixed_store(s):
        return pltpu.make_async_copy(mixed_stage, mixed_all.at[s], mixed_sem)

    def chunk(s, carry):
        @pl.when(s > 0)
        def _():
            pass_rows(s - 1).wait_recv()

        @pl.when(s < ring - 1)
        def _():
            pass_rows(s).start()

        @pl.when(s > 0)
        def _():
            keep(s - 1).wait()
            grad_keep(s - 1).wait()

        turned[0] = held[s].T
        keep(s).start()
        for k in range(ring):

            @pl.when(s == k)
            def _(k=k):
                grad_load(k).wait()
                if k < ring - 1:
                    grad_load(k + 1).start()

        slot = lax.rem(s, 2)
        turned[1] = grads_held[slot].T
        grad_keep(s).start()
        acc_n[...] = jnp.zeros_like(acc_n)
        acc_m[...] = jnp.zeros_like(acc_m)

        def body(w_gate, w_up, w_down, act, grad_gate, grad_up):
            rows = held[s]
            gate = dot_nn(rows, w_gate[...])
            up = dot_nn(rows, w_up[...])
            grad_act = dot_nn(grads_held[slot], w_down[...])
            sig = 1.0 / (1.0 + jnp.exp(-gate))
            silu = gate * sig
            low_act = (silu * up).astype(bf16)
            low_up = (grad_act * silu).astype(bf16)
            low_gate = (grad_act * up * sig * (1.0 + gate * (1.0 - sig))).astype(bf16)
            act[...] = low_act
            grad_gate[...] = low_gate
            grad_up[...] = low_up
            acc_m[...] += dot_nt(low_act, w_down[...])
            acc_n[...] += dot_nt(low_gate, w_gate[...]) + dot_nt(low_up, w_up[...])

        width, count = own_rows.shape[1], own_rows.shape[0]
        pltpu.emit_pipeline(
            body,
            grid=(tiles,),
            in_specs=[
                pl.BlockSpec((width, tile), lambda k: (0, k)),
                pl.BlockSpec((width, tile), lambda k: (0, k + tiles)),
                pl.BlockSpec((width, tile), lambda k: (0, k + 2 * tiles)),
            ],
            out_specs=[
                pl.BlockSpec((count, tile), lambda k: (0, k)),
                pl.BlockSpec((count, tile), lambda k: (0, k)),
                pl.BlockSpec((count, tile), lambda k: (0, k + tiles)),
            ],
        )(weights, weights, weights, act_all.at[s], grads_all.at[s], grads_all.at[s])

        @pl.when(s > 0)
        def _():
            mixed_store(s - 1).wait()

        mixed_stage[...] = acc_m[...].astype(bf16)
        mixed_store(s).start()

        @pl.when(s == 0)
        def _():
            first_part[...] = acc_n[...]

        @pl.when(s == 1)
        def _():
            outgoing[0] = acc_n[...].astype(bf16)

        @pl.when(s > 1)
        def _():
            pass_sum(s - 1).wait_recv()
            outgoing[s - 1] = (acc_n[...] + arrived[s - 2].astype(f32)).astype(bf16)

        @pl.when(s > 0)
        def _():
            pass_sum(s).start()

        return carry

    lax.fori_loop(0, ring, chunk, 0)
    mixed_store(ring - 1).wait()
    pass_sum(ring - 1).wait_recv()
    final_stage[...] = (first_part[...] + arrived[ring - 2].astype(f32)).astype(bf16)
    final = pltpu.make_async_copy(final_stage, grad_own, final_sem)
    final.start()

    def settle(s, carry):
        @pl.when(s < ring - 1)
        def _():
            pass_rows(s).wait_send()

        @pl.when(s > 0)
        def _():
            pass_sum(s).wait_send()

        return carry

    lax.fori_loop(0, ring, settle, 0)
    keep(ring - 1).wait()
    grad_keep(ring - 1).wait()
    final.wait()


def feed(own_rows, grad_rows, weights, ring, tile=256, collective_id=7):
    count, width = own_rows.shape
    hidden = weights.shape[1] // 3
    any_spec = pl.BlockSpec(memory_space=pl.ANY)
    dma = pltpu.SemaphoreType.DMA
    return pl.pallas_call(
        functools.partial(feed_kernel, ring, min(tile, hidden)),
        out_shape=[
            jax.ShapeDtypeStruct((width, ring * count), bf16),
            jax.ShapeDtypeStruct((width, ring * count), bf16),
            jax.ShapeDtypeStruct((ring, count, hidden), bf16),
            jax.ShapeDtypeStruct((ring, count, 2 * hidden), bf16),
            jax.ShapeDtypeStruct((ring, count, width), bf16),
            jax.ShapeDtypeStruct((count, width), bf16),
        ],
        in_specs=[any_spec] * (2 + ring),
        out_specs=[any_spec] * 6,
        scratch_shapes=[
            pltpu.VMEM((ring, count, width), bf16),
            pltpu.VMEM((2, count, width), bf16),
            pltpu.VMEM((count, width), f32),
            pltpu.VMEM((count, width), f32),
            pltpu.VMEM((count, width), f32),
            pltpu.VMEM((ring - 1, count, width), bf16),
            pltpu.VMEM((ring - 1, count, width), bf16),
            pltpu.VMEM((count, width), bf16),
            pltpu.VMEM((count, width), bf16),
            pltpu.VMEM((2, width, count), bf16),
            dma,
            dma,
            dma((2,)),
            dma,
            dma,
            dma((ring - 1,)),
            dma((ring - 1,)),
            dma((ring - 1,)),
            dma((ring - 1,)),
            dma,
        ],
        compiler_params=pltpu.CompilerParams(
            collective_id=collective_id, has_side_effects=True, vmem_limit_bytes=64 * 1024 * 1024 - 65536,
        ),
        cost_estimate=pl.CostEstimate(
            flops=12 * ring * count * width * hidden,
            bytes_accessed=8 * ring * count * width,
            transcendentals=ring * count * hidden,
        ),
        name="feed_forward",
    )(own_rows, *grad_rows, weights)


def weigh_kernel(
    tp_count, dp_count, tile, grads, rows_t, grads_t, gate_up, act, slots, out,
    left, left_sem, own_sem, send, recv,
):
    count = dp_count * tp_count
    my_dp = lax.axis_index("dp")
    my_tp = lax.axis_index("tensor")
    me = my_dp * tp_count + my_tp
    page_rows = slots.shape[1]

    loads = [
        pltpu.make_async_copy(source, left.at[k], left_sem.at[k])
        for k, source in enumerate((rows_t, grads_t))
    ]
    for load in loads:
        load.start()

    barrier = pltpu.get_barrier_semaphore()

    def place(peer):
        return {"dp": lax.div(peer, tp_count), "tensor": lax.rem(peer, tp_count)}

    def greet(j, carry):
        peer = lax.rem(me + j, count)
        pl.semaphore_signal(barrier, inc=1, device_id=place(peer), device_id_type=MESH)
        return carry

    lax.fori_loop(1, count, greet, 0)
    pl.semaphore_wait(barrier, count - 1)

    home = slots.at[my_tp * dp_count + my_dp]

    def block(p_dp, p_tp):
        return grads.at[p_tp, pl.ds(p_dp * page_rows, page_rows), :]

    own = pltpu.make_async_copy(block(my_dp, my_tp), home, own_sem)
    own.start()

    def copy_to(j):
        peer = lax.rem(me + j, count)
        return pltpu.make_async_remote_copy(
            src_ref=block(lax.div(peer, tp_count), lax.rem(peer, tp_count)),
            dst_ref=home,
            send_sem=send.at[j],
            recv_sem=recv.at[j],
            device_id=place(peer),
            device_id_type=MESH,
        )

    def start(j, carry):
        copy_to(j).start()
        return carry

    def finish(j, carry):
        copy_to(j).wait()
        return carry

    lax.fori_loop(1, count, start, 0)

    width = rows_t.shape[0]
    step = min(512, width)

    def multiply(k, right, first):
        ring, rows, cols = right.shape

        def body(part, result):
            values = part[...].reshape(ring * rows, tile)
            for m in range(0, width, step):
                result[m : m + step, :] = dot_nn(left[k, m : m + step, :], values).astype(bf16)

        pltpu.emit_pipeline(
            body,
            grid=(cols // tile,),
            in_specs=[pl.BlockSpec((ring, rows, tile), lambda n: (0, 0, n))],
            out_specs=[pl.BlockSpec((width, tile), lambda n: (0, n + first))],
        )(right, out)

    loads[0].wait()
    multiply(0, gate_up, 0)
    loads[1].wait()
    multiply(1, act, gate_up.shape[2] // tile)
    own.wait()
    lax.fori_loop(1, count, finish, 0)


def weigh(grads, rows_t, grads_t, gate_up, act, tp_count, dp_count, collective_id):
    count = tp_count * dp_count
    cols = grads.shape[2]
    page_rows = grads.shape[1] // dp_count
    width, rows = rows_t.shape
    hidden = act.shape[2]
    any_spec = pl.BlockSpec(memory_space=pl.ANY)
    dma = pltpu.SemaphoreType.DMA
    return pl.pallas_call(
        functools.partial(weigh_kernel, tp_count, dp_count, min(512, hidden)),
        out_shape=[
            jax.ShapeDtypeStruct((count, page_rows, cols), bf16),
            jax.ShapeDtypeStruct((width, 3 * hidden), bf16),
        ],
        in_specs=[any_spec] * 5,
        out_specs=[any_spec] * 2,
        scratch_shapes=[
            pltpu.VMEM((2, width, rows), bf16),
            dma((2,)),
            dma,
            dma((count,)),
            dma((count,)),
        ],
        compiler_params=pltpu.CompilerParams(
            collective_id=collective_id, has_side_effects=True, vmem_limit_bytes=48 * 1024 * 1024
        ),
        cost_estimate=pl.CostEstimate(
            flops=6 * rows * width * hidden,
            bytes_accessed=2 * width * (2 * rows + 3 * hidden),
            transcendentals=0,
        ),
        name="weigh",
    )(grads, rows_t, grads_t, gate_up, act)


def flip(index, bit):
    return index + bit - 2 * bit * lax.rem(lax.div(index, bit), 2)


def collect_kernel(
    tp_count, dp_count, hops, shard, second, gains, chunk, out, second_out, gains_out, chunks_out,
    second_send, second_recv, own_sem, ring_send, ring_recv, send, recv, gain_send, gain_recv, chunk_send, chunk_recv,
):
    my_dp = lax.axis_index("dp")
    my_tp = lax.axis_index("tensor")
    rows = shard.shape[0]
    half = rows // 2
    bits = [1 << b for b in reversed(range(dp_count.bit_length() - 1))]
    orders = [bits, bits[:-1][::-1] + bits[-1:]]
    steps = len(bits)

    barrier = pltpu.get_barrier_semaphore()
    for j in range(1, tp_count):
        pl.semaphore_signal(
            barrier, inc=1, device_id={"tensor": lax.rem(my_tp + j, tp_count)}, device_id_type=MESH
        )
    for j in range(1, dp_count):
        pl.semaphore_signal(
            barrier, inc=1, device_id={"dp": lax.rem(my_dp + j, dp_count)}, device_id_type=MESH
        )
    pl.semaphore_wait(barrier, tp_count + dp_count - 2)

    home = out.at[my_tp, pl.ds(my_dp * rows, rows), :]
    own = pltpu.make_async_copy(shard, home, own_sem.at[0])
    own.start()
    own_gain = pltpu.make_async_copy(gains, gains_out.at[my_dp], own_sem.at[1])
    own_gain.start()
    own_second = pltpu.make_async_copy(second, second_out.at[my_tp], own_sem.at[2])
    own_second.start()

    def second_copy(j):
        return pltpu.make_async_remote_copy(
            src_ref=second,
            dst_ref=second_out.at[my_tp],
            send_sem=second_send.at[j],
            recv_sem=second_recv.at[j],
            device_id={"tensor": lax.rem(my_tp + j, tp_count)},
            device_id_type=MESH,
        )

    def across(j):
        return pltpu.make_async_remote_copy(
            src_ref=shard,
            dst_ref=home,
            send_sem=ring_send.at[j],
            recv_sem=ring_recv.at[j],
            device_id={"tensor": lax.rem(my_tp + j, tp_count)},
            device_id_type=MESH,
        )

    def gain_copy(j):
        return pltpu.make_async_remote_copy(
            src_ref=gains,
            dst_ref=gains_out.at[my_dp],
            send_sem=gain_send.at[j],
            recv_sem=gain_recv.at[j],
            device_id={"dp": lax.rem(my_dp + j, dp_count)},
            device_id_type=MESH,
        )

    def onward(hop):
        return pltpu.make_async_remote_copy(
            src_ref=chunk if hop == 0 else chunks_out.at[hop - 1],
            dst_ref=chunks_out.at[hop],
            send_sem=chunk_send.at[hop],
            recv_sem=chunk_recv.at[hop],
            device_id={"tensor": lax.rem(my_tp + 1, tp_count)},
            device_id_type=MESH,
        )

    def within(j, s, k, m):
        order = orders[s]
        owner = my_dp
        for b in range(k):
            if m >> b & 1:
                owner = flip(owner, order[b])
        block = out.at[
            lax.rem(my_tp - j + tp_count, tp_count), pl.ds(owner * rows + s * half, half), :
        ]
        at = (1 << k) - 1 + m
        return pltpu.make_async_remote_copy(
            src_ref=block,
            dst_ref=block,
            send_sem=send.at[j, s, at],
            recv_sem=recv.at[j, s, at],
            device_id={"dp": flip(my_dp, order[k])},
            device_id_type=MESH,
        )

    for j in range(1, tp_count):
        across(j).start()
    for j in range(1, dp_count):
        gain_copy(j).start()
    onward(0).start()
    own.wait()
    for phase in range(tp_count + steps):
        for k in reversed(range(steps + 1)):
            j = phase - k
            if not 0 <= j < tp_count:
                continue
            if k == 0:
                if j > 0:
                    across(j).wait_recv()
            else:
                for s in range(2):
                    for m in range(1 << (k - 1)):
                        within(j, s, k - 1, m).wait_recv()
            if k < steps:
                for s in range(2):
                    for m in range(1 << k):
                        within(j, s, k, m).start()
        if phase == tp_count:
            for j in range(1, tp_count):
                second_copy(j).start()
        if tp_count <= phase < tp_count + hops - 1:
            onward(phase - tp_count).wait_recv()
            onward(phase - tp_count + 1).start()
    for j in range(tp_count):
        if j > 0:
            across(j).wait_send()
        for s in range(2):
            for k in range(steps):
                for m in range(1 << k):
                    within(j, s, k, m).wait_send()
    own_gain.wait()
    own_second.wait()
    for j in range(1, tp_count):
        second_copy(j).wait()
    for j in range(1, dp_count):
        gain_copy(j).wait()
    for hop in range(hops):
        if hop == hops - 1:
            onward(hop).wait_recv()
        onward(hop).wait_send()


def collect(shard, second, gains, chunk, tp_count, dp_count, hops, collective_id):
    rows, cols = shard.shape
    dma = pltpu.SemaphoreType.DMA
    vmem_spec = pl.BlockSpec(memory_space=pltpu.VMEM)
    any_spec = pl.BlockSpec(memory_space=pl.ANY)
    return pl.pallas_call(
        functools.partial(collect_kernel, tp_count, dp_count, hops),
        out_shape=[
            jax.ShapeDtypeStruct((tp_count, dp_count * rows, cols), shard.dtype),
            jax.ShapeDtypeStruct((tp_count,) + second.shape, second.dtype),
            jax.ShapeDtypeStruct((dp_count,) + gains.shape, gains.dtype),
            jax.ShapeDtypeStruct((hops,) + chunk.shape, chunk.dtype),
        ],
        in_specs=[vmem_spec, vmem_spec, vmem_spec, any_spec],
        out_specs=[any_spec] * 4,
        scratch_shapes=[
            dma((tp_count,)),
            dma((tp_count,)),
            dma((3,)),
            dma((tp_count,)),
            dma((tp_count,)),
            dma((tp_count, 2, dp_count - 1)),
            dma((tp_count, 2, dp_count - 1)),
            dma((dp_count,)),
            dma((dp_count,)),
            dma((hops,)),
            dma((hops,)),
        ],
        compiler_params=pltpu.CompilerParams(collective_id=collective_id, has_side_effects=True),
        cost_estimate=pl.CostEstimate(
            flops=0, bytes_accessed=16 * tp_count * dp_count * shard.size, transcendentals=0
        ),
        name="collect",
    )(shard, second, gains, chunk)


def spread_kernel(rows, weight, out):
    out[0] = dot_nn(rows[...], weight[0]).astype(out.dtype)


def spread(rows, weights, part, cols):
    shards, width, _ = weights.shape
    count = rows.shape[0]
    return pl.pallas_call(
        spread_kernel,
        grid=(shards,),
        in_specs=[
            pl.BlockSpec((count, width), lambda t: (0, 0)),
            pl.BlockSpec((1, width, cols), lambda t: (t, 0, part)),
        ],
        out_specs=pl.BlockSpec((1, count, cols), lambda t: (t, 0, 0)),
        out_shape=jax.ShapeDtypeStruct((shards, count, cols), bf16),
        cost_estimate=pl.CostEstimate(
            flops=2 * shards * count * width * cols,
            bytes_accessed=2 * shards * width * cols,
            transcendentals=0,
        ),
        name="spread",
    )(rows, weights)


def gather_kernel(has_begin, part, weight, *refs):
    out = refs[-1]

    @pl.when(pl.program_id(0) == 0)
    def _():
        out[...] = refs[0][...] if has_begin else jnp.zeros_like(out)

    out[...] += dot_nt(part[0], weight[0])


def gather_sum(parts, weights, part, begin):
    shards, count, cols = parts.shape
    width = weights.shape[1]
    whole = pl.BlockSpec((count, width), lambda t: (0, 0))
    begins = [] if begin is None else [begin]
    return pl.pallas_call(
        functools.partial(gather_kernel, begin is not None),
        grid=(shards,),
        in_specs=[
            pl.BlockSpec((1, count, cols), lambda t: (t, 0, 0)),
            pl.BlockSpec((1, width, cols), lambda t: (t, 0, part)),
        ]
        + [whole] * len(begins),
        out_specs=whole,
        out_shape=jax.ShapeDtypeStruct((count, width), f32),
        cost_estimate=pl.CostEstimate(
            flops=2 * shards * count * width * cols,
            bytes_accessed=2 * shards * width * cols,
            transcendentals=0,
        ),
        name="gather_sum",
    )(parts, weights, *begins)


def outer_kernel(rows, *refs):
    parts, out, turned = refs[:-2], refs[-2], refs[-1]

    @pl.when(pl.program_id(0) == 0)
    def _():
        turned[...] = rows[...].T

    at = 0
    for part in parts:
        cols = part.shape[2]
        out[:, at : at + cols] = dot_nn(turned[...], part[0]).astype(out.dtype)
        at += cols


def outer(rows, parts):
    shards, count, _ = parts[0].shape
    cols = sum(part.shape[2] for part in parts)
    width = rows.shape[1]
    return pl.pallas_call(
        outer_kernel,
        grid=(shards,),
        in_specs=[pl.BlockSpec((count, width), lambda t: (0, 0))]
        + [pl.BlockSpec((1, count, part.shape[2]), lambda t: (t, 0, 0)) for part in parts],
        out_specs=pl.BlockSpec((width, cols), lambda t: (0, t)),
        out_shape=jax.ShapeDtypeStruct((width, shards * cols), bf16),
        scratch_shapes=[pltpu.VMEM((width, count), bf16)],
        cost_estimate=pl.CostEstimate(
            flops=2 * shards * count * width * cols,
            bytes_accessed=2 * shards * width * cols,
            transcendentals=0,
        ),
        name="outer",
    )(rows, *parts)


def rms_scale(hidden):
    return lax.rsqrt(jnp.mean(hidden * hidden, axis=1, keepdims=True) + epsilon)


def norm_back(grad_norm, hidden, scale_rows, gain):
    normed = hidden * scale_rows
    gain_part = jnp.sum(grad_norm * normed, axis=0)
    inner = grad_norm * gain
    grad_hidden = scale_rows * (inner - normed * jnp.mean(inner * normed, axis=1, keepdims=True))
    return (grad_hidden, gain_part)


def after(value, other):
    return lax.optimization_barrier((value, other))[0]


def local(
    tokens,
    upstream,
    lengths,
    positions,
    pages,
    attn_gain,
    w_query,
    w_key,
    w_value,
    w_out,
    mlp_gain,
    w_gate,
    w_up,
    w_down,
):
    dp_count = lax.axis_size("dp")
    tp_count = lax.axis_size("tensor")
    dp_index = lax.axis_index("dp")
    tp_index = lax.axis_index("tensor")
    tok_dev, width = tokens.shape
    tok_group = tok_dev * tp_count
    page_rows = tok_dev // dp_count
    group_pages = tp_count * dp_count
    page_count = pages.shape[0]
    device = dp_index * tp_count + tp_index
    everyone = ("tensor", "dp")

    local_ids = jnp.arange(dp_count, dtype=jnp.int32)
    inverse = (
        jnp.zeros((page_count,), jnp.int32).at[pages].set(jnp.arange(page_count, dtype=jnp.int32))
    )
    dealt = lax.dynamic_slice_in_dim(inverse, device * dp_count, dp_count)
    dest_group = dealt // group_pages
    send_order = jnp.zeros((dp_count,), jnp.int32).at[dest_group].set(local_ids)
    group_sources = lax.dynamic_slice_in_dim(pages, dp_index * group_pages, group_pages)
    perm = (
        (jnp.arange(group_pages, dtype=jnp.int32) // dp_count) * dp_count
        + group_sources // group_pages
    ).astype(jnp.int32)

    def reorder(rows, order):
        blocks = rows.reshape(dp_count, page_rows, rows.shape[1])
        return jnp.take(blocks, order, axis=0, mode="clip").reshape(rows.shape)

    hidden_in = reorder(tokens, send_order).astype(f32)
    grad_top = reorder(upstream, send_order).astype(f32)
    seq_lens = lengths[0]
    seq_ends = jnp.cumsum(seq_lens)
    place = (jnp.take(dealt, send_order, mode="clip") % group_pages) * page_rows
    place_rows = (place[:, None] + jnp.arange(page_rows, dtype=jnp.int32)[None, :]).reshape(-1)
    valid_rows = (place_rows < seq_ends[-1]).astype(f32)[:, None]

    row_ids = jnp.arange(tok_group, dtype=jnp.int32)
    begin = jnp.max(
        jnp.where(row_ids[:, None] >= seq_ends[None, :], seq_ends[None, :], 0), axis=1
    ).astype(jnp.int32)
    block_len = min(block_rows, tok_group)
    first_block = begin[::block_len] // min(key_rows, tok_group)
    begin = begin[None, :]
    inverse_freq = theta_base ** (-(jnp.arange(HALF, dtype=f32) * 2.0) / HD)
    angles = inverse_freq[:, None] * positions.astype(f32)
    cos_t, sin_t = jnp.cos(angles), jnp.sin(angles)

    q_cols, kv_cols = w_query.shape[1], w_key.shape[1]
    kv_heads = kv_cols // HD
    per_group = q_cols // kv_cols
    group_q = per_group * HD
    groups = range(kv_heads)
    qkv_shard = jnp.concatenate(
        [
            part
            for g in groups
            for part in (
                w_query[:, g * group_q : (g + 1) * group_q],
                w_key[:, g * HD : (g + 1) * HD],
                w_value[:, g * HD : (g + 1) * HD],
            )
        ],
        axis=1,
    )

    def trade(value):
        blocks = value.reshape(group_pages, page_rows, value.shape[-1])
        return lax.all_to_all(blocks, everyone, split_axis=0, concat_axis=0, tiled=True)

    def trade_back(value):
        return trade(value).reshape(tp_count, tok_dev, value.shape[-1])

    ring_next = [(t, (t + 1) % tp_count) for t in range(tp_count)]

    def pass_on(value):
        return lax.ppermute(value, "tensor", ring_next)

    grad_out = grad_top * valid_rows
    grad_chunks = [grad_out.astype(bf16)]
    mlp_shard = jnp.concatenate([w_gate, w_up, w_down.T], axis=1)
    w_mlp = lax.all_gather(mlp_shard, "dp", axis=0, tiled=True)
    hops = min(2, tp_count - 1)
    w_qkv, out_shards, gains, got_chunks = collect(
        qkv_shard, w_out.T, jnp.stack([attn_gain, mlp_gain]), grad_chunks[0], tp_count, dp_count,
        hops, 1,
    )
    w_out_t = lax.all_gather(out_shards, "dp", axis=1, tiled=True)
    grad_chunks += [got_chunks[hop] for hop in range(hops)]
    gains = gains.transpose(1, 0, 2).reshape(2, -1).astype(f32)
    gain_one, gain_two = gains[0], gains[1]

    scale_one = rms_scale(hidden_in)
    normed_one = (hidden_in * scale_one * gain_one).astype(bf16)
    slots = project(normed_one, w_qkv, dp_count, 3)
    for hop in range(hops + 1, tp_count):
        grad_chunks.append(pass_on(after(grad_chunks[-1], slots)))
    saved, mixed = [], []
    for g in groups:
        q_t, k_t, k_rows, v_t, v_rows = prepare(
            after(slots, (o_slots, w_mlp)) if g else slots, g, perm, cos_t, sin_t, per_group, 1
        )
        o_t, lse, o_slots = attend_forward(
            q_t, k_rows, v_t, begin, first_block, perm, page_rows, block_len
        )
        saved.append((q_t, k_rows, k_t, v_rows, o_t, lse))
        mixed.append(trade_back(after(o_slots, grad_chunks[-1]) if g else o_slots))
    hidden_mid = hidden_in
    for g in groups:
        hidden_mid = gather_sum(mixed[g], w_out_t, g, hidden_mid)

    scale_two = rms_scale(hidden_mid)
    normed_two = (hidden_mid * scale_two * gain_two).astype(bf16)
    grads_t, rows_t, inner_act, grad_gate_up, partial_two, grad_normed_two = feed(
        normed_two, grad_chunks, w_mlp, tp_count
    )
    grad_normed_two = grad_normed_two.astype(f32)
    grad_mid_norm, gain_two_part = norm_back(grad_normed_two, hidden_mid, scale_two, gain_two)
    grad_mid = grad_out + grad_mid_norm

    def add_on(arrived, s):
        return (arrived.astype(f32) + partial_two[s].astype(f32)).astype(bf16)

    def reduce_dp(grad):
        return lax.psum_scatter(grad.astype(bf16), "dp", scatter_dimension=0, tiled=True)

    def reduce_tensor(value):
        cols = value.shape[1] // tp_count
        total = lax.dynamic_slice_in_dim(value, tp_index * cols, cols, 1).astype(f32)
        for s in range(1, tp_count):
            target = lax.rem(tp_index + s, tp_count)
            block = lax.dynamic_slice_in_dim(value, target * cols, cols, 1)
            pairs = [(t, (t + s) % tp_count) for t in range(tp_count)]
            total = total + lax.ppermute(block, "tensor", pairs).astype(f32)
        return total

    grad_z = grad_mid.astype(bf16)
    grad_wout = outer(grad_z, mixed)
    sum_out = reduce_dp(grad_wout)
    grad_slots, grad_wmlp = weigh(
        spread(after(grad_z, grad_wout), w_out_t, 0, q_cols),
        rows_t, grads_t, grad_gate_up, inner_act, tp_count, dp_count, 2,
    )
    sum_mlp = reduce_dp(grad_wmlp)
    branch_two = pass_on(after(partial_two[1], grad_slots))
    grad_qkv = []
    for g in groups:
        q_t, k_rows, k_t, v_rows, o_t, lse = saved[g]
        back = attend_backward(
            grad_slots if g == 0 else after(grad_slots, (back, sum_out)), g, q_t,
            k_rows, k_t, v_rows, o_t, lse, begin, cos_t, sin_t, first_block, perm, page_rows,
            block_len,
        )
        grad_qkv.append(trade_back(after(back, (grad_qkv[-1], branch_two)) if grad_qkv else back))
    hidden = sum_mlp.shape[1] // 3
    sum_out = reduce_tensor(sum_out)
    for s in range(2, tp_count - 1):
        branch_two = pass_on(add_on(after(branch_two, tuple(grad_qkv)), s))
    grad_wqkv = outer(after(normed_one, (sum_mlp, sum_out)), grad_qkv)
    sum_qkv = reduce_tensor(reduce_dp(grad_wqkv))
    each = group_q + 2 * HD
    sum_qkv = [sum_qkv[:, g * each : (g + 1) * each] for g in groups]
    grad_normed_one = None
    for g in groups:
        grad_normed_one = gather_sum(after(grad_qkv[g], grad_wqkv), w_qkv, g, grad_normed_one)
    branch_two = pass_on(add_on(after(branch_two, grad_normed_one), tp_count - 1))
    result = (
        (after(hidden_mid, back) + branch_two.astype(f32) + partial_two[0].astype(f32)) * valid_rows
    ).astype(bf16)
    grad_in_norm, gain_one_part = norm_back(grad_normed_one, hidden_in, scale_one, gain_one)
    grad_in = (grad_mid + grad_in_norm).astype(bf16)

    gain_parts = jnp.stack([gain_one_part, gain_two_part]).reshape(2, dp_count, -1)
    gain_parts = jnp.broadcast_to(
        gain_parts.transpose(1, 0, 2)[None], (tp_count, dp_count, 2, gain_parts.shape[2])
    ).reshape(group_pages, 2, -1)
    gain_sums = jnp.sum(
        lax.all_to_all(gain_parts, everyone, split_axis=0, concat_axis=0, tiled=True), axis=0
    )
    return (
        reorder(result, dest_group),
        reorder(grad_in, dest_group),
        gain_sums[0],
        jnp.concatenate([part[:, :group_q] for part in sum_qkv], axis=1),
        jnp.concatenate([part[:, group_q : group_q + HD] for part in sum_qkv], axis=1),
        jnp.concatenate([part[:, group_q + HD :] for part in sum_qkv], axis=1),
        sum_out.T,
        gain_sums[1],
        sum_mlp[:, :hidden].astype(f32),
        sum_mlp[:, hidden : 2 * hidden].astype(f32),
        sum_mlp[:, 2 * hidden :].astype(f32).T,
    )


def solution(mesh):
    rows = P(("dp", "tensor"), None)
    weight = P("dp", "tensor")
    weight_t = P("tensor", "dp")
    return jax.shard_map(
        local,
        mesh=mesh,
        in_specs=(
            rows,
            rows,
            P("dp", None),
            P("dp", None),
            P(),
            P("dp"),
            weight,
            weight,
            weight,
            weight_t,
            P("dp"),
            weight,
            weight,
            weight_t,
        ),
        out_specs=(
            rows,
            rows,
            P("dp"),
            weight,
            weight,
            weight,
            weight_t,
            P("dp"),
            weight,
            weight,
            weight_t,
        ),
        check_vma=False,
    )
```

```python
import functools

import jax
import jax.numpy as jnp
from jax import lax
from jax.experimental import pallas as pl
from jax.experimental.pallas import tpu as pltpu
from jax.sharding import PartitionSpec as P

HD = 64
HALF = HD // 2

epsilon = 1e-05
theta_base = 500000.0
masked_score = -1e30
score_scale = HD**-0.5
block_rows = 512
key_rows = 256
MESH = pl.DeviceIdType.MESH
f32 = jnp.float32
bf16 = jnp.bfloat16


def dot_nn(left, right):
    return lax.dot_general(left, right, (((1,), (0,)), ((), ())), preferred_element_type=f32)


def dot_nt(left, right):
    return lax.dot_general(left, right, (((1,), (1,)), ((), ())), preferred_element_type=f32)


def dot_tn(left, right):
    return lax.dot_general(left, right, (((0,), (0,)), ((), ())), preferred_element_type=f32)


def prep_kernel(pages_per, q_heads, kv_heads, perm, *refs):
    page_refs = refs[:pages_per]
    cos_ref, sin_ref, q_t, k_t, k_rows, v_t, v_rows = refs[pages_per:]
    rows = jnp.concatenate([r[0].astype(f32) for r in page_refs], axis=0)
    turned = rows.T
    cos, sin = cos_ref[...], sin_ref[...]

    def rope(base):
        first, second = turned[base : base + HALF], turned[base + HALF : base + HD]
        return jnp.concatenate([first * cos - second * sin, second * cos + first * sin], axis=0)

    for h in range(q_heads):
        roped = rope(h * HD).astype(bf16)
        q_t[h * HD : (h + 1) * HD, :] = (roped.astype(f32) * score_scale).astype(bf16)
    k_base = q_heads * HD
    v_base = k_base + kv_heads * HD
    for g in range(kv_heads):
        roped = rope(k_base + g * HD)
        k_t[g * HD : (g + 1) * HD, :] = roped.astype(bf16)
        k_rows[g] = roped.T.astype(bf16)
        v_t[g * HD : (g + 1) * HD, :] = turned[v_base + g * HD : v_base + (g + 1) * HD].astype(bf16)
        v_rows[g] = rows[:, v_base + g * HD : v_base + (g + 1) * HD].astype(bf16)


def prepare(slots, part, perm, cos_t, sin_t, q_heads, kv_heads):
    page_rows = slots.shape[1]
    cols = (q_heads + 2 * kv_heads) * HD
    total_rows = slots.shape[0] * page_rows
    lanes = min(256, total_rows)
    pages_per = lanes // page_rows

    def page_spec(a):
        return pl.BlockSpec(
            (1, page_rows, cols), lambda i, perm_ref, a=a: (perm_ref[i * pages_per + a], 0, part)
        )

    table = pl.BlockSpec((HALF, lanes), lambda i, perm_ref: (0, i))
    return pl.pallas_call(
        functools.partial(prep_kernel, pages_per, q_heads, kv_heads),
        grid_spec=pltpu.PrefetchScalarGridSpec(
            num_scalar_prefetch=1,
            grid=(total_rows // lanes,),
            in_specs=[page_spec(a) for a in range(pages_per)] + [table, table],
            out_specs=[
                pl.BlockSpec((q_heads * HD, lanes), lambda i, perm_ref: (0, i)),
                pl.BlockSpec((kv_heads * HD, lanes), lambda i, perm_ref: (0, i)),
                pl.BlockSpec((kv_heads, lanes, HD), lambda i, perm_ref: (0, i, 0)),
                pl.BlockSpec((kv_heads * HD, lanes), lambda i, perm_ref: (0, i)),
                pl.BlockSpec((kv_heads, lanes, HD), lambda i, perm_ref: (0, i, 0)),
            ],
        ),
        out_shape=[
            jax.ShapeDtypeStruct((q_heads * HD, total_rows), bf16),
            jax.ShapeDtypeStruct((kv_heads * HD, total_rows), bf16),
            jax.ShapeDtypeStruct((kv_heads, total_rows, HD), bf16),
            jax.ShapeDtypeStruct((kv_heads * HD, total_rows), bf16),
            jax.ShapeDtypeStruct((kv_heads, total_rows, HD), bf16),
        ],
        cost_estimate=pl.CostEstimate(
            flops=8 * slots.size, bytes_accessed=6 * slots.size, transcendentals=0
        ),
        name="prepare",
    )(perm, *([slots] * pages_per), cos_t, sin_t)


def block_bias(i, j, begin_row, block_len, key_len):
    keys = j * key_len + lax.broadcasted_iota(jnp.int32, (key_len, block_len), 0)
    queries = i * block_len + lax.broadcasted_iota(jnp.int32, (key_len, block_len), 1)
    allowed = (keys >= begin_row) & (keys <= queries)
    return jnp.where(allowed, 0.0, masked_score)


def forward_kernel(
    q_heads, kv_heads, page_rows, first_block, perm,
    q_t, k_rows, v_t, begin, o_t, lse, o_slots, acc, stage, sems,
):
    i = pl.program_id(0)
    block_len = q_t.shape[1]
    key_len = min(key_rows, k_rows.shape[1])
    per_group = q_heads // kv_heads
    acc[...] = jnp.zeros_like(acc)
    begin_row = begin[...]

    def visit(j, carry):
        bias = block_bias(i, j, begin_row, block_len, key_len)
        at = pl.ds(pl.multiple_of(j * key_len, key_len), key_len)
        scores = [
            dot_nn(k_rows[h // per_group, at, :], q_t[h * HD : (h + 1) * HD, :]) + bias
            for h in range(q_heads)
        ]
        tops = [
            jnp.maximum(carry[h][0], jnp.max(scores[h], axis=0, keepdims=True))
            for h in range(q_heads)
        ]
        weights = [jnp.exp(scores[h] - tops[h]) for h in range(q_heads)]
        fades = [jnp.exp(carry[h][0] - tops[h]) for h in range(q_heads)]
        totals = [
            carry[h][1] * fades[h] + jnp.sum(weights[h], axis=0, keepdims=True)
            for h in range(q_heads)
        ]
        for h in range(q_heads):
            g = h // per_group
            span = slice(h * HD, (h + 1) * HD)
            acc[span, :] = acc[span, :] * fades[h] + dot_nn(
                v_t[g * HD : (g + 1) * HD, at], weights[h].astype(bf16)
            )
        return tuple(zip(tops, totals))

    start = tuple(
        (jnp.full((1, block_len), masked_score, f32), jnp.zeros((1, block_len), f32))
        for _ in range(q_heads)
    )
    stats = lax.fori_loop(
        first_block[i], lax.div((i + 1) * block_len - 1, key_len) + 1, visit, start
    )
    for h in range(q_heads):
        lse[h : h + 1, :] = stats[h][0] + jnp.log(stats[h][1])
    mixed = jnp.concatenate(
        [acc[h * HD : (h + 1) * HD, :] / stats[h][1] for h in range(q_heads)], axis=0
    )
    o_t[...] = mixed.astype(bf16)
    pages = block_len // page_rows
    stage[...] = mixed.T.astype(bf16).reshape(pages, page_rows, q_heads * HD)
    copies = [
        pltpu.make_async_copy(stage.at[a], o_slots.at[perm[i * pages + a]], sems.at[a])
        for a in range(pages)
    ]
    for copy in copies:
        copy.start()
    for copy in copies:
        copy.wait()


def attend_forward(q_t, k_rows, v_t, begin, first_block, perm, page_rows, block_len):
    total_rows = q_t.shape[1]
    kv_heads = k_rows.shape[0]
    q_heads = q_t.shape[0] // HD
    pages = block_len // page_rows
    return pl.pallas_call(
        functools.partial(forward_kernel, q_heads, kv_heads, page_rows),
        grid_spec=pltpu.PrefetchScalarGridSpec(
            num_scalar_prefetch=2,
            grid=(total_rows // block_len,),
            in_specs=[
                pl.BlockSpec((q_heads * HD, block_len), lambda i, *_: (0, i)),
                pl.BlockSpec((kv_heads, total_rows, HD), lambda i, *_: (0, 0, 0)),
                pl.BlockSpec((kv_heads * HD, total_rows), lambda i, *_: (0, 0)),
                pl.BlockSpec((1, block_len), lambda i, *_: (0, i)),
            ],
            out_specs=[
                pl.BlockSpec((q_heads * HD, block_len), lambda i, *_: (0, i)),
                pl.BlockSpec((q_heads, block_len), lambda i, *_: (0, i)),
                pl.BlockSpec(memory_space=pl.ANY),
            ],
            scratch_shapes=[
                pltpu.VMEM((q_heads * HD, block_len), f32),
                pltpu.VMEM((pages, page_rows, q_heads * HD), bf16),
                pltpu.SemaphoreType.DMA((pages,)),
            ],
        ),
        out_shape=[
            jax.ShapeDtypeStruct((q_heads * HD, total_rows), bf16),
            jax.ShapeDtypeStruct((q_heads, total_rows), f32),
            jax.ShapeDtypeStruct((total_rows // page_rows, page_rows, q_heads * HD), bf16),
        ],
        cost_estimate=pl.CostEstimate(
            flops=q_heads * total_rows * total_rows * HD,
            bytes_accessed=8 * q_t.size,
            transcendentals=q_heads * total_rows * total_rows // 4,
        ),
        name="attend_forward",
    )(first_block, perm, q_t, k_rows, v_t, begin)


def backward_kernel(
    q_heads, kv_heads, page_rows, pages, first_block, perm, *refs
):
    grad_pages = refs[:pages]
    (
        q_t, k_rows, k_t, v_rows, o_t, lse, begin, cos_ref, sin_ref, cos_all, sin_all,
        out, grad_q, grad_k, grad_v, stage, kv_stage, sems, kv_sems,
    ) = refs[pages:]
    i = pl.program_id(0)
    steps = pl.num_programs(0)
    block_len = q_t.shape[1]
    key_len = min(key_rows, k_rows.shape[1])
    per_group = q_heads // kv_heads
    q_cols = q_heads * HD
    kv_cols = kv_heads * HD

    @pl.when(i == 0)
    def _():
        grad_k[...] = jnp.zeros_like(grad_k)
        grad_v[...] = jnp.zeros_like(grad_v)

    grad_rows = jnp.concatenate([r[0].astype(f32) for r in grad_pages], axis=0)
    grad_t = grad_rows.T
    grad_low = grad_t.astype(bf16)
    inner = [
        jnp.sum(
            grad_t[h * HD : (h + 1) * HD] * o_t[h * HD : (h + 1) * HD, :].astype(f32),
            axis=0,
            keepdims=True,
        )
        for h in range(q_heads)
    ]
    grad_q[...] = jnp.zeros_like(grad_q)
    begin_row = begin[...]

    def visit(j, carry):
        bias = block_bias(i, j, begin_row, block_len, key_len)
        at = pl.ds(pl.multiple_of(j * key_len, key_len), key_len)
        for g in range(kv_heads):
            kv_span = slice(g * HD, (g + 1) * HD)
            keys, vals, keys_t = k_rows[g, at, :], v_rows[g, at, :], k_t[kv_span, at]
            heads = range(g * per_group, (g + 1) * per_group)
            spans = [slice(h * HD, (h + 1) * HD) for h in heads]
            scores = [dot_nn(keys, q_t[span, :]) + bias for span in spans]
            grad_probs = [dot_nn(vals, grad_low[span]) for span in spans]
            probs = [jnp.exp(s - lse[h : h + 1, :]) for s, h in zip(scores, heads)]
            grad_scores = [
                (p * (d - inner[h])).astype(bf16) for p, d, h in zip(probs, grad_probs, heads)
            ]
            low_probs = [p.astype(bf16) for p in probs]
            grad_v[kv_span, at] += sum(
                dot_nt(grad_low[span], p) for span, p in zip(spans, low_probs)
            )
            grad_k[kv_span, at] += sum(
                dot_nt(q_t[span, :], d) for span, d in zip(spans, grad_scores)
            )
            for span, d in zip(spans, grad_scores):
                grad_q[span, :] += dot_nn(keys_t, d)
        return carry

    lax.fori_loop(first_block[i], lax.div((i + 1) * block_len - 1, key_len) + 1, visit, 0)

    def unrope(value, cos, sin):
        first, second = value[:HALF], value[HALF:]
        return jnp.concatenate([first * cos + second * sin, second * cos - first * sin], axis=0)

    cos, sin = cos_ref[...], sin_ref[...]
    parts = [
        unrope(grad_q[h * HD : (h + 1) * HD, :] * score_scale, cos, sin) for h in range(q_heads)
    ]
    stage[...] = jnp.concatenate(parts, axis=0).T.astype(bf16).reshape(pages, page_rows, q_cols)
    copies = [
        pltpu.make_async_copy(
            stage.at[a], out.at[perm[i * pages + a], :, pl.ds(0, q_cols)], sems.at[a]
        )
        for a in range(pages)
    ]
    for copy in copies:
        copy.start()
    for copy in copies:
        copy.wait()

    @pl.when(i == steps - 1)
    def _():
        all_pages = kv_stage.shape[0]
        cos, sin = cos_all[...], sin_all[...]
        parts = [unrope(grad_k[g * HD : (g + 1) * HD, :], cos, sin) for g in range(kv_heads)]
        both = jnp.concatenate(parts + [grad_v[...]], axis=0)
        kv_stage[...] = both.T.astype(bf16).reshape(all_pages, page_rows, 2 * kv_cols)
        copies = [
            pltpu.make_async_copy(
                kv_stage.at[a], out.at[perm[a], :, pl.ds(q_cols, 2 * kv_cols)], kv_sems.at[a]
            )
            for a in range(all_pages)
        ]
        for copy in copies:
            copy.start()
        for copy in copies:
            copy.wait()


def attend_backward(
    grad_slots, part, q_t, k_rows, k_t, v_rows, o_t, lse, begin, cos_t, sin_t, first_block, perm,
    page_rows, block_len,
):
    total_rows = q_t.shape[1]
    kv_heads = k_rows.shape[0]
    q_heads = q_t.shape[0] // HD
    pages = block_len // page_rows
    all_pages = total_rows // page_rows
    q_cols = q_heads * HD
    kv_cols = kv_heads * HD

    def page_spec(a):
        return pl.BlockSpec(
            (1, page_rows, q_cols),
            lambda i, first_ref, perm_ref, a=a: (perm_ref[i * pages + a], 0, part),
        )

    def whole(shape):
        return pl.BlockSpec(shape, lambda i, *_: (0,) * len(shape))

    def column(rows):
        return pl.BlockSpec((rows, block_len), lambda i, *_: (0, i))

    return pl.pallas_call(
        functools.partial(backward_kernel, q_heads, kv_heads, page_rows, pages),
        grid_spec=pltpu.PrefetchScalarGridSpec(
            num_scalar_prefetch=2,
            grid=(total_rows // block_len,),
            in_specs=[page_spec(a) for a in range(pages)]
            + [
                column(q_cols),
                whole((kv_heads, total_rows, HD)),
                whole((kv_cols, total_rows)),
                whole((kv_heads, total_rows, HD)),
                column(q_cols),
                column(q_heads),
                column(1),
                column(HALF),
                column(HALF),
                whole((HALF, total_rows)),
                whole((HALF, total_rows)),
            ],
            out_specs=pl.BlockSpec(memory_space=pl.ANY),
            scratch_shapes=[
                pltpu.VMEM((q_cols, block_len), f32),
                pltpu.VMEM((kv_cols, total_rows), f32),
                pltpu.VMEM((kv_cols, total_rows), f32),
                pltpu.VMEM((pages, page_rows, q_cols), bf16),
                pltpu.VMEM((all_pages, page_rows, 2 * kv_cols), bf16),
                pltpu.SemaphoreType.DMA((pages,)),
                pltpu.SemaphoreType.DMA((all_pages,)),
            ],
        ),
        out_shape=jax.ShapeDtypeStruct((all_pages, page_rows, q_cols + 2 * kv_cols), bf16),
        cost_estimate=pl.CostEstimate(
            flops=3 * q_heads * total_rows * total_rows * HD,
            bytes_accessed=12 * q_t.size,
            transcendentals=q_heads * total_rows * total_rows // 4,
        ),
        name="attend_backward",
    )(
        first_block, perm, *([grad_slots] * pages), q_t, k_rows, k_t, v_rows, o_t, lse, begin,
        cos_t, sin_t, cos_t, sin_t,
    )


def project_kernel(
    tp_count, dp_count, rows, weights, slots, held, stage, load_sem, own_sem, send, recv
):
    count = dp_count * tp_count
    my_dp = lax.axis_index("dp")
    my_tp = lax.axis_index("tensor")
    me = my_dp * tp_count + my_tp
    page_rows = slots.shape[1]

    def load(j):
        shard = lax.rem(my_tp + 1 + j, tp_count)
        return pltpu.make_async_copy(weights.at[shard], held.at[j % 2], load_sem.at[j % 2])

    load(0).start()
    barrier = pltpu.get_barrier_semaphore()

    def greet(j, carry):
        peer = lax.rem(me + j, count)
        pl.semaphore_signal(
            barrier,
            inc=1,
            device_id={"dp": lax.div(peer, tp_count), "tensor": lax.rem(peer, tp_count)},
            device_id_type=MESH,
        )
        return carry

    lax.fori_loop(1, count, greet, 0)
    pl.semaphore_wait(barrier, count - 1)
    home = slots.at[my_tp * dp_count + my_dp]

    def copy_to(j, off):
        p_dp = lax.rem(my_dp + off, dp_count)
        return pltpu.make_async_remote_copy(
            src_ref=stage.at[j, pl.ds(p_dp * page_rows, page_rows), :],
            dst_ref=home,
            send_sem=send.at[j, off],
            recv_sem=recv.at[j, off],
            device_id={"dp": p_dp, "tensor": lax.rem(my_tp + 1 + j, tp_count)},
            device_id_type=MESH,
        )

    def each(j, act):
        def one(off, carry):
            act(copy_to(j, off))
            return carry

        lax.fori_loop(1 if j == tp_count - 1 else 0, dp_count, one, 0)

    for j in range(tp_count):
        load(j).wait()
        if j + 1 < tp_count:
            load(j + 1).start()
        stage[j] = dot_nn(rows[...], held[j % 2]).astype(bf16)
        if j > 0:
            each(j - 1, lambda copy: copy.start())
    each(tp_count - 1, lambda copy: copy.start())
    own = pltpu.make_async_copy(
        stage.at[tp_count - 1, pl.ds(my_dp * page_rows, page_rows), :], home, own_sem
    )
    own.start()
    own.wait()
    for j in range(tp_count):
        each(j, lambda copy: copy.wait())


def project(rows, weights, dp_count, collective_id):
    tp_count, width, cols = weights.shape
    total = rows.shape[0]
    page_rows = total // dp_count
    any_spec = pl.BlockSpec(memory_space=pl.ANY)
    dma = pltpu.SemaphoreType.DMA
    return pl.pallas_call(
        functools.partial(project_kernel, tp_count, dp_count),
        out_shape=jax.ShapeDtypeStruct((tp_count * dp_count, page_rows, cols), bf16),
        in_specs=[pl.BlockSpec(memory_space=pltpu.VMEM), any_spec],
        out_specs=any_spec,
        scratch_shapes=[
            pltpu.VMEM((2, width, cols), bf16),
            pltpu.VMEM((tp_count, total, cols), bf16),
            dma((2,)),
            dma,
            dma((tp_count, dp_count)),
            dma((tp_count, dp_count)),
        ],
        compiler_params=pltpu.CompilerParams(
            collective_id=collective_id, has_side_effects=True, vmem_limit_bytes=32 * 1024 * 1024
        ),
        cost_estimate=pl.CostEstimate(
            flops=2 * tp_count * total * width * cols,
            bytes_accessed=16 * tp_count * width * cols,
            transcendentals=0,
        ),
        name="project",
    )(rows, weights)


def feed_kernel(
    ring, tile, own_rows, *refs
):
    grad_rows = refs[:ring]
    (
        weights, grads_t, rows_t, act_all, grads_all, mixed_all, grad_own,
    held, grads_held, acc_n, acc_m, first_part, arrived, outgoing, mixed_stage, final_stage,
    turned, load_sem, keep_sem, grad_sem, mixed_sem, final_sem,
    row_send, row_recv, sum_send, sum_recv, all_sem,
    ) = refs[ring:]
    me = lax.axis_index("tensor")
    right = lax.rem(me + 1, ring)
    left = lax.rem(me + ring - 1, ring)
    hidden = weights.shape[1] // 3
    tiles = hidden // tile

    barrier = pltpu.get_barrier_semaphore()
    for neighbour in (left, right):
        pl.semaphore_signal(barrier, inc=1, device_id={"tensor": neighbour}, device_id_type=MESH)
    pl.semaphore_wait(barrier, 2)

    load = pltpu.make_async_copy(own_rows, held.at[0], load_sem)
    load.start()

    def grad_load(s):
        return pltpu.make_async_copy(grad_rows[s], grads_held.at[s % 2], grad_sem.at[s % 2])

    def part_of(array, s):
        count = own_rows.shape[0]
        return array.at[:, pl.ds(pl.multiple_of(s * count, 128), count)]

    def grad_keep(s):
        return pltpu.make_async_copy(turned.at[1], part_of(grads_t, s), all_sem)

    grad_load(0).start()
    load.wait()

    def pass_rows(s):
        return pltpu.make_async_remote_copy(
            src_ref=held.at[s],
            dst_ref=held.at[s + 1],
            send_sem=row_send.at[s],
            recv_sem=row_recv.at[s],
            device_id={"tensor": right},
            device_id_type=MESH,
        )

    def pass_sum(s):
        return pltpu.make_async_remote_copy(
            src_ref=outgoing.at[s - 1],
            dst_ref=arrived.at[s - 1],
            send_sem=sum_send.at[s - 1],
            recv_sem=sum_recv.at[s - 1],
            device_id={"tensor": right},
            device_id_type=MESH,
        )

    def keep(s):
        return pltpu.make_async_copy(turned.at[0], part_of(rows_t, s), keep_sem)

    def mixed_store(s):
        return pltpu.make_async_copy(mixed_stage, mixed_all.at[s], mixed_sem)

    def chunk(s, carry):
        @pl.when(s > 0)
        def _():
            pass_rows(s - 1).wait_recv()

        @pl.when(s < ring - 1)
        def _():
            pass_rows(s).start()

        @pl.when(s > 0)
        def _():
            keep(s - 1).wait()
            grad_keep(s - 1).wait()

        turned[0] = held[s].T
        keep(s).start()
        for k in range(ring):

            @pl.when(s == k)
            def _(k=k):
                grad_load(k).wait()
                if k < ring - 1:
                    grad_load(k + 1).start()

        slot = lax.rem(s, 2)
        turned[1] = grads_held[slot].T
        grad_keep(s).start()
        acc_n[...] = jnp.zeros_like(acc_n)
        acc_m[...] = jnp.zeros_like(acc_m)

        def body(w_gate, w_up, w_down, act, grad_gate, grad_up):
            rows = held[s]
            gate = dot_nn(rows, w_gate[...])
            up = dot_nn(rows, w_up[...])
            grad_act = dot_nn(grads_held[slot], w_down[...])
            sig = 1.0 / (1.0 + jnp.exp(-gate))
            silu = gate * sig
            low_act = (silu * up).astype(bf16)
            low_up = (grad_act * silu).astype(bf16)
            low_gate = (grad_act * up * sig * (1.0 + gate * (1.0 - sig))).astype(bf16)
            act[...] = low_act
            grad_gate[...] = low_gate
            grad_up[...] = low_up
            acc_m[...] += dot_nt(low_act, w_down[...])
            acc_n[...] += dot_nt(low_gate, w_gate[...]) + dot_nt(low_up, w_up[...])

        width, count = own_rows.shape[1], own_rows.shape[0]
        pltpu.emit_pipeline(
            body,
            grid=(tiles,),
            in_specs=[
                pl.BlockSpec((width, tile), lambda k: (0, k)),
                pl.BlockSpec((width, tile), lambda k: (0, k + tiles)),
                pl.BlockSpec((width, tile), lambda k: (0, k + 2 * tiles)),
            ],
            out_specs=[
                pl.BlockSpec((count, tile), lambda k: (0, k)),
                pl.BlockSpec((count, tile), lambda k: (0, k)),
                pl.BlockSpec((count, tile), lambda k: (0, k + tiles)),
            ],
        )(weights, weights, weights, act_all.at[s], grads_all.at[s], grads_all.at[s])

        @pl.when(s > 0)
        def _():
            mixed_store(s - 1).wait()

        mixed_stage[...] = acc_m[...].astype(bf16)
        mixed_store(s).start()

        @pl.when(s == 0)
        def _():
            first_part[...] = acc_n[...]

        @pl.when(s == 1)
        def _():
            outgoing[0] = acc_n[...].astype(bf16)

        @pl.when(s > 1)
        def _():
            pass_sum(s - 1).wait_recv()
            outgoing[s - 1] = (acc_n[...] + arrived[s - 2].astype(f32)).astype(bf16)

        @pl.when(s > 0)
        def _():
            pass_sum(s).start()

        return carry

    lax.fori_loop(0, ring, chunk, 0)
    mixed_store(ring - 1).wait()
    pass_sum(ring - 1).wait_recv()
    final_stage[...] = (first_part[...] + arrived[ring - 2].astype(f32)).astype(bf16)
    final = pltpu.make_async_copy(final_stage, grad_own, final_sem)
    final.start()

    def settle(s, carry):
        @pl.when(s < ring - 1)
        def _():
            pass_rows(s).wait_send()

        @pl.when(s > 0)
        def _():
            pass_sum(s).wait_send()

        return carry

    lax.fori_loop(0, ring, settle, 0)
    keep(ring - 1).wait()
    grad_keep(ring - 1).wait()
    final.wait()


def feed(own_rows, grad_rows, weights, ring, tile=256, collective_id=7):
    count, width = own_rows.shape
    hidden = weights.shape[1] // 3
    any_spec = pl.BlockSpec(memory_space=pl.ANY)
    dma = pltpu.SemaphoreType.DMA
    return pl.pallas_call(
        functools.partial(feed_kernel, ring, min(tile, hidden)),
        out_shape=[
            jax.ShapeDtypeStruct((width, ring * count), bf16),
            jax.ShapeDtypeStruct((width, ring * count), bf16),
            jax.ShapeDtypeStruct((ring, count, hidden), bf16),
            jax.ShapeDtypeStruct((ring, count, 2 * hidden), bf16),
            jax.ShapeDtypeStruct((ring, count, width), bf16),
            jax.ShapeDtypeStruct((count, width), bf16),
        ],
        in_specs=[any_spec] * (2 + ring),
        out_specs=[any_spec] * 6,
        scratch_shapes=[
            pltpu.VMEM((ring, count, width), bf16),
            pltpu.VMEM((2, count, width), bf16),
            pltpu.VMEM((count, width), f32),
            pltpu.VMEM((count, width), f32),
            pltpu.VMEM((count, width), f32),
            pltpu.VMEM((ring - 1, count, width), bf16),
            pltpu.VMEM((ring - 1, count, width), bf16),
            pltpu.VMEM((count, width), bf16),
            pltpu.VMEM((count, width), bf16),
            pltpu.VMEM((2, width, count), bf16),
            dma,
            dma,
            dma((2,)),
            dma,
            dma,
            dma((ring - 1,)),
            dma((ring - 1,)),
            dma((ring - 1,)),
            dma((ring - 1,)),
            dma,
        ],
        compiler_params=pltpu.CompilerParams(
            collective_id=collective_id, has_side_effects=True, vmem_limit_bytes=64 * 1024 * 1024 - 65536,
        ),
        cost_estimate=pl.CostEstimate(
            flops=12 * ring * count * width * hidden,
            bytes_accessed=8 * ring * count * width,
            transcendentals=ring * count * hidden,
        ),
        name="feed_forward",
    )(own_rows, *grad_rows, weights)


def weigh_kernel(
    tp_count, dp_count, tile, grads, rows_t, grads_t, gate_up, act, slots, out,
    left, left_sem, own_sem, send, recv,
):
    count = dp_count * tp_count
    my_dp = lax.axis_index("dp")
    my_tp = lax.axis_index("tensor")
    me = my_dp * tp_count + my_tp
    page_rows = slots.shape[1]

    loads = [
        pltpu.make_async_copy(source, left.at[k], left_sem.at[k])
        for k, source in enumerate((rows_t, grads_t))
    ]
    for load in loads:
        load.start()

    barrier = pltpu.get_barrier_semaphore()

    def place(peer):
        return {"dp": lax.div(peer, tp_count), "tensor": lax.rem(peer, tp_count)}

    def greet(j, carry):
        peer = lax.rem(me + j, count)
        pl.semaphore_signal(barrier, inc=1, device_id=place(peer), device_id_type=MESH)
        return carry

    lax.fori_loop(1, count, greet, 0)
    pl.semaphore_wait(barrier, count - 1)

    home = slots.at[my_tp * dp_count + my_dp]

    def block(p_dp, p_tp):
        return grads.at[p_tp, pl.ds(p_dp * page_rows, page_rows), :]

    own = pltpu.make_async_copy(block(my_dp, my_tp), home, own_sem)
    own.start()

    def copy_to(j):
        peer = lax.rem(me + j, count)
        return pltpu.make_async_remote_copy(
            src_ref=block(lax.div(peer, tp_count), lax.rem(peer, tp_count)),
            dst_ref=home,
            send_sem=send.at[j],
            recv_sem=recv.at[j],
            device_id=place(peer),
            device_id_type=MESH,
        )

    def start(j, carry):
        copy_to(j).start()
        return carry

    def finish(j, carry):
        copy_to(j).wait()
        return carry

    lax.fori_loop(1, count, start, 0)

    width = rows_t.shape[0]
    step = min(512, width)

    def multiply(k, right, first):
        ring, rows, cols = right.shape

        def body(part, result):
            values = part[...].reshape(ring * rows, tile)
            for m in range(0, width, step):
                result[m : m + step, :] = dot_nn(left[k, m : m + step, :], values).astype(bf16)

        pltpu.emit_pipeline(
            body,
            grid=(cols // tile,),
            in_specs=[pl.BlockSpec((ring, rows, tile), lambda n: (0, 0, n))],
            out_specs=[pl.BlockSpec((width, tile), lambda n: (0, n + first))],
        )(right, out)

    loads[0].wait()
    multiply(0, gate_up, 0)
    loads[1].wait()
    multiply(1, act, gate_up.shape[2] // tile)
    own.wait()
    lax.fori_loop(1, count, finish, 0)


def weigh(grads, rows_t, grads_t, gate_up, act, tp_count, dp_count, collective_id):
    count = tp_count * dp_count
    cols = grads.shape[2]
    page_rows = grads.shape[1] // dp_count
    width, rows = rows_t.shape
    hidden = act.shape[2]
    any_spec = pl.BlockSpec(memory_space=pl.ANY)
    dma = pltpu.SemaphoreType.DMA
    return pl.pallas_call(
        functools.partial(weigh_kernel, tp_count, dp_count, min(512, hidden)),
        out_shape=[
            jax.ShapeDtypeStruct((count, page_rows, cols), bf16),
            jax.ShapeDtypeStruct((width, 3 * hidden), bf16),
        ],
        in_specs=[any_spec] * 5,
        out_specs=[any_spec] * 2,
        scratch_shapes=[
            pltpu.VMEM((2, width, rows), bf16),
            dma((2,)),
            dma,
            dma((count,)),
            dma((count,)),
        ],
        compiler_params=pltpu.CompilerParams(
            collective_id=collective_id, has_side_effects=True, vmem_limit_bytes=48 * 1024 * 1024
        ),
        cost_estimate=pl.CostEstimate(
            flops=6 * rows * width * hidden,
            bytes_accessed=2 * width * (2 * rows + 3 * hidden),
            transcendentals=0,
        ),
        name="weigh",
    )(grads, rows_t, grads_t, gate_up, act)


def flip(index, bit):
    return index + bit - 2 * bit * lax.rem(lax.div(index, bit), 2)


def collect_kernel(
    tp_count, dp_count, hops, shard, second, gains, chunk, out, second_out, gains_out, chunks_out,
    second_send, second_recv, own_sem, ring_send, ring_recv, send, recv, gain_send, gain_recv, chunk_send, chunk_recv,
):
    my_dp = lax.axis_index("dp")
    my_tp = lax.axis_index("tensor")
    rows = shard.shape[0]
    half = rows // 2
    bits = [1 << b for b in reversed(range(dp_count.bit_length() - 1))]
    orders = [bits, bits[:-1][::-1] + bits[-1:]]
    steps = len(bits)

    barrier = pltpu.get_barrier_semaphore()
    for j in range(1, tp_count):
        pl.semaphore_signal(
            barrier, inc=1, device_id={"tensor": lax.rem(my_tp + j, tp_count)}, device_id_type=MESH
        )
    for j in range(1, dp_count):
        pl.semaphore_signal(
            barrier, inc=1, device_id={"dp": lax.rem(my_dp + j, dp_count)}, device_id_type=MESH
        )
    pl.semaphore_wait(barrier, tp_count + dp_count - 2)

    home = out.at[my_tp, pl.ds(my_dp * rows, rows), :]
    own = pltpu.make_async_copy(shard, home, own_sem.at[0])
    own.start()
    own_gain = pltpu.make_async_copy(gains, gains_out.at[my_dp], own_sem.at[1])
    own_gain.start()
    own_second = pltpu.make_async_copy(second, second_out.at[my_tp], own_sem.at[2])
    own_second.start()

    def second_copy(j):
        return pltpu.make_async_remote_copy(
            src_ref=second,
            dst_ref=second_out.at[my_tp],
            send_sem=second_send.at[j],
            recv_sem=second_recv.at[j],
            device_id={"tensor": lax.rem(my_tp + j, tp_count)},
            device_id_type=MESH,
        )

    def across(j):
        return pltpu.make_async_remote_copy(
            src_ref=shard,
            dst_ref=home,
            send_sem=ring_send.at[j],
            recv_sem=ring_recv.at[j],
            device_id={"tensor": lax.rem(my_tp + j, tp_count)},
            device_id_type=MESH,
        )

    def gain_copy(j):
        return pltpu.make_async_remote_copy(
            src_ref=gains,
            dst_ref=gains_out.at[my_dp],
            send_sem=gain_send.at[j],
            recv_sem=gain_recv.at[j],
            device_id={"dp": lax.rem(my_dp + j, dp_count)},
            device_id_type=MESH,
        )

    def onward(hop):
        return pltpu.make_async_remote_copy(
            src_ref=chunk if hop == 0 else chunks_out.at[hop - 1],
            dst_ref=chunks_out.at[hop],
            send_sem=chunk_send.at[hop],
            recv_sem=chunk_recv.at[hop],
            device_id={"tensor": lax.rem(my_tp + 1, tp_count)},
            device_id_type=MESH,
        )

    def within(j, s, k, m):
        order = orders[s]
        owner = my_dp
        for b in range(k):
            if m >> b & 1:
                owner = flip(owner, order[b])
        block = out.at[
            lax.rem(my_tp - j + tp_count, tp_count), pl.ds(owner * rows + s * half, half), :
        ]
        at = (1 << k) - 1 + m
        return pltpu.make_async_remote_copy(
            src_ref=block,
            dst_ref=block,
            send_sem=send.at[j, s, at],
            recv_sem=recv.at[j, s, at],
            device_id={"dp": flip(my_dp, order[k])},
            device_id_type=MESH,
        )

    for j in range(1, tp_count):
        across(j).start()
    for j in range(1, dp_count):
        gain_copy(j).start()
    onward(0).start()
    own.wait()
    for phase in range(tp_count + steps):
        for k in reversed(range(steps + 1)):
            j = phase - k
            if not 0 <= j < tp_count:
                continue
            if k == 0:
                if j > 0:
                    across(j).wait_recv()
            else:
                for s in range(2):
                    for m in range(1 << (k - 1)):
                        within(j, s, k - 1, m).wait_recv()
            if k < steps:
                for s in range(2):
                    for m in range(1 << k):
                        within(j, s, k, m).start()
        if phase == tp_count:
            for j in range(1, tp_count):
                second_copy(j).start()
        if tp_count <= phase < tp_count + hops - 1:
            onward(phase - tp_count).wait_recv()
            onward(phase - tp_count + 1).start()
    for j in range(tp_count):
        if j > 0:
            across(j).wait_send()
        for s in range(2):
            for k in range(steps):
                for m in range(1 << k):
                    within(j, s, k, m).wait_send()
    own_gain.wait()
    own_second.wait()
    for j in range(1, tp_count):
        second_copy(j).wait()
    for j in range(1, dp_count):
        gain_copy(j).wait()
    for hop in range(hops):
        if hop == hops - 1:
            onward(hop).wait_recv()
        onward(hop).wait_send()


def collect(shard, second, gains, chunk, tp_count, dp_count, hops, collective_id):
    rows, cols = shard.shape
    dma = pltpu.SemaphoreType.DMA
    vmem_spec = pl.BlockSpec(memory_space=pltpu.VMEM)
    any_spec = pl.BlockSpec(memory_space=pl.ANY)
    return pl.pallas_call(
        functools.partial(collect_kernel, tp_count, dp_count, hops),
        out_shape=[
            jax.ShapeDtypeStruct((tp_count, dp_count * rows, cols), shard.dtype),
            jax.ShapeDtypeStruct((tp_count,) + second.shape, second.dtype),
            jax.ShapeDtypeStruct((dp_count,) + gains.shape, gains.dtype),
            jax.ShapeDtypeStruct((hops,) + chunk.shape, chunk.dtype),
        ],
        in_specs=[vmem_spec, vmem_spec, vmem_spec, any_spec],
        out_specs=[any_spec] * 4,
        scratch_shapes=[
            dma((tp_count,)),
            dma((tp_count,)),
            dma((3,)),
            dma((tp_count,)),
            dma((tp_count,)),
            dma((tp_count, 2, dp_count - 1)),
            dma((tp_count, 2, dp_count - 1)),
            dma((dp_count,)),
            dma((dp_count,)),
            dma((hops,)),
            dma((hops,)),
        ],
        compiler_params=pltpu.CompilerParams(collective_id=collective_id, has_side_effects=True),
        cost_estimate=pl.CostEstimate(
            flops=0, bytes_accessed=16 * tp_count * dp_count * shard.size, transcendentals=0
        ),
        name="collect",
    )(shard, second, gains, chunk)


def spread_kernel(rows, weight, out):
    out[0] = dot_nn(rows[...], weight[0]).astype(out.dtype)


def spread(rows, weights, part, cols):
    shards, width, _ = weights.shape
    count = rows.shape[0]
    return pl.pallas_call(
        spread_kernel,
        grid=(shards,),
        in_specs=[
            pl.BlockSpec((count, width), lambda t: (0, 0)),
            pl.BlockSpec((1, width, cols), lambda t: (t, 0, part)),
        ],
        out_specs=pl.BlockSpec((1, count, cols), lambda t: (t, 0, 0)),
        out_shape=jax.ShapeDtypeStruct((shards, count, cols), bf16),
        cost_estimate=pl.CostEstimate(
            flops=2 * shards * count * width * cols,
            bytes_accessed=2 * shards * width * cols,
            transcendentals=0,
        ),
        name="spread",
    )(rows, weights)


def gather_kernel(has_begin, part, weight, *refs):
    out = refs[-1]

    @pl.when(pl.program_id(0) == 0)
    def _():
        out[...] = refs[0][...] if has_begin else jnp.zeros_like(out)

    out[...] += dot_nt(part[0], weight[0])


def gather_sum(parts, weights, part, begin):
    shards, count, cols = parts.shape
    width = weights.shape[1]
    whole = pl.BlockSpec((count, width), lambda t: (0, 0))
    begins = [] if begin is None else [begin]
    return pl.pallas_call(
        functools.partial(gather_kernel, begin is not None),
        grid=(shards,),
        in_specs=[
            pl.BlockSpec((1, count, cols), lambda t: (t, 0, 0)),
            pl.BlockSpec((1, width, cols), lambda t: (t, 0, part)),
        ]
        + [whole] * len(begins),
        out_specs=whole,
        out_shape=jax.ShapeDtypeStruct((count, width), f32),
        cost_estimate=pl.CostEstimate(
            flops=2 * shards * count * width * cols,
            bytes_accessed=2 * shards * width * cols,
            transcendentals=0,
        ),
        name="gather_sum",
    )(parts, weights, *begins)


def outer_kernel(rows, *refs):
    parts, out, turned = refs[:-2], refs[-2], refs[-1]

    @pl.when(pl.program_id(0) == 0)
    def _():
        turned[...] = rows[...].T

    at = 0
    for part in parts:
        cols = part.shape[2]
        out[:, at : at + cols] = dot_nn(turned[...], part[0]).astype(out.dtype)
        at += cols


def outer(rows, parts):
    shards, count, _ = parts[0].shape
    cols = sum(part.shape[2] for part in parts)
    width = rows.shape[1]
    return pl.pallas_call(
        outer_kernel,
        grid=(shards,),
        in_specs=[pl.BlockSpec((count, width), lambda t: (0, 0))]
        + [pl.BlockSpec((1, count, part.shape[2]), lambda t: (t, 0, 0)) for part in parts],
        out_specs=pl.BlockSpec((width, cols), lambda t: (0, t)),
        out_shape=jax.ShapeDtypeStruct((width, shards * cols), bf16),
        scratch_shapes=[pltpu.VMEM((width, count), bf16)],
        cost_estimate=pl.CostEstimate(
            flops=2 * shards * count * width * cols,
            bytes_accessed=2 * shards * width * cols,
            transcendentals=0,
        ),
        name="outer",
    )(rows, *parts)


def total_kernel(
    tp_count, dp_count, hops, groups, rows, *refs
):
    parts = refs[:groups]
    running = refs[groups]
    addends = refs[groups + 1 : groups + hops]
    (
        weights, out, grad_rows, last_chunk,
        turned, mine, got, got_across, held, chunks, onward,
        load_sem, send, recv, across_send, across_recv, chunk_send, chunk_recv,
    ) = refs[groups + hops :]
    my_dp = lax.axis_index("dp")
    my_tp = lax.axis_index("tensor")
    own_rows = out.shape[0]
    half = own_rows // 2
    bits = [1 << b for b in range(dp_count.bit_length() - 1)]
    orders = [bits, bits[:1] + bits[1:][::-1]]
    steps = len(bits)

    def shard_of(j):
        return lax.rem(my_tp + 1 + j, tp_count)

    def load(j):
        return pltpu.make_async_copy(weights.at[shard_of(j)], held.at[j % 2], load_sem.at[j % 2])

    load(0).start()
    barrier = pltpu.get_barrier_semaphore()
    for j in range(1, tp_count):
        pl.semaphore_signal(
            barrier, inc=1, device_id={"tensor": lax.rem(my_tp + j, tp_count)}, device_id_type=MESH
        )
    for bit in bits:
        pl.semaphore_signal(
            barrier, inc=1, device_id={"dp": flip(my_dp, bit)}, device_id_type=MESH
        )
    pl.semaphore_wait(barrier, tp_count - 1 + steps)

    def hop(n):
        source = running if n == 0 else onward.at[n - 1]
        return pltpu.make_async_remote_copy(
            src_ref=source,
            dst_ref=last_chunk if n == hops - 1 else chunks.at[n],
            send_sem=chunk_send.at[n],
            recv_sem=chunk_recv.at[n],
            device_id={"tensor": lax.rem(my_tp + 1, tp_count)},
            device_id_type=MESH,
        )

    hop(0).start()

    def block(j, s, owner):
        return j, pl.ds(pl.multiple_of(owner * own_rows + s * half, half), half)

    def place(k, m):
        return sum(1 << (steps - 1 - e) for e in range(k)) + m

    def fellow(s, k, m, start):
        owner = start
        for b in range(steps - 1 - k):
            if m >> b & 1:
                owner = flip(owner, orders[s][k + 1 + b])
        return owner

    def exchange_part(j, s, k, m):
        partner = flip(my_dp, orders[s][k])
        at = place(k, m)
        index, span = block(j, s, fellow(s, k, m, partner))
        return pltpu.make_async_remote_copy(
            src_ref=mine.at[index, span, :],
            dst_ref=got.at[j, s, at],
            send_sem=send.at[j, s, at],
            recv_sem=recv.at[j, s, at],
            device_id={"dp": partner},
            device_id_type=MESH,
        )

    def across(j):
        return pltpu.make_async_remote_copy(
            src_ref=mine.at[j, pl.ds(pl.multiple_of(my_dp * own_rows, own_rows), own_rows), :],
            dst_ref=got_across.at[j],
            send_sem=across_send.at[j],
            recv_sem=across_recv.at[j],
            device_id={"tensor": shard_of(j)},
            device_id_type=MESH,
        )

    def every(k):
        return [(s, m) for s in range(2) for m in range(1 << (steps - 1 - k))]

    turned[...] = rows[...].T
    for phase in range(tp_count + steps + 1):
        if phase < tp_count:
            shard = shard_of(phase)
            at = 0
            load(phase).wait()
            if phase + 1 < tp_count:
                load(phase + 1).start()
            for g, part in enumerate(parts):
                cols = part.shape[2]
                value = part[shard]
                mine[phase, :, at : at + cols] = dot_nn(turned[...], value).astype(bf16)
                product = dot_nt(value, held[phase % 2, :, at : at + cols])
                if phase == 0 and g == 0:
                    grad_rows[...] = product
                else:
                    grad_rows[...] += product
                at += cols
        for k in reversed(range(steps + 1)):
            j = phase - k
            if not 0 <= j < tp_count:
                continue
            if k > 0:
                for s, m in every(k - 1):
                    exchange_part(j, s, k - 1, m).wait_recv()
                    index, span = block(j, s, fellow(s, k - 1, m, my_dp))
                    mine[index, span, :] = (
                        mine[index, span, :].astype(f32)
                        + got[j, s, place(k - 1, m)].astype(f32)
                    ).astype(bf16)
            if k < steps:
                for s, m in every(k):
                    exchange_part(j, s, k, m).start()
            elif j < tp_count - 1:
                across(j).start()
        if tp_count <= phase < tp_count + hops - 1:
            n = phase - tp_count
            hop(n).wait_recv()
            onward[n] = (chunks[n].astype(f32) + addends[n][...].astype(f32)).astype(bf16)
            hop(n + 1).start()
    total = mine[
        tp_count - 1, pl.ds(pl.multiple_of(my_dp * own_rows, own_rows), own_rows), :
    ].astype(f32)
    for j in range(tp_count - 1):
        across(j).wait_recv()
        total += got_across[j].astype(f32)
    out[...] = total
    hop(hops - 1).wait_recv()
    for n in range(hops):
        hop(n).wait_send()
    for j in range(tp_count):
        if j < tp_count - 1:
            across(j).wait_send()
        for k in range(steps):
            for s, m in every(k):
                exchange_part(j, s, k, m).wait_send()


def total_grads(rows, parts, running, addends, weights, dp_count, collective_id):
    tp_count, width, cols = weights.shape
    count = rows.shape[0]
    own_rows = width // dp_count
    hops = len(addends) + 1
    vmem_spec = pl.BlockSpec(memory_space=pltpu.VMEM)
    any_spec = pl.BlockSpec(memory_space=pl.ANY)
    dma = pltpu.SemaphoreType.DMA
    return pl.pallas_call(
        functools.partial(total_kernel, tp_count, dp_count, hops, len(parts)),
        out_shape=[
            jax.ShapeDtypeStruct((own_rows, cols), f32),
            jax.ShapeDtypeStruct((count, width), f32),
            jax.ShapeDtypeStruct((count, width), bf16),
        ],
        in_specs=[vmem_spec] * (1 + len(parts) + hops) + [any_spec],
        out_specs=[vmem_spec, vmem_spec, any_spec],
        scratch_shapes=[
            pltpu.VMEM((width, count), bf16),
            pltpu.VMEM((tp_count, width, cols), bf16),
            pltpu.VMEM((tp_count, 2, dp_count - 1, own_rows // 2, cols), bf16),
            pltpu.VMEM((tp_count - 1, own_rows, cols), bf16),
            pltpu.VMEM((2, width, cols), bf16),
            pltpu.VMEM((max(hops - 1, 1), count, width), bf16),
            pltpu.VMEM((max(hops - 1, 1), count, width), bf16),
            dma((2,)),
            dma((tp_count, 2, dp_count - 1)),
            dma((tp_count, 2, dp_count - 1)),
            dma((tp_count,)),
            dma((tp_count,)),
            dma((hops,)),
            dma((hops,)),
        ],
        compiler_params=pltpu.CompilerParams(
            collective_id=collective_id, has_side_effects=True, vmem_limit_bytes=62 * 1024 * 1024
        ),
        cost_estimate=pl.CostEstimate(
            flops=4 * tp_count * count * width * cols,
            bytes_accessed=16 * tp_count * width * cols,
            transcendentals=0,
        ),
        name="total_grads",
    )(rows, *parts, running, *addends, weights)


def rms_scale(hidden):
    return lax.rsqrt(jnp.mean(hidden * hidden, axis=1, keepdims=True) + epsilon)


def norm_back(grad_norm, hidden, scale_rows, gain):
    normed = hidden * scale_rows
    gain_part = jnp.sum(grad_norm * normed, axis=0)
    inner = grad_norm * gain
    grad_hidden = scale_rows * (inner - normed * jnp.mean(inner * normed, axis=1, keepdims=True))
    return (grad_hidden, gain_part)


def after(value, other):
    return lax.optimization_barrier((value, other))[0]


def local(
    tokens,
    upstream,
    lengths,
    positions,
    pages,
    attn_gain,
    w_query,
    w_key,
    w_value,
    w_out,
    mlp_gain,
    w_gate,
    w_up,
    w_down,
):
    dp_count = lax.axis_size("dp")
    tp_count = lax.axis_size("tensor")
    dp_index = lax.axis_index("dp")
    tp_index = lax.axis_index("tensor")
    tok_dev, width = tokens.shape
    tok_group = tok_dev * tp_count
    page_rows = tok_dev // dp_count
    group_pages = tp_count * dp_count
    page_count = pages.shape[0]
    device = dp_index * tp_count + tp_index
    everyone = ("tensor", "dp")

    local_ids = jnp.arange(dp_count, dtype=jnp.int32)
    inverse = (
        jnp.zeros((page_count,), jnp.int32).at[pages].set(jnp.arange(page_count, dtype=jnp.int32))
    )
    dealt = lax.dynamic_slice_in_dim(inverse, device * dp_count, dp_count)
    dest_group = dealt // group_pages
    send_order = jnp.zeros((dp_count,), jnp.int32).at[dest_group].set(local_ids)
    group_sources = lax.dynamic_slice_in_dim(pages, dp_index * group_pages, group_pages)
    perm = (
        (jnp.arange(group_pages, dtype=jnp.int32) // dp_count) * dp_count
        + group_sources // group_pages
    ).astype(jnp.int32)

    def reorder(rows, order):
        blocks = rows.reshape(dp_count, page_rows, rows.shape[1])
        return jnp.take(blocks, order, axis=0, mode="clip").reshape(rows.shape)

    hidden_in = reorder(tokens, send_order).astype(f32)
    grad_top = reorder(upstream, send_order).astype(f32)
    seq_lens = lengths[0]
    seq_ends = jnp.cumsum(seq_lens)
    place = (jnp.take(dealt, send_order, mode="clip") % group_pages) * page_rows
    place_rows = (place[:, None] + jnp.arange(page_rows, dtype=jnp.int32)[None, :]).reshape(-1)
    valid_rows = (place_rows < seq_ends[-1]).astype(f32)[:, None]

    row_ids = jnp.arange(tok_group, dtype=jnp.int32)
    begin = jnp.max(
        jnp.where(row_ids[:, None] >= seq_ends[None, :], seq_ends[None, :], 0), axis=1
    ).astype(jnp.int32)
    block_len = min(block_rows, tok_group)
    first_block = begin[::block_len] // min(key_rows, tok_group)
    begin = begin[None, :]
    inverse_freq = theta_base ** (-(jnp.arange(HALF, dtype=f32) * 2.0) / HD)
    angles = inverse_freq[:, None] * positions.astype(f32)
    cos_t, sin_t = jnp.cos(angles), jnp.sin(angles)

    q_cols, kv_cols = w_query.shape[1], w_key.shape[1]
    kv_heads = kv_cols // HD
    per_group = q_cols // kv_cols
    group_q = per_group * HD
    groups = range(kv_heads)
    qkv_shard = jnp.concatenate(
        [
            part
            for g in groups
            for part in (
                w_query[:, g * group_q : (g + 1) * group_q],
                w_key[:, g * HD : (g + 1) * HD],
                w_value[:, g * HD : (g + 1) * HD],
            )
        ],
        axis=1,
    )

    def trade(value):
        blocks = value.reshape(group_pages, page_rows, value.shape[-1])
        return lax.all_to_all(blocks, everyone, split_axis=0, concat_axis=0, tiled=True)

    def trade_back(value):
        return trade(value).reshape(tp_count, tok_dev, value.shape[-1])

    ring_next = [(t, (t + 1) % tp_count) for t in range(tp_count)]

    def pass_on(value):
        return lax.ppermute(value, "tensor", ring_next)

    grad_out = grad_top * valid_rows
    grad_chunks = [grad_out.astype(bf16)]
    mlp_shard = jnp.concatenate([w_gate, w_up, w_down.T], axis=1)
    w_mlp = lax.all_gather(mlp_shard, "dp", axis=0, tiled=True)
    hops = min(2, tp_count - 1)
    w_qkv, out_shards, gains, got_chunks = collect(
        qkv_shard, w_out.T, jnp.stack([attn_gain, mlp_gain]), grad_chunks[0], tp_count, dp_count,
        hops, 1,
    )
    w_out_t = lax.all_gather(out_shards, "dp", axis=1, tiled=True)
    grad_chunks += [got_chunks[hop] for hop in range(hops)]
    gains = gains.transpose(1, 0, 2).reshape(2, -1).astype(f32)
    gain_one, gain_two = gains[0], gains[1]

    scale_one = rms_scale(hidden_in)
    normed_one = (hidden_in * scale_one * gain_one).astype(bf16)
    slots = project(normed_one, w_qkv, dp_count, 3)
    for hop in range(hops + 1, tp_count):
        grad_chunks.append(pass_on(after(grad_chunks[-1], slots)))
    saved, mixed = [], []
    for g in groups:
        q_t, k_t, k_rows, v_t, v_rows = prepare(
            after(slots, (o_slots, w_mlp)) if g else slots, g, perm, cos_t, sin_t, per_group, 1
        )
        o_t, lse, o_slots = attend_forward(
            q_t, k_rows, v_t, begin, first_block, perm, page_rows, block_len
        )
        saved.append((q_t, k_rows, k_t, v_rows, o_t, lse))
        mixed.append(trade_back(after(o_slots, grad_chunks[-1]) if g else o_slots))
    hidden_mid = hidden_in
    for g in groups:
        hidden_mid = gather_sum(mixed[g], w_out_t, g, hidden_mid)

    scale_two = rms_scale(hidden_mid)
    normed_two = (hidden_mid * scale_two * gain_two).astype(bf16)
    grads_t, rows_t, inner_act, grad_gate_up, partial_two, grad_normed_two = feed(
        normed_two, grad_chunks, w_mlp, tp_count
    )
    grad_normed_two = grad_normed_two.astype(f32)
    grad_mid_norm, gain_two_part = norm_back(grad_normed_two, hidden_mid, scale_two, gain_two)
    grad_mid = grad_out + grad_mid_norm

    def add_on(arrived, s):
        return (arrived.astype(f32) + partial_two[s].astype(f32)).astype(bf16)

    def reduce_dp(grad):
        return lax.psum_scatter(grad.astype(bf16), "dp", scatter_dimension=0, tiled=True)

    def reduce_tensor(value):
        cols = value.shape[1] // tp_count
        total = lax.dynamic_slice_in_dim(value, tp_index * cols, cols, 1).astype(f32)
        for s in range(1, tp_count):
            target = lax.rem(tp_index + s, tp_count)
            block = lax.dynamic_slice_in_dim(value, target * cols, cols, 1)
            pairs = [(t, (t + s) % tp_count) for t in range(tp_count)]
            total = total + lax.ppermute(block, "tensor", pairs).astype(f32)
        return total

    grad_z = grad_mid.astype(bf16)
    grad_wout = outer(grad_z, mixed)
    sum_out = reduce_dp(grad_wout)
    grad_slots, grad_wmlp = weigh(
        spread(after(grad_z, grad_wout), w_out_t, 0, q_cols),
        rows_t, grads_t, grad_gate_up, inner_act, tp_count, dp_count, 2,
    )
    sum_mlp = reduce_dp(grad_wmlp)
    first_part = after(partial_two[1], grad_slots)
    branch_two = pass_on(first_part)
    grad_qkv = []
    for g in groups:
        q_t, k_rows, k_t, v_rows, o_t, lse = saved[g]
        back = attend_backward(
            after(grad_slots, (back, sum_out) if g else first_part), g, q_t, k_rows, k_t, v_rows,
            o_t, lse, begin, cos_t, sin_t, first_block, perm, page_rows, block_len,
        )
        grad_qkv.append(trade_back(after(back, (grad_qkv[-1], branch_two)) if g else back))
    hidden = sum_mlp.shape[1] // 3
    hops = min(2, tp_count - 2)
    sum_qkv, grad_normed_one, branch_two = total_grads(
        normed_one,
        grad_qkv,
        add_on(branch_two, 2),
        [partial_two[2 + n] for n in range(1, hops)],
        w_qkv,
        dp_count,
        4,
    )
    each = group_q + 2 * HD
    sum_qkv = [sum_qkv[:, g * each : (g + 1) * each] for g in groups]
    for s in range(2 + hops, tp_count):
        branch_two = pass_on(add_on(branch_two, s))
    sum_out = reduce_tensor(sum_out)
    result = (
        (after(hidden_mid, back) + branch_two.astype(f32) + partial_two[0].astype(f32)) * valid_rows
    ).astype(bf16)
    grad_in_norm, gain_one_part = norm_back(grad_normed_one, hidden_in, scale_one, gain_one)
    grad_in = (grad_mid + grad_in_norm).astype(bf16)

    gain_parts = jnp.stack([gain_one_part, gain_two_part]).reshape(2, dp_count, -1)
    gain_parts = jnp.broadcast_to(
        gain_parts.transpose(1, 0, 2)[None], (tp_count, dp_count, 2, gain_parts.shape[2])
    ).reshape(group_pages, 2, -1)
    gain_sums = jnp.sum(
        lax.all_to_all(gain_parts, everyone, split_axis=0, concat_axis=0, tiled=True), axis=0
    )
    return (
        reorder(result, dest_group),
        reorder(grad_in, dest_group),
        gain_sums[0],
        jnp.concatenate([part[:, :group_q] for part in sum_qkv], axis=1),
        jnp.concatenate([part[:, group_q : group_q + HD] for part in sum_qkv], axis=1),
        jnp.concatenate([part[:, group_q + HD :] for part in sum_qkv], axis=1),
        sum_out.T,
        gain_sums[1],
        sum_mlp[:, :hidden].astype(f32),
        sum_mlp[:, hidden : 2 * hidden].astype(f32),
        sum_mlp[:, 2 * hidden :].astype(f32).T,
    )


def solution(mesh):
    rows = P(("dp", "tensor"), None)
    weight = P("dp", "tensor")
    weight_t = P("tensor", "dp")
    return jax.shard_map(
        local,
        mesh=mesh,
        in_specs=(
            rows,
            rows,
            P("dp", None),
            P("dp", None),
            P(),
            P("dp"),
            weight,
            weight,
            weight,
            weight_t,
            P("dp"),
            weight,
            weight,
            weight_t,
        ),
        out_specs=(
            rows,
            rows,
            P("dp"),
            weight,
            weight,
            weight,
            weight_t,
            P("dp"),
            weight,
            weight,
            weight_t,
        ),
        check_vma=False,
    )
```

```python
import functools

import jax
import jax.numpy as jnp
from jax import lax
from jax.experimental import pallas as pl
from jax.experimental.pallas import tpu as pltpu
from jax.sharding import PartitionSpec as P

HD = 64
HALF = HD // 2

epsilon = 1e-05
theta_base = 500000.0
masked_score = -1e30
score_scale = HD**-0.5
block_rows = 512
key_rows = 256
MESH = pl.DeviceIdType.MESH
f32 = jnp.float32
bf16 = jnp.bfloat16


def dot_nn(left, right):
    return lax.dot_general(left, right, (((1,), (0,)), ((), ())), preferred_element_type=f32)


def dot_nt(left, right):
    return lax.dot_general(left, right, (((1,), (1,)), ((), ())), preferred_element_type=f32)


def dot_tn(left, right):
    return lax.dot_general(left, right, (((0,), (0,)), ((), ())), preferred_element_type=f32)


def prep_kernel(pages_per, q_heads, kv_heads, perm, *refs):
    page_refs = refs[:pages_per]
    cos_ref, sin_ref, q_t, k_t, k_rows, v_t, v_rows = refs[pages_per:]
    rows = jnp.concatenate([r[0].astype(f32) for r in page_refs], axis=0)
    turned = rows.T
    cos, sin = cos_ref[...], sin_ref[...]

    def rope(base):
        first, second = turned[base : base + HALF], turned[base + HALF : base + HD]
        return jnp.concatenate([first * cos - second * sin, second * cos + first * sin], axis=0)

    for h in range(q_heads):
        roped = rope(h * HD).astype(bf16)
        q_t[h * HD : (h + 1) * HD, :] = (roped.astype(f32) * score_scale).astype(bf16)
    k_base = q_heads * HD
    v_base = k_base + kv_heads * HD
    for g in range(kv_heads):
        roped = rope(k_base + g * HD)
        k_t[g * HD : (g + 1) * HD, :] = roped.astype(bf16)
        k_rows[g] = roped.T.astype(bf16)
        v_t[g * HD : (g + 1) * HD, :] = turned[v_base + g * HD : v_base + (g + 1) * HD].astype(bf16)
        v_rows[g] = rows[:, v_base + g * HD : v_base + (g + 1) * HD].astype(bf16)


def prepare(slots, part, perm, cos_t, sin_t, q_heads, kv_heads):
    page_rows = slots.shape[1]
    cols = (q_heads + 2 * kv_heads) * HD
    total_rows = slots.shape[0] * page_rows
    lanes = min(256, total_rows)
    pages_per = lanes // page_rows

    def page_spec(a):
        return pl.BlockSpec(
            (1, page_rows, cols), lambda i, perm_ref, a=a: (perm_ref[i * pages_per + a], 0, part)
        )

    table = pl.BlockSpec((HALF, lanes), lambda i, perm_ref: (0, i))
    return pl.pallas_call(
        functools.partial(prep_kernel, pages_per, q_heads, kv_heads),
        grid_spec=pltpu.PrefetchScalarGridSpec(
            num_scalar_prefetch=1,
            grid=(total_rows // lanes,),
            in_specs=[page_spec(a) for a in range(pages_per)] + [table, table],
            out_specs=[
                pl.BlockSpec((q_heads * HD, lanes), lambda i, perm_ref: (0, i)),
                pl.BlockSpec((kv_heads * HD, lanes), lambda i, perm_ref: (0, i)),
                pl.BlockSpec((kv_heads, lanes, HD), lambda i, perm_ref: (0, i, 0)),
                pl.BlockSpec((kv_heads * HD, lanes), lambda i, perm_ref: (0, i)),
                pl.BlockSpec((kv_heads, lanes, HD), lambda i, perm_ref: (0, i, 0)),
            ],
        ),
        out_shape=[
            jax.ShapeDtypeStruct((q_heads * HD, total_rows), bf16),
            jax.ShapeDtypeStruct((kv_heads * HD, total_rows), bf16),
            jax.ShapeDtypeStruct((kv_heads, total_rows, HD), bf16),
            jax.ShapeDtypeStruct((kv_heads * HD, total_rows), bf16),
            jax.ShapeDtypeStruct((kv_heads, total_rows, HD), bf16),
        ],
        cost_estimate=pl.CostEstimate(
            flops=8 * slots.size, bytes_accessed=6 * slots.size, transcendentals=0
        ),
        name="prepare",
    )(perm, *([slots] * pages_per), cos_t, sin_t)


def block_bias(i, j, begin_row, block_len, key_len):
    keys = j * key_len + lax.broadcasted_iota(jnp.int32, (key_len, block_len), 0)
    queries = i * block_len + lax.broadcasted_iota(jnp.int32, (key_len, block_len), 1)
    allowed = (keys >= begin_row) & (keys <= queries)
    return jnp.where(allowed, 0.0, masked_score)


def forward_kernel(
    q_heads, kv_heads, page_rows, first_block, perm,
    q_t, k_rows, v_t, begin, o_t, lse, o_slots, acc, stage, sems,
):
    i = pl.program_id(0)
    block_len = q_t.shape[1]
    key_len = min(key_rows, k_rows.shape[1])
    per_group = q_heads // kv_heads
    acc[...] = jnp.zeros_like(acc)
    begin_row = begin[...]

    def visit(j, carry):
        bias = block_bias(i, j, begin_row, block_len, key_len)
        at = pl.ds(pl.multiple_of(j * key_len, key_len), key_len)
        scores = [
            dot_nn(k_rows[h // per_group, at, :], q_t[h * HD : (h + 1) * HD, :]) + bias
            for h in range(q_heads)
        ]
        tops = [
            jnp.maximum(carry[h][0], jnp.max(scores[h], axis=0, keepdims=True))
            for h in range(q_heads)
        ]
        weights = [jnp.exp(scores[h] - tops[h]) for h in range(q_heads)]
        fades = [jnp.exp(carry[h][0] - tops[h]) for h in range(q_heads)]
        totals = [
            carry[h][1] * fades[h] + jnp.sum(weights[h], axis=0, keepdims=True)
            for h in range(q_heads)
        ]
        for h in range(q_heads):
            g = h // per_group
            span = slice(h * HD, (h + 1) * HD)
            acc[span, :] = acc[span, :] * fades[h] + dot_nn(
                v_t[g * HD : (g + 1) * HD, at], weights[h].astype(bf16)
            )
        return tuple(zip(tops, totals))

    start = tuple(
        (jnp.full((1, block_len), masked_score, f32), jnp.zeros((1, block_len), f32))
        for _ in range(q_heads)
    )
    stats = lax.fori_loop(
        first_block[i], lax.div((i + 1) * block_len - 1, key_len) + 1, visit, start
    )
    for h in range(q_heads):
        lse[h : h + 1, :] = stats[h][0] + jnp.log(stats[h][1])
    mixed = jnp.concatenate(
        [acc[h * HD : (h + 1) * HD, :] / stats[h][1] for h in range(q_heads)], axis=0
    )
    o_t[...] = mixed.astype(bf16)
    pages = block_len // page_rows
    stage[...] = mixed.T.astype(bf16).reshape(pages, page_rows, q_heads * HD)
    copies = [
        pltpu.make_async_copy(stage.at[a], o_slots.at[perm[i * pages + a]], sems.at[a])
        for a in range(pages)
    ]
    for copy in copies:
        copy.start()
    for copy in copies:
        copy.wait()


def attend_forward(q_t, k_rows, v_t, begin, first_block, perm, page_rows, block_len):
    total_rows = q_t.shape[1]
    kv_heads = k_rows.shape[0]
    q_heads = q_t.shape[0] // HD
    pages = block_len // page_rows
    return pl.pallas_call(
        functools.partial(forward_kernel, q_heads, kv_heads, page_rows),
        grid_spec=pltpu.PrefetchScalarGridSpec(
            num_scalar_prefetch=2,
            grid=(total_rows // block_len,),
            in_specs=[
                pl.BlockSpec((q_heads * HD, block_len), lambda i, *_: (0, i)),
                pl.BlockSpec((kv_heads, total_rows, HD), lambda i, *_: (0, 0, 0)),
                pl.BlockSpec((kv_heads * HD, total_rows), lambda i, *_: (0, 0)),
                pl.BlockSpec((1, block_len), lambda i, *_: (0, i)),
            ],
            out_specs=[
                pl.BlockSpec((q_heads * HD, block_len), lambda i, *_: (0, i)),
                pl.BlockSpec((q_heads, block_len), lambda i, *_: (0, i)),
                pl.BlockSpec(memory_space=pl.ANY),
            ],
            scratch_shapes=[
                pltpu.VMEM((q_heads * HD, block_len), f32),
                pltpu.VMEM((pages, page_rows, q_heads * HD), bf16),
                pltpu.SemaphoreType.DMA((pages,)),
            ],
        ),
        out_shape=[
            jax.ShapeDtypeStruct((q_heads * HD, total_rows), bf16),
            jax.ShapeDtypeStruct((q_heads, total_rows), f32),
            jax.ShapeDtypeStruct((total_rows // page_rows, page_rows, q_heads * HD), bf16),
        ],
        cost_estimate=pl.CostEstimate(
            flops=q_heads * total_rows * total_rows * HD,
            bytes_accessed=8 * q_t.size,
            transcendentals=q_heads * total_rows * total_rows // 4,
        ),
        name="attend_forward",
    )(first_block, perm, q_t, k_rows, v_t, begin)


def backward_kernel(
    q_heads, kv_heads, page_rows, pages, first_block, perm, *refs
):
    grad_pages = refs[:pages]
    (
        q_t, k_rows, k_t, v_rows, o_t, lse, begin, cos_ref, sin_ref, cos_all, sin_all,
        out, grad_q, grad_k, grad_v, stage, kv_stage, sems, kv_sems,
    ) = refs[pages:]
    i = pl.program_id(0)
    steps = pl.num_programs(0)
    block_len = q_t.shape[1]
    key_len = min(key_rows, k_rows.shape[1])
    per_group = q_heads // kv_heads
    q_cols = q_heads * HD
    kv_cols = kv_heads * HD

    @pl.when(i == 0)
    def _():
        grad_k[...] = jnp.zeros_like(grad_k)
        grad_v[...] = jnp.zeros_like(grad_v)

    grad_rows = jnp.concatenate([r[0].astype(f32) for r in grad_pages], axis=0)
    grad_t = grad_rows.T
    grad_low = grad_t.astype(bf16)
    inner = [
        jnp.sum(
            grad_t[h * HD : (h + 1) * HD] * o_t[h * HD : (h + 1) * HD, :].astype(f32),
            axis=0,
            keepdims=True,
        )
        for h in range(q_heads)
    ]
    grad_q[...] = jnp.zeros_like(grad_q)
    begin_row = begin[...]

    def visit(j, carry):
        bias = block_bias(i, j, begin_row, block_len, key_len)
        at = pl.ds(pl.multiple_of(j * key_len, key_len), key_len)
        for g in range(kv_heads):
            kv_span = slice(g * HD, (g + 1) * HD)
            keys, vals, keys_t = k_rows[g, at, :], v_rows[g, at, :], k_t[kv_span, at]
            heads = range(g * per_group, (g + 1) * per_group)
            spans = [slice(h * HD, (h + 1) * HD) for h in heads]
            scores = [dot_nn(keys, q_t[span, :]) + bias for span in spans]
            grad_probs = [dot_nn(vals, grad_low[span]) for span in spans]
            probs = [jnp.exp(s - lse[h : h + 1, :]) for s, h in zip(scores, heads)]
            grad_scores = [
                (p * (d - inner[h])).astype(bf16) for p, d, h in zip(probs, grad_probs, heads)
            ]
            low_probs = [p.astype(bf16) for p in probs]
            grad_v[kv_span, at] += sum(
                dot_nt(grad_low[span], p) for span, p in zip(spans, low_probs)
            )
            grad_k[kv_span, at] += sum(
                dot_nt(q_t[span, :], d) for span, d in zip(spans, grad_scores)
            )
            for span, d in zip(spans, grad_scores):
                grad_q[span, :] += dot_nn(keys_t, d)
        return carry

    lax.fori_loop(first_block[i], lax.div((i + 1) * block_len - 1, key_len) + 1, visit, 0)

    def unrope(value, cos, sin):
        first, second = value[:HALF], value[HALF:]
        return jnp.concatenate([first * cos + second * sin, second * cos - first * sin], axis=0)

    cos, sin = cos_ref[...], sin_ref[...]
    parts = [
        unrope(grad_q[h * HD : (h + 1) * HD, :] * score_scale, cos, sin) for h in range(q_heads)
    ]
    stage[...] = jnp.concatenate(parts, axis=0).T.astype(bf16).reshape(pages, page_rows, q_cols)
    copies = [
        pltpu.make_async_copy(
            stage.at[a], out.at[perm[i * pages + a], :, pl.ds(0, q_cols)], sems.at[a]
        )
        for a in range(pages)
    ]
    for copy in copies:
        copy.start()
    for copy in copies:
        copy.wait()

    @pl.when(i == steps - 1)
    def _():
        all_pages = kv_stage.shape[0]
        cos, sin = cos_all[...], sin_all[...]
        parts = [unrope(grad_k[g * HD : (g + 1) * HD, :], cos, sin) for g in range(kv_heads)]
        both = jnp.concatenate(parts + [grad_v[...]], axis=0)
        kv_stage[...] = both.T.astype(bf16).reshape(all_pages, page_rows, 2 * kv_cols)
        copies = [
            pltpu.make_async_copy(
                kv_stage.at[a], out.at[perm[a], :, pl.ds(q_cols, 2 * kv_cols)], kv_sems.at[a]
            )
            for a in range(all_pages)
        ]
        for copy in copies:
            copy.start()
        for copy in copies:
            copy.wait()


def attend_backward(
    grad_slots, part, q_t, k_rows, k_t, v_rows, o_t, lse, begin, cos_t, sin_t, first_block, perm,
    page_rows, block_len,
):
    total_rows = q_t.shape[1]
    kv_heads = k_rows.shape[0]
    q_heads = q_t.shape[0] // HD
    pages = block_len // page_rows
    all_pages = total_rows // page_rows
    q_cols = q_heads * HD
    kv_cols = kv_heads * HD

    def page_spec(a):
        return pl.BlockSpec(
            (1, page_rows, q_cols),
            lambda i, first_ref, perm_ref, a=a: (perm_ref[i * pages + a], 0, part),
        )

    def whole(shape):
        return pl.BlockSpec(shape, lambda i, *_: (0,) * len(shape))

    def column(rows):
        return pl.BlockSpec((rows, block_len), lambda i, *_: (0, i))

    return pl.pallas_call(
        functools.partial(backward_kernel, q_heads, kv_heads, page_rows, pages),
        grid_spec=pltpu.PrefetchScalarGridSpec(
            num_scalar_prefetch=2,
            grid=(total_rows // block_len,),
            in_specs=[page_spec(a) for a in range(pages)]
            + [
                column(q_cols),
                whole((kv_heads, total_rows, HD)),
                whole((kv_cols, total_rows)),
                whole((kv_heads, total_rows, HD)),
                column(q_cols),
                column(q_heads),
                column(1),
                column(HALF),
                column(HALF),
                whole((HALF, total_rows)),
                whole((HALF, total_rows)),
            ],
            out_specs=pl.BlockSpec(memory_space=pl.ANY),
            scratch_shapes=[
                pltpu.VMEM((q_cols, block_len), f32),
                pltpu.VMEM((kv_cols, total_rows), f32),
                pltpu.VMEM((kv_cols, total_rows), f32),
                pltpu.VMEM((pages, page_rows, q_cols), bf16),
                pltpu.VMEM((all_pages, page_rows, 2 * kv_cols), bf16),
                pltpu.SemaphoreType.DMA((pages,)),
                pltpu.SemaphoreType.DMA((all_pages,)),
            ],
        ),
        out_shape=jax.ShapeDtypeStruct((all_pages, page_rows, q_cols + 2 * kv_cols), bf16),
        cost_estimate=pl.CostEstimate(
            flops=3 * q_heads * total_rows * total_rows * HD,
            bytes_accessed=12 * q_t.size,
            transcendentals=q_heads * total_rows * total_rows // 4,
        ),
        name="attend_backward",
    )(
        first_block, perm, *([grad_slots] * pages), q_t, k_rows, k_t, v_rows, o_t, lse, begin,
        cos_t, sin_t, cos_t, sin_t,
    )


def project_kernel(
    tp_count, dp_count, rows, weights, slots, held, stage, load_sem, own_sem, send, recv
):
    count = dp_count * tp_count
    my_dp = lax.axis_index("dp")
    my_tp = lax.axis_index("tensor")
    me = my_dp * tp_count + my_tp
    page_rows = slots.shape[1]

    def load(j):
        shard = lax.rem(my_tp + 1 + j, tp_count)
        return pltpu.make_async_copy(weights.at[shard], held.at[j % 2], load_sem.at[j % 2])

    load(0).start()
    barrier = pltpu.get_barrier_semaphore()

    def greet(j, carry):
        peer = lax.rem(me + j, count)
        pl.semaphore_signal(
            barrier,
            inc=1,
            device_id={"dp": lax.div(peer, tp_count), "tensor": lax.rem(peer, tp_count)},
            device_id_type=MESH,
        )
        return carry

    lax.fori_loop(1, count, greet, 0)
    pl.semaphore_wait(barrier, count - 1)
    home = slots.at[my_tp * dp_count + my_dp]

    def copy_to(j, off):
        p_dp = lax.rem(my_dp + off, dp_count)
        return pltpu.make_async_remote_copy(
            src_ref=stage.at[j, pl.ds(p_dp * page_rows, page_rows), :],
            dst_ref=home,
            send_sem=send.at[j, off],
            recv_sem=recv.at[j, off],
            device_id={"dp": p_dp, "tensor": lax.rem(my_tp + 1 + j, tp_count)},
            device_id_type=MESH,
        )

    def each(j, act):
        def one(off, carry):
            act(copy_to(j, off))
            return carry

        lax.fori_loop(1 if j == tp_count - 1 else 0, dp_count, one, 0)

    for j in range(tp_count):
        load(j).wait()
        if j + 1 < tp_count:
            load(j + 1).start()
        stage[j] = dot_nn(rows[...], held[j % 2]).astype(bf16)
        if j > 0:
            each(j - 1, lambda copy: copy.start())
    each(tp_count - 1, lambda copy: copy.start())
    own = pltpu.make_async_copy(
        stage.at[tp_count - 1, pl.ds(my_dp * page_rows, page_rows), :], home, own_sem
    )
    own.start()
    own.wait()
    for j in range(tp_count):
        each(j, lambda copy: copy.wait())


def project(rows, weights, dp_count, collective_id):
    tp_count, width, cols = weights.shape
    total = rows.shape[0]
    page_rows = total // dp_count
    any_spec = pl.BlockSpec(memory_space=pl.ANY)
    dma = pltpu.SemaphoreType.DMA
    return pl.pallas_call(
        functools.partial(project_kernel, tp_count, dp_count),
        out_shape=jax.ShapeDtypeStruct((tp_count * dp_count, page_rows, cols), bf16),
        in_specs=[pl.BlockSpec(memory_space=pltpu.VMEM), any_spec],
        out_specs=any_spec,
        scratch_shapes=[
            pltpu.VMEM((2, width, cols), bf16),
            pltpu.VMEM((tp_count, total, cols), bf16),
            dma((2,)),
            dma,
            dma((tp_count, dp_count)),
            dma((tp_count, dp_count)),
        ],
        compiler_params=pltpu.CompilerParams(
            collective_id=collective_id, has_side_effects=True, vmem_limit_bytes=32 * 1024 * 1024
        ),
        cost_estimate=pl.CostEstimate(
            flops=2 * tp_count * total * width * cols,
            bytes_accessed=16 * tp_count * width * cols,
            transcendentals=0,
        ),
        name="project",
    )(rows, weights)


def feed_kernel(
    ring, tile, own_rows, *refs
):
    grad_rows = refs[: 2 * ring - 1]
    (
        weights, grads_t, rows_t, act_all, grads_all, mixed_all, grad_own,
    held, grads_held, acc_n, acc_m, first_part, arrived, outgoing, mixed_stage, final_stage,
    turned, load_sem, keep_sem, grad_sem, mixed_sem, final_sem,
    row_send, row_recv, sum_send, sum_recv, all_sem,
    ) = refs[2 * ring - 1 :]
    me = lax.axis_index("tensor")
    right = lax.rem(me + 1, ring)
    left = lax.rem(me + ring - 1, ring)
    hidden = weights.shape[1] // 3
    tiles = hidden // tile

    barrier = pltpu.get_barrier_semaphore()
    for neighbour in (left, right):
        pl.semaphore_signal(barrier, inc=1, device_id={"tensor": neighbour}, device_id_type=MESH)
    pl.semaphore_wait(barrier, 2)

    load = pltpu.make_async_copy(own_rows, held.at[0], load_sem)
    load.start()

    def grad_load(s):
        def copy_of(source):
            return pltpu.make_async_copy(
                grad_rows[source], grads_held.at[s % 2], grad_sem.at[s % 2]
            )

        if s == 0:
            copy_of(0).start()
            return

        @pl.when(me >= s)
        def _():
            copy_of(s).start()

        @pl.when(me < s)
        def _():
            copy_of(ring - 1 + ring - s).start()

    def grad_wait(s):
        pltpu.make_async_copy(grad_rows[0], grads_held.at[s % 2], grad_sem.at[s % 2]).wait()

    def part_of(array, s):
        count = own_rows.shape[0]
        return array.at[:, pl.ds(pl.multiple_of(s * count, 128), count)]

    def grad_keep(s):
        return pltpu.make_async_copy(turned.at[1], part_of(grads_t, s), all_sem)

    grad_load(0)
    load.wait()

    def pass_rows(s):
        return pltpu.make_async_remote_copy(
            src_ref=held.at[s],
            dst_ref=held.at[s + 1],
            send_sem=row_send.at[s],
            recv_sem=row_recv.at[s],
            device_id={"tensor": right},
            device_id_type=MESH,
        )

    def pass_sum(s):
        return pltpu.make_async_remote_copy(
            src_ref=outgoing.at[s - 1],
            dst_ref=arrived.at[s - 1],
            send_sem=sum_send.at[s - 1],
            recv_sem=sum_recv.at[s - 1],
            device_id={"tensor": right},
            device_id_type=MESH,
        )

    def keep(s):
        return pltpu.make_async_copy(turned.at[0], part_of(rows_t, s), keep_sem)

    def mixed_store(s):
        return pltpu.make_async_copy(mixed_stage, mixed_all.at[s], mixed_sem)

    def chunk(s, carry):
        @pl.when(s > 0)
        def _():
            pass_rows(s - 1).wait_recv()

        @pl.when(s < ring - 1)
        def _():
            pass_rows(s).start()

        @pl.when(s > 0)
        def _():
            keep(s - 1).wait()
            grad_keep(s - 1).wait()

        turned[0] = held[s].T
        keep(s).start()
        for k in range(ring):

            @pl.when(s == k)
            def _(k=k):
                grad_wait(k)
                if k < ring - 1:
                    grad_load(k + 1)

        slot = lax.rem(s, 2)
        turned[1] = grads_held[slot].T
        grad_keep(s).start()
        acc_n[...] = jnp.zeros_like(acc_n)
        acc_m[...] = jnp.zeros_like(acc_m)

        def body(w_gate, w_up, w_down, act, grad_gate, grad_up):
            rows = held[s]
            gate = dot_nn(rows, w_gate[...])
            up = dot_nn(rows, w_up[...])
            grad_act = dot_nn(grads_held[slot], w_down[...])
            sig = 1.0 / (1.0 + jnp.exp(-gate))
            silu = gate * sig
            low_act = (silu * up).astype(bf16)
            low_up = (grad_act * silu).astype(bf16)
            low_gate = (grad_act * up * sig * (1.0 + gate * (1.0 - sig))).astype(bf16)
            act[...] = low_act
            grad_gate[...] = low_gate
            grad_up[...] = low_up
            acc_m[...] += dot_nt(low_act, w_down[...])
            acc_n[...] += dot_nt(low_gate, w_gate[...]) + dot_nt(low_up, w_up[...])

        width, count = own_rows.shape[1], own_rows.shape[0]
        pltpu.emit_pipeline(
            body,
            grid=(tiles,),
            in_specs=[
                pl.BlockSpec((width, tile), lambda k: (0, k)),
                pl.BlockSpec((width, tile), lambda k: (0, k + tiles)),
                pl.BlockSpec((width, tile), lambda k: (0, k + 2 * tiles)),
            ],
            out_specs=[
                pl.BlockSpec((count, tile), lambda k: (0, k)),
                pl.BlockSpec((count, tile), lambda k: (0, k)),
                pl.BlockSpec((count, tile), lambda k: (0, k + tiles)),
            ],
        )(weights, weights, weights, act_all.at[s], grads_all.at[s], grads_all.at[s])

        @pl.when(s > 0)
        def _():
            mixed_store(s - 1).wait()

        mixed_stage[...] = acc_m[...].astype(bf16)
        mixed_store(s).start()

        @pl.when(s == 0)
        def _():
            first_part[...] = acc_n[...]

        @pl.when(s == 1)
        def _():
            outgoing[0] = acc_n[...].astype(bf16)

        @pl.when(s > 1)
        def _():
            pass_sum(s - 1).wait_recv()
            outgoing[s - 1] = (acc_n[...] + arrived[s - 2].astype(f32)).astype(bf16)

        @pl.when(s > 0)
        def _():
            pass_sum(s).start()

        return carry

    lax.fori_loop(0, ring, chunk, 0)
    mixed_store(ring - 1).wait()
    pass_sum(ring - 1).wait_recv()
    final_stage[...] = (first_part[...] + arrived[ring - 2].astype(f32)).astype(bf16)
    final = pltpu.make_async_copy(final_stage, grad_own, final_sem)
    final.start()

    def settle(s, carry):
        @pl.when(s < ring - 1)
        def _():
            pass_rows(s).wait_send()

        @pl.when(s > 0)
        def _():
            pass_sum(s).wait_send()

        return carry

    lax.fori_loop(0, ring, settle, 0)
    keep(ring - 1).wait()
    grad_keep(ring - 1).wait()
    final.wait()


def feed(own_rows, grad_rows, weights, ring, tile=256, collective_id=7):
    count, width = own_rows.shape
    hidden = weights.shape[1] // 3
    any_spec = pl.BlockSpec(memory_space=pl.ANY)
    dma = pltpu.SemaphoreType.DMA
    return pl.pallas_call(
        functools.partial(feed_kernel, ring, min(tile, hidden)),
        out_shape=[
            jax.ShapeDtypeStruct((width, ring * count), bf16),
            jax.ShapeDtypeStruct((width, ring * count), bf16),
            jax.ShapeDtypeStruct((ring, count, hidden), bf16),
            jax.ShapeDtypeStruct((ring, count, 2 * hidden), bf16),
            jax.ShapeDtypeStruct((ring, count, width), bf16),
            jax.ShapeDtypeStruct((count, width), bf16),
        ],
        in_specs=[any_spec] * (1 + 2 * ring),
        out_specs=[any_spec] * 6,
        scratch_shapes=[
            pltpu.VMEM((ring, count, width), bf16),
            pltpu.VMEM((2, count, width), bf16),
            pltpu.VMEM((count, width), f32),
            pltpu.VMEM((count, width), f32),
            pltpu.VMEM((count, width), f32),
            pltpu.VMEM((ring - 1, count, width), bf16),
            pltpu.VMEM((ring - 1, count, width), bf16),
            pltpu.VMEM((count, width), bf16),
            pltpu.VMEM((count, width), bf16),
            pltpu.VMEM((2, width, count), bf16),
            dma,
            dma,
            dma((2,)),
            dma,
            dma,
            dma((ring - 1,)),
            dma((ring - 1,)),
            dma((ring - 1,)),
            dma((ring - 1,)),
            dma,
        ],
        compiler_params=pltpu.CompilerParams(
            collective_id=collective_id, has_side_effects=True, vmem_limit_bytes=64 * 1024 * 1024 - 65536,
        ),
        cost_estimate=pl.CostEstimate(
            flops=12 * ring * count * width * hidden,
            bytes_accessed=8 * ring * count * width,
            transcendentals=ring * count * hidden,
        ),
        name="feed_forward",
    )(own_rows, *grad_rows, weights)


def weigh_kernel(
    tp_count, dp_count, tile, grads, rows_t, grads_t, gate_up, act, slots, out,
    left, left_sem, own_sem, send, recv,
):
    count = dp_count * tp_count
    my_dp = lax.axis_index("dp")
    my_tp = lax.axis_index("tensor")
    me = my_dp * tp_count + my_tp
    page_rows = slots.shape[1]

    loads = [
        pltpu.make_async_copy(source, left.at[k], left_sem.at[k])
        for k, source in enumerate((rows_t, grads_t))
    ]
    for load in loads:
        load.start()

    barrier = pltpu.get_barrier_semaphore()

    def place(peer):
        return {"dp": lax.div(peer, tp_count), "tensor": lax.rem(peer, tp_count)}

    def greet(j, carry):
        peer = lax.rem(me + j, count)
        pl.semaphore_signal(barrier, inc=1, device_id=place(peer), device_id_type=MESH)
        return carry

    lax.fori_loop(1, count, greet, 0)
    pl.semaphore_wait(barrier, count - 1)

    home = slots.at[my_tp * dp_count + my_dp]

    def block(p_dp, p_tp):
        return grads.at[p_tp, pl.ds(p_dp * page_rows, page_rows), :]

    own = pltpu.make_async_copy(block(my_dp, my_tp), home, own_sem)
    own.start()

    def copy_to(j):
        peer = lax.rem(me + j, count)
        return pltpu.make_async_remote_copy(
            src_ref=block(lax.div(peer, tp_count), lax.rem(peer, tp_count)),
            dst_ref=home,
            send_sem=send.at[j],
            recv_sem=recv.at[j],
            device_id=place(peer),
            device_id_type=MESH,
        )

    def start(j, carry):
        copy_to(j).start()
        return carry

    def finish(j, carry):
        copy_to(j).wait()
        return carry

    lax.fori_loop(1, count, start, 0)

    width = rows_t.shape[0]
    step = min(512, width)

    def multiply(k, right, first):
        ring, rows, cols = right.shape

        def body(part, result):
            values = part[...].reshape(ring * rows, tile)
            for m in range(0, width, step):
                result[m : m + step, :] = dot_nn(left[k, m : m + step, :], values).astype(bf16)

        pltpu.emit_pipeline(
            body,
            grid=(cols // tile,),
            in_specs=[pl.BlockSpec((ring, rows, tile), lambda n: (0, 0, n))],
            out_specs=[pl.BlockSpec((width, tile), lambda n: (0, n + first))],
        )(right, out)

    loads[0].wait()
    multiply(0, gate_up, 0)
    loads[1].wait()
    multiply(1, act, gate_up.shape[2] // tile)
    own.wait()
    lax.fori_loop(1, count, finish, 0)


def weigh(grads, rows_t, grads_t, gate_up, act, tp_count, dp_count, collective_id):
    count = tp_count * dp_count
    cols = grads.shape[2]
    page_rows = grads.shape[1] // dp_count
    width, rows = rows_t.shape
    hidden = act.shape[2]
    any_spec = pl.BlockSpec(memory_space=pl.ANY)
    dma = pltpu.SemaphoreType.DMA
    return pl.pallas_call(
        functools.partial(weigh_kernel, tp_count, dp_count, min(512, hidden)),
        out_shape=[
            jax.ShapeDtypeStruct((count, page_rows, cols), bf16),
            jax.ShapeDtypeStruct((width, 3 * hidden), bf16),
        ],
        in_specs=[any_spec] * 5,
        out_specs=[any_spec] * 2,
        scratch_shapes=[
            pltpu.VMEM((2, width, rows), bf16),
            dma((2,)),
            dma,
            dma((count,)),
            dma((count,)),
        ],
        compiler_params=pltpu.CompilerParams(
            collective_id=collective_id, has_side_effects=True, vmem_limit_bytes=48 * 1024 * 1024
        ),
        cost_estimate=pl.CostEstimate(
            flops=6 * rows * width * hidden,
            bytes_accessed=2 * width * (2 * rows + 3 * hidden),
            transcendentals=0,
        ),
        name="weigh",
    )(grads, rows_t, grads_t, gate_up, act)


def flip(index, bit):
    return index + bit - 2 * bit * lax.rem(lax.div(index, bit), 2)


def collect_kernel(
    tp_count, dp_count, shard, second, gains, chunk, out, second_out, gains_out, chunks_out,
    second_send, second_recv, own_sem, ring_send, ring_recv, send, recv, gain_send, gain_recv, chunk_send, chunk_recv,
):
    my_dp = lax.axis_index("dp")
    my_tp = lax.axis_index("tensor")
    rows = shard.shape[0]
    half = rows // 2
    bits = [1 << b for b in reversed(range(dp_count.bit_length() - 1))]
    orders = [bits, bits[:-1][::-1] + bits[-1:]]
    steps = len(bits)

    barrier = pltpu.get_barrier_semaphore()
    for j in range(1, tp_count):
        pl.semaphore_signal(
            barrier, inc=1, device_id={"tensor": lax.rem(my_tp + j, tp_count)}, device_id_type=MESH
        )
    for j in range(1, dp_count):
        pl.semaphore_signal(
            barrier, inc=1, device_id={"dp": lax.rem(my_dp + j, dp_count)}, device_id_type=MESH
        )
    pl.semaphore_wait(barrier, tp_count + dp_count - 2)

    home = out.at[my_tp, pl.ds(my_dp * rows, rows), :]
    own = pltpu.make_async_copy(shard, home, own_sem.at[0])
    own.start()
    own_gain = pltpu.make_async_copy(gains, gains_out.at[my_dp], own_sem.at[1])
    own_gain.start()
    own_second = pltpu.make_async_copy(second, second_out.at[my_tp], own_sem.at[2])
    own_second.start()

    def second_copy(j):
        return pltpu.make_async_remote_copy(
            src_ref=second,
            dst_ref=second_out.at[my_tp],
            send_sem=second_send.at[j],
            recv_sem=second_recv.at[j],
            device_id={"tensor": lax.rem(my_tp + j, tp_count)},
            device_id_type=MESH,
        )

    def across(j):
        return pltpu.make_async_remote_copy(
            src_ref=shard,
            dst_ref=home,
            send_sem=ring_send.at[j],
            recv_sem=ring_recv.at[j],
            device_id={"tensor": lax.rem(my_tp + j, tp_count)},
            device_id_type=MESH,
        )

    def gain_copy(j):
        return pltpu.make_async_remote_copy(
            src_ref=gains,
            dst_ref=gains_out.at[my_dp],
            send_sem=gain_send.at[j],
            recv_sem=gain_recv.at[j],
            device_id={"dp": lax.rem(my_dp + j, dp_count)},
            device_id_type=MESH,
        )

    def step(way):
        return pltpu.make_async_remote_copy(
            src_ref=chunk,
            dst_ref=chunks_out.at[way],
            send_sem=chunk_send.at[way],
            recv_sem=chunk_recv.at[way],
            device_id={"tensor": lax.rem(my_tp + (1, tp_count - 1)[way], tp_count)},
            device_id_type=MESH,
        )

    has_right, has_left = my_tp < tp_count - 1, my_tp > 0

    def within(j, s, k, m):
        order = orders[s]
        owner = my_dp
        for b in range(k):
            if m >> b & 1:
                owner = flip(owner, order[b])
        block = out.at[
            lax.rem(my_tp - j + tp_count, tp_count), pl.ds(owner * rows + s * half, half), :
        ]
        at = (1 << k) - 1 + m
        return pltpu.make_async_remote_copy(
            src_ref=block,
            dst_ref=block,
            send_sem=send.at[j, s, at],
            recv_sem=recv.at[j, s, at],
            device_id={"dp": flip(my_dp, order[k])},
            device_id_type=MESH,
        )

    for j in range(1, tp_count):
        across(j).start()
    for j in range(1, dp_count):
        gain_copy(j).start()

    @pl.when(has_right)
    def _():
        step(0).start()

    @pl.when(has_left)
    def _():
        step(1).start()

    own.wait()
    for phase in range(tp_count + steps):
        for k in reversed(range(steps + 1)):
            j = phase - k
            if not 0 <= j < tp_count:
                continue
            if k == 0:
                if j > 0:
                    across(j).wait_recv()
            else:
                for s in range(2):
                    for m in range(1 << (k - 1)):
                        within(j, s, k - 1, m).wait_recv()
            if k < steps:
                for s in range(2):
                    for m in range(1 << k):
                        within(j, s, k, m).start()
        if phase == tp_count:
            for j in range(1, tp_count):
                second_copy(j).start()
    for j in range(tp_count):
        if j > 0:
            across(j).wait_send()
        for s in range(2):
            for k in range(steps):
                for m in range(1 << k):
                    within(j, s, k, m).wait_send()
    own_gain.wait()
    own_second.wait()
    for j in range(1, tp_count):
        second_copy(j).wait()
    for j in range(1, dp_count):
        gain_copy(j).wait()

    @pl.when(has_right)
    def _():
        step(0).wait_send()
        step(1).wait_recv()

    @pl.when(has_left)
    def _():
        step(1).wait_send()
        step(0).wait_recv()


def collect(shard, second, gains, chunk, tp_count, dp_count, collective_id):
    rows, cols = shard.shape
    dma = pltpu.SemaphoreType.DMA
    vmem_spec = pl.BlockSpec(memory_space=pltpu.VMEM)
    any_spec = pl.BlockSpec(memory_space=pl.ANY)
    return pl.pallas_call(
        functools.partial(collect_kernel, tp_count, dp_count),
        out_shape=[
            jax.ShapeDtypeStruct((tp_count, dp_count * rows, cols), shard.dtype),
            jax.ShapeDtypeStruct((tp_count,) + second.shape, second.dtype),
            jax.ShapeDtypeStruct((dp_count,) + gains.shape, gains.dtype),
            jax.ShapeDtypeStruct((2,) + chunk.shape, chunk.dtype),
        ],
        in_specs=[vmem_spec, vmem_spec, vmem_spec, any_spec],
        out_specs=[any_spec] * 4,
        scratch_shapes=[
            dma((tp_count,)),
            dma((tp_count,)),
            dma((3,)),
            dma((tp_count,)),
            dma((tp_count,)),
            dma((tp_count, 2, dp_count - 1)),
            dma((tp_count, 2, dp_count - 1)),
            dma((dp_count,)),
            dma((dp_count,)),
            dma((2,)),
            dma((2,)),
        ],
        compiler_params=pltpu.CompilerParams(collective_id=collective_id, has_side_effects=True),
        cost_estimate=pl.CostEstimate(
            flops=0, bytes_accessed=16 * tp_count * dp_count * shard.size, transcendentals=0
        ),
        name="collect",
    )(shard, second, gains, chunk)


def spread_kernel(rows, weight, out):
    out[0] = dot_nn(rows[...], weight[0]).astype(out.dtype)


def spread(rows, weights, part, cols):
    shards, width, _ = weights.shape
    count = rows.shape[0]
    return pl.pallas_call(
        spread_kernel,
        grid=(shards,),
        in_specs=[
            pl.BlockSpec((count, width), lambda t: (0, 0)),
            pl.BlockSpec((1, width, cols), lambda t: (t, 0, part)),
        ],
        out_specs=pl.BlockSpec((1, count, cols), lambda t: (t, 0, 0)),
        out_shape=jax.ShapeDtypeStruct((shards, count, cols), bf16),
        cost_estimate=pl.CostEstimate(
            flops=2 * shards * count * width * cols,
            bytes_accessed=2 * shards * width * cols,
            transcendentals=0,
        ),
        name="spread",
    )(rows, weights)


def gather_kernel(has_begin, part, weight, *refs):
    out = refs[-1]

    @pl.when(pl.program_id(0) == 0)
    def _():
        out[...] = refs[0][...] if has_begin else jnp.zeros_like(out)

    out[...] += dot_nt(part[0], weight[0])


def gather_sum(parts, weights, part, begin):
    shards, count, cols = parts.shape
    width = weights.shape[1]
    whole = pl.BlockSpec((count, width), lambda t: (0, 0))
    begins = [] if begin is None else [begin]
    return pl.pallas_call(
        functools.partial(gather_kernel, begin is not None),
        grid=(shards,),
        in_specs=[
            pl.BlockSpec((1, count, cols), lambda t: (t, 0, 0)),
            pl.BlockSpec((1, width, cols), lambda t: (t, 0, part)),
        ]
        + [whole] * len(begins),
        out_specs=whole,
        out_shape=jax.ShapeDtypeStruct((count, width), f32),
        cost_estimate=pl.CostEstimate(
            flops=2 * shards * count * width * cols,
            bytes_accessed=2 * shards * width * cols,
            transcendentals=0,
        ),
        name="gather_sum",
    )(parts, weights, *begins)


def outer_kernel(rows, *refs):
    parts, out, turned = refs[:-2], refs[-2], refs[-1]

    @pl.when(pl.program_id(0) == 0)
    def _():
        turned[...] = rows[...].T

    at = 0
    for part in parts:
        cols = part.shape[2]
        out[:, at : at + cols] = dot_nn(turned[...], part[0]).astype(out.dtype)
        at += cols


def outer(rows, parts):
    shards, count, _ = parts[0].shape
    cols = sum(part.shape[2] for part in parts)
    width = rows.shape[1]
    return pl.pallas_call(
        outer_kernel,
        grid=(shards,),
        in_specs=[pl.BlockSpec((count, width), lambda t: (0, 0))]
        + [pl.BlockSpec((1, count, part.shape[2]), lambda t: (t, 0, 0)) for part in parts],
        out_specs=pl.BlockSpec((width, cols), lambda t: (0, t)),
        out_shape=jax.ShapeDtypeStruct((width, shards * cols), bf16),
        scratch_shapes=[pltpu.VMEM((width, count), bf16)],
        cost_estimate=pl.CostEstimate(
            flops=2 * shards * count * width * cols,
            bytes_accessed=2 * shards * width * cols,
            transcendentals=0,
        ),
        name="outer",
    )(rows, *parts)


def total_kernel(
    tp_count, dp_count, groups, rows, *refs
):
    parts = refs[:groups]
    (
        to_right, to_left, weights, out, grad_rows, from_sides,
        turned, mine, got, got_across, held, load_sem, send, recv,
        across_send, across_recv, chunk_send, chunk_recv,
    ) = refs[groups:]
    my_dp = lax.axis_index("dp")
    my_tp = lax.axis_index("tensor")
    own_rows = out.shape[0]
    half = own_rows // 2
    bits = [1 << b for b in range(dp_count.bit_length() - 1)]
    orders = [bits, bits[:1] + bits[1:][::-1]]
    steps = len(bits)

    def shard_of(j):
        return lax.rem(my_tp + 1 + j, tp_count)

    def load(j):
        return pltpu.make_async_copy(weights.at[shard_of(j)], held.at[j % 2], load_sem.at[j % 2])

    load(0).start()
    barrier = pltpu.get_barrier_semaphore()
    for j in range(1, tp_count):
        pl.semaphore_signal(
            barrier, inc=1, device_id={"tensor": lax.rem(my_tp + j, tp_count)}, device_id_type=MESH
        )
    for bit in bits:
        pl.semaphore_signal(
            barrier, inc=1, device_id={"dp": flip(my_dp, bit)}, device_id_type=MESH
        )
    pl.semaphore_wait(barrier, tp_count - 1 + steps)

    def step(way):
        return pltpu.make_async_remote_copy(
            src_ref=(to_right, to_left)[way],
            dst_ref=from_sides.at[way],
            send_sem=chunk_send.at[way],
            recv_sem=chunk_recv.at[way],
            device_id={"tensor": lax.rem(my_tp + (1, tp_count - 1)[way], tp_count)},
            device_id_type=MESH,
        )

    has_right, has_left = my_tp < tp_count - 1, my_tp > 0

    @pl.when(has_right)
    def _():
        step(0).start()

    @pl.when(has_left)
    def _():
        step(1).start()

    def block(j, s, owner):
        return j, pl.ds(pl.multiple_of(owner * own_rows + s * half, half), half)

    def place(k, m):
        return sum(1 << (steps - 1 - e) for e in range(k)) + m

    def fellow(s, k, m, start):
        owner = start
        for b in range(steps - 1 - k):
            if m >> b & 1:
                owner = flip(owner, orders[s][k + 1 + b])
        return owner

    def exchange_part(j, s, k, m):
        partner = flip(my_dp, orders[s][k])
        at = place(k, m)
        index, span = block(j, s, fellow(s, k, m, partner))
        return pltpu.make_async_remote_copy(
            src_ref=mine.at[index, span, :],
            dst_ref=got.at[j, s, at],
            send_sem=send.at[j, s, at],
            recv_sem=recv.at[j, s, at],
            device_id={"dp": partner},
            device_id_type=MESH,
        )

    def across(j):
        return pltpu.make_async_remote_copy(
            src_ref=mine.at[j, pl.ds(pl.multiple_of(my_dp * own_rows, own_rows), own_rows), :],
            dst_ref=got_across.at[j],
            send_sem=across_send.at[j],
            recv_sem=across_recv.at[j],
            device_id={"tensor": shard_of(j)},
            device_id_type=MESH,
        )

    def every(k):
        return [(s, m) for s in range(2) for m in range(1 << (steps - 1 - k))]

    turned[...] = rows[...].T
    for phase in range(tp_count + steps + 1):
        if phase < tp_count:
            shard = shard_of(phase)
            at = 0
            load(phase).wait()
            if phase + 1 < tp_count:
                load(phase + 1).start()
            for g, part in enumerate(parts):
                cols = part.shape[2]
                value = part[shard]
                mine[phase, :, at : at + cols] = dot_nn(turned[...], value).astype(bf16)
                product = dot_nt(value, held[phase % 2, :, at : at + cols])
                if phase == 0 and g == 0:
                    grad_rows[...] = product
                else:
                    grad_rows[...] += product
                at += cols
        for k in reversed(range(steps + 1)):
            j = phase - k
            if not 0 <= j < tp_count:
                continue
            if k > 0:
                for s, m in every(k - 1):
                    exchange_part(j, s, k - 1, m).wait_recv()
                    index, span = block(j, s, fellow(s, k - 1, m, my_dp))
                    mine[index, span, :] = (
                        mine[index, span, :].astype(f32)
                        + got[j, s, place(k - 1, m)].astype(f32)
                    ).astype(bf16)
            if k < steps:
                for s, m in every(k):
                    exchange_part(j, s, k, m).start()
            elif j < tp_count - 1:
                across(j).start()
    total = mine[
        tp_count - 1, pl.ds(pl.multiple_of(my_dp * own_rows, own_rows), own_rows), :
    ].astype(f32)
    for j in range(tp_count - 1):
        across(j).wait_recv()
        total += got_across[j].astype(f32)
    out[...] = total

    @pl.when(has_right)
    def _():
        step(0).wait_send()
        step(1).wait_recv()

    @pl.when(has_left)
    def _():
        step(1).wait_send()
        step(0).wait_recv()

    for j in range(tp_count):
        if j < tp_count - 1:
            across(j).wait_send()
        for k in range(steps):
            for s, m in every(k):
                exchange_part(j, s, k, m).wait_send()


def total_grads(rows, parts, to_right, to_left, weights, dp_count, collective_id):
    tp_count, width, cols = weights.shape
    count = rows.shape[0]
    own_rows = width // dp_count
    vmem_spec = pl.BlockSpec(memory_space=pltpu.VMEM)
    any_spec = pl.BlockSpec(memory_space=pl.ANY)
    dma = pltpu.SemaphoreType.DMA
    return pl.pallas_call(
        functools.partial(total_kernel, tp_count, dp_count, len(parts)),
        out_shape=[
            jax.ShapeDtypeStruct((own_rows, cols), f32),
            jax.ShapeDtypeStruct((count, width), f32),
            jax.ShapeDtypeStruct((2, count, width), bf16),
        ],
        in_specs=[vmem_spec] * (1 + len(parts)) + [any_spec] * 3,
        out_specs=[vmem_spec, vmem_spec, any_spec],
        scratch_shapes=[
            pltpu.VMEM((width, count), bf16),
            pltpu.VMEM((tp_count, width, cols), bf16),
            pltpu.VMEM((tp_count, 2, dp_count - 1, own_rows // 2, cols), bf16),
            pltpu.VMEM((tp_count - 1, own_rows, cols), bf16),
            pltpu.VMEM((2, width, cols), bf16),
            dma((2,)),
            dma((tp_count, 2, dp_count - 1)),
            dma((tp_count, 2, dp_count - 1)),
            dma((tp_count,)),
            dma((tp_count,)),
            dma((2,)),
            dma((2,)),
        ],
        compiler_params=pltpu.CompilerParams(
            collective_id=collective_id, has_side_effects=True, vmem_limit_bytes=62 * 1024 * 1024
        ),
        cost_estimate=pl.CostEstimate(
            flops=4 * tp_count * count * width * cols,
            bytes_accessed=16 * tp_count * width * cols,
            transcendentals=0,
        ),
        name="total_grads",
    )(rows, *parts, to_right, to_left, weights)


def rms_scale(hidden):
    return lax.rsqrt(jnp.mean(hidden * hidden, axis=1, keepdims=True) + epsilon)


def norm_back(grad_norm, hidden, scale_rows, gain):
    normed = hidden * scale_rows
    gain_part = jnp.sum(grad_norm * normed, axis=0)
    inner = grad_norm * gain
    grad_hidden = scale_rows * (inner - normed * jnp.mean(inner * normed, axis=1, keepdims=True))
    return (grad_hidden, gain_part)


def after(value, other):
    return lax.optimization_barrier((value, other))[0]


def local(
    tokens,
    upstream,
    lengths,
    positions,
    pages,
    attn_gain,
    w_query,
    w_key,
    w_value,
    w_out,
    mlp_gain,
    w_gate,
    w_up,
    w_down,
):
    dp_count = lax.axis_size("dp")
    tp_count = lax.axis_size("tensor")
    dp_index = lax.axis_index("dp")
    tp_index = lax.axis_index("tensor")
    tok_dev, width = tokens.shape
    tok_group = tok_dev * tp_count
    page_rows = tok_dev // dp_count
    group_pages = tp_count * dp_count
    page_count = pages.shape[0]
    device = dp_index * tp_count + tp_index
    everyone = ("tensor", "dp")

    local_ids = jnp.arange(dp_count, dtype=jnp.int32)
    inverse = (
        jnp.zeros((page_count,), jnp.int32).at[pages].set(jnp.arange(page_count, dtype=jnp.int32))
    )
    dealt = lax.dynamic_slice_in_dim(inverse, device * dp_count, dp_count)
    dest_group = dealt // group_pages
    send_order = jnp.zeros((dp_count,), jnp.int32).at[dest_group].set(local_ids)
    group_sources = lax.dynamic_slice_in_dim(pages, dp_index * group_pages, group_pages)
    perm = (
        (jnp.arange(group_pages, dtype=jnp.int32) // dp_count) * dp_count
        + group_sources // group_pages
    ).astype(jnp.int32)

    def reorder(rows, order):
        blocks = rows.reshape(dp_count, page_rows, rows.shape[1])
        return jnp.take(blocks, order, axis=0, mode="clip").reshape(rows.shape)

    hidden_in = reorder(tokens, send_order).astype(f32)
    grad_top = reorder(upstream, send_order).astype(f32)
    seq_lens = lengths[0]
    seq_ends = jnp.cumsum(seq_lens)
    place = (jnp.take(dealt, send_order, mode="clip") % group_pages) * page_rows
    place_rows = (place[:, None] + jnp.arange(page_rows, dtype=jnp.int32)[None, :]).reshape(-1)
    valid_rows = (place_rows < seq_ends[-1]).astype(f32)[:, None]

    row_ids = jnp.arange(tok_group, dtype=jnp.int32)
    begin = jnp.max(
        jnp.where(row_ids[:, None] >= seq_ends[None, :], seq_ends[None, :], 0), axis=1
    ).astype(jnp.int32)
    block_len = min(block_rows, tok_group)
    first_block = begin[::block_len] // min(key_rows, tok_group)
    begin = begin[None, :]
    inverse_freq = theta_base ** (-(jnp.arange(HALF, dtype=f32) * 2.0) / HD)
    angles = inverse_freq[:, None] * positions.astype(f32)
    cos_t, sin_t = jnp.cos(angles), jnp.sin(angles)

    q_cols, kv_cols = w_query.shape[1], w_key.shape[1]
    kv_heads = kv_cols // HD
    per_group = q_cols // kv_cols
    group_q = per_group * HD
    groups = range(kv_heads)
    qkv_shard = jnp.concatenate(
        [
            part
            for g in groups
            for part in (
                w_query[:, g * group_q : (g + 1) * group_q],
                w_key[:, g * HD : (g + 1) * HD],
                w_value[:, g * HD : (g + 1) * HD],
            )
        ],
        axis=1,
    )

    def trade(value):
        blocks = value.reshape(group_pages, page_rows, value.shape[-1])
        return lax.all_to_all(blocks, everyone, split_axis=0, concat_axis=0, tiled=True)

    def trade_back(value):
        return trade(value).reshape(tp_count, tok_dev, value.shape[-1])

    def pass_on(values, first, last):
        return (
            lax.ppermute(values[0], "tensor", [(t, t + 1) for t in range(*first)]),
            lax.ppermute(values[1], "tensor", [(t, t - 1) for t in range(*last)]),
        )

    grad_out = grad_top * valid_rows
    own_chunk = grad_out.astype(bf16)
    mlp_shard = jnp.concatenate([w_gate, w_up, w_down.T], axis=1)
    w_mlp = lax.all_gather(mlp_shard, "dp", axis=0, tiled=True)
    w_qkv, out_shards, gains, sides = collect(
        qkv_shard, w_out.T, jnp.stack([attn_gain, mlp_gain]), own_chunk, tp_count, dp_count, 1
    )
    w_out_t = lax.all_gather(out_shards, "dp", axis=1, tiled=True)
    chunks = [(sides[0], sides[1])]
    gains = gains.transpose(1, 0, 2).reshape(2, -1).astype(f32)
    gain_one, gain_two = gains[0], gains[1]

    scale_one = rms_scale(hidden_in)
    normed_one = (hidden_in * scale_one * gain_one).astype(bf16)
    slots = project(normed_one, w_qkv, dp_count, 3)
    for n in range(2, tp_count):
        passed = after(chunks[-1], slots) if n == 2 else chunks[-1]
        chunks.append(pass_on(passed, (n - 1, tp_count - 1), (1, tp_count - n + 1)))
    saved, mixed = [], []
    for g in groups:
        q_t, k_t, k_rows, v_t, v_rows = prepare(
            after(slots, (o_slots, w_mlp)) if g else slots, g, perm, cos_t, sin_t, per_group, 1
        )
        o_t, lse, o_slots = attend_forward(
            q_t, k_rows, v_t, begin, first_block, perm, page_rows, block_len
        )
        saved.append((q_t, k_rows, k_t, v_rows, o_t, lse))
        mixed.append(trade_back(after(o_slots, chunks[1]) if g else o_slots))
    hidden_mid = hidden_in
    for g in groups:
        hidden_mid = gather_sum(mixed[g], w_out_t, g, hidden_mid)

    scale_two = rms_scale(hidden_mid)
    normed_two = (hidden_mid * scale_two * gain_two).astype(bf16)
    grads_t, rows_t, inner_act, grad_gate_up, partial_two, grad_normed_two = feed(
        normed_two, [own_chunk] + [c[0] for c in chunks] + [c[1] for c in chunks], w_mlp, tp_count
    )
    grad_normed_two = grad_normed_two.astype(f32)
    grad_mid_norm, gain_two_part = norm_back(grad_normed_two, hidden_mid, scale_two, gain_two)
    grad_mid = grad_out + grad_mid_norm

    def add_on(arrived, s):
        return tuple(
            (value.astype(f32) + partial_two[at].astype(f32)).astype(bf16)
            for value, at in zip(arrived, (s, tp_count - s))
        )

    def reduce_dp(grad):
        return lax.psum_scatter(grad.astype(bf16), "dp", scatter_dimension=0, tiled=True)

    def reduce_tensor(value):
        cols = value.shape[1] // tp_count
        total = lax.dynamic_slice_in_dim(value, tp_index * cols, cols, 1).astype(f32)
        for s in range(1, tp_count):
            target = lax.rem(tp_index + s, tp_count)
            block = lax.dynamic_slice_in_dim(value, target * cols, cols, 1)
            pairs = [(t, (t + s) % tp_count) for t in range(tp_count)]
            total = total + lax.ppermute(block, "tensor", pairs).astype(f32)
        return total

    grad_z = grad_mid.astype(bf16)
    grad_wout = outer(grad_z, mixed)
    sum_out = reduce_dp(grad_wout)
    grad_slots, grad_wmlp = weigh(
        spread(after(grad_z, grad_wout), w_out_t, 0, q_cols),
        rows_t, grads_t, grad_gate_up, inner_act, tp_count, dp_count, 2,
    )
    sum_mlp = reduce_dp(grad_wmlp)
    first_part = after((partial_two[1], partial_two[tp_count - 1]), grad_slots)
    passing = pass_on(first_part, (0, 1), (tp_count - 1, tp_count))
    grad_qkv = []
    for g in groups:
        q_t, k_rows, k_t, v_rows, o_t, lse = saved[g]
        back = attend_backward(
            after(grad_slots, (back, sum_out) if g else first_part), g, q_t, k_rows, k_t, v_rows,
            o_t, lse, begin, cos_t, sin_t, first_block, perm, page_rows, block_len,
        )
        grad_qkv.append(trade_back(after(back, (grad_qkv[-1], passing)) if g else back))
    hidden = sum_mlp.shape[1] // 3
    for s in range(2, tp_count - 1):
        passing = pass_on(add_on(passing, s), (0, s), (tp_count - s, tp_count))
    passing = add_on(passing, tp_count - 1)
    sum_qkv, grad_normed_one, sides = total_grads(
        normed_one, grad_qkv, passing[0], passing[1], w_qkv, dp_count, 4
    )
    branch_two = jnp.where(tp_index > 0, sides[0].astype(f32), 0.0)
    branch_two += jnp.where(tp_index < tp_count - 1, sides[1].astype(f32), 0.0)
    each = group_q + 2 * HD
    sum_qkv = [sum_qkv[:, g * each : (g + 1) * each] for g in groups]
    sum_out = reduce_tensor(sum_out)
    result = (
        (after(hidden_mid, back) + branch_two + partial_two[0].astype(f32)) * valid_rows
    ).astype(bf16)
    grad_in_norm, gain_one_part = norm_back(grad_normed_one, hidden_in, scale_one, gain_one)
    grad_in = (grad_mid + grad_in_norm).astype(bf16)

    gain_parts = jnp.stack([gain_one_part, gain_two_part]).reshape(2, dp_count, -1)
    gain_parts = jnp.broadcast_to(
        gain_parts.transpose(1, 0, 2)[None], (tp_count, dp_count, 2, gain_parts.shape[2])
    ).reshape(group_pages, 2, -1)
    gain_sums = jnp.sum(
        lax.all_to_all(gain_parts, everyone, split_axis=0, concat_axis=0, tiled=True), axis=0
    )
    return (
        reorder(result, dest_group),
        reorder(grad_in, dest_group),
        gain_sums[0],
        jnp.concatenate([part[:, :group_q] for part in sum_qkv], axis=1),
        jnp.concatenate([part[:, group_q : group_q + HD] for part in sum_qkv], axis=1),
        jnp.concatenate([part[:, group_q + HD :] for part in sum_qkv], axis=1),
        sum_out.T,
        gain_sums[1],
        sum_mlp[:, :hidden].astype(f32),
        sum_mlp[:, hidden : 2 * hidden].astype(f32),
        sum_mlp[:, 2 * hidden :].astype(f32).T,
    )


def solution(mesh):
    rows = P(("dp", "tensor"), None)
    weight = P("dp", "tensor")
    weight_t = P("tensor", "dp")
    return jax.shard_map(
        local,
        mesh=mesh,
        in_specs=(
            rows,
            rows,
            P("dp", None),
            P("dp", None),
            P(),
            P("dp"),
            weight,
            weight,
            weight,
            weight_t,
            P("dp"),
            weight,
            weight,
            weight_t,
        ),
        out_specs=(
            rows,
            rows,
            P("dp"),
            weight,
            weight,
            weight,
            weight_t,
            P("dp"),
            weight,
            weight,
            weight_t,
        ),
        check_vma=False,
    )
```

```python
import functools

import jax
import jax.numpy as jnp
from jax import lax
from jax.experimental import pallas as pl
from jax.experimental.pallas import tpu as pltpu
from jax.sharding import PartitionSpec as P

HD = 64
HALF = HD // 2

epsilon = 1e-05
theta_base = 500000.0
masked_score = -1e30
score_scale = HD**-0.5
block_rows = 512
key_rows = 256
MESH = pl.DeviceIdType.MESH
f32 = jnp.float32
bf16 = jnp.bfloat16


def dot_nn(left, right):
    return lax.dot_general(left, right, (((1,), (0,)), ((), ())), preferred_element_type=f32)


def dot_nt(left, right):
    return lax.dot_general(left, right, (((1,), (1,)), ((), ())), preferred_element_type=f32)


def dot_tn(left, right):
    return lax.dot_general(left, right, (((0,), (0,)), ((), ())), preferred_element_type=f32)


def prep_kernel(pages_per, q_heads, kv_heads, perm, *refs):
    page_refs = refs[:pages_per]
    cos_ref, sin_ref, q_t, k_t, k_rows, v_t, v_rows = refs[pages_per:]
    rows = jnp.concatenate([r[0].astype(f32) for r in page_refs], axis=0)
    turned = rows.T
    cos, sin = cos_ref[...], sin_ref[...]

    def rope(base):
        first, second = turned[base : base + HALF], turned[base + HALF : base + HD]
        return jnp.concatenate([first * cos - second * sin, second * cos + first * sin], axis=0)

    for h in range(q_heads):
        roped = rope(h * HD).astype(bf16)
        q_t[h * HD : (h + 1) * HD, :] = (roped.astype(f32) * score_scale).astype(bf16)
    k_base = q_heads * HD
    v_base = k_base + kv_heads * HD
    for g in range(kv_heads):
        roped = rope(k_base + g * HD)
        k_t[g * HD : (g + 1) * HD, :] = roped.astype(bf16)
        k_rows[g] = roped.T.astype(bf16)
        v_t[g * HD : (g + 1) * HD, :] = turned[v_base + g * HD : v_base + (g + 1) * HD].astype(bf16)
        v_rows[g] = rows[:, v_base + g * HD : v_base + (g + 1) * HD].astype(bf16)


def prepare(slots, part, perm, cos_t, sin_t, q_heads, kv_heads):
    page_rows = slots.shape[1]
    cols = (q_heads + 2 * kv_heads) * HD
    total_rows = slots.shape[0] * page_rows
    lanes = min(256, total_rows)
    pages_per = lanes // page_rows

    def page_spec(a):
        return pl.BlockSpec(
            (1, page_rows, cols), lambda i, perm_ref, a=a: (perm_ref[i * pages_per + a], 0, part)
        )

    table = pl.BlockSpec((HALF, lanes), lambda i, perm_ref: (0, i))
    return pl.pallas_call(
        functools.partial(prep_kernel, pages_per, q_heads, kv_heads),
        grid_spec=pltpu.PrefetchScalarGridSpec(
            num_scalar_prefetch=1,
            grid=(total_rows // lanes,),
            in_specs=[page_spec(a) for a in range(pages_per)] + [table, table],
            out_specs=[
                pl.BlockSpec((q_heads * HD, lanes), lambda i, perm_ref: (0, i)),
                pl.BlockSpec((kv_heads * HD, lanes), lambda i, perm_ref: (0, i)),
                pl.BlockSpec((kv_heads, lanes, HD), lambda i, perm_ref: (0, i, 0)),
                pl.BlockSpec((kv_heads * HD, lanes), lambda i, perm_ref: (0, i)),
                pl.BlockSpec((kv_heads, lanes, HD), lambda i, perm_ref: (0, i, 0)),
            ],
        ),
        out_shape=[
            jax.ShapeDtypeStruct((q_heads * HD, total_rows), bf16),
            jax.ShapeDtypeStruct((kv_heads * HD, total_rows), bf16),
            jax.ShapeDtypeStruct((kv_heads, total_rows, HD), bf16),
            jax.ShapeDtypeStruct((kv_heads * HD, total_rows), bf16),
            jax.ShapeDtypeStruct((kv_heads, total_rows, HD), bf16),
        ],
        cost_estimate=pl.CostEstimate(
            flops=8 * slots.size, bytes_accessed=6 * slots.size, transcendentals=0
        ),
        name="prepare",
    )(perm, *([slots] * pages_per), cos_t, sin_t)


def block_bias(i, j, begin_row, block_len, key_len):
    keys = j * key_len + lax.broadcasted_iota(jnp.int32, (key_len, block_len), 0)
    queries = i * block_len + lax.broadcasted_iota(jnp.int32, (key_len, block_len), 1)
    allowed = (keys >= begin_row) & (keys <= queries)
    return jnp.where(allowed, 0.0, masked_score)


def forward_kernel(
    q_heads, kv_heads, page_rows, first_block, perm,
    q_t, k_rows, v_t, begin, o_t, lse, o_slots, acc, stage, sems,
):
    i = pl.program_id(0)
    block_len = q_t.shape[1]
    key_len = min(key_rows, k_rows.shape[1])
    per_group = q_heads // kv_heads
    acc[...] = jnp.zeros_like(acc)
    begin_row = begin[...]

    def visit(j, carry):
        bias = block_bias(i, j, begin_row, block_len, key_len)
        at = pl.ds(pl.multiple_of(j * key_len, key_len), key_len)
        scores = [
            dot_nn(k_rows[h // per_group, at, :], q_t[h * HD : (h + 1) * HD, :]) + bias
            for h in range(q_heads)
        ]
        tops = [
            jnp.maximum(carry[h][0], jnp.max(scores[h], axis=0, keepdims=True))
            for h in range(q_heads)
        ]
        weights = [jnp.exp(scores[h] - tops[h]) for h in range(q_heads)]
        fades = [jnp.exp(carry[h][0] - tops[h]) for h in range(q_heads)]
        totals = [
            carry[h][1] * fades[h] + jnp.sum(weights[h], axis=0, keepdims=True)
            for h in range(q_heads)
        ]
        for h in range(q_heads):
            g = h // per_group
            span = slice(h * HD, (h + 1) * HD)
            acc[span, :] = acc[span, :] * fades[h] + dot_nn(
                v_t[g * HD : (g + 1) * HD, at], weights[h].astype(bf16)
            )
        return tuple(zip(tops, totals))

    start = tuple(
        (jnp.full((1, block_len), masked_score, f32), jnp.zeros((1, block_len), f32))
        for _ in range(q_heads)
    )
    stats = lax.fori_loop(
        first_block[i], lax.div((i + 1) * block_len - 1, key_len) + 1, visit, start
    )
    for h in range(q_heads):
        lse[h : h + 1, :] = stats[h][0] + jnp.log(stats[h][1])
    mixed = jnp.concatenate(
        [acc[h * HD : (h + 1) * HD, :] / stats[h][1] for h in range(q_heads)], axis=0
    )
    o_t[...] = mixed.astype(bf16)
    pages = block_len // page_rows
    stage[...] = mixed.T.astype(bf16).reshape(pages, page_rows, q_heads * HD)
    copies = [
        pltpu.make_async_copy(stage.at[a], o_slots.at[perm[i * pages + a]], sems.at[a])
        for a in range(pages)
    ]
    for copy in copies:
        copy.start()
    for copy in copies:
        copy.wait()


def attend_forward(q_t, k_rows, v_t, begin, first_block, perm, page_rows, block_len):
    total_rows = q_t.shape[1]
    kv_heads = k_rows.shape[0]
    q_heads = q_t.shape[0] // HD
    pages = block_len // page_rows
    return pl.pallas_call(
        functools.partial(forward_kernel, q_heads, kv_heads, page_rows),
        grid_spec=pltpu.PrefetchScalarGridSpec(
            num_scalar_prefetch=2,
            grid=(total_rows // block_len,),
            in_specs=[
                pl.BlockSpec((q_heads * HD, block_len), lambda i, *_: (0, i)),
                pl.BlockSpec((kv_heads, total_rows, HD), lambda i, *_: (0, 0, 0)),
                pl.BlockSpec((kv_heads * HD, total_rows), lambda i, *_: (0, 0)),
                pl.BlockSpec((1, block_len), lambda i, *_: (0, i)),
            ],
            out_specs=[
                pl.BlockSpec((q_heads * HD, block_len), lambda i, *_: (0, i)),
                pl.BlockSpec((q_heads, block_len), lambda i, *_: (0, i)),
                pl.BlockSpec(memory_space=pl.ANY),
            ],
            scratch_shapes=[
                pltpu.VMEM((q_heads * HD, block_len), f32),
                pltpu.VMEM((pages, page_rows, q_heads * HD), bf16),
                pltpu.SemaphoreType.DMA((pages,)),
            ],
        ),
        out_shape=[
            jax.ShapeDtypeStruct((q_heads * HD, total_rows), bf16),
            jax.ShapeDtypeStruct((q_heads, total_rows), f32),
            jax.ShapeDtypeStruct((total_rows // page_rows, page_rows, q_heads * HD), bf16),
        ],
        cost_estimate=pl.CostEstimate(
            flops=q_heads * total_rows * total_rows * HD,
            bytes_accessed=8 * q_t.size,
            transcendentals=q_heads * total_rows * total_rows // 4,
        ),
        name="attend_forward",
    )(first_block, perm, q_t, k_rows, v_t, begin)


def backward_kernel(
    q_heads, kv_heads, page_rows, pages, first_block, perm, *refs
):
    grad_pages = refs[:pages]
    (
        q_t, k_rows, k_t, v_rows, o_t, lse, begin, cos_ref, sin_ref, cos_all, sin_all,
        out, grad_q, grad_k, grad_v, stage, kv_stage, sems, kv_sems,
    ) = refs[pages:]
    i = pl.program_id(0)
    steps = pl.num_programs(0)
    block_len = q_t.shape[1]
    key_len = min(key_rows, k_rows.shape[1])
    per_group = q_heads // kv_heads
    q_cols = q_heads * HD
    kv_cols = kv_heads * HD

    @pl.when(i == 0)
    def _():
        grad_k[...] = jnp.zeros_like(grad_k)
        grad_v[...] = jnp.zeros_like(grad_v)

    grad_rows = jnp.concatenate([r[0].astype(f32) for r in grad_pages], axis=0)
    grad_t = grad_rows.T
    grad_low = grad_t.astype(bf16)
    inner = [
        jnp.sum(
            grad_t[h * HD : (h + 1) * HD] * o_t[h * HD : (h + 1) * HD, :].astype(f32),
            axis=0,
            keepdims=True,
        )
        for h in range(q_heads)
    ]
    grad_q[...] = jnp.zeros_like(grad_q)
    begin_row = begin[...]

    def visit(j, carry):
        bias = block_bias(i, j, begin_row, block_len, key_len)
        at = pl.ds(pl.multiple_of(j * key_len, key_len), key_len)
        for g in range(kv_heads):
            kv_span = slice(g * HD, (g + 1) * HD)
            keys, vals, keys_t = k_rows[g, at, :], v_rows[g, at, :], k_t[kv_span, at]
            heads = range(g * per_group, (g + 1) * per_group)
            spans = [slice(h * HD, (h + 1) * HD) for h in heads]
            scores = [dot_nn(keys, q_t[span, :]) + bias for span in spans]
            grad_probs = [dot_nn(vals, grad_low[span]) for span in spans]
            probs = [jnp.exp(s - lse[h : h + 1, :]) for s, h in zip(scores, heads)]
            grad_scores = [
                (p * (d - inner[h])).astype(bf16) for p, d, h in zip(probs, grad_probs, heads)
            ]
            low_probs = [p.astype(bf16) for p in probs]
            grad_v[kv_span, at] += sum(
                dot_nt(grad_low[span], p) for span, p in zip(spans, low_probs)
            )
            grad_k[kv_span, at] += sum(
                dot_nt(q_t[span, :], d) for span, d in zip(spans, grad_scores)
            )
            for span, d in zip(spans, grad_scores):
                grad_q[span, :] += dot_nn(keys_t, d)
        return carry

    lax.fori_loop(first_block[i], lax.div((i + 1) * block_len - 1, key_len) + 1, visit, 0)

    def unrope(value, cos, sin):
        first, second = value[:HALF], value[HALF:]
        return jnp.concatenate([first * cos + second * sin, second * cos - first * sin], axis=0)

    cos, sin = cos_ref[...], sin_ref[...]
    parts = [
        unrope(grad_q[h * HD : (h + 1) * HD, :] * score_scale, cos, sin) for h in range(q_heads)
    ]
    stage[...] = jnp.concatenate(parts, axis=0).T.astype(bf16).reshape(pages, page_rows, q_cols)
    copies = [
        pltpu.make_async_copy(
            stage.at[a], out.at[perm[i * pages + a], :, pl.ds(0, q_cols)], sems.at[a]
        )
        for a in range(pages)
    ]
    for copy in copies:
        copy.start()
    for copy in copies:
        copy.wait()

    @pl.when(i == steps - 1)
    def _():
        all_pages = kv_stage.shape[0]
        cos, sin = cos_all[...], sin_all[...]
        parts = [unrope(grad_k[g * HD : (g + 1) * HD, :], cos, sin) for g in range(kv_heads)]
        both = jnp.concatenate(parts + [grad_v[...]], axis=0)
        kv_stage[...] = both.T.astype(bf16).reshape(all_pages, page_rows, 2 * kv_cols)
        copies = [
            pltpu.make_async_copy(
                kv_stage.at[a], out.at[perm[a], :, pl.ds(q_cols, 2 * kv_cols)], kv_sems.at[a]
            )
            for a in range(all_pages)
        ]
        for copy in copies:
            copy.start()
        for copy in copies:
            copy.wait()


def attend_backward(
    grad_slots, part, q_t, k_rows, k_t, v_rows, o_t, lse, begin, cos_t, sin_t, first_block, perm,
    page_rows, block_len,
):
    total_rows = q_t.shape[1]
    kv_heads = k_rows.shape[0]
    q_heads = q_t.shape[0] // HD
    pages = block_len // page_rows
    all_pages = total_rows // page_rows
    q_cols = q_heads * HD
    kv_cols = kv_heads * HD

    def page_spec(a):
        return pl.BlockSpec(
            (1, page_rows, q_cols),
            lambda i, first_ref, perm_ref, a=a: (perm_ref[i * pages + a], 0, part),
        )

    def whole(shape):
        return pl.BlockSpec(shape, lambda i, *_: (0,) * len(shape))

    def column(rows):
        return pl.BlockSpec((rows, block_len), lambda i, *_: (0, i))

    return pl.pallas_call(
        functools.partial(backward_kernel, q_heads, kv_heads, page_rows, pages),
        grid_spec=pltpu.PrefetchScalarGridSpec(
            num_scalar_prefetch=2,
            grid=(total_rows // block_len,),
            in_specs=[page_spec(a) for a in range(pages)]
            + [
                column(q_cols),
                whole((kv_heads, total_rows, HD)),
                whole((kv_cols, total_rows)),
                whole((kv_heads, total_rows, HD)),
                column(q_cols),
                column(q_heads),
                column(1),
                column(HALF),
                column(HALF),
                whole((HALF, total_rows)),
                whole((HALF, total_rows)),
            ],
            out_specs=pl.BlockSpec(memory_space=pl.ANY),
            scratch_shapes=[
                pltpu.VMEM((q_cols, block_len), f32),
                pltpu.VMEM((kv_cols, total_rows), f32),
                pltpu.VMEM((kv_cols, total_rows), f32),
                pltpu.VMEM((pages, page_rows, q_cols), bf16),
                pltpu.VMEM((all_pages, page_rows, 2 * kv_cols), bf16),
                pltpu.SemaphoreType.DMA((pages,)),
                pltpu.SemaphoreType.DMA((all_pages,)),
            ],
        ),
        out_shape=jax.ShapeDtypeStruct((all_pages, page_rows, q_cols + 2 * kv_cols), bf16),
        cost_estimate=pl.CostEstimate(
            flops=3 * q_heads * total_rows * total_rows * HD,
            bytes_accessed=12 * q_t.size,
            transcendentals=q_heads * total_rows * total_rows // 4,
        ),
        name="attend_backward",
    )(
        first_block, perm, *([grad_slots] * pages), q_t, k_rows, k_t, v_rows, o_t, lse, begin,
        cos_t, sin_t, cos_t, sin_t,
    )


def project_kernel(
    tp_count, dp_count, rows, weights, slots, held, stage, load_sem, own_sem, send, recv
):
    count = dp_count * tp_count
    my_dp = lax.axis_index("dp")
    my_tp = lax.axis_index("tensor")
    me = my_dp * tp_count + my_tp
    page_rows = slots.shape[1]

    def load(j):
        shard = lax.rem(my_tp + 1 + j, tp_count)
        return pltpu.make_async_copy(weights.at[shard], held.at[j % 2], load_sem.at[j % 2])

    load(0).start()
    barrier = pltpu.get_barrier_semaphore()

    def greet(j, carry):
        peer = lax.rem(me + j, count)
        pl.semaphore_signal(
            barrier,
            inc=1,
            device_id={"dp": lax.div(peer, tp_count), "tensor": lax.rem(peer, tp_count)},
            device_id_type=MESH,
        )
        return carry

    lax.fori_loop(1, count, greet, 0)
    pl.semaphore_wait(barrier, count - 1)
    home = slots.at[my_tp * dp_count + my_dp]

    def copy_to(j, off):
        p_dp = lax.rem(my_dp + off, dp_count)
        return pltpu.make_async_remote_copy(
            src_ref=stage.at[j, pl.ds(p_dp * page_rows, page_rows), :],
            dst_ref=home,
            send_sem=send.at[j, off],
            recv_sem=recv.at[j, off],
            device_id={"dp": p_dp, "tensor": lax.rem(my_tp + 1 + j, tp_count)},
            device_id_type=MESH,
        )

    def each(j, act):
        def one(off, carry):
            act(copy_to(j, off))
            return carry

        lax.fori_loop(1 if j == tp_count - 1 else 0, dp_count, one, 0)

    for j in range(tp_count):
        load(j).wait()
        if j + 1 < tp_count:
            load(j + 1).start()
        stage[j] = dot_nn(rows[...], held[j % 2]).astype(bf16)
        if j > 0:
            each(j - 1, lambda copy: copy.start())
    each(tp_count - 1, lambda copy: copy.start())
    own = pltpu.make_async_copy(
        stage.at[tp_count - 1, pl.ds(my_dp * page_rows, page_rows), :], home, own_sem
    )
    own.start()
    own.wait()
    for j in range(tp_count):
        each(j, lambda copy: copy.wait())


def project(rows, weights, dp_count, collective_id):
    tp_count, width, cols = weights.shape
    total = rows.shape[0]
    page_rows = total // dp_count
    any_spec = pl.BlockSpec(memory_space=pl.ANY)
    dma = pltpu.SemaphoreType.DMA
    return pl.pallas_call(
        functools.partial(project_kernel, tp_count, dp_count),
        out_shape=jax.ShapeDtypeStruct((tp_count * dp_count, page_rows, cols), bf16),
        in_specs=[
            pl.BlockSpec(memory_space=pltpu.VMEM),
            pl.BlockSpec(memory_space=pltpu.HBM),
        ],
        out_specs=any_spec,
        scratch_shapes=[
            pltpu.VMEM((2, width, cols), bf16),
            pltpu.VMEM((tp_count, total, cols), bf16),
            dma((2,)),
            dma,
            dma((tp_count, dp_count)),
            dma((tp_count, dp_count)),
        ],
        compiler_params=pltpu.CompilerParams(
            collective_id=collective_id, has_side_effects=True, vmem_limit_bytes=32 * 1024 * 1024
        ),
        cost_estimate=pl.CostEstimate(
            flops=2 * tp_count * total * width * cols,
            bytes_accessed=16 * tp_count * width * cols,
            transcendentals=0,
        ),
        name="project",
    )(rows, weights)


def feed_kernel(
    ring, tile, own_rows, *refs
):
    grad_rows = refs[: 2 * ring - 1]
    weights, grads_t, rows_t, act_all, grads_all = refs[2 * ring - 1 : 2 * ring + 4]
    mixed_all = refs[2 * ring + 4 : 3 * ring + 4]
    (
        grad_own, held, grads_held, acc_n, acc_m, first_part, arrived, outgoing, mixed_stage,
        final_stage, turned, load_sem, keep_sem, grad_sem, mixed_sem, final_sem,
        row_send, row_recv, sum_send, sum_recv, all_sem,
    ) = refs[3 * ring + 4 :]
    me = lax.axis_index("tensor")
    right = lax.rem(me + 1, ring)
    left = lax.rem(me + ring - 1, ring)
    hidden = weights.shape[1] // 3
    tiles = hidden // tile

    barrier = pltpu.get_barrier_semaphore()
    for neighbour in (left, right):
        pl.semaphore_signal(barrier, inc=1, device_id={"tensor": neighbour}, device_id_type=MESH)
    pl.semaphore_wait(barrier, 2)

    load = pltpu.make_async_copy(own_rows, held.at[0], load_sem)
    load.start()

    def grad_load(s):
        def copy_of(source):
            return pltpu.make_async_copy(
                grad_rows[source], grads_held.at[s % 2], grad_sem.at[s % 2]
            )

        if s == 0:
            copy_of(0).start()
            return

        @pl.when(me >= s)
        def _():
            copy_of(s).start()

        @pl.when(me < s)
        def _():
            copy_of(ring - 1 + ring - s).start()

    def grad_wait(s):
        pltpu.make_async_copy(grad_rows[0], grads_held.at[s % 2], grad_sem.at[s % 2]).wait()

    def part_of(array, s):
        count = own_rows.shape[0]
        return array.at[:, pl.ds(pl.multiple_of(s * count, 128), count)]

    def grad_keep(s):
        return pltpu.make_async_copy(turned.at[1], part_of(grads_t, s), all_sem)

    grad_load(0)
    load.wait()

    def pass_rows(s):
        return pltpu.make_async_remote_copy(
            src_ref=held.at[s],
            dst_ref=held.at[s + 1],
            send_sem=row_send.at[s],
            recv_sem=row_recv.at[s],
            device_id={"tensor": right},
            device_id_type=MESH,
        )

    def pass_sum(s):
        return pltpu.make_async_remote_copy(
            src_ref=outgoing.at[s - 1],
            dst_ref=arrived.at[s - 1],
            send_sem=sum_send.at[s - 1],
            recv_sem=sum_recv.at[s - 1],
            device_id={"tensor": right},
            device_id_type=MESH,
        )

    def keep(s):
        return pltpu.make_async_copy(turned.at[0], part_of(rows_t, s), keep_sem)

    def mixed_store(s):
        return pltpu.make_async_copy(mixed_stage, mixed_all[s], mixed_sem)

    def chunk(s, carry):
        @pl.when(s > 0)
        def _():
            pass_rows(s - 1).wait_recv()

        @pl.when(s < ring - 1)
        def _():
            pass_rows(s).start()

        @pl.when(s > 0)
        def _():
            keep(s - 1).wait()
            grad_keep(s - 1).wait()

        turned[0] = held[s].T
        keep(s).start()
        for k in range(ring):

            @pl.when(s == k)
            def _(k=k):
                grad_wait(k)
                if k < ring - 1:
                    grad_load(k + 1)

        slot = lax.rem(s, 2)
        turned[1] = grads_held[slot].T
        grad_keep(s).start()
        acc_n[...] = jnp.zeros_like(acc_n)
        acc_m[...] = jnp.zeros_like(acc_m)

        def body(w_gate, w_up, w_down, act, grad_gate, grad_up):
            rows = held[s]
            gate = dot_nn(rows, w_gate[...])
            up = dot_nn(rows, w_up[...])
            grad_act = dot_nn(grads_held[slot], w_down[...])
            sig = 1.0 / (1.0 + jnp.exp(-gate))
            silu = gate * sig
            low_act = (silu * up).astype(bf16)
            low_up = (grad_act * silu).astype(bf16)
            low_gate = (grad_act * up * sig * (1.0 + gate * (1.0 - sig))).astype(bf16)
            act[...] = low_act
            grad_gate[...] = low_gate
            grad_up[...] = low_up
            acc_m[...] += dot_nt(low_act, w_down[...])
            acc_n[...] += dot_nt(low_gate, w_gate[...]) + dot_nt(low_up, w_up[...])

        width, count = own_rows.shape[1], own_rows.shape[0]
        pltpu.emit_pipeline(
            body,
            grid=(tiles,),
            in_specs=[
                pl.BlockSpec((width, tile), lambda k: (0, k)),
                pl.BlockSpec((width, tile), lambda k: (0, k + tiles)),
                pl.BlockSpec((width, tile), lambda k: (0, k + 2 * tiles)),
            ],
            out_specs=[
                pl.BlockSpec((count, tile), lambda k: (0, k)),
                pl.BlockSpec((count, tile), lambda k: (0, k)),
                pl.BlockSpec((count, tile), lambda k: (0, k + tiles)),
            ],
        )(weights, weights, weights, act_all.at[s], grads_all.at[s], grads_all.at[s])

        @pl.when(s > 0)
        def _():
            mixed_store(0).wait()

        mixed_stage[...] = acc_m[...].astype(bf16)
        for k in range(ring):

            @pl.when(s == k)
            def _(k=k):
                mixed_store(k).start()

        @pl.when(s == 0)
        def _():
            first_part[...] = acc_n[...]

        @pl.when(s == 1)
        def _():
            outgoing[0] = acc_n[...].astype(bf16)

        @pl.when(s > 1)
        def _():
            pass_sum(s - 1).wait_recv()
            outgoing[s - 1] = (acc_n[...] + arrived[s - 2].astype(f32)).astype(bf16)

        @pl.when(s > 0)
        def _():
            pass_sum(s).start()

        return carry

    lax.fori_loop(0, ring, chunk, 0)
    mixed_store(0).wait()
    pass_sum(ring - 1).wait_recv()
    final_stage[...] = (first_part[...] + arrived[ring - 2].astype(f32)).astype(bf16)
    final = pltpu.make_async_copy(final_stage, grad_own, final_sem)
    final.start()

    def settle(s, carry):
        @pl.when(s < ring - 1)
        def _():
            pass_rows(s).wait_send()

        @pl.when(s > 0)
        def _():
            pass_sum(s).wait_send()

        return carry

    lax.fori_loop(0, ring, settle, 0)
    keep(ring - 1).wait()
    grad_keep(ring - 1).wait()
    final.wait()


def feed(own_rows, grad_rows, weights, ring, tile=256, collective_id=7):
    count, width = own_rows.shape
    hidden = weights.shape[1] // 3
    any_spec = pl.BlockSpec(memory_space=pl.ANY)
    dma = pltpu.SemaphoreType.DMA
    return pl.pallas_call(
        functools.partial(feed_kernel, ring, min(tile, hidden)),
        out_shape=[
            jax.ShapeDtypeStruct((width, ring * count), bf16),
            jax.ShapeDtypeStruct((width, ring * count), bf16),
            jax.ShapeDtypeStruct((ring, count, hidden), bf16),
            jax.ShapeDtypeStruct((ring, count, 2 * hidden), bf16),
        ]
        + [jax.ShapeDtypeStruct((count, width), bf16)] * (ring + 1),
        in_specs=[any_spec] * (1 + 2 * ring),
        out_specs=[any_spec] * (5 + ring),
        scratch_shapes=[
            pltpu.VMEM((ring, count, width), bf16),
            pltpu.VMEM((2, count, width), bf16),
            pltpu.VMEM((count, width), f32),
            pltpu.VMEM((count, width), f32),
            pltpu.VMEM((count, width), f32),
            pltpu.VMEM((ring - 1, count, width), bf16),
            pltpu.VMEM((ring - 1, count, width), bf16),
            pltpu.VMEM((count, width), bf16),
            pltpu.VMEM((count, width), bf16),
            pltpu.VMEM((2, width, count), bf16),
            dma,
            dma,
            dma((2,)),
            dma,
            dma,
            dma((ring - 1,)),
            dma((ring - 1,)),
            dma((ring - 1,)),
            dma((ring - 1,)),
            dma,
        ],
        compiler_params=pltpu.CompilerParams(
            collective_id=collective_id, has_side_effects=True, vmem_limit_bytes=64 * 1024 * 1024 - 65536,
        ),
        cost_estimate=pl.CostEstimate(
            flops=12 * ring * count * width * hidden,
            bytes_accessed=8 * ring * count * width,
            transcendentals=ring * count * hidden,
        ),
        name="feed_forward",
    )(own_rows, *grad_rows, weights)


def weigh_kernel(
    tp_count, dp_count, tile, grads, rows_t, grads_t, gate_up, act, slots, out,
    left, left_sem, own_sem, send, recv,
):
    count = dp_count * tp_count
    my_dp = lax.axis_index("dp")
    my_tp = lax.axis_index("tensor")
    me = my_dp * tp_count + my_tp
    page_rows = slots.shape[1]

    loads = [
        pltpu.make_async_copy(source, left.at[k], left_sem.at[k])
        for k, source in enumerate((rows_t, grads_t))
    ]
    for load in loads:
        load.start()

    barrier = pltpu.get_barrier_semaphore()

    def place(peer):
        return {"dp": lax.div(peer, tp_count), "tensor": lax.rem(peer, tp_count)}

    def greet(j, carry):
        peer = lax.rem(me + j, count)
        pl.semaphore_signal(barrier, inc=1, device_id=place(peer), device_id_type=MESH)
        return carry

    lax.fori_loop(1, count, greet, 0)
    pl.semaphore_wait(barrier, count - 1)

    home = slots.at[my_tp * dp_count + my_dp]

    def block(p_dp, p_tp):
        return grads.at[p_tp, pl.ds(p_dp * page_rows, page_rows), :]

    own = pltpu.make_async_copy(block(my_dp, my_tp), home, own_sem)
    own.start()

    def copy_to(j):
        peer = lax.rem(me + j, count)
        return pltpu.make_async_remote_copy(
            src_ref=block(lax.div(peer, tp_count), lax.rem(peer, tp_count)),
            dst_ref=home,
            send_sem=send.at[j],
            recv_sem=recv.at[j],
            device_id=place(peer),
            device_id_type=MESH,
        )

    def start(j, carry):
        copy_to(j).start()
        return carry

    def finish(j, carry):
        copy_to(j).wait()
        return carry

    lax.fori_loop(1, count, start, 0)

    width = rows_t.shape[0]
    step = min(512, width)

    def multiply(k, right, first):
        ring, rows, cols = right.shape

        def body(part, result):
            values = part[...].reshape(ring * rows, tile)
            for m in range(0, width, step):
                result[m : m + step, :] = dot_nn(left[k, m : m + step, :], values).astype(bf16)

        pltpu.emit_pipeline(
            body,
            grid=(cols // tile,),
            in_specs=[pl.BlockSpec((ring, rows, tile), lambda n: (0, 0, n))],
            out_specs=[pl.BlockSpec((width, tile), lambda n: (0, n + first))],
        )(right, out)

    loads[0].wait()
    multiply(0, gate_up, 0)
    loads[1].wait()
    multiply(1, act, gate_up.shape[2] // tile)
    own.wait()
    lax.fori_loop(1, count, finish, 0)


def weigh(grads, rows_t, grads_t, gate_up, act, tp_count, dp_count, collective_id):
    count = tp_count * dp_count
    cols = grads.shape[2]
    page_rows = grads.shape[1] // dp_count
    width, rows = rows_t.shape
    hidden = act.shape[2]
    any_spec = pl.BlockSpec(memory_space=pl.ANY)
    dma = pltpu.SemaphoreType.DMA
    return pl.pallas_call(
        functools.partial(weigh_kernel, tp_count, dp_count, min(512, hidden)),
        out_shape=[
            jax.ShapeDtypeStruct((count, page_rows, cols), bf16),
            jax.ShapeDtypeStruct((width, 3 * hidden), bf16),
        ],
        in_specs=[pl.BlockSpec(memory_space=pltpu.HBM)] * 5,
        out_specs=[any_spec] * 2,
        scratch_shapes=[
            pltpu.VMEM((2, width, rows), bf16),
            dma((2,)),
            dma,
            dma((count,)),
            dma((count,)),
        ],
        compiler_params=pltpu.CompilerParams(
            collective_id=collective_id, has_side_effects=True, vmem_limit_bytes=48 * 1024 * 1024
        ),
        cost_estimate=pl.CostEstimate(
            flops=6 * rows * width * hidden,
            bytes_accessed=2 * width * (2 * rows + 3 * hidden),
            transcendentals=0,
        ),
        name="weigh",
    )(grads, rows_t, grads_t, gate_up, act)


def flip(index, bit):
    return index + bit - 2 * bit * lax.rem(lax.div(index, bit), 2)


def collect_kernel(
    tp_count, dp_count, shard, second, gains, chunk, out, second_out, gains_out, from_left, from_right,
    second_send, second_recv, own_sem, ring_send, ring_recv, send, recv, gain_send, gain_recv, chunk_send, chunk_recv,
):
    my_dp = lax.axis_index("dp")
    my_tp = lax.axis_index("tensor")
    rows = shard.shape[0]
    half = rows // 2
    bits = [1 << b for b in reversed(range(dp_count.bit_length() - 1))]
    orders = [bits, bits[:-1][::-1] + bits[-1:]]
    steps = len(bits)

    barrier = pltpu.get_barrier_semaphore()
    for j in range(1, tp_count):
        pl.semaphore_signal(
            barrier, inc=1, device_id={"tensor": lax.rem(my_tp + j, tp_count)}, device_id_type=MESH
        )
    for j in range(1, dp_count):
        pl.semaphore_signal(
            barrier, inc=1, device_id={"dp": lax.rem(my_dp + j, dp_count)}, device_id_type=MESH
        )
    pl.semaphore_wait(barrier, tp_count + dp_count - 2)

    home = out.at[my_tp, pl.ds(my_dp * rows, rows), :]
    own = pltpu.make_async_copy(shard, home, own_sem.at[0])
    own.start()
    own_gain = pltpu.make_async_copy(gains, gains_out.at[my_dp], own_sem.at[1])
    own_gain.start()
    own_second = pltpu.make_async_copy(second, second_out.at[my_tp], own_sem.at[2])
    own_second.start()

    def second_copy(j):
        return pltpu.make_async_remote_copy(
            src_ref=second,
            dst_ref=second_out.at[my_tp],
            send_sem=second_send.at[j],
            recv_sem=second_recv.at[j],
            device_id={"tensor": lax.rem(my_tp + j, tp_count)},
            device_id_type=MESH,
        )

    def across(j):
        return pltpu.make_async_remote_copy(
            src_ref=shard,
            dst_ref=home,
            send_sem=ring_send.at[j],
            recv_sem=ring_recv.at[j],
            device_id={"tensor": lax.rem(my_tp + j, tp_count)},
            device_id_type=MESH,
        )

    def gain_copy(j):
        return pltpu.make_async_remote_copy(
            src_ref=gains,
            dst_ref=gains_out.at[my_dp],
            send_sem=gain_send.at[j],
            recv_sem=gain_recv.at[j],
            device_id={"dp": lax.rem(my_dp + j, dp_count)},
            device_id_type=MESH,
        )

    def step(way):
        return pltpu.make_async_remote_copy(
            src_ref=chunk,
            dst_ref=(from_left, from_right)[way],
            send_sem=chunk_send.at[way],
            recv_sem=chunk_recv.at[way],
            device_id={"tensor": lax.rem(my_tp + (1, tp_count - 1)[way], tp_count)},
            device_id_type=MESH,
        )

    has_right, has_left = my_tp < tp_count - 1, my_tp > 0

    def within(j, s, k, m):
        order = orders[s]
        owner = my_dp
        for b in range(k):
            if m >> b & 1:
                owner = flip(owner, order[b])
        block = out.at[
            lax.rem(my_tp - j + tp_count, tp_count), pl.ds(owner * rows + s * half, half), :
        ]
        at = (1 << k) - 1 + m
        return pltpu.make_async_remote_copy(
            src_ref=block,
            dst_ref=block,
            send_sem=send.at[j, s, at],
            recv_sem=recv.at[j, s, at],
            device_id={"dp": flip(my_dp, order[k])},
            device_id_type=MESH,
        )

    for j in range(1, tp_count):
        across(j).start()
    for j in range(1, dp_count):
        gain_copy(j).start()

    @pl.when(has_right)
    def _():
        step(0).start()

    @pl.when(has_left)
    def _():
        step(1).start()

    own.wait()
    for phase in range(tp_count + steps):
        for k in reversed(range(steps + 1)):
            j = phase - k
            if not 0 <= j < tp_count:
                continue
            if k == 0:
                if j > 0:
                    across(j).wait_recv()
            else:
                for s in range(2):
                    for m in range(1 << (k - 1)):
                        within(j, s, k - 1, m).wait_recv()
            if k < steps:
                for s in range(2):
                    for m in range(1 << k):
                        within(j, s, k, m).start()
        if phase == tp_count:
            for j in range(1, tp_count):
                second_copy(j).start()
    for j in range(tp_count):
        if j > 0:
            across(j).wait_send()
        for s in range(2):
            for k in range(steps):
                for m in range(1 << k):
                    within(j, s, k, m).wait_send()
    own_gain.wait()
    own_second.wait()
    for j in range(1, tp_count):
        second_copy(j).wait()
    for j in range(1, dp_count):
        gain_copy(j).wait()

    @pl.when(has_right)
    def _():
        step(0).wait_send()
        step(1).wait_recv()

    @pl.when(has_left)
    def _():
        step(1).wait_send()
        step(0).wait_recv()


def collect(shard, second, gains, chunk, tp_count, dp_count, collective_id):
    rows, cols = shard.shape
    dma = pltpu.SemaphoreType.DMA
    vmem_spec = pl.BlockSpec(memory_space=pltpu.VMEM)
    any_spec = pl.BlockSpec(memory_space=pl.ANY)
    return pl.pallas_call(
        functools.partial(collect_kernel, tp_count, dp_count),
        out_shape=[
            jax.ShapeDtypeStruct((tp_count, dp_count * rows, cols), shard.dtype),
            jax.ShapeDtypeStruct((tp_count,) + second.shape, second.dtype),
            jax.ShapeDtypeStruct((dp_count,) + gains.shape, gains.dtype),
            jax.ShapeDtypeStruct(chunk.shape, chunk.dtype),
            jax.ShapeDtypeStruct(chunk.shape, chunk.dtype),
        ],
        in_specs=[vmem_spec, vmem_spec, vmem_spec, any_spec],
        out_specs=[any_spec] * 5,
        scratch_shapes=[
            dma((tp_count,)),
            dma((tp_count,)),
            dma((3,)),
            dma((tp_count,)),
            dma((tp_count,)),
            dma((tp_count, 2, dp_count - 1)),
            dma((tp_count, 2, dp_count - 1)),
            dma((dp_count,)),
            dma((dp_count,)),
            dma((2,)),
            dma((2,)),
        ],
        compiler_params=pltpu.CompilerParams(collective_id=collective_id, has_side_effects=True),
        cost_estimate=pl.CostEstimate(
            flops=0, bytes_accessed=16 * tp_count * dp_count * shard.size, transcendentals=0
        ),
        name="collect",
    )(shard, second, gains, chunk)


def spread_kernel(rows, weight, out):
    out[0] = dot_nn(rows[...], weight[0]).astype(out.dtype)


def spread(rows, weights, part, cols):
    shards, width, _ = weights.shape
    count = rows.shape[0]
    return pl.pallas_call(
        spread_kernel,
        grid=(shards,),
        in_specs=[
            pl.BlockSpec((count, width), lambda t: (0, 0)),
            pl.BlockSpec((1, width, cols), lambda t: (t, 0, part)),
        ],
        out_specs=pl.BlockSpec((1, count, cols), lambda t: (t, 0, 0)),
        out_shape=jax.ShapeDtypeStruct((shards, count, cols), bf16),
        cost_estimate=pl.CostEstimate(
            flops=2 * shards * count * width * cols,
            bytes_accessed=2 * shards * width * cols,
            transcendentals=0,
        ),
        name="spread",
    )(rows, weights)


def gather_kernel(has_begin, part, weight, *refs):
    out = refs[-1]

    @pl.when(pl.program_id(0) == 0)
    def _():
        out[...] = refs[0][...] if has_begin else jnp.zeros_like(out)

    out[...] += dot_nt(part[0], weight[0])


def gather_sum(parts, weights, part, begin):
    shards, count, cols = parts.shape
    width = weights.shape[1]
    whole = pl.BlockSpec((count, width), lambda t: (0, 0))
    begins = [] if begin is None else [begin]
    return pl.pallas_call(
        functools.partial(gather_kernel, begin is not None),
        grid=(shards,),
        in_specs=[
            pl.BlockSpec((1, count, cols), lambda t: (t, 0, 0)),
            pl.BlockSpec((1, width, cols), lambda t: (t, 0, part)),
        ]
        + [whole] * len(begins),
        out_specs=whole,
        out_shape=jax.ShapeDtypeStruct((count, width), f32),
        cost_estimate=pl.CostEstimate(
            flops=2 * shards * count * width * cols,
            bytes_accessed=2 * shards * width * cols,
            transcendentals=0,
        ),
        name="gather_sum",
    )(parts, weights, *begins)


def outer_kernel(rows, *refs):
    parts, out, turned = refs[:-2], refs[-2], refs[-1]

    @pl.when(pl.program_id(0) == 0)
    def _():
        turned[...] = rows[...].T

    at = 0
    for part in parts:
        cols = part.shape[2]
        out[:, at : at + cols] = dot_nn(turned[...], part[0]).astype(out.dtype)
        at += cols


def outer(rows, parts):
    shards, count, _ = parts[0].shape
    cols = sum(part.shape[2] for part in parts)
    width = rows.shape[1]
    return pl.pallas_call(
        outer_kernel,
        grid=(shards,),
        in_specs=[pl.BlockSpec((count, width), lambda t: (0, 0))]
        + [pl.BlockSpec((1, count, part.shape[2]), lambda t: (t, 0, 0)) for part in parts],
        out_specs=pl.BlockSpec((width, cols), lambda t: (0, t)),
        out_shape=jax.ShapeDtypeStruct((width, shards * cols), bf16),
        scratch_shapes=[pltpu.VMEM((width, count), bf16)],
        cost_estimate=pl.CostEstimate(
            flops=2 * shards * count * width * cols,
            bytes_accessed=2 * shards * width * cols,
            transcendentals=0,
        ),
        name="outer",
    )(rows, *parts)


def total_kernel(
    tp_count, dp_count, groups, rows, *refs
):
    parts = refs[:groups]
    (
        to_right, to_left, weights, out, grad_rows, from_sides,
        turned, mine, got, got_across, held, load_sem, send, recv,
        across_send, across_recv, chunk_send, chunk_recv,
    ) = refs[groups:]
    my_dp = lax.axis_index("dp")
    my_tp = lax.axis_index("tensor")
    own_rows = out.shape[0]
    half = own_rows // 2
    bits = [1 << b for b in range(dp_count.bit_length() - 1)]
    orders = [bits, bits[:1] + bits[1:][::-1]]
    steps = len(bits)

    def shard_of(j):
        return lax.rem(my_tp + 1 + j, tp_count)

    def load(j):
        return pltpu.make_async_copy(weights.at[shard_of(j)], held.at[j % 2], load_sem.at[j % 2])

    load(0).start()
    barrier = pltpu.get_barrier_semaphore()
    for j in range(1, tp_count):
        pl.semaphore_signal(
            barrier, inc=1, device_id={"tensor": lax.rem(my_tp + j, tp_count)}, device_id_type=MESH
        )
    for bit in bits:
        pl.semaphore_signal(
            barrier, inc=1, device_id={"dp": flip(my_dp, bit)}, device_id_type=MESH
        )
    pl.semaphore_wait(barrier, tp_count - 1 + steps)

    def step(way):
        return pltpu.make_async_remote_copy(
            src_ref=(to_right, to_left)[way],
            dst_ref=from_sides.at[way],
            send_sem=chunk_send.at[way],
            recv_sem=chunk_recv.at[way],
            device_id={"tensor": lax.rem(my_tp + (1, tp_count - 1)[way], tp_count)},
            device_id_type=MESH,
        )

    has_right, has_left = my_tp < tp_count - 1, my_tp > 0

    @pl.when(has_right)
    def _():
        step(0).start()

    @pl.when(has_left)
    def _():
        step(1).start()

    def block(j, s, owner):
        return j, pl.ds(pl.multiple_of(owner * own_rows + s * half, half), half)

    def place(k, m):
        return sum(1 << (steps - 1 - e) for e in range(k)) + m

    def fellow(s, k, m, start):
        owner = start
        for b in range(steps - 1 - k):
            if m >> b & 1:
                owner = flip(owner, orders[s][k + 1 + b])
        return owner

    def exchange_part(j, s, k, m):
        partner = flip(my_dp, orders[s][k])
        at = place(k, m)
        index, span = block(j, s, fellow(s, k, m, partner))
        return pltpu.make_async_remote_copy(
            src_ref=mine.at[index, span, :],
            dst_ref=got.at[j, s, at],
            send_sem=send.at[j, s, at],
            recv_sem=recv.at[j, s, at],
            device_id={"dp": partner},
            device_id_type=MESH,
        )

    def across(j):
        return pltpu.make_async_remote_copy(
            src_ref=mine.at[j, pl.ds(pl.multiple_of(my_dp * own_rows, own_rows), own_rows), :],
            dst_ref=got_across.at[j],
            send_sem=across_send.at[j],
            recv_sem=across_recv.at[j],
            device_id={"tensor": shard_of(j)},
            device_id_type=MESH,
        )

    def every(k):
        return [(s, m) for s in range(2) for m in range(1 << (steps - 1 - k))]

    turned[...] = rows[...].T
    for phase in range(tp_count + steps + 1):
        if phase < tp_count:
            shard = shard_of(phase)
            at = 0
            load(phase).wait()
            if phase + 1 < tp_count:
                load(phase + 1).start()
            for g, part in enumerate(parts):
                cols = part.shape[2]
                value = part[shard]
                mine[phase, :, at : at + cols] = dot_nn(turned[...], value).astype(bf16)
                product = dot_nt(value, held[phase % 2, :, at : at + cols])
                if phase == 0 and g == 0:
                    grad_rows[...] = product
                else:
                    grad_rows[...] += product
                at += cols
        for k in reversed(range(steps + 1)):
            j = phase - k
            if not 0 <= j < tp_count:
                continue
            if k > 0:
                for s, m in every(k - 1):
                    exchange_part(j, s, k - 1, m).wait_recv()
                    index, span = block(j, s, fellow(s, k - 1, m, my_dp))
                    mine[index, span, :] = (
                        mine[index, span, :].astype(f32)
                        + got[j, s, place(k - 1, m)].astype(f32)
                    ).astype(bf16)
            if k < steps:
                for s, m in every(k):
                    exchange_part(j, s, k, m).start()
            elif j < tp_count - 1:
                across(j).start()
    total = mine[
        tp_count - 1, pl.ds(pl.multiple_of(my_dp * own_rows, own_rows), own_rows), :
    ].astype(f32)
    for j in range(tp_count - 1):
        across(j).wait_recv()
        total += got_across[j].astype(f32)
    out[...] = total

    @pl.when(has_right)
    def _():
        step(0).wait_send()
        step(1).wait_recv()

    @pl.when(has_left)
    def _():
        step(1).wait_send()
        step(0).wait_recv()

    for j in range(tp_count):
        if j < tp_count - 1:
            across(j).wait_send()
        for k in range(steps):
            for s, m in every(k):
                exchange_part(j, s, k, m).wait_send()


def total_grads(rows, parts, to_right, to_left, weights, dp_count, collective_id):
    tp_count, width, cols = weights.shape
    count = rows.shape[0]
    own_rows = width // dp_count
    vmem_spec = pl.BlockSpec(memory_space=pltpu.VMEM)
    any_spec = pl.BlockSpec(memory_space=pl.ANY)
    dma = pltpu.SemaphoreType.DMA
    return pl.pallas_call(
        functools.partial(total_kernel, tp_count, dp_count, len(parts)),
        out_shape=[
            jax.ShapeDtypeStruct((own_rows, cols), f32),
            jax.ShapeDtypeStruct((count, width), f32),
            jax.ShapeDtypeStruct((2, count, width), bf16),
        ],
        in_specs=[vmem_spec] * (1 + len(parts)) + [any_spec] * 3,
        out_specs=[vmem_spec, vmem_spec, any_spec],
        scratch_shapes=[
            pltpu.VMEM((width, count), bf16),
            pltpu.VMEM((tp_count, width, cols), bf16),
            pltpu.VMEM((tp_count, 2, dp_count - 1, own_rows // 2, cols), bf16),
            pltpu.VMEM((tp_count - 1, own_rows, cols), bf16),
            pltpu.VMEM((2, width, cols), bf16),
            dma((2,)),
            dma((tp_count, 2, dp_count - 1)),
            dma((tp_count, 2, dp_count - 1)),
            dma((tp_count,)),
            dma((tp_count,)),
            dma((2,)),
            dma((2,)),
        ],
        compiler_params=pltpu.CompilerParams(
            collective_id=collective_id, has_side_effects=True, vmem_limit_bytes=62 * 1024 * 1024
        ),
        cost_estimate=pl.CostEstimate(
            flops=4 * tp_count * count * width * cols,
            bytes_accessed=16 * tp_count * width * cols,
            transcendentals=0,
        ),
        name="total_grads",
    )(rows, *parts, to_right, to_left, weights)


def rms_scale(hidden):
    return lax.rsqrt(jnp.mean(hidden * hidden, axis=1, keepdims=True) + epsilon)


def norm_back(grad_norm, hidden, scale_rows, gain):
    normed = hidden * scale_rows
    gain_part = jnp.sum(grad_norm * normed, axis=0)
    inner = grad_norm * gain
    grad_hidden = scale_rows * (inner - normed * jnp.mean(inner * normed, axis=1, keepdims=True))
    return (grad_hidden, gain_part)


def after(value, other):
    return lax.optimization_barrier((value, other))[0]


def local(
    tokens,
    upstream,
    lengths,
    positions,
    pages,
    attn_gain,
    w_query,
    w_key,
    w_value,
    w_out,
    mlp_gain,
    w_gate,
    w_up,
    w_down,
):
    dp_count = lax.axis_size("dp")
    tp_count = lax.axis_size("tensor")
    dp_index = lax.axis_index("dp")
    tp_index = lax.axis_index("tensor")
    tok_dev, width = tokens.shape
    tok_group = tok_dev * tp_count
    page_rows = tok_dev // dp_count
    group_pages = tp_count * dp_count
    page_count = pages.shape[0]
    device = dp_index * tp_count + tp_index
    everyone = ("tensor", "dp")

    local_ids = jnp.arange(dp_count, dtype=jnp.int32)
    inverse = (
        jnp.zeros((page_count,), jnp.int32).at[pages].set(jnp.arange(page_count, dtype=jnp.int32))
    )
    dealt = lax.dynamic_slice_in_dim(inverse, device * dp_count, dp_count)
    dest_group = dealt // group_pages
    send_order = jnp.zeros((dp_count,), jnp.int32).at[dest_group].set(local_ids)
    group_sources = lax.dynamic_slice_in_dim(pages, dp_index * group_pages, group_pages)
    perm = (
        (jnp.arange(group_pages, dtype=jnp.int32) // dp_count) * dp_count
        + group_sources // group_pages
    ).astype(jnp.int32)

    def reorder(rows, order):
        blocks = rows.reshape(dp_count, page_rows, rows.shape[1])
        return jnp.take(blocks, order, axis=0, mode="clip").reshape(rows.shape)

    hidden_in = reorder(tokens, send_order).astype(f32)
    grad_top = reorder(upstream, send_order).astype(f32)
    seq_lens = lengths[0]
    seq_ends = jnp.cumsum(seq_lens)
    place = (jnp.take(dealt, send_order, mode="clip") % group_pages) * page_rows
    place_rows = (place[:, None] + jnp.arange(page_rows, dtype=jnp.int32)[None, :]).reshape(-1)
    valid_rows = (place_rows < seq_ends[-1]).astype(f32)[:, None]

    row_ids = jnp.arange(tok_group, dtype=jnp.int32)
    begin = jnp.max(
        jnp.where(row_ids[:, None] >= seq_ends[None, :], seq_ends[None, :], 0), axis=1
    ).astype(jnp.int32)
    block_len = min(block_rows, tok_group)
    first_block = begin[::block_len] // min(key_rows, tok_group)
    begin = begin[None, :]
    inverse_freq = theta_base ** (-(jnp.arange(HALF, dtype=f32) * 2.0) / HD)
    angles = inverse_freq[:, None] * positions.astype(f32)
    cos_t, sin_t = jnp.cos(angles), jnp.sin(angles)

    q_cols, kv_cols = w_query.shape[1], w_key.shape[1]
    kv_heads = kv_cols // HD
    per_group = q_cols // kv_cols
    group_q = per_group * HD
    groups = range(kv_heads)
    qkv_shard = jnp.concatenate(
        [
            part
            for g in groups
            for part in (
                w_query[:, g * group_q : (g + 1) * group_q],
                w_key[:, g * HD : (g + 1) * HD],
                w_value[:, g * HD : (g + 1) * HD],
            )
        ],
        axis=1,
    )

    def trade(value):
        blocks = value.reshape(group_pages, page_rows, value.shape[-1])
        return lax.all_to_all(blocks, everyone, split_axis=0, concat_axis=0, tiled=True)

    def trade_back(value):
        return trade(value).reshape(tp_count, tok_dev, value.shape[-1])

    def pass_on(values, first, last):
        return (
            lax.ppermute(values[0], "tensor", [(t, t + 1) for t in range(*first)]),
            lax.ppermute(values[1], "tensor", [(t, t - 1) for t in range(*last)]),
        )

    grad_out = grad_top * valid_rows
    own_chunk = grad_out.astype(bf16)
    mlp_shard = jnp.concatenate([w_gate, w_up, w_down.T], axis=1)
    w_mlp = lax.all_gather(mlp_shard, "dp", axis=0, tiled=True)
    w_qkv, out_shards, gains, *sides = collect(
        qkv_shard, w_out.T, jnp.stack([attn_gain, mlp_gain]), own_chunk, tp_count, dp_count, 1
    )
    w_out_t = lax.all_gather(out_shards, "dp", axis=1, tiled=True)
    chunks = [(sides[0], sides[1])]
    gains = gains.transpose(1, 0, 2).reshape(2, -1).astype(f32)
    gain_one, gain_two = gains[0], gains[1]

    scale_one = rms_scale(hidden_in)
    normed_one = (hidden_in * scale_one * gain_one).astype(bf16)
    slots = project(normed_one, w_qkv, dp_count, 3)
    for n in range(2, tp_count):
        passed = after(chunks[-1], slots) if n == 2 else chunks[-1]
        chunks.append(pass_on(passed, (n - 1, tp_count - 1), (1, tp_count - n + 1)))
    saved, mixed = [], []
    for g in groups:
        q_t, k_t, k_rows, v_t, v_rows = prepare(
            after(slots, (o_slots, w_mlp, chunks[1])) if g else slots, g, perm, cos_t, sin_t, per_group, 1
        )
        o_t, lse, o_slots = attend_forward(
            q_t, k_rows, v_t, begin, first_block, perm, page_rows, block_len
        )
        saved.append((q_t, k_rows, k_t, v_rows, o_t, lse))
        mixed.append(trade_back(after(o_slots, chunks[1]) if g else o_slots))
    hidden_mid = hidden_in
    mixed[0] = after(mixed[0], chunks[-1])
    for g in groups:
        hidden_mid = gather_sum(mixed[g], w_out_t, g, hidden_mid)

    scale_two = rms_scale(hidden_mid)
    normed_two = (hidden_mid * scale_two * gain_two).astype(bf16)
    grads_t, rows_t, inner_act, grad_gate_up, *partial_two, grad_normed_two = feed(
        normed_two, [own_chunk] + [c[0] for c in chunks] + [c[1] for c in chunks], w_mlp, tp_count
    )
    grad_normed_two = grad_normed_two.astype(f32)
    grad_mid_norm, gain_two_part = norm_back(grad_normed_two, hidden_mid, scale_two, gain_two)
    grad_mid = grad_out + grad_mid_norm

    def add_on(arrived, s):
        return tuple(
            (value.astype(f32) + partial_two[at].astype(f32)).astype(bf16)
            for value, at in zip(arrived, (s, tp_count - s))
        )

    def reduce_dp(grad):
        return lax.psum_scatter(grad.astype(bf16), "dp", scatter_dimension=0, tiled=True)

    def reduce_tensor(value):
        cols = value.shape[1] // tp_count
        total = lax.dynamic_slice_in_dim(value, tp_index * cols, cols, 1).astype(f32)
        for s in range(1, tp_count):
            target = lax.rem(tp_index + s, tp_count)
            block = lax.dynamic_slice_in_dim(value, target * cols, cols, 1)
            pairs = [(t, (t + s) % tp_count) for t in range(tp_count)]
            total = total + lax.ppermute(block, "tensor", pairs).astype(f32)
        return total

    grad_z = grad_mid.astype(bf16)
    grad_wout = outer(grad_z, mixed)
    sum_out = reduce_dp(grad_wout)
    grad_slots, grad_wmlp = weigh(
        spread(after(grad_z, grad_wout), w_out_t, 0, q_cols),
        rows_t, grads_t, grad_gate_up, inner_act, tp_count, dp_count, 2,
    )
    sum_mlp = reduce_dp(grad_wmlp)
    first_part = after((partial_two[1], partial_two[tp_count - 1]), grad_slots)
    passing = pass_on(first_part, (0, 1), (tp_count - 1, tp_count))
    grad_qkv = []
    for g in groups:
        q_t, k_rows, k_t, v_rows, o_t, lse = saved[g]
        back = attend_backward(
            after(grad_slots, (back, sum_out) if g else first_part), g, q_t, k_rows, k_t, v_rows,
            o_t, lse, begin, cos_t, sin_t, first_block, perm, page_rows, block_len,
        )
        if g == len(groups) - 1:
            steps = 2
            if tp_count > 3:
                passing = pass_on(add_on(passing, 2), (0, 2), (tp_count - 2, tp_count))
                steps = 3
            back = after(back, (grad_qkv, passing))
        grad_qkv.append(trade_back(back))
    hidden = sum_mlp.shape[1] // 3
    for s in range(steps, tp_count - 1):
        passing = pass_on(add_on(passing, s), (0, s), (tp_count - s, tp_count))
    passing = add_on(passing, tp_count - 1)
    sum_qkv, grad_normed_one, sides = total_grads(
        normed_one, grad_qkv, passing[0], passing[1], w_qkv, dp_count, 4
    )
    branch_two = jnp.where(tp_index > 0, sides[0].astype(f32), 0.0)
    branch_two += jnp.where(tp_index < tp_count - 1, sides[1].astype(f32), 0.0)
    each = group_q + 2 * HD
    sum_qkv = [sum_qkv[:, g * each : (g + 1) * each] for g in groups]
    sum_out = reduce_tensor(after(sum_out, grad_normed_one))
    result = (
        (after(hidden_mid, back) + branch_two + partial_two[0].astype(f32)) * valid_rows
    ).astype(bf16)
    grad_in_norm, gain_one_part = norm_back(grad_normed_one, hidden_in, scale_one, gain_one)
    grad_in = (grad_mid + grad_in_norm).astype(bf16)

    gain_parts = jnp.stack([gain_one_part, gain_two_part]).reshape(2, dp_count, -1)
    gain_parts = jnp.broadcast_to(
        gain_parts.transpose(1, 0, 2)[None], (tp_count, dp_count, 2, gain_parts.shape[2])
    ).reshape(group_pages, 2, -1)
    gain_sums = jnp.sum(
        lax.all_to_all(gain_parts, everyone, split_axis=0, concat_axis=0, tiled=True), axis=0
    )
    return (
        reorder(result, dest_group),
        reorder(grad_in, dest_group),
        gain_sums[0],
        jnp.concatenate([part[:, :group_q] for part in sum_qkv], axis=1),
        jnp.concatenate([part[:, group_q : group_q + HD] for part in sum_qkv], axis=1),
        jnp.concatenate([part[:, group_q + HD :] for part in sum_qkv], axis=1),
        sum_out.T,
        gain_sums[1],
        sum_mlp[:, :hidden].astype(f32),
        sum_mlp[:, hidden : 2 * hidden].astype(f32),
        sum_mlp[:, 2 * hidden :].astype(f32).T,
    )


def solution(mesh):
    rows = P(("dp", "tensor"), None)
    weight = P("dp", "tensor")
    weight_t = P("tensor", "dp")
    return jax.shard_map(
        local,
        mesh=mesh,
        in_specs=(
            rows,
            rows,
            P("dp", None),
            P("dp", None),
            P(),
            P("dp"),
            weight,
            weight,
            weight,
            weight_t,
            P("dp"),
            weight,
            weight,
            weight_t,
        ),
        out_specs=(
            rows,
            rows,
            P("dp"),
            weight,
            weight,
            weight,
            weight_t,
            P("dp"),
            weight,
            weight,
            weight_t,
        ),
        check_vma=False,
    )
```

```python
import functools

import jax
import jax.numpy as jnp
from jax import lax
from jax.experimental import pallas as pl
from jax.experimental.pallas import tpu as pltpu
from jax.sharding import PartitionSpec as P

HD = 64
HALF = HD // 2

epsilon = 1e-05
theta_base = 500000.0
masked_score = -1e30
score_scale = HD**-0.5
block_rows = 512
key_rows = 256
MESH = pl.DeviceIdType.MESH
f32 = jnp.float32
bf16 = jnp.bfloat16


def dot_nn(left, right):
    return lax.dot_general(left, right, (((1,), (0,)), ((), ())), preferred_element_type=f32)


def dot_nt(left, right):
    return lax.dot_general(left, right, (((1,), (1,)), ((), ())), preferred_element_type=f32)


def dot_tn(left, right):
    return lax.dot_general(left, right, (((0,), (0,)), ((), ())), preferred_element_type=f32)


def prep_kernel(pages_per, q_heads, kv_heads, perm, *refs):
    page_refs = refs[:pages_per]
    cos_ref, sin_ref, q_t, k_t, k_rows, v_t, v_rows = refs[pages_per:]
    rows = jnp.concatenate([r[0].astype(f32) for r in page_refs], axis=0)
    turned = rows.T
    cos, sin = cos_ref[...], sin_ref[...]

    def rope(base):
        first, second = turned[base : base + HALF], turned[base + HALF : base + HD]
        return jnp.concatenate([first * cos - second * sin, second * cos + first * sin], axis=0)

    for h in range(q_heads):
        roped = rope(h * HD).astype(bf16)
        q_t[h * HD : (h + 1) * HD, :] = (roped.astype(f32) * score_scale).astype(bf16)
    k_base = q_heads * HD
    v_base = k_base + kv_heads * HD
    for g in range(kv_heads):
        roped = rope(k_base + g * HD)
        k_t[g * HD : (g + 1) * HD, :] = roped.astype(bf16)
        k_rows[g] = roped.T.astype(bf16)
        v_t[g * HD : (g + 1) * HD, :] = turned[v_base + g * HD : v_base + (g + 1) * HD].astype(bf16)
        v_rows[g] = rows[:, v_base + g * HD : v_base + (g + 1) * HD].astype(bf16)


def prepare(slots, part, perm, cos_t, sin_t, q_heads, kv_heads):
    page_rows = slots.shape[1]
    cols = (q_heads + 2 * kv_heads) * HD
    total_rows = slots.shape[0] * page_rows
    lanes = min(256, total_rows)
    pages_per = lanes // page_rows

    def page_spec(a):
        return pl.BlockSpec(
            (1, page_rows, cols), lambda i, perm_ref, a=a: (perm_ref[i * pages_per + a], 0, part)
        )

    table = pl.BlockSpec((HALF, lanes), lambda i, perm_ref: (0, i))
    return pl.pallas_call(
        functools.partial(prep_kernel, pages_per, q_heads, kv_heads),
        grid_spec=pltpu.PrefetchScalarGridSpec(
            num_scalar_prefetch=1,
            grid=(total_rows // lanes,),
            in_specs=[page_spec(a) for a in range(pages_per)] + [table, table],
            out_specs=[
                pl.BlockSpec((q_heads * HD, lanes), lambda i, perm_ref: (0, i)),
                pl.BlockSpec((kv_heads * HD, lanes), lambda i, perm_ref: (0, i)),
                pl.BlockSpec((kv_heads, lanes, HD), lambda i, perm_ref: (0, i, 0)),
                pl.BlockSpec((kv_heads * HD, lanes), lambda i, perm_ref: (0, i)),
                pl.BlockSpec((kv_heads, lanes, HD), lambda i, perm_ref: (0, i, 0)),
            ],
        ),
        out_shape=[
            jax.ShapeDtypeStruct((q_heads * HD, total_rows), bf16),
            jax.ShapeDtypeStruct((kv_heads * HD, total_rows), bf16),
            jax.ShapeDtypeStruct((kv_heads, total_rows, HD), bf16),
            jax.ShapeDtypeStruct((kv_heads * HD, total_rows), bf16),
            jax.ShapeDtypeStruct((kv_heads, total_rows, HD), bf16),
        ],
        cost_estimate=pl.CostEstimate(
            flops=8 * slots.size, bytes_accessed=6 * slots.size, transcendentals=0
        ),
        name="prepare",
    )(perm, *([slots] * pages_per), cos_t, sin_t)


def block_bias(i, j, begin_row, block_len, key_len):
    keys = j * key_len + lax.broadcasted_iota(jnp.int32, (key_len, block_len), 0)
    queries = i * block_len + lax.broadcasted_iota(jnp.int32, (key_len, block_len), 1)
    allowed = (keys >= begin_row) & (keys <= queries)
    return jnp.where(allowed, 0.0, masked_score)


def forward_kernel(
    q_heads, kv_heads, page_rows, first_block, perm,
    q_t, k_rows, v_t, begin, o_t, lse, o_slots, acc, stage, sems,
):
    i = pl.program_id(0)
    block_len = q_t.shape[1]
    key_len = min(key_rows, k_rows.shape[1])
    per_group = q_heads // kv_heads
    acc[...] = jnp.zeros_like(acc)
    begin_row = begin[...]

    def visit(j, carry):
        bias = block_bias(i, j, begin_row, block_len, key_len)
        at = pl.ds(pl.multiple_of(j * key_len, key_len), key_len)
        scores = [
            dot_nn(k_rows[h // per_group, at, :], q_t[h * HD : (h + 1) * HD, :]) + bias
            for h in range(q_heads)
        ]
        tops = [
            jnp.maximum(carry[h][0], jnp.max(scores[h], axis=0, keepdims=True))
            for h in range(q_heads)
        ]
        weights = [jnp.exp(scores[h] - tops[h]) for h in range(q_heads)]
        fades = [jnp.exp(carry[h][0] - tops[h]) for h in range(q_heads)]
        totals = [
            carry[h][1] * fades[h] + jnp.sum(weights[h], axis=0, keepdims=True)
            for h in range(q_heads)
        ]
        for h in range(q_heads):
            g = h // per_group
            span = slice(h * HD, (h + 1) * HD)
            acc[span, :] = acc[span, :] * fades[h] + dot_nn(
                v_t[g * HD : (g + 1) * HD, at], weights[h].astype(bf16)
            )
        return tuple(zip(tops, totals))

    start = tuple(
        (jnp.full((1, block_len), masked_score, f32), jnp.zeros((1, block_len), f32))
        for _ in range(q_heads)
    )
    stats = lax.fori_loop(
        first_block[i], lax.div((i + 1) * block_len - 1, key_len) + 1, visit, start
    )
    for h in range(q_heads):
        lse[h : h + 1, :] = stats[h][0] + jnp.log(stats[h][1])
    mixed = jnp.concatenate(
        [acc[h * HD : (h + 1) * HD, :] / stats[h][1] for h in range(q_heads)], axis=0
    )
    o_t[...] = mixed.astype(bf16)
    pages = block_len // page_rows
    stage[...] = mixed.T.astype(bf16).reshape(pages, page_rows, q_heads * HD)
    copies = [
        pltpu.make_async_copy(stage.at[a], o_slots.at[perm[i * pages + a]], sems.at[a])
        for a in range(pages)
    ]
    for copy in copies:
        copy.start()
    for copy in copies:
        copy.wait()


def attend_forward(q_t, k_rows, v_t, begin, first_block, perm, page_rows, block_len):
    total_rows = q_t.shape[1]
    kv_heads = k_rows.shape[0]
    q_heads = q_t.shape[0] // HD
    pages = block_len // page_rows
    return pl.pallas_call(
        functools.partial(forward_kernel, q_heads, kv_heads, page_rows),
        grid_spec=pltpu.PrefetchScalarGridSpec(
            num_scalar_prefetch=2,
            grid=(total_rows // block_len,),
            in_specs=[
                pl.BlockSpec((q_heads * HD, block_len), lambda i, *_: (0, i)),
                pl.BlockSpec((kv_heads, total_rows, HD), lambda i, *_: (0, 0, 0)),
                pl.BlockSpec((kv_heads * HD, total_rows), lambda i, *_: (0, 0)),
                pl.BlockSpec((1, block_len), lambda i, *_: (0, i)),
            ],
            out_specs=[
                pl.BlockSpec((q_heads * HD, block_len), lambda i, *_: (0, i)),
                pl.BlockSpec((q_heads, block_len), lambda i, *_: (0, i)),
                pl.BlockSpec(memory_space=pl.ANY),
            ],
            scratch_shapes=[
                pltpu.VMEM((q_heads * HD, block_len), f32),
                pltpu.VMEM((pages, page_rows, q_heads * HD), bf16),
                pltpu.SemaphoreType.DMA((pages,)),
            ],
        ),
        out_shape=[
            jax.ShapeDtypeStruct((q_heads * HD, total_rows), bf16),
            jax.ShapeDtypeStruct((q_heads, total_rows), f32),
            jax.ShapeDtypeStruct((total_rows // page_rows, page_rows, q_heads * HD), bf16),
        ],
        cost_estimate=pl.CostEstimate(
            flops=q_heads * total_rows * total_rows * HD,
            bytes_accessed=8 * q_t.size,
            transcendentals=q_heads * total_rows * total_rows // 4,
        ),
        name="attend_forward",
    )(first_block, perm, q_t, k_rows, v_t, begin)


def backward_kernel(
    q_heads, kv_heads, page_rows, pages, first_block, perm, *refs
):
    grad_pages = refs[:pages]
    (
        q_t, k_rows, k_t, v_rows, o_t, lse, begin, cos_ref, sin_ref, cos_all, sin_all,
        out, grad_q, grad_k, grad_v, stage, kv_stage, sems, kv_sems,
    ) = refs[pages:]
    i = pl.program_id(0)
    steps = pl.num_programs(0)
    block_len = q_t.shape[1]
    key_len = min(key_rows, k_rows.shape[1])
    per_group = q_heads // kv_heads
    q_cols = q_heads * HD
    kv_cols = kv_heads * HD

    @pl.when(i == 0)
    def _():
        grad_k[...] = jnp.zeros_like(grad_k)
        grad_v[...] = jnp.zeros_like(grad_v)

    grad_rows = jnp.concatenate([r[0].astype(f32) for r in grad_pages], axis=0)
    grad_t = grad_rows.T
    grad_low = grad_t.astype(bf16)
    inner = [
        jnp.sum(
            grad_t[h * HD : (h + 1) * HD] * o_t[h * HD : (h + 1) * HD, :].astype(f32),
            axis=0,
            keepdims=True,
        )
        for h in range(q_heads)
    ]
    grad_q[...] = jnp.zeros_like(grad_q)
    begin_row = begin[...]

    def visit(j, carry):
        bias = block_bias(i, j, begin_row, block_len, key_len)
        at = pl.ds(pl.multiple_of(j * key_len, key_len), key_len)
        for g in range(kv_heads):
            kv_span = slice(g * HD, (g + 1) * HD)
            keys, vals, keys_t = k_rows[g, at, :], v_rows[g, at, :], k_t[kv_span, at]
            heads = range(g * per_group, (g + 1) * per_group)
            spans = [slice(h * HD, (h + 1) * HD) for h in heads]
            scores = [dot_nn(keys, q_t[span, :]) + bias for span in spans]
            grad_probs = [dot_nn(vals, grad_low[span]) for span in spans]
            probs = [jnp.exp(s - lse[h : h + 1, :]) for s, h in zip(scores, heads)]
            grad_scores = [
                (p * (d - inner[h])).astype(bf16) for p, d, h in zip(probs, grad_probs, heads)
            ]
            low_probs = [p.astype(bf16) for p in probs]
            grad_v[kv_span, at] += sum(
                dot_nt(grad_low[span], p) for span, p in zip(spans, low_probs)
            )
            grad_k[kv_span, at] += sum(
                dot_nt(q_t[span, :], d) for span, d in zip(spans, grad_scores)
            )
            for span, d in zip(spans, grad_scores):
                grad_q[span, :] += dot_nn(keys_t, d)
        return carry

    lax.fori_loop(first_block[i], lax.div((i + 1) * block_len - 1, key_len) + 1, visit, 0)

    def unrope(value, cos, sin):
        first, second = value[:HALF], value[HALF:]
        return jnp.concatenate([first * cos + second * sin, second * cos - first * sin], axis=0)

    cos, sin = cos_ref[...], sin_ref[...]
    parts = [
        unrope(grad_q[h * HD : (h + 1) * HD, :] * score_scale, cos, sin) for h in range(q_heads)
    ]
    stage[...] = jnp.concatenate(parts, axis=0).T.astype(bf16).reshape(pages, page_rows, q_cols)
    copies = [
        pltpu.make_async_copy(
            stage.at[a], out.at[perm[i * pages + a], :, pl.ds(0, q_cols)], sems.at[a]
        )
        for a in range(pages)
    ]
    for copy in copies:
        copy.start()
    for copy in copies:
        copy.wait()

    @pl.when(i == steps - 1)
    def _():
        all_pages = kv_stage.shape[0]
        cos, sin = cos_all[...], sin_all[...]
        parts = [unrope(grad_k[g * HD : (g + 1) * HD, :], cos, sin) for g in range(kv_heads)]
        both = jnp.concatenate(parts + [grad_v[...]], axis=0)
        kv_stage[...] = both.T.astype(bf16).reshape(all_pages, page_rows, 2 * kv_cols)
        copies = [
            pltpu.make_async_copy(
                kv_stage.at[a], out.at[perm[a], :, pl.ds(q_cols, 2 * kv_cols)], kv_sems.at[a]
            )
            for a in range(all_pages)
        ]
        for copy in copies:
            copy.start()
        for copy in copies:
            copy.wait()


def attend_backward(
    grad_slots, part, q_t, k_rows, k_t, v_rows, o_t, lse, begin, cos_t, sin_t, first_block, perm,
    page_rows, block_len,
):
    total_rows = q_t.shape[1]
    kv_heads = k_rows.shape[0]
    q_heads = q_t.shape[0] // HD
    pages = block_len // page_rows
    all_pages = total_rows // page_rows
    q_cols = q_heads * HD
    kv_cols = kv_heads * HD

    def page_spec(a):
        return pl.BlockSpec(
            (1, page_rows, q_cols),
            lambda i, first_ref, perm_ref, a=a: (perm_ref[i * pages + a], 0, part),
        )

    def whole(shape):
        return pl.BlockSpec(shape, lambda i, *_: (0,) * len(shape))

    def column(rows):
        return pl.BlockSpec((rows, block_len), lambda i, *_: (0, i))

    return pl.pallas_call(
        functools.partial(backward_kernel, q_heads, kv_heads, page_rows, pages),
        grid_spec=pltpu.PrefetchScalarGridSpec(
            num_scalar_prefetch=2,
            grid=(total_rows // block_len,),
            in_specs=[page_spec(a) for a in range(pages)]
            + [
                column(q_cols),
                whole((kv_heads, total_rows, HD)),
                whole((kv_cols, total_rows)),
                whole((kv_heads, total_rows, HD)),
                column(q_cols),
                column(q_heads),
                column(1),
                column(HALF),
                column(HALF),
                whole((HALF, total_rows)),
                whole((HALF, total_rows)),
            ],
            out_specs=pl.BlockSpec(memory_space=pl.ANY),
            scratch_shapes=[
                pltpu.VMEM((q_cols, block_len), f32),
                pltpu.VMEM((kv_cols, total_rows), f32),
                pltpu.VMEM((kv_cols, total_rows), f32),
                pltpu.VMEM((pages, page_rows, q_cols), bf16),
                pltpu.VMEM((all_pages, page_rows, 2 * kv_cols), bf16),
                pltpu.SemaphoreType.DMA((pages,)),
                pltpu.SemaphoreType.DMA((all_pages,)),
            ],
        ),
        out_shape=jax.ShapeDtypeStruct((all_pages, page_rows, q_cols + 2 * kv_cols), bf16),
        cost_estimate=pl.CostEstimate(
            flops=3 * q_heads * total_rows * total_rows * HD,
            bytes_accessed=12 * q_t.size,
            transcendentals=q_heads * total_rows * total_rows // 4,
        ),
        name="attend_backward",
    )(
        first_block, perm, *([grad_slots] * pages), q_t, k_rows, k_t, v_rows, o_t, lse, begin,
        cos_t, sin_t, cos_t, sin_t,
    )


def project_kernel(
    tp_count, dp_count, rows, weights, slots, held, stage, load_sem, own_sem, send, recv
):
    count = dp_count * tp_count
    my_dp = lax.axis_index("dp")
    my_tp = lax.axis_index("tensor")
    me = my_dp * tp_count + my_tp
    page_rows = slots.shape[1]

    def load(j):
        shard = lax.rem(my_tp + 1 + j, tp_count)
        return pltpu.make_async_copy(weights.at[shard], held.at[j % 2], load_sem.at[j % 2])

    load(0).start()
    barrier = pltpu.get_barrier_semaphore()

    def greet(j, carry):
        peer = lax.rem(me + j, count)
        pl.semaphore_signal(
            barrier,
            inc=1,
            device_id={"dp": lax.div(peer, tp_count), "tensor": lax.rem(peer, tp_count)},
            device_id_type=MESH,
        )
        return carry

    lax.fori_loop(1, count, greet, 0)
    pl.semaphore_wait(barrier, count - 1)
    home = slots.at[my_tp * dp_count + my_dp]

    def copy_to(j, off):
        p_dp = lax.rem(my_dp + off, dp_count)
        return pltpu.make_async_remote_copy(
            src_ref=stage.at[j, pl.ds(p_dp * page_rows, page_rows), :],
            dst_ref=home,
            send_sem=send.at[j, off],
            recv_sem=recv.at[j, off],
            device_id={"dp": p_dp, "tensor": lax.rem(my_tp + 1 + j, tp_count)},
            device_id_type=MESH,
        )

    def each(j, act):
        def one(off, carry):
            act(copy_to(j, off))
            return carry

        lax.fori_loop(1 if j == tp_count - 1 else 0, dp_count, one, 0)

    for j in range(tp_count):
        load(j).wait()
        if j + 1 < tp_count:
            load(j + 1).start()
        stage[j] = dot_nn(rows[...], held[j % 2]).astype(bf16)
        if j > 0:
            each(j - 1, lambda copy: copy.start())
    each(tp_count - 1, lambda copy: copy.start())
    own = pltpu.make_async_copy(
        stage.at[tp_count - 1, pl.ds(my_dp * page_rows, page_rows), :], home, own_sem
    )
    own.start()
    own.wait()
    for j in range(tp_count):
        each(j, lambda copy: copy.wait())


def project(rows, weights, dp_count, collective_id):
    tp_count, width, cols = weights.shape
    total = rows.shape[0]
    page_rows = total // dp_count
    any_spec = pl.BlockSpec(memory_space=pl.ANY)
    dma = pltpu.SemaphoreType.DMA
    return pl.pallas_call(
        functools.partial(project_kernel, tp_count, dp_count),
        out_shape=jax.ShapeDtypeStruct((tp_count * dp_count, page_rows, cols), bf16),
        in_specs=[
            pl.BlockSpec(memory_space=pltpu.VMEM),
            pl.BlockSpec(memory_space=pltpu.HBM),
        ],
        out_specs=any_spec,
        scratch_shapes=[
            pltpu.VMEM((2, width, cols), bf16),
            pltpu.VMEM((tp_count, total, cols), bf16),
            dma((2,)),
            dma,
            dma((tp_count, dp_count)),
            dma((tp_count, dp_count)),
        ],
        compiler_params=pltpu.CompilerParams(
            collective_id=collective_id, has_side_effects=True, vmem_limit_bytes=62 * 1024 * 1024
        ),
        cost_estimate=pl.CostEstimate(
            flops=2 * tp_count * total * width * cols,
            bytes_accessed=16 * tp_count * width * cols,
            transcendentals=0,
        ),
        name="project",
    )(rows, weights)


def feed_kernel(
    ring, tile, own_rows, *refs
):
    grad_rows = refs[: 2 * ring - 1]
    weights, grads_t, rows_t, act_all, grads_all = refs[2 * ring - 1 : 2 * ring + 4]
    mixed_all = refs[2 * ring + 4 : 3 * ring + 4]
    (
        grad_own, held, grads_held, acc_n, acc_m, first_part, arrived, outgoing, mixed_stage,
        final_stage, turned, load_sem, keep_sem, grad_sem, mixed_sem, final_sem,
        row_send, row_recv, sum_send, sum_recv, all_sem,
    ) = refs[3 * ring + 4 :]
    me = lax.axis_index("tensor")
    right = lax.rem(me + 1, ring)
    left = lax.rem(me + ring - 1, ring)
    hidden = weights.shape[1] // 3
    tiles = hidden // tile

    barrier = pltpu.get_barrier_semaphore()
    for neighbour in (left, right):
        pl.semaphore_signal(barrier, inc=1, device_id={"tensor": neighbour}, device_id_type=MESH)
    pl.semaphore_wait(barrier, 2)

    load = pltpu.make_async_copy(own_rows, held.at[0], load_sem)
    load.start()

    def grad_load(s):
        def copy_of(source):
            return pltpu.make_async_copy(
                grad_rows[source], grads_held.at[s % 2], grad_sem.at[s % 2]
            )

        if s == 0:
            copy_of(0).start()
            return

        @pl.when(me >= s)
        def _():
            copy_of(s).start()

        @pl.when(me < s)
        def _():
            copy_of(ring - 1 + ring - s).start()

    def grad_wait(s):
        pltpu.make_async_copy(grad_rows[0], grads_held.at[s % 2], grad_sem.at[s % 2]).wait()

    def part_of(array, s):
        count = own_rows.shape[0]
        return array.at[:, pl.ds(pl.multiple_of(s * count, 128), count)]

    def grad_keep(s):
        return pltpu.make_async_copy(turned.at[1], part_of(grads_t, s), all_sem)

    grad_load(0)
    load.wait()

    def pass_rows(s):
        return pltpu.make_async_remote_copy(
            src_ref=held.at[s],
            dst_ref=held.at[s + 1],
            send_sem=row_send.at[s],
            recv_sem=row_recv.at[s],
            device_id={"tensor": right},
            device_id_type=MESH,
        )

    def pass_sum(s):
        return pltpu.make_async_remote_copy(
            src_ref=outgoing.at[s - 1],
            dst_ref=arrived.at[s - 1],
            send_sem=sum_send.at[s - 1],
            recv_sem=sum_recv.at[s - 1],
            device_id={"tensor": right},
            device_id_type=MESH,
        )

    def keep(s):
        return pltpu.make_async_copy(turned.at[0], part_of(rows_t, s), keep_sem)

    def mixed_store(s):
        return pltpu.make_async_copy(mixed_stage, mixed_all[s], mixed_sem)

    def chunk(s, carry):
        @pl.when(s > 0)
        def _():
            pass_rows(s - 1).wait_recv()

        @pl.when(s < ring - 1)
        def _():
            pass_rows(s).start()

        @pl.when(s > 0)
        def _():
            keep(s - 1).wait()
            grad_keep(s - 1).wait()

        turned[0] = held[s].T
        keep(s).start()
        for k in range(ring):

            @pl.when(s == k)
            def _(k=k):
                grad_wait(k)
                if k < ring - 1:
                    grad_load(k + 1)

        slot = lax.rem(s, 2)
        turned[1] = grads_held[slot].T
        grad_keep(s).start()
        acc_n[...] = jnp.zeros_like(acc_n)
        acc_m[...] = jnp.zeros_like(acc_m)

        def body(w_gate, w_up, w_down, act, grad_gate, grad_up):
            rows = held[s]
            gate = dot_nn(rows, w_gate[...])
            up = dot_nn(rows, w_up[...])
            grad_act = dot_nn(grads_held[slot], w_down[...])
            sig = 1.0 / (1.0 + jnp.exp(-gate))
            silu = gate * sig
            low_act = (silu * up).astype(bf16)
            low_up = (grad_act * silu).astype(bf16)
            low_gate = (grad_act * up * sig * (1.0 + gate * (1.0 - sig))).astype(bf16)
            act[...] = low_act
            grad_gate[...] = low_gate
            grad_up[...] = low_up
            acc_m[...] += dot_nt(low_act, w_down[...])
            acc_n[...] += dot_nt(low_gate, w_gate[...]) + dot_nt(low_up, w_up[...])

        width, count = own_rows.shape[1], own_rows.shape[0]
        pltpu.emit_pipeline(
            body,
            grid=(tiles,),
            in_specs=[
                pl.BlockSpec((width, tile), lambda k: (0, k)),
                pl.BlockSpec((width, tile), lambda k: (0, k + tiles)),
                pl.BlockSpec((width, tile), lambda k: (0, k + 2 * tiles)),
            ],
            out_specs=[
                pl.BlockSpec((count, tile), lambda k: (0, k)),
                pl.BlockSpec((count, tile), lambda k: (0, k)),
                pl.BlockSpec((count, tile), lambda k: (0, k + tiles)),
            ],
        )(weights, weights, weights, act_all.at[s], grads_all.at[s], grads_all.at[s])

        @pl.when(s > 0)
        def _():
            mixed_store(0).wait()

        mixed_stage[...] = acc_m[...].astype(bf16)
        for k in range(ring):

            @pl.when(s == k)
            def _(k=k):
                mixed_store(k).start()

        @pl.when(s == 0)
        def _():
            first_part[...] = acc_n[...]

        @pl.when(s == 1)
        def _():
            outgoing[0] = acc_n[...].astype(bf16)

        @pl.when(s > 1)
        def _():
            pass_sum(s - 1).wait_recv()
            outgoing[s - 1] = (acc_n[...] + arrived[s - 2].astype(f32)).astype(bf16)

        @pl.when(s > 0)
        def _():
            pass_sum(s).start()

        return carry

    lax.fori_loop(0, ring, chunk, 0)
    mixed_store(0).wait()
    pass_sum(ring - 1).wait_recv()
    final_stage[...] = (first_part[...] + arrived[ring - 2].astype(f32)).astype(bf16)
    final = pltpu.make_async_copy(final_stage, grad_own, final_sem)
    final.start()

    def settle(s, carry):
        @pl.when(s < ring - 1)
        def _():
            pass_rows(s).wait_send()

        @pl.when(s > 0)
        def _():
            pass_sum(s).wait_send()

        return carry

    lax.fori_loop(0, ring, settle, 0)
    keep(ring - 1).wait()
    grad_keep(ring - 1).wait()
    final.wait()


def feed(own_rows, grad_rows, weights, ring, tile=256, collective_id=7):
    count, width = own_rows.shape
    hidden = weights.shape[1] // 3
    any_spec = pl.BlockSpec(memory_space=pl.ANY)
    dma = pltpu.SemaphoreType.DMA
    return pl.pallas_call(
        functools.partial(feed_kernel, ring, min(tile, hidden)),
        out_shape=[
            jax.ShapeDtypeStruct((width, ring * count), bf16),
            jax.ShapeDtypeStruct((width, ring * count), bf16),
            jax.ShapeDtypeStruct((ring, count, hidden), bf16),
            jax.ShapeDtypeStruct((ring, count, 2 * hidden), bf16),
        ]
        + [jax.ShapeDtypeStruct((count, width), bf16)] * (ring + 1),
        in_specs=[any_spec] * (1 + 2 * ring),
        out_specs=[any_spec] * (5 + ring),
        scratch_shapes=[
            pltpu.VMEM((ring, count, width), bf16),
            pltpu.VMEM((2, count, width), bf16),
            pltpu.VMEM((count, width), f32),
            pltpu.VMEM((count, width), f32),
            pltpu.VMEM((count, width), f32),
            pltpu.VMEM((ring - 1, count, width), bf16),
            pltpu.VMEM((ring - 1, count, width), bf16),
            pltpu.VMEM((count, width), bf16),
            pltpu.VMEM((count, width), bf16),
            pltpu.VMEM((2, width, count), bf16),
            dma,
            dma,
            dma((2,)),
            dma,
            dma,
            dma((ring - 1,)),
            dma((ring - 1,)),
            dma((ring - 1,)),
            dma((ring - 1,)),
            dma,
        ],
        compiler_params=pltpu.CompilerParams(
            collective_id=collective_id, has_side_effects=True, vmem_limit_bytes=64 * 1024 * 1024 - 65536,
        ),
        cost_estimate=pl.CostEstimate(
            flops=12 * ring * count * width * hidden,
            bytes_accessed=8 * ring * count * width,
            transcendentals=ring * count * hidden,
        ),
        name="feed_forward",
    )(own_rows, *grad_rows, weights)


def weigh_kernel(
    tp_count, dp_count, tile, grads, rows_t, grads_t, gate_up, act, slots, out,
    left, left_sem, own_sem, send, recv,
):
    count = dp_count * tp_count
    my_dp = lax.axis_index("dp")
    my_tp = lax.axis_index("tensor")
    me = my_dp * tp_count + my_tp
    page_rows = slots.shape[1]

    loads = [
        pltpu.make_async_copy(source, left.at[k], left_sem.at[k])
        for k, source in enumerate((rows_t, grads_t))
    ]
    for load in loads:
        load.start()

    barrier = pltpu.get_barrier_semaphore()

    def place(peer):
        return {"dp": lax.div(peer, tp_count), "tensor": lax.rem(peer, tp_count)}

    def greet(j, carry):
        peer = lax.rem(me + j, count)
        pl.semaphore_signal(barrier, inc=1, device_id=place(peer), device_id_type=MESH)
        return carry

    lax.fori_loop(1, count, greet, 0)
    pl.semaphore_wait(barrier, count - 1)

    home = slots.at[my_tp * dp_count + my_dp]

    def block(p_dp, p_tp):
        return grads.at[p_tp, pl.ds(p_dp * page_rows, page_rows), :]

    own = pltpu.make_async_copy(block(my_dp, my_tp), home, own_sem)
    own.start()

    def copy_to(j):
        peer = lax.rem(me + j, count)
        return pltpu.make_async_remote_copy(
            src_ref=block(lax.div(peer, tp_count), lax.rem(peer, tp_count)),
            dst_ref=home,
            send_sem=send.at[j],
            recv_sem=recv.at[j],
            device_id=place(peer),
            device_id_type=MESH,
        )

    def start(j, carry):
        copy_to(j).start()
        return carry

    def finish(j, carry):
        copy_to(j).wait()
        return carry

    lax.fori_loop(1, count, start, 0)

    width = rows_t.shape[0]
    step = min(512, width)

    def multiply(k, right, first):
        ring, rows, cols = right.shape

        def body(part, result):
            values = part[...].reshape(ring * rows, tile)
            for m in range(0, width, step):
                result[m : m + step, :] = dot_nn(left[k, m : m + step, :], values).astype(bf16)

        pltpu.emit_pipeline(
            body,
            grid=(cols // tile,),
            in_specs=[pl.BlockSpec((ring, rows, tile), lambda n: (0, 0, n))],
            out_specs=[pl.BlockSpec((width, tile), lambda n: (0, n + first))],
        )(right, out)

    loads[0].wait()
    multiply(0, gate_up, 0)
    loads[1].wait()
    multiply(1, act, gate_up.shape[2] // tile)
    own.wait()
    lax.fori_loop(1, count, finish, 0)


def weigh(grads, rows_t, grads_t, gate_up, act, tp_count, dp_count, collective_id):
    count = tp_count * dp_count
    cols = grads.shape[2]
    page_rows = grads.shape[1] // dp_count
    width, rows = rows_t.shape
    hidden = act.shape[2]
    any_spec = pl.BlockSpec(memory_space=pl.ANY)
    dma = pltpu.SemaphoreType.DMA
    return pl.pallas_call(
        functools.partial(weigh_kernel, tp_count, dp_count, min(512, hidden)),
        out_shape=[
            jax.ShapeDtypeStruct((count, page_rows, cols), bf16),
            jax.ShapeDtypeStruct((width, 3 * hidden), bf16),
        ],
        in_specs=[pl.BlockSpec(memory_space=pltpu.HBM)] * 5,
        out_specs=[any_spec] * 2,
        scratch_shapes=[
            pltpu.VMEM((2, width, rows), bf16),
            dma((2,)),
            dma,
            dma((count,)),
            dma((count,)),
        ],
        compiler_params=pltpu.CompilerParams(
            collective_id=collective_id, has_side_effects=True, vmem_limit_bytes=62 * 1024 * 1024
        ),
        cost_estimate=pl.CostEstimate(
            flops=6 * rows * width * hidden,
            bytes_accessed=2 * width * (2 * rows + 3 * hidden),
            transcendentals=0,
        ),
        name="weigh",
    )(grads, rows_t, grads_t, gate_up, act)


def flip(index, bit):
    return index + bit - 2 * bit * lax.rem(lax.div(index, bit), 2)


def collect_kernel(
    tp_count, dp_count, shard, second, gains, chunk, out, second_out, gains_out, from_left, from_right,
    second_send, second_recv, own_sem, ring_send, ring_recv, send, recv, gain_send, gain_recv, chunk_send, chunk_recv,
):
    my_dp = lax.axis_index("dp")
    my_tp = lax.axis_index("tensor")
    rows = shard.shape[0]
    half = rows // 2
    bits = [1 << b for b in reversed(range(dp_count.bit_length() - 1))]
    orders = [bits, bits[:-1][::-1] + bits[-1:]]
    steps = len(bits)

    barrier = pltpu.get_barrier_semaphore()
    for j in range(1, tp_count):
        pl.semaphore_signal(
            barrier, inc=1, device_id={"tensor": lax.rem(my_tp + j, tp_count)}, device_id_type=MESH
        )
    for j in range(1, dp_count):
        pl.semaphore_signal(
            barrier, inc=1, device_id={"dp": lax.rem(my_dp + j, dp_count)}, device_id_type=MESH
        )
    pl.semaphore_wait(barrier, tp_count + dp_count - 2)

    home = out.at[my_tp, pl.ds(my_dp * rows, rows), :]
    own = pltpu.make_async_copy(shard, home, own_sem.at[0])
    own.start()
    own_gain = pltpu.make_async_copy(gains, gains_out.at[my_dp], own_sem.at[1])
    own_gain.start()
    own_second = pltpu.make_async_copy(second, second_out.at[my_tp], own_sem.at[2])
    own_second.start()

    def second_copy(j):
        return pltpu.make_async_remote_copy(
            src_ref=second,
            dst_ref=second_out.at[my_tp],
            send_sem=second_send.at[j],
            recv_sem=second_recv.at[j],
            device_id={"tensor": lax.rem(my_tp + j, tp_count)},
            device_id_type=MESH,
        )

    def across(j):
        return pltpu.make_async_remote_copy(
            src_ref=shard,
            dst_ref=home,
            send_sem=ring_send.at[j],
            recv_sem=ring_recv.at[j],
            device_id={"tensor": lax.rem(my_tp + j, tp_count)},
            device_id_type=MESH,
        )

    def gain_copy(j):
        return pltpu.make_async_remote_copy(
            src_ref=gains,
            dst_ref=gains_out.at[my_dp],
            send_sem=gain_send.at[j],
            recv_sem=gain_recv.at[j],
            device_id={"dp": lax.rem(my_dp + j, dp_count)},
            device_id_type=MESH,
        )

    def step(way):
        return pltpu.make_async_remote_copy(
            src_ref=chunk,
            dst_ref=(from_left, from_right)[way],
            send_sem=chunk_send.at[way],
            recv_sem=chunk_recv.at[way],
            device_id={"tensor": lax.rem(my_tp + (1, tp_count - 1)[way], tp_count)},
            device_id_type=MESH,
        )

    has_right, has_left = my_tp < tp_count - 1, my_tp > 0

    def within(j, s, k, m):
        order = orders[s]
        owner = my_dp
        for b in range(k):
            if m >> b & 1:
                owner = flip(owner, order[b])
        block = out.at[
            lax.rem(my_tp - j + tp_count, tp_count), pl.ds(owner * rows + s * half, half), :
        ]
        at = (1 << k) - 1 + m
        return pltpu.make_async_remote_copy(
            src_ref=block,
            dst_ref=block,
            send_sem=send.at[j, s, at],
            recv_sem=recv.at[j, s, at],
            device_id={"dp": flip(my_dp, order[k])},
            device_id_type=MESH,
        )

    for j in range(1, tp_count):
        across(j).start()
    for j in range(1, dp_count):
        gain_copy(j).start()

    @pl.when(has_right)
    def _():
        step(0).start()

    @pl.when(has_left)
    def _():
        step(1).start()

    own.wait()
    for phase in range(tp_count + steps):
        for k in reversed(range(steps + 1)):
            j = phase - k
            if not 0 <= j < tp_count:
                continue
            if k == 0:
                if j > 0:
                    across(j).wait_recv()
            else:
                for s in range(2):
                    for m in range(1 << (k - 1)):
                        within(j, s, k - 1, m).wait_recv()
            if k < steps:
                for s in range(2):
                    for m in range(1 << k):
                        within(j, s, k, m).start()
        if phase == tp_count:
            for j in range(1, tp_count):
                second_copy(j).start()
    for j in range(tp_count):
        if j > 0:
            across(j).wait_send()
        for s in range(2):
            for k in range(steps):
                for m in range(1 << k):
                    within(j, s, k, m).wait_send()
    own_gain.wait()
    own_second.wait()
    for j in range(1, tp_count):
        second_copy(j).wait()
    for j in range(1, dp_count):
        gain_copy(j).wait()

    @pl.when(has_right)
    def _():
        step(0).wait_send()
        step(1).wait_recv()

    @pl.when(has_left)
    def _():
        step(1).wait_send()
        step(0).wait_recv()


def collect(shard, second, gains, chunk, tp_count, dp_count, collective_id):
    rows, cols = shard.shape
    dma = pltpu.SemaphoreType.DMA
    vmem_spec = pl.BlockSpec(memory_space=pltpu.VMEM)
    any_spec = pl.BlockSpec(memory_space=pl.ANY)
    return pl.pallas_call(
        functools.partial(collect_kernel, tp_count, dp_count),
        out_shape=[
            jax.ShapeDtypeStruct((tp_count, dp_count * rows, cols), shard.dtype),
            jax.ShapeDtypeStruct((tp_count,) + second.shape, second.dtype),
            jax.ShapeDtypeStruct((dp_count,) + gains.shape, gains.dtype),
            jax.ShapeDtypeStruct(chunk.shape, chunk.dtype),
            jax.ShapeDtypeStruct(chunk.shape, chunk.dtype),
        ],
        in_specs=[vmem_spec, vmem_spec, vmem_spec, any_spec],
        out_specs=[any_spec] * 5,
        scratch_shapes=[
            dma((tp_count,)),
            dma((tp_count,)),
            dma((3,)),
            dma((tp_count,)),
            dma((tp_count,)),
            dma((tp_count, 2, dp_count - 1)),
            dma((tp_count, 2, dp_count - 1)),
            dma((dp_count,)),
            dma((dp_count,)),
            dma((2,)),
            dma((2,)),
        ],
        compiler_params=pltpu.CompilerParams(collective_id=collective_id, has_side_effects=True),
        cost_estimate=pl.CostEstimate(
            flops=0, bytes_accessed=16 * tp_count * dp_count * shard.size, transcendentals=0
        ),
        name="collect",
    )(shard, second, gains, chunk)


def spread_kernel(rows, weight, out):
    out[0] = dot_nn(rows[...], weight[0]).astype(out.dtype)


def spread(rows, weights, part, cols):
    shards, width, _ = weights.shape
    count = rows.shape[0]
    return pl.pallas_call(
        spread_kernel,
        grid=(shards,),
        in_specs=[
            pl.BlockSpec((count, width), lambda t: (0, 0)),
            pl.BlockSpec((1, width, cols), lambda t: (t, 0, part)),
        ],
        out_specs=pl.BlockSpec((1, count, cols), lambda t: (t, 0, 0)),
        out_shape=jax.ShapeDtypeStruct((shards, count, cols), bf16),
        cost_estimate=pl.CostEstimate(
            flops=2 * shards * count * width * cols,
            bytes_accessed=2 * shards * width * cols,
            transcendentals=0,
        ),
        name="spread",
    )(rows, weights)


def gather_kernel(has_begin, part, weight, *refs):
    out = refs[-1]

    @pl.when(pl.program_id(0) == 0)
    def _():
        out[...] = refs[0][...] if has_begin else jnp.zeros_like(out)

    out[...] += dot_nt(part[0], weight[0])


def gather_sum(parts, weights, part, begin):
    shards, count, cols = parts.shape
    width = weights.shape[1]
    whole = pl.BlockSpec((count, width), lambda t: (0, 0))
    begins = [] if begin is None else [begin]
    return pl.pallas_call(
        functools.partial(gather_kernel, begin is not None),
        grid=(shards,),
        in_specs=[
            pl.BlockSpec((1, count, cols), lambda t: (t, 0, 0)),
            pl.BlockSpec((1, width, cols), lambda t: (t, 0, part)),
        ]
        + [whole] * len(begins),
        out_specs=whole,
        out_shape=jax.ShapeDtypeStruct((count, width), f32),
        cost_estimate=pl.CostEstimate(
            flops=2 * shards * count * width * cols,
            bytes_accessed=2 * shards * width * cols,
            transcendentals=0,
        ),
        name="gather_sum",
    )(parts, weights, *begins)


def outer_kernel(rows, *refs):
    parts, out, turned = refs[:-2], refs[-2], refs[-1]

    @pl.when(pl.program_id(0) == 0)
    def _():
        turned[...] = rows[...].T

    at = 0
    for part in parts:
        cols = part.shape[2]
        out[:, at : at + cols] = dot_nn(turned[...], part[0]).astype(out.dtype)
        at += cols


def outer(rows, parts):
    shards, count, _ = parts[0].shape
    cols = sum(part.shape[2] for part in parts)
    width = rows.shape[1]
    return pl.pallas_call(
        outer_kernel,
        grid=(shards,),
        in_specs=[pl.BlockSpec((count, width), lambda t: (0, 0))]
        + [pl.BlockSpec((1, count, part.shape[2]), lambda t: (t, 0, 0)) for part in parts],
        out_specs=pl.BlockSpec((width, cols), lambda t: (0, t)),
        out_shape=jax.ShapeDtypeStruct((width, shards * cols), bf16),
        scratch_shapes=[pltpu.VMEM((width, count), bf16)],
        cost_estimate=pl.CostEstimate(
            flops=2 * shards * count * width * cols,
            bytes_accessed=2 * shards * width * cols,
            transcendentals=0,
        ),
        name="outer",
    )(rows, *parts)


def total_kernel(
    tp_count, dp_count, groups, rows, *refs
):
    parts = refs[:groups]
    (
        to_right, to_left, weights, out, grad_rows, from_sides,
        turned, mine, got, got_across, held, load_sem, send, recv,
        across_send, across_recv, chunk_send, chunk_recv,
    ) = refs[groups:]
    my_dp = lax.axis_index("dp")
    my_tp = lax.axis_index("tensor")
    own_rows = out.shape[0]
    half = own_rows // 2
    bits = [1 << b for b in range(dp_count.bit_length() - 1)]
    orders = [bits, bits[:1] + bits[1:][::-1]]
    steps = len(bits)

    def shard_of(j):
        return lax.rem(my_tp + 1 + j, tp_count)

    def load(j):
        return pltpu.make_async_copy(weights.at[shard_of(j)], held.at[j % 2], load_sem.at[j % 2])

    load(0).start()
    barrier = pltpu.get_barrier_semaphore()
    for j in range(1, tp_count):
        pl.semaphore_signal(
            barrier, inc=1, device_id={"tensor": lax.rem(my_tp + j, tp_count)}, device_id_type=MESH
        )
    for bit in bits:
        pl.semaphore_signal(
            barrier, inc=1, device_id={"dp": flip(my_dp, bit)}, device_id_type=MESH
        )
    pl.semaphore_wait(barrier, tp_count - 1 + steps)

    def step(way):
        return pltpu.make_async_remote_copy(
            src_ref=(to_right, to_left)[way],
            dst_ref=from_sides.at[way],
            send_sem=chunk_send.at[way],
            recv_sem=chunk_recv.at[way],
            device_id={"tensor": lax.rem(my_tp + (1, tp_count - 1)[way], tp_count)},
            device_id_type=MESH,
        )

    has_right, has_left = my_tp < tp_count - 1, my_tp > 0

    @pl.when(has_right)
    def _():
        step(0).start()

    @pl.when(has_left)
    def _():
        step(1).start()

    def block(j, s, owner):
        return j, pl.ds(pl.multiple_of(owner * own_rows + s * half, half), half)

    def place(k, m):
        return sum(1 << (steps - 1 - e) for e in range(k)) + m

    def fellow(s, k, m, start):
        owner = start
        for b in range(steps - 1 - k):
            if m >> b & 1:
                owner = flip(owner, orders[s][k + 1 + b])
        return owner

    def exchange_part(j, s, k, m):
        partner = flip(my_dp, orders[s][k])
        at = place(k, m)
        index, span = block(j, s, fellow(s, k, m, partner))
        return pltpu.make_async_remote_copy(
            src_ref=mine.at[index, span, :],
            dst_ref=got.at[j, s, at],
            send_sem=send.at[j, s, at],
            recv_sem=recv.at[j, s, at],
            device_id={"dp": partner},
            device_id_type=MESH,
        )

    def across(j):
        return pltpu.make_async_remote_copy(
            src_ref=mine.at[j, pl.ds(pl.multiple_of(my_dp * own_rows, own_rows), own_rows), :],
            dst_ref=got_across.at[j],
            send_sem=across_send.at[j],
            recv_sem=across_recv.at[j],
            device_id={"tensor": shard_of(j)},
            device_id_type=MESH,
        )

    def every(k):
        return [(s, m) for s in range(2) for m in range(1 << (steps - 1 - k))]

    turned[...] = rows[...].T
    for phase in range(tp_count + steps + 1):
        if phase < tp_count:
            shard = shard_of(phase)
            at = 0
            load(phase).wait()
            if phase + 1 < tp_count:
                load(phase + 1).start()
            for g, part in enumerate(parts):
                cols = part.shape[2]
                value = part[shard]
                mine[phase, :, at : at + cols] = dot_nn(turned[...], value).astype(bf16)
                product = dot_nt(value, held[phase % 2, :, at : at + cols])
                if phase == 0 and g == 0:
                    grad_rows[...] = product
                else:
                    grad_rows[...] += product
                at += cols
        for k in reversed(range(steps + 1)):
            j = phase - k
            if not 0 <= j < tp_count:
                continue
            if k > 0:
                for s, m in every(k - 1):
                    exchange_part(j, s, k - 1, m).wait_recv()
                    index, span = block(j, s, fellow(s, k - 1, m, my_dp))
                    mine[index, span, :] = (
                        mine[index, span, :].astype(f32)
                        + got[j, s, place(k - 1, m)].astype(f32)
                    ).astype(bf16)
            if k < steps:
                for s, m in every(k):
                    exchange_part(j, s, k, m).start()
            elif j < tp_count - 1:
                across(j).start()
    total = mine[
        tp_count - 1, pl.ds(pl.multiple_of(my_dp * own_rows, own_rows), own_rows), :
    ].astype(f32)
    for j in range(tp_count - 1):
        across(j).wait_recv()
        total += got_across[j].astype(f32)
    out[...] = total

    @pl.when(has_right)
    def _():
        step(0).wait_send()
        step(1).wait_recv()

    @pl.when(has_left)
    def _():
        step(1).wait_send()
        step(0).wait_recv()

    for j in range(tp_count):
        if j < tp_count - 1:
            across(j).wait_send()
        for k in range(steps):
            for s, m in every(k):
                exchange_part(j, s, k, m).wait_send()


def total_grads(rows, parts, to_right, to_left, weights, dp_count, collective_id):
    tp_count, width, cols = weights.shape
    count = rows.shape[0]
    own_rows = width // dp_count
    vmem_spec = pl.BlockSpec(memory_space=pltpu.VMEM)
    any_spec = pl.BlockSpec(memory_space=pl.ANY)
    dma = pltpu.SemaphoreType.DMA
    return pl.pallas_call(
        functools.partial(total_kernel, tp_count, dp_count, len(parts)),
        out_shape=[
            jax.ShapeDtypeStruct((own_rows, cols), f32),
            jax.ShapeDtypeStruct((count, width), f32),
            jax.ShapeDtypeStruct((2, count, width), bf16),
        ],
        in_specs=[vmem_spec] * (1 + len(parts)) + [any_spec] * 3,
        out_specs=[vmem_spec, vmem_spec, any_spec],
        scratch_shapes=[
            pltpu.VMEM((width, count), bf16),
            pltpu.VMEM((tp_count, width, cols), bf16),
            pltpu.VMEM((tp_count, 2, dp_count - 1, own_rows // 2, cols), bf16),
            pltpu.VMEM((tp_count - 1, own_rows, cols), bf16),
            pltpu.VMEM((2, width, cols), bf16),
            dma((2,)),
            dma((tp_count, 2, dp_count - 1)),
            dma((tp_count, 2, dp_count - 1)),
            dma((tp_count,)),
            dma((tp_count,)),
            dma((2,)),
            dma((2,)),
        ],
        compiler_params=pltpu.CompilerParams(
            collective_id=collective_id, has_side_effects=True, vmem_limit_bytes=62 * 1024 * 1024
        ),
        cost_estimate=pl.CostEstimate(
            flops=4 * tp_count * count * width * cols,
            bytes_accessed=16 * tp_count * width * cols,
            transcendentals=0,
        ),
        name="total_grads",
    )(rows, *parts, to_right, to_left, weights)


def rms_scale(hidden):
    return lax.rsqrt(jnp.mean(hidden * hidden, axis=1, keepdims=True) + epsilon)


def norm_back(grad_norm, hidden, scale_rows, gain):
    normed = hidden * scale_rows
    gain_part = jnp.sum(grad_norm * normed, axis=0)
    inner = grad_norm * gain
    grad_hidden = scale_rows * (inner - normed * jnp.mean(inner * normed, axis=1, keepdims=True))
    return (grad_hidden, gain_part)


def after(value, other):
    return lax.optimization_barrier((value, other))[0]


def local(
    tokens,
    upstream,
    lengths,
    positions,
    pages,
    attn_gain,
    w_query,
    w_key,
    w_value,
    w_out,
    mlp_gain,
    w_gate,
    w_up,
    w_down,
):
    dp_count = lax.axis_size("dp")
    tp_count = lax.axis_size("tensor")
    dp_index = lax.axis_index("dp")
    tp_index = lax.axis_index("tensor")
    tok_dev, width = tokens.shape
    tok_group = tok_dev * tp_count
    page_rows = tok_dev // dp_count
    group_pages = tp_count * dp_count
    page_count = pages.shape[0]
    device = dp_index * tp_count + tp_index
    everyone = ("tensor", "dp")

    local_ids = jnp.arange(dp_count, dtype=jnp.int32)
    inverse = (
        jnp.zeros((page_count,), jnp.int32).at[pages].set(jnp.arange(page_count, dtype=jnp.int32))
    )
    dealt = lax.dynamic_slice_in_dim(inverse, device * dp_count, dp_count)
    dest_group = dealt // group_pages
    send_order = jnp.zeros((dp_count,), jnp.int32).at[dest_group].set(local_ids)
    group_sources = lax.dynamic_slice_in_dim(pages, dp_index * group_pages, group_pages)
    perm = (
        (jnp.arange(group_pages, dtype=jnp.int32) // dp_count) * dp_count
        + group_sources // group_pages
    ).astype(jnp.int32)

    def reorder(rows, order):
        blocks = rows.reshape(dp_count, page_rows, rows.shape[1])
        return jnp.take(blocks, order, axis=0, mode="clip").reshape(rows.shape)

    hidden_in = reorder(tokens, send_order).astype(f32)
    grad_top = reorder(upstream, send_order).astype(f32)
    seq_lens = lengths[0]
    seq_ends = jnp.cumsum(seq_lens)
    place = (jnp.take(dealt, send_order, mode="clip") % group_pages) * page_rows
    place_rows = (place[:, None] + jnp.arange(page_rows, dtype=jnp.int32)[None, :]).reshape(-1)
    valid_rows = (place_rows < seq_ends[-1]).astype(f32)[:, None]

    row_ids = jnp.arange(tok_group, dtype=jnp.int32)
    begin = jnp.max(
        jnp.where(row_ids[:, None] >= seq_ends[None, :], seq_ends[None, :], 0), axis=1
    ).astype(jnp.int32)
    block_len = min(block_rows, tok_group)
    first_block = begin[::block_len] // min(key_rows, tok_group)
    begin = begin[None, :]
    inverse_freq = theta_base ** (-(jnp.arange(HALF, dtype=f32) * 2.0) / HD)
    angles = inverse_freq[:, None] * positions.astype(f32)
    cos_t, sin_t = jnp.cos(angles), jnp.sin(angles)

    q_cols, kv_cols = w_query.shape[1], w_key.shape[1]
    kv_heads = kv_cols // HD
    per_group = q_cols // kv_cols
    group_q = per_group * HD
    groups = range(kv_heads)
    qkv_shard = jnp.concatenate(
        [
            part
            for g in groups
            for part in (
                w_query[:, g * group_q : (g + 1) * group_q],
                w_key[:, g * HD : (g + 1) * HD],
                w_value[:, g * HD : (g + 1) * HD],
            )
        ],
        axis=1,
    )

    def trade(value):
        blocks = value.reshape(group_pages, page_rows, value.shape[-1])
        return lax.all_to_all(blocks, everyone, split_axis=0, concat_axis=0, tiled=True)

    def trade_back(value):
        return trade(value).reshape(tp_count, tok_dev, value.shape[-1])

    def pass_on(values, first, last):
        return (
            lax.ppermute(values[0], "tensor", [(t, t + 1) for t in range(*first)]),
            lax.ppermute(values[1], "tensor", [(t, t - 1) for t in range(*last)]),
        )

    grad_out = grad_top * valid_rows
    own_chunk = grad_out.astype(bf16)
    mlp_shard = jnp.concatenate([w_gate, w_up, w_down.T], axis=1)
    w_qkv, out_shards, gains, *sides = collect(
        qkv_shard, w_out.T, jnp.stack([attn_gain, mlp_gain]), own_chunk, tp_count, dp_count, 1
    )
    w_out_t = lax.all_gather(out_shards, "dp", axis=1, tiled=True)
    w_mlp = lax.all_gather(after(mlp_shard, gains), "dp", axis=0, tiled=True)
    chunks = [(sides[0], sides[1])]
    gains = gains.transpose(1, 0, 2).reshape(2, -1).astype(f32)
    gain_one, gain_two = gains[0], gains[1]

    scale_one = rms_scale(hidden_in)
    normed_one = (hidden_in * scale_one * gain_one).astype(bf16)
    slots = project(normed_one, w_qkv, dp_count, 3)
    for n in range(2, tp_count):
        passed = after(chunks[-1], slots) if n == 2 else chunks[-1]
        chunks.append(pass_on(passed, (n - 1, tp_count - 1), (1, tp_count - n + 1)))
    saved, mixed = [], []
    for g in groups:
        q_t, k_t, k_rows, v_t, v_rows = prepare(
            after(slots, (o_slots, w_out_t, chunks[1])) if g else slots, g, perm, cos_t, sin_t, per_group, 1
        )
        o_t, lse, o_slots = attend_forward(
            q_t, k_rows, v_t, begin, first_block, perm, page_rows, block_len
        )
        saved.append((q_t, k_rows, k_t, v_rows, o_t, lse))
        mixed.append(trade_back(after(o_slots, chunks[1]) if g else o_slots))
    hidden_mid = hidden_in
    mixed[0] = after(mixed[0], chunks[-1])
    for g in groups:
        hidden_mid = gather_sum(mixed[g], w_out_t, g, hidden_mid)

    scale_two = rms_scale(hidden_mid)
    normed_two = (hidden_mid * scale_two * gain_two).astype(bf16)
    grads_t, rows_t, inner_act, grad_gate_up, *partial_two, grad_normed_two = feed(
        normed_two, [own_chunk] + [c[0] for c in chunks] + [c[1] for c in chunks], w_mlp, tp_count
    )
    grad_normed_two = grad_normed_two.astype(f32)
    grad_mid_norm, gain_two_part = norm_back(grad_normed_two, hidden_mid, scale_two, gain_two)
    grad_mid = grad_out + grad_mid_norm

    def add_on(arrived, s):
        return tuple(
            (value.astype(f32) + partial_two[at].astype(f32)).astype(bf16)
            for value, at in zip(arrived, (s, tp_count - s))
        )

    def reduce_dp(grad):
        return lax.psum_scatter(grad.astype(bf16), "dp", scatter_dimension=0, tiled=True)

    def reduce_tensor(value):
        cols = value.shape[1] // tp_count
        total = lax.dynamic_slice_in_dim(value, tp_index * cols, cols, 1).astype(f32)
        for s in range(1, tp_count):
            target = lax.rem(tp_index + s, tp_count)
            block = lax.dynamic_slice_in_dim(value, target * cols, cols, 1)
            pairs = [(t, (t + s) % tp_count) for t in range(tp_count)]
            total = total + lax.ppermute(block, "tensor", pairs).astype(f32)
        return total

    grad_z = grad_mid.astype(bf16)
    grad_wout = outer(grad_z, mixed)
    sum_out = reduce_dp(grad_wout)
    grad_slots, grad_wmlp = weigh(
        spread(after(grad_z, grad_wout), w_out_t, 0, q_cols),
        rows_t, grads_t, grad_gate_up, inner_act, tp_count, dp_count, 2,
    )
    sum_mlp = reduce_dp(grad_wmlp)
    first_part = after((partial_two[1], partial_two[tp_count - 1]), grad_slots)
    passing = pass_on(first_part, (0, 1), (tp_count - 1, tp_count))
    grad_qkv = []
    for g in groups:
        q_t, k_rows, k_t, v_rows, o_t, lse = saved[g]
        back = attend_backward(
            after(grad_slots, (back, sum_out) if g else first_part), g, q_t, k_rows, k_t, v_rows,
            o_t, lse, begin, cos_t, sin_t, first_block, perm, page_rows, block_len,
        )
        if g == len(groups) - 1:
            steps = 2
            if tp_count > 3:
                passing = pass_on(add_on(passing, 2), (0, 2), (tp_count - 2, tp_count))
                steps = 3
            back = after(back, (grad_qkv, passing))
        grad_qkv.append(trade_back(back))
    hidden = sum_mlp.shape[1] // 3
    for s in range(steps, tp_count - 1):
        passing = pass_on(add_on(passing, s), (0, s), (tp_count - s, tp_count))
    passing = add_on(passing, tp_count - 1)
    sum_qkv, grad_normed_one, sides = total_grads(
        normed_one, grad_qkv, passing[0], passing[1], w_qkv, dp_count, 4
    )
    branch_two = jnp.where(tp_index > 0, sides[0].astype(f32), 0.0)
    branch_two += jnp.where(tp_index < tp_count - 1, sides[1].astype(f32), 0.0)
    each = group_q + 2 * HD
    sum_qkv = [sum_qkv[:, g * each : (g + 1) * each] for g in groups]
    sum_out = reduce_tensor(after(sum_out, grad_normed_one))
    result = (
        (after(hidden_mid, back) + branch_two + partial_two[0].astype(f32)) * valid_rows
    ).astype(bf16)
    grad_in_norm, gain_one_part = norm_back(grad_normed_one, hidden_in, scale_one, gain_one)
    grad_in = (grad_mid + grad_in_norm).astype(bf16)

    gain_parts = jnp.stack([gain_one_part, gain_two_part]).reshape(2, dp_count, -1)
    gain_parts = jnp.broadcast_to(
        gain_parts.transpose(1, 0, 2)[None], (tp_count, dp_count, 2, gain_parts.shape[2])
    ).reshape(group_pages, 2, -1)
    gain_sums = jnp.sum(
        lax.all_to_all(gain_parts, everyone, split_axis=0, concat_axis=0, tiled=True), axis=0
    )
    return (
        reorder(result, dest_group),
        reorder(grad_in, dest_group),
        gain_sums[0],
        jnp.concatenate([part[:, :group_q] for part in sum_qkv], axis=1),
        jnp.concatenate([part[:, group_q : group_q + HD] for part in sum_qkv], axis=1),
        jnp.concatenate([part[:, group_q + HD :] for part in sum_qkv], axis=1),
        sum_out.T,
        gain_sums[1],
        sum_mlp[:, :hidden].astype(f32),
        sum_mlp[:, hidden : 2 * hidden].astype(f32),
        sum_mlp[:, 2 * hidden :].astype(f32).T,
    )


def solution(mesh):
    rows = P(("dp", "tensor"), None)
    weight = P("dp", "tensor")
    weight_t = P("tensor", "dp")
    return jax.shard_map(
        local,
        mesh=mesh,
        in_specs=(
            rows,
            rows,
            P("dp", None),
            P("dp", None),
            P(),
            P("dp"),
            weight,
            weight,
            weight,
            weight_t,
            P("dp"),
            weight,
            weight,
            weight_t,
        ),
        out_specs=(
            rows,
            rows,
            P("dp"),
            weight,
            weight,
            weight,
            weight_t,
            P("dp"),
            weight,
            weight,
            weight_t,
        ),
        check_vma=False,
    )
```

```python
import functools

import jax
import jax.numpy as jnp
from jax import lax
from jax.experimental import pallas as pl
from jax.experimental.pallas import tpu as pltpu
from jax.sharding import PartitionSpec as P

HD = 64
HALF = HD // 2

epsilon = 1e-05
theta_base = 500000.0
masked_score = -1e30
score_scale = HD**-0.5
block_rows = 512
key_rows = 256
MESH = pl.DeviceIdType.MESH
f32 = jnp.float32
bf16 = jnp.bfloat16


def dot_nn(left, right):
    return lax.dot_general(left, right, (((1,), (0,)), ((), ())), preferred_element_type=f32)


def dot_nt(left, right):
    return lax.dot_general(left, right, (((1,), (1,)), ((), ())), preferred_element_type=f32)


def dot_tn(left, right):
    return lax.dot_general(left, right, (((0,), (0,)), ((), ())), preferred_element_type=f32)


def prep_kernel(pages_per, q_heads, kv_heads, perm, *refs):
    page_refs = refs[:pages_per]
    cos_ref, sin_ref, q_t, k_t, k_rows, v_t, v_rows = refs[pages_per:]
    rows = jnp.concatenate([r[0].astype(f32) for r in page_refs], axis=0)
    turned = rows.T
    cos, sin = cos_ref[...], sin_ref[...]

    def rope(base):
        first, second = turned[base : base + HALF], turned[base + HALF : base + HD]
        return jnp.concatenate([first * cos - second * sin, second * cos + first * sin], axis=0)

    for h in range(q_heads):
        roped = rope(h * HD).astype(bf16)
        q_t[h * HD : (h + 1) * HD, :] = (roped.astype(f32) * score_scale).astype(bf16)
    k_base = q_heads * HD
    v_base = k_base + kv_heads * HD
    for g in range(kv_heads):
        roped = rope(k_base + g * HD)
        k_t[g * HD : (g + 1) * HD, :] = roped.astype(bf16)
        k_rows[g] = roped.T.astype(bf16)
        v_t[g * HD : (g + 1) * HD, :] = turned[v_base + g * HD : v_base + (g + 1) * HD].astype(bf16)
        v_rows[g] = rows[:, v_base + g * HD : v_base + (g + 1) * HD].astype(bf16)


def prepare(slots, part, perm, cos_t, sin_t, q_heads, kv_heads):
    page_rows = slots.shape[1]
    cols = (q_heads + 2 * kv_heads) * HD
    total_rows = slots.shape[0] * page_rows
    lanes = min(256, total_rows)
    pages_per = lanes // page_rows

    def page_spec(a):
        return pl.BlockSpec(
            (1, page_rows, cols), lambda i, perm_ref, a=a: (perm_ref[i * pages_per + a], 0, part)
        )

    table = pl.BlockSpec((HALF, lanes), lambda i, perm_ref: (0, i))
    return pl.pallas_call(
        functools.partial(prep_kernel, pages_per, q_heads, kv_heads),
        grid_spec=pltpu.PrefetchScalarGridSpec(
            num_scalar_prefetch=1,
            grid=(total_rows // lanes,),
            in_specs=[page_spec(a) for a in range(pages_per)] + [table, table],
            out_specs=[
                pl.BlockSpec((q_heads * HD, lanes), lambda i, perm_ref: (0, i)),
                pl.BlockSpec((kv_heads * HD, lanes), lambda i, perm_ref: (0, i)),
                pl.BlockSpec((kv_heads, lanes, HD), lambda i, perm_ref: (0, i, 0)),
                pl.BlockSpec((kv_heads * HD, lanes), lambda i, perm_ref: (0, i)),
                pl.BlockSpec((kv_heads, lanes, HD), lambda i, perm_ref: (0, i, 0)),
            ],
        ),
        out_shape=[
            jax.ShapeDtypeStruct((q_heads * HD, total_rows), bf16),
            jax.ShapeDtypeStruct((kv_heads * HD, total_rows), bf16),
            jax.ShapeDtypeStruct((kv_heads, total_rows, HD), bf16),
            jax.ShapeDtypeStruct((kv_heads * HD, total_rows), bf16),
            jax.ShapeDtypeStruct((kv_heads, total_rows, HD), bf16),
        ],
        cost_estimate=pl.CostEstimate(
            flops=8 * slots.size, bytes_accessed=6 * slots.size, transcendentals=0
        ),
        name="prepare",
    )(perm, *([slots] * pages_per), cos_t, sin_t)


def block_bias(i, j, begin_row, block_len, key_len):
    keys = j * key_len + lax.broadcasted_iota(jnp.int32, (key_len, block_len), 0)
    queries = i * block_len + lax.broadcasted_iota(jnp.int32, (key_len, block_len), 1)
    allowed = (keys >= begin_row) & (keys <= queries)
    return jnp.where(allowed, 0.0, masked_score)


def forward_kernel(
    q_heads, kv_heads, page_rows, first_block, perm,
    q_t, k_rows, v_t, begin, o_t, lse, o_slots, acc, stage, sems,
):
    i = pl.program_id(0)
    block_len = q_t.shape[1]
    key_len = min(key_rows, k_rows.shape[1])
    per_group = q_heads // kv_heads
    acc[...] = jnp.zeros_like(acc)
    begin_row = begin[...]

    def visit(j, carry):
        bias = block_bias(i, j, begin_row, block_len, key_len)
        at = pl.ds(pl.multiple_of(j * key_len, key_len), key_len)
        scores = [
            dot_nn(k_rows[h // per_group, at, :], q_t[h * HD : (h + 1) * HD, :]) + bias
            for h in range(q_heads)
        ]
        tops = [
            jnp.maximum(carry[h][0], jnp.max(scores[h], axis=0, keepdims=True))
            for h in range(q_heads)
        ]
        weights = [jnp.exp(scores[h] - tops[h]) for h in range(q_heads)]
        fades = [jnp.exp(carry[h][0] - tops[h]) for h in range(q_heads)]
        totals = [
            carry[h][1] * fades[h] + jnp.sum(weights[h], axis=0, keepdims=True)
            for h in range(q_heads)
        ]
        for h in range(q_heads):
            g = h // per_group
            span = slice(h * HD, (h + 1) * HD)
            acc[span, :] = acc[span, :] * fades[h] + dot_nn(
                v_t[g * HD : (g + 1) * HD, at], weights[h].astype(bf16)
            )
        return tuple(zip(tops, totals))

    start = tuple(
        (jnp.full((1, block_len), masked_score, f32), jnp.zeros((1, block_len), f32))
        for _ in range(q_heads)
    )
    stats = lax.fori_loop(
        first_block[i], lax.div((i + 1) * block_len - 1, key_len) + 1, visit, start
    )
    for h in range(q_heads):
        lse[h : h + 1, :] = stats[h][0] + jnp.log(stats[h][1])
    mixed = jnp.concatenate(
        [acc[h * HD : (h + 1) * HD, :] / stats[h][1] for h in range(q_heads)], axis=0
    )
    o_t[...] = mixed.astype(bf16)
    pages = block_len // page_rows
    stage[...] = mixed.T.astype(bf16).reshape(pages, page_rows, q_heads * HD)
    copies = [
        pltpu.make_async_copy(stage.at[a], o_slots.at[perm[i * pages + a]], sems.at[a])
        for a in range(pages)
    ]
    for copy in copies:
        copy.start()
    for copy in copies:
        copy.wait()


def attend_forward(q_t, k_rows, v_t, begin, first_block, perm, page_rows, block_len):
    total_rows = q_t.shape[1]
    kv_heads = k_rows.shape[0]
    q_heads = q_t.shape[0] // HD
    pages = block_len // page_rows
    return pl.pallas_call(
        functools.partial(forward_kernel, q_heads, kv_heads, page_rows),
        grid_spec=pltpu.PrefetchScalarGridSpec(
            num_scalar_prefetch=2,
            grid=(total_rows // block_len,),
            in_specs=[
                pl.BlockSpec((q_heads * HD, block_len), lambda i, *_: (0, i)),
                pl.BlockSpec((kv_heads, total_rows, HD), lambda i, *_: (0, 0, 0)),
                pl.BlockSpec((kv_heads * HD, total_rows), lambda i, *_: (0, 0)),
                pl.BlockSpec((1, block_len), lambda i, *_: (0, i)),
            ],
            out_specs=[
                pl.BlockSpec((q_heads * HD, block_len), lambda i, *_: (0, i)),
                pl.BlockSpec((q_heads, block_len), lambda i, *_: (0, i)),
                pl.BlockSpec(memory_space=pl.ANY),
            ],
            scratch_shapes=[
                pltpu.VMEM((q_heads * HD, block_len), f32),
                pltpu.VMEM((pages, page_rows, q_heads * HD), bf16),
                pltpu.SemaphoreType.DMA((pages,)),
            ],
        ),
        out_shape=[
            jax.ShapeDtypeStruct((q_heads * HD, total_rows), bf16),
            jax.ShapeDtypeStruct((q_heads, total_rows), f32),
            jax.ShapeDtypeStruct((total_rows // page_rows, page_rows, q_heads * HD), bf16),
        ],
        cost_estimate=pl.CostEstimate(
            flops=q_heads * total_rows * total_rows * HD,
            bytes_accessed=8 * q_t.size,
            transcendentals=q_heads * total_rows * total_rows // 4,
        ),
        name="attend_forward",
    )(first_block, perm, q_t, k_rows, v_t, begin)


def backward_kernel(
    q_heads, kv_heads, page_rows, pages, first_block, perm, *refs
):
    grad_pages = refs[:pages]
    (
        q_t, k_rows, k_t, v_rows, o_t, lse, begin, cos_ref, sin_ref, cos_all, sin_all,
        out, grad_q, grad_k, grad_v, stage, kv_stage, sems, kv_sems,
    ) = refs[pages:]
    i = pl.program_id(0)
    steps = pl.num_programs(0)
    block_len = q_t.shape[1]
    key_len = min(key_rows, k_rows.shape[1])
    per_group = q_heads // kv_heads
    q_cols = q_heads * HD
    kv_cols = kv_heads * HD

    @pl.when(i == 0)
    def _():
        grad_k[...] = jnp.zeros_like(grad_k)
        grad_v[...] = jnp.zeros_like(grad_v)

    grad_rows = jnp.concatenate([r[0].astype(f32) for r in grad_pages], axis=0)
    grad_t = grad_rows.T
    grad_low = grad_t.astype(bf16)
    inner = [
        jnp.sum(
            grad_t[h * HD : (h + 1) * HD] * o_t[h * HD : (h + 1) * HD, :].astype(f32),
            axis=0,
            keepdims=True,
        )
        for h in range(q_heads)
    ]
    grad_q[...] = jnp.zeros_like(grad_q)
    begin_row = begin[...]

    def visit(j, carry):
        bias = block_bias(i, j, begin_row, block_len, key_len)
        at = pl.ds(pl.multiple_of(j * key_len, key_len), key_len)
        for g in range(kv_heads):
            kv_span = slice(g * HD, (g + 1) * HD)
            keys, vals, keys_t = k_rows[g, at, :], v_rows[g, at, :], k_t[kv_span, at]
            heads = range(g * per_group, (g + 1) * per_group)
            spans = [slice(h * HD, (h + 1) * HD) for h in heads]
            scores = [dot_nn(keys, q_t[span, :]) + bias for span in spans]
            grad_probs = [dot_nn(vals, grad_low[span]) for span in spans]
            probs = [jnp.exp(s - lse[h : h + 1, :]) for s, h in zip(scores, heads)]
            grad_scores = [
                (p * (d - inner[h])).astype(bf16) for p, d, h in zip(probs, grad_probs, heads)
            ]
            low_probs = [p.astype(bf16) for p in probs]
            grad_v[kv_span, at] += sum(
                dot_nt(grad_low[span], p) for span, p in zip(spans, low_probs)
            )
            grad_k[kv_span, at] += sum(
                dot_nt(q_t[span, :], d) for span, d in zip(spans, grad_scores)
            )
            for span, d in zip(spans, grad_scores):
                grad_q[span, :] += dot_nn(keys_t, d)
        return carry

    lax.fori_loop(first_block[i], lax.div((i + 1) * block_len - 1, key_len) + 1, visit, 0)

    def unrope(value, cos, sin):
        first, second = value[:HALF], value[HALF:]
        return jnp.concatenate([first * cos + second * sin, second * cos - first * sin], axis=0)

    cos, sin = cos_ref[...], sin_ref[...]
    parts = [
        unrope(grad_q[h * HD : (h + 1) * HD, :] * score_scale, cos, sin) for h in range(q_heads)
    ]
    stage[...] = jnp.concatenate(parts, axis=0).T.astype(bf16).reshape(pages, page_rows, q_cols)
    copies = [
        pltpu.make_async_copy(
            stage.at[a], out.at[perm[i * pages + a], :, pl.ds(0, q_cols)], sems.at[a]
        )
        for a in range(pages)
    ]
    for copy in copies:
        copy.start()
    for copy in copies:
        copy.wait()

    @pl.when(i == steps - 1)
    def _():
        all_pages = kv_stage.shape[0]
        cos, sin = cos_all[...], sin_all[...]
        parts = [unrope(grad_k[g * HD : (g + 1) * HD, :], cos, sin) for g in range(kv_heads)]
        both = jnp.concatenate(parts + [grad_v[...]], axis=0)
        kv_stage[...] = both.T.astype(bf16).reshape(all_pages, page_rows, 2 * kv_cols)
        copies = [
            pltpu.make_async_copy(
                kv_stage.at[a], out.at[perm[a], :, pl.ds(q_cols, 2 * kv_cols)], kv_sems.at[a]
            )
            for a in range(all_pages)
        ]
        for copy in copies:
            copy.start()
        for copy in copies:
            copy.wait()


def attend_backward(
    grad_slots, part, q_t, k_rows, k_t, v_rows, o_t, lse, begin, cos_t, sin_t, first_block, perm,
    page_rows, block_len,
):
    total_rows = q_t.shape[1]
    kv_heads = k_rows.shape[0]
    q_heads = q_t.shape[0] // HD
    pages = block_len // page_rows
    all_pages = total_rows // page_rows
    q_cols = q_heads * HD
    kv_cols = kv_heads * HD

    def page_spec(a):
        return pl.BlockSpec(
            (1, page_rows, q_cols),
            lambda i, first_ref, perm_ref, a=a: (perm_ref[i * pages + a], 0, part),
        )

    def whole(shape):
        return pl.BlockSpec(shape, lambda i, *_: (0,) * len(shape))

    def column(rows):
        return pl.BlockSpec((rows, block_len), lambda i, *_: (0, i))

    return pl.pallas_call(
        functools.partial(backward_kernel, q_heads, kv_heads, page_rows, pages),
        grid_spec=pltpu.PrefetchScalarGridSpec(
            num_scalar_prefetch=2,
            grid=(total_rows // block_len,),
            in_specs=[page_spec(a) for a in range(pages)]
            + [
                column(q_cols),
                whole((kv_heads, total_rows, HD)),
                whole((kv_cols, total_rows)),
                whole((kv_heads, total_rows, HD)),
                column(q_cols),
                column(q_heads),
                column(1),
                column(HALF),
                column(HALF),
                whole((HALF, total_rows)),
                whole((HALF, total_rows)),
            ],
            out_specs=pl.BlockSpec(memory_space=pl.ANY),
            scratch_shapes=[
                pltpu.VMEM((q_cols, block_len), f32),
                pltpu.VMEM((kv_cols, total_rows), f32),
                pltpu.VMEM((kv_cols, total_rows), f32),
                pltpu.VMEM((pages, page_rows, q_cols), bf16),
                pltpu.VMEM((all_pages, page_rows, 2 * kv_cols), bf16),
                pltpu.SemaphoreType.DMA((pages,)),
                pltpu.SemaphoreType.DMA((all_pages,)),
            ],
        ),
        out_shape=jax.ShapeDtypeStruct((all_pages, page_rows, q_cols + 2 * kv_cols), bf16),
        cost_estimate=pl.CostEstimate(
            flops=3 * q_heads * total_rows * total_rows * HD,
            bytes_accessed=12 * q_t.size,
            transcendentals=q_heads * total_rows * total_rows // 4,
        ),
        name="attend_backward",
    )(
        first_block, perm, *([grad_slots] * pages), q_t, k_rows, k_t, v_rows, o_t, lse, begin,
        cos_t, sin_t, cos_t, sin_t,
    )


def project_kernel(
    tp_count, dp_count, rows, weights, slots, held, stage, load_sem, own_sem, send, recv
):
    count = dp_count * tp_count
    my_dp = lax.axis_index("dp")
    my_tp = lax.axis_index("tensor")
    me = my_dp * tp_count + my_tp
    page_rows = slots.shape[1]

    def load(j):
        shard = lax.rem(my_tp + 1 + j, tp_count)
        return pltpu.make_async_copy(weights.at[shard], held.at[j % 2], load_sem.at[j % 2])

    load(0).start()
    barrier = pltpu.get_barrier_semaphore()

    def greet(j, carry):
        peer = lax.rem(me + j, count)
        pl.semaphore_signal(
            barrier,
            inc=1,
            device_id={"dp": lax.div(peer, tp_count), "tensor": lax.rem(peer, tp_count)},
            device_id_type=MESH,
        )
        return carry

    lax.fori_loop(1, count, greet, 0)
    pl.semaphore_wait(barrier, count - 1)
    home = slots.at[my_tp * dp_count + my_dp]

    def copy_to(j, off):
        p_dp = lax.rem(my_dp + off, dp_count)
        return pltpu.make_async_remote_copy(
            src_ref=stage.at[j, pl.ds(p_dp * page_rows, page_rows), :],
            dst_ref=home,
            send_sem=send.at[j, off],
            recv_sem=recv.at[j, off],
            device_id={"dp": p_dp, "tensor": lax.rem(my_tp + 1 + j, tp_count)},
            device_id_type=MESH,
        )

    def each(j, act):
        def one(off, carry):
            act(copy_to(j, off))
            return carry

        lax.fori_loop(1 if j == tp_count - 1 else 0, dp_count, one, 0)

    for j in range(tp_count):
        load(j).wait()
        if j + 1 < tp_count:
            load(j + 1).start()
        stage[j] = dot_nn(rows[...], held[j % 2]).astype(bf16)
        if j > 0:
            each(j - 1, lambda copy: copy.start())
    each(tp_count - 1, lambda copy: copy.start())
    own = pltpu.make_async_copy(
        stage.at[tp_count - 1, pl.ds(my_dp * page_rows, page_rows), :], home, own_sem
    )
    own.start()
    own.wait()
    for j in range(tp_count):
        each(j, lambda copy: copy.wait())


def project(rows, weights, dp_count, collective_id):
    tp_count, width, cols = weights.shape
    total = rows.shape[0]
    page_rows = total // dp_count
    any_spec = pl.BlockSpec(memory_space=pl.ANY)
    dma = pltpu.SemaphoreType.DMA
    return pl.pallas_call(
        functools.partial(project_kernel, tp_count, dp_count),
        out_shape=jax.ShapeDtypeStruct((tp_count * dp_count, page_rows, cols), bf16),
        in_specs=[
            pl.BlockSpec(memory_space=pltpu.VMEM),
            pl.BlockSpec(memory_space=pltpu.HBM),
        ],
        out_specs=any_spec,
        scratch_shapes=[
            pltpu.VMEM((2, width, cols), bf16),
            pltpu.VMEM((tp_count, total, cols), bf16),
            dma((2,)),
            dma,
            dma((tp_count, dp_count)),
            dma((tp_count, dp_count)),
        ],
        compiler_params=pltpu.CompilerParams(
            collective_id=collective_id, has_side_effects=True, vmem_limit_bytes=62 * 1024 * 1024
        ),
        cost_estimate=pl.CostEstimate(
            flops=2 * tp_count * total * width * cols,
            bytes_accessed=16 * tp_count * width * cols,
            transcendentals=0,
        ),
        name="project",
    )(rows, weights)


def feed_kernel(
    ring, tile, own_rows, *refs
):
    grad_rows = refs[: 2 * ring - 1]
    weights, grads_t, rows_t, act_all, grads_all = refs[2 * ring - 1 : 2 * ring + 4]
    mixed_all = refs[2 * ring + 4 : 3 * ring + 4]
    (
        grad_own, held, grads_held, acc_n, acc_m, first_part, arrived, outgoing, mixed_stage,
        final_stage, turned, load_sem, keep_sem, grad_sem, mixed_sem, final_sem,
        row_send, row_recv, sum_send, sum_recv, all_sem,
    ) = refs[3 * ring + 4 :]
    me = lax.axis_index("tensor")
    right = lax.rem(me + 1, ring)
    left = lax.rem(me + ring - 1, ring)
    hidden = weights.shape[1] // 3
    tiles = hidden // tile

    barrier = pltpu.get_barrier_semaphore()
    for neighbour in (left, right):
        pl.semaphore_signal(barrier, inc=1, device_id={"tensor": neighbour}, device_id_type=MESH)
    pl.semaphore_wait(barrier, 2)

    load = pltpu.make_async_copy(own_rows, held.at[0], load_sem)
    load.start()

    def grad_load(s):
        def copy_of(source):
            return pltpu.make_async_copy(
                grad_rows[source], grads_held.at[s % 2], grad_sem.at[s % 2]
            )

        if s == 0:
            copy_of(0).start()
            return

        @pl.when(me >= s)
        def _():
            copy_of(s).start()

        @pl.when(me < s)
        def _():
            copy_of(ring - 1 + ring - s).start()

    def grad_wait(s):
        pltpu.make_async_copy(grad_rows[0], grads_held.at[s % 2], grad_sem.at[s % 2]).wait()

    def part_of(array, s):
        count = own_rows.shape[0]
        return array.at[:, pl.ds(pl.multiple_of(s * count, 128), count)]

    def grad_keep(s):
        return pltpu.make_async_copy(turned.at[1], part_of(grads_t, s), all_sem)

    grad_load(0)
    load.wait()

    def pass_rows(s):
        return pltpu.make_async_remote_copy(
            src_ref=held.at[s],
            dst_ref=held.at[s + 1],
            send_sem=row_send.at[s],
            recv_sem=row_recv.at[s],
            device_id={"tensor": right},
            device_id_type=MESH,
        )

    def pass_sum(s):
        return pltpu.make_async_remote_copy(
            src_ref=outgoing.at[s - 1],
            dst_ref=arrived.at[s - 1],
            send_sem=sum_send.at[s - 1],
            recv_sem=sum_recv.at[s - 1],
            device_id={"tensor": right},
            device_id_type=MESH,
        )

    def keep(s):
        return pltpu.make_async_copy(turned.at[0], part_of(rows_t, s), keep_sem)

    def mixed_store(s):
        return pltpu.make_async_copy(mixed_stage, mixed_all[s], mixed_sem)

    def chunk(s, carry):
        @pl.when(s > 0)
        def _():
            pass_rows(s - 1).wait_recv()

        @pl.when(s < ring - 1)
        def _():
            pass_rows(s).start()

        @pl.when(s > 0)
        def _():
            keep(s - 1).wait()
            grad_keep(s - 1).wait()

        turned[0] = held[s].T
        keep(s).start()
        for k in range(ring):

            @pl.when(s == k)
            def _(k=k):
                grad_wait(k)
                if k < ring - 1:
                    grad_load(k + 1)

        slot = lax.rem(s, 2)
        turned[1] = grads_held[slot].T
        grad_keep(s).start()
        acc_n[...] = jnp.zeros_like(acc_n)
        acc_m[...] = jnp.zeros_like(acc_m)

        def body(w_gate, w_up, w_down, act, grad_gate, grad_up):
            rows = held[s]
            gate = dot_nn(rows, w_gate[...])
            up = dot_nn(rows, w_up[...])
            grad_act = dot_nn(grads_held[slot], w_down[...])
            sig = 1.0 / (1.0 + jnp.exp(-gate))
            silu = gate * sig
            low_act = (silu * up).astype(bf16)
            low_up = (grad_act * silu).astype(bf16)
            low_gate = (grad_act * up * sig * (1.0 + gate * (1.0 - sig))).astype(bf16)
            act[...] = low_act
            grad_gate[...] = low_gate
            grad_up[...] = low_up
            acc_m[...] += dot_nt(low_act, w_down[...])
            acc_n[...] += dot_nt(low_gate, w_gate[...]) + dot_nt(low_up, w_up[...])

        width, count = own_rows.shape[1], own_rows.shape[0]
        pltpu.emit_pipeline(
            body,
            grid=(tiles,),
            in_specs=[
                pl.BlockSpec((width, tile), lambda k: (0, k)),
                pl.BlockSpec((width, tile), lambda k: (0, k + tiles)),
                pl.BlockSpec((width, tile), lambda k: (0, k + 2 * tiles)),
            ],
            out_specs=[
                pl.BlockSpec((count, tile), lambda k: (0, k)),
                pl.BlockSpec((count, tile), lambda k: (0, k)),
                pl.BlockSpec((count, tile), lambda k: (0, k + tiles)),
            ],
        )(weights, weights, weights, act_all.at[s], grads_all.at[s], grads_all.at[s])

        @pl.when(s > 0)
        def _():
            mixed_store(0).wait()

        mixed_stage[...] = acc_m[...].astype(bf16)
        for k in range(ring):

            @pl.when(s == k)
            def _(k=k):
                mixed_store(k).start()

        @pl.when(s == 0)
        def _():
            first_part[...] = acc_n[...]

        @pl.when(s == 1)
        def _():
            outgoing[0] = acc_n[...].astype(bf16)

        @pl.when(s > 1)
        def _():
            pass_sum(s - 1).wait_recv()
            outgoing[s - 1] = (acc_n[...] + arrived[s - 2].astype(f32)).astype(bf16)

        @pl.when(s > 0)
        def _():
            pass_sum(s).start()

        return carry

    lax.fori_loop(0, ring, chunk, 0)
    mixed_store(0).wait()
    pass_sum(ring - 1).wait_recv()
    final_stage[...] = (first_part[...] + arrived[ring - 2].astype(f32)).astype(bf16)
    final = pltpu.make_async_copy(final_stage, grad_own, final_sem)
    final.start()

    def settle(s, carry):
        @pl.when(s < ring - 1)
        def _():
            pass_rows(s).wait_send()

        @pl.when(s > 0)
        def _():
            pass_sum(s).wait_send()

        return carry

    lax.fori_loop(0, ring, settle, 0)
    keep(ring - 1).wait()
    grad_keep(ring - 1).wait()
    final.wait()


def feed(own_rows, grad_rows, weights, ring, tile=256, collective_id=7):
    count, width = own_rows.shape
    hidden = weights.shape[1] // 3
    any_spec = pl.BlockSpec(memory_space=pl.ANY)
    dma = pltpu.SemaphoreType.DMA
    return pl.pallas_call(
        functools.partial(feed_kernel, ring, min(tile, hidden)),
        out_shape=[
            jax.ShapeDtypeStruct((width, ring * count), bf16),
            jax.ShapeDtypeStruct((width, ring * count), bf16),
            jax.ShapeDtypeStruct((ring, count, hidden), bf16),
            jax.ShapeDtypeStruct((ring, count, 2 * hidden), bf16),
        ]
        + [jax.ShapeDtypeStruct((count, width), bf16)] * (ring + 1),
        in_specs=[any_spec] * (1 + 2 * ring),
        out_specs=[any_spec] * (5 + ring),
        scratch_shapes=[
            pltpu.VMEM((ring, count, width), bf16),
            pltpu.VMEM((2, count, width), bf16),
            pltpu.VMEM((count, width), f32),
            pltpu.VMEM((count, width), f32),
            pltpu.VMEM((count, width), f32),
            pltpu.VMEM((ring - 1, count, width), bf16),
            pltpu.VMEM((ring - 1, count, width), bf16),
            pltpu.VMEM((count, width), bf16),
            pltpu.VMEM((count, width), bf16),
            pltpu.VMEM((2, width, count), bf16),
            dma,
            dma,
            dma((2,)),
            dma,
            dma,
            dma((ring - 1,)),
            dma((ring - 1,)),
            dma((ring - 1,)),
            dma((ring - 1,)),
            dma,
        ],
        compiler_params=pltpu.CompilerParams(
            collective_id=collective_id, has_side_effects=True, vmem_limit_bytes=64 * 1024 * 1024 - 65536,
        ),
        cost_estimate=pl.CostEstimate(
            flops=12 * ring * count * width * hidden,
            bytes_accessed=8 * ring * count * width,
            transcendentals=ring * count * hidden,
        ),
        name="feed_forward",
    )(own_rows, *grad_rows, weights)


def weigh_kernel(
    tp_count, dp_count, tile, grads, rows_t, grads_t, gate_up, act, slots, out,
    left, left_sem, own_sem, send, recv,
):
    count = dp_count * tp_count
    my_dp = lax.axis_index("dp")
    my_tp = lax.axis_index("tensor")
    me = my_dp * tp_count + my_tp
    page_rows = slots.shape[1]

    loads = [
        pltpu.make_async_copy(source, left.at[k], left_sem.at[k])
        for k, source in enumerate((rows_t, grads_t))
    ]
    for load in loads:
        load.start()

    barrier = pltpu.get_barrier_semaphore()

    def place(peer):
        return {"dp": lax.div(peer, tp_count), "tensor": lax.rem(peer, tp_count)}

    def greet(j, carry):
        peer = lax.rem(me + j, count)
        pl.semaphore_signal(barrier, inc=1, device_id=place(peer), device_id_type=MESH)
        return carry

    lax.fori_loop(1, count, greet, 0)
    pl.semaphore_wait(barrier, count - 1)

    home = slots.at[my_tp * dp_count + my_dp]

    def block(p_dp, p_tp):
        return grads.at[p_tp, pl.ds(p_dp * page_rows, page_rows), :]

    own = pltpu.make_async_copy(block(my_dp, my_tp), home, own_sem)
    own.start()

    def copy_to(j):
        peer = lax.rem(me + j, count)
        return pltpu.make_async_remote_copy(
            src_ref=block(lax.div(peer, tp_count), lax.rem(peer, tp_count)),
            dst_ref=home,
            send_sem=send.at[j],
            recv_sem=recv.at[j],
            device_id=place(peer),
            device_id_type=MESH,
        )

    def start(j, carry):
        copy_to(j).start()
        return carry

    def finish(j, carry):
        copy_to(j).wait()
        return carry

    lax.fori_loop(1, count, start, 0)

    width = rows_t.shape[0]
    step = min(512, width)

    def multiply(k, right, first):
        ring, rows, cols = right.shape

        def body(part, result):
            values = part[...].reshape(ring * rows, tile)
            for m in range(0, width, step):
                result[m : m + step, :] = dot_nn(left[k, m : m + step, :], values).astype(bf16)

        pltpu.emit_pipeline(
            body,
            grid=(cols // tile,),
            in_specs=[pl.BlockSpec((ring, rows, tile), lambda n: (0, 0, n))],
            out_specs=[pl.BlockSpec((width, tile), lambda n: (0, n + first))],
        )(right, out)

    loads[0].wait()
    multiply(0, gate_up, 0)
    loads[1].wait()
    multiply(1, act, gate_up.shape[2] // tile)
    own.wait()
    lax.fori_loop(1, count, finish, 0)


def weigh(grads, rows_t, grads_t, gate_up, act, tp_count, dp_count, collective_id):
    count = tp_count * dp_count
    cols = grads.shape[2]
    page_rows = grads.shape[1] // dp_count
    width, rows = rows_t.shape
    hidden = act.shape[2]
    any_spec = pl.BlockSpec(memory_space=pl.ANY)
    dma = pltpu.SemaphoreType.DMA
    return pl.pallas_call(
        functools.partial(weigh_kernel, tp_count, dp_count, min(512, hidden)),
        out_shape=[
            jax.ShapeDtypeStruct((count, page_rows, cols), bf16),
            jax.ShapeDtypeStruct((width, 3 * hidden), bf16),
        ],
        in_specs=[pl.BlockSpec(memory_space=pltpu.HBM)] * 5,
        out_specs=[any_spec] * 2,
        scratch_shapes=[
            pltpu.VMEM((2, width, rows), bf16),
            dma((2,)),
            dma,
            dma((count,)),
            dma((count,)),
        ],
        compiler_params=pltpu.CompilerParams(
            collective_id=collective_id, has_side_effects=True, vmem_limit_bytes=62 * 1024 * 1024
        ),
        cost_estimate=pl.CostEstimate(
            flops=6 * rows * width * hidden,
            bytes_accessed=2 * width * (2 * rows + 3 * hidden),
            transcendentals=0,
        ),
        name="weigh",
    )(grads, rows_t, grads_t, gate_up, act)


def flip(index, bit):
    return index + bit - 2 * bit * lax.rem(lax.div(index, bit), 2)


def collect_kernel(
    tp_count, dp_count, shard, second, gains, chunk, out, second_out, gains_out, from_left, from_right,
    second_send, second_recv, own_sem, ring_send, ring_recv, send, recv, gain_send, gain_recv, chunk_send, chunk_recv,
):
    my_dp = lax.axis_index("dp")
    my_tp = lax.axis_index("tensor")
    rows = shard.shape[0]
    half = rows // 2
    bits = [1 << b for b in reversed(range(dp_count.bit_length() - 1))]
    orders = [bits, bits[:-1][::-1] + bits[-1:]]
    steps = len(bits)

    barrier = pltpu.get_barrier_semaphore()
    for j in range(1, tp_count):
        pl.semaphore_signal(
            barrier, inc=1, device_id={"tensor": lax.rem(my_tp + j, tp_count)}, device_id_type=MESH
        )
    for j in range(1, dp_count):
        pl.semaphore_signal(
            barrier, inc=1, device_id={"dp": lax.rem(my_dp + j, dp_count)}, device_id_type=MESH
        )
    pl.semaphore_wait(barrier, tp_count + dp_count - 2)

    home = out.at[my_tp, pl.ds(my_dp * rows, rows), :]
    own = pltpu.make_async_copy(shard, home, own_sem.at[0])
    own.start()
    own_gain = pltpu.make_async_copy(gains, gains_out.at[my_dp], own_sem.at[1])
    own_gain.start()
    own_second = pltpu.make_async_copy(second, second_out.at[my_tp], own_sem.at[2])
    own_second.start()

    def second_copy(j):
        return pltpu.make_async_remote_copy(
            src_ref=second,
            dst_ref=second_out.at[my_tp],
            send_sem=second_send.at[j],
            recv_sem=second_recv.at[j],
            device_id={"tensor": lax.rem(my_tp + j, tp_count)},
            device_id_type=MESH,
        )

    def across(j):
        return pltpu.make_async_remote_copy(
            src_ref=shard,
            dst_ref=home,
            send_sem=ring_send.at[j],
            recv_sem=ring_recv.at[j],
            device_id={"tensor": lax.rem(my_tp + j, tp_count)},
            device_id_type=MESH,
        )

    def gain_copy(j):
        return pltpu.make_async_remote_copy(
            src_ref=gains,
            dst_ref=gains_out.at[my_dp],
            send_sem=gain_send.at[j],
            recv_sem=gain_recv.at[j],
            device_id={"dp": lax.rem(my_dp + j, dp_count)},
            device_id_type=MESH,
        )

    def step(way):
        return pltpu.make_async_remote_copy(
            src_ref=chunk,
            dst_ref=(from_left, from_right)[way],
            send_sem=chunk_send.at[way],
            recv_sem=chunk_recv.at[way],
            device_id={"tensor": lax.rem(my_tp + (1, tp_count - 1)[way], tp_count)},
            device_id_type=MESH,
        )

    has_right, has_left = my_tp < tp_count - 1, my_tp > 0

    def within(j, s, k, m):
        order = orders[s]
        owner = my_dp
        for b in range(k):
            if m >> b & 1:
                owner = flip(owner, order[b])
        block = out.at[
            lax.rem(my_tp - j + tp_count, tp_count), pl.ds(owner * rows + s * half, half), :
        ]
        at = (1 << k) - 1 + m
        return pltpu.make_async_remote_copy(
            src_ref=block,
            dst_ref=block,
            send_sem=send.at[j, s, at],
            recv_sem=recv.at[j, s, at],
            device_id={"dp": flip(my_dp, order[k])},
            device_id_type=MESH,
        )

    for j in range(1, tp_count):
        across(j).start()
    for j in range(1, dp_count):
        gain_copy(j).start()

    @pl.when(has_right)
    def _():
        step(0).start()

    @pl.when(has_left)
    def _():
        step(1).start()

    own.wait()
    for phase in range(tp_count + steps):
        for k in reversed(range(steps + 1)):
            j = phase - k
            if not 0 <= j < tp_count:
                continue
            if k == 0:
                if j > 0:
                    across(j).wait_recv()
            else:
                for s in range(2):
                    for m in range(1 << (k - 1)):
                        within(j, s, k - 1, m).wait_recv()
            if k < steps:
                for s in range(2):
                    for m in range(1 << k):
                        within(j, s, k, m).start()
        if phase == tp_count:
            for j in range(1, tp_count):
                second_copy(j).start()
    for j in range(tp_count):
        if j > 0:
            across(j).wait_send()
        for s in range(2):
            for k in range(steps):
                for m in range(1 << k):
                    within(j, s, k, m).wait_send()
    own_gain.wait()
    own_second.wait()
    for j in range(1, tp_count):
        second_copy(j).wait()
    for j in range(1, dp_count):
        gain_copy(j).wait()

    @pl.when(has_right)
    def _():
        step(0).wait_send()
        step(1).wait_recv()

    @pl.when(has_left)
    def _():
        step(1).wait_send()
        step(0).wait_recv()


def collect(shard, second, gains, chunk, tp_count, dp_count, collective_id):
    rows, cols = shard.shape
    dma = pltpu.SemaphoreType.DMA
    vmem_spec = pl.BlockSpec(memory_space=pltpu.VMEM)
    any_spec = pl.BlockSpec(memory_space=pl.ANY)
    return pl.pallas_call(
        functools.partial(collect_kernel, tp_count, dp_count),
        out_shape=[
            jax.ShapeDtypeStruct((tp_count, dp_count * rows, cols), shard.dtype),
            jax.ShapeDtypeStruct((tp_count,) + second.shape, second.dtype),
            jax.ShapeDtypeStruct((dp_count,) + gains.shape, gains.dtype),
            jax.ShapeDtypeStruct(chunk.shape, chunk.dtype),
            jax.ShapeDtypeStruct(chunk.shape, chunk.dtype),
        ],
        in_specs=[vmem_spec, vmem_spec, vmem_spec, any_spec],
        out_specs=[any_spec] * 5,
        scratch_shapes=[
            dma((tp_count,)),
            dma((tp_count,)),
            dma((3,)),
            dma((tp_count,)),
            dma((tp_count,)),
            dma((tp_count, 2, dp_count - 1)),
            dma((tp_count, 2, dp_count - 1)),
            dma((dp_count,)),
            dma((dp_count,)),
            dma((2,)),
            dma((2,)),
        ],
        compiler_params=pltpu.CompilerParams(collective_id=collective_id, has_side_effects=True),
        cost_estimate=pl.CostEstimate(
            flops=0, bytes_accessed=16 * tp_count * dp_count * shard.size, transcendentals=0
        ),
        name="collect",
    )(shard, second, gains, chunk)


def spread_kernel(rows, weight, out):
    out[0] = dot_nn(rows[...], weight[0]).astype(out.dtype)


def spread(rows, weights, part, cols):
    shards, width, _ = weights.shape
    count = rows.shape[0]
    return pl.pallas_call(
        spread_kernel,
        grid=(shards,),
        in_specs=[
            pl.BlockSpec((count, width), lambda t: (0, 0)),
            pl.BlockSpec((1, width, cols), lambda t: (t, 0, part)),
        ],
        out_specs=pl.BlockSpec((1, count, cols), lambda t: (t, 0, 0)),
        out_shape=jax.ShapeDtypeStruct((shards, count, cols), bf16),
        cost_estimate=pl.CostEstimate(
            flops=2 * shards * count * width * cols,
            bytes_accessed=2 * shards * width * cols,
            transcendentals=0,
        ),
        name="spread",
    )(rows, weights)


def gather_kernel(has_begin, part, weight, *refs):
    out = refs[-1]

    @pl.when(pl.program_id(0) == 0)
    def _():
        out[...] = refs[0][...] if has_begin else jnp.zeros_like(out)

    out[...] += dot_nt(part[0], weight[0])


def gather_sum(parts, weights, part, begin):
    shards, count, cols = parts.shape
    width = weights.shape[1]
    whole = pl.BlockSpec((count, width), lambda t: (0, 0))
    begins = [] if begin is None else [begin]
    return pl.pallas_call(
        functools.partial(gather_kernel, begin is not None),
        grid=(shards,),
        in_specs=[
            pl.BlockSpec((1, count, cols), lambda t: (t, 0, 0)),
            pl.BlockSpec((1, width, cols), lambda t: (t, 0, part)),
        ]
        + [whole] * len(begins),
        out_specs=whole,
        out_shape=jax.ShapeDtypeStruct((count, width), f32),
        cost_estimate=pl.CostEstimate(
            flops=2 * shards * count * width * cols,
            bytes_accessed=2 * shards * width * cols,
            transcendentals=0,
        ),
        name="gather_sum",
    )(parts, weights, *begins)


def outer_kernel(rows, *refs):
    parts, out, turned = refs[:-2], refs[-2], refs[-1]

    @pl.when(pl.program_id(0) == 0)
    def _():
        turned[...] = rows[...].T

    at = 0
    for part in parts:
        cols = part.shape[2]
        out[:, at : at + cols] = dot_nn(turned[...], part[0]).astype(out.dtype)
        at += cols


def outer(rows, parts):
    shards, count, _ = parts[0].shape
    cols = sum(part.shape[2] for part in parts)
    width = rows.shape[1]
    return pl.pallas_call(
        outer_kernel,
        grid=(shards,),
        in_specs=[pl.BlockSpec((count, width), lambda t: (0, 0))]
        + [pl.BlockSpec((1, count, part.shape[2]), lambda t: (t, 0, 0)) for part in parts],
        out_specs=pl.BlockSpec((width, cols), lambda t: (0, t)),
        out_shape=jax.ShapeDtypeStruct((width, shards * cols), bf16),
        scratch_shapes=[pltpu.VMEM((width, count), bf16)],
        cost_estimate=pl.CostEstimate(
            flops=2 * shards * count * width * cols,
            bytes_accessed=2 * shards * width * cols,
            transcendentals=0,
        ),
        name="outer",
    )(rows, *parts)


def total_kernel(
    tp_count, dp_count, groups, rows, *refs
):
    parts = refs[:groups]
    (
        to_right, to_left, weights, out, grad_rows, from_sides,
        turned, mine, got, got_across, held, load_sem, send, recv,
        across_send, across_recv, chunk_send, chunk_recv,
    ) = refs[groups:]
    my_dp = lax.axis_index("dp")
    my_tp = lax.axis_index("tensor")
    own_rows = out.shape[0]
    half = own_rows // 2
    bits = [1 << b for b in range(dp_count.bit_length() - 1)]
    orders = [bits, bits[:1] + bits[1:][::-1]]
    steps = len(bits)

    def shard_of(j):
        return lax.rem(my_tp + 1 + j, tp_count)

    def load(j):
        return pltpu.make_async_copy(weights.at[shard_of(j)], held.at[j % 2], load_sem.at[j % 2])

    load(0).start()
    barrier = pltpu.get_barrier_semaphore()
    for j in range(1, tp_count):
        pl.semaphore_signal(
            barrier, inc=1, device_id={"tensor": lax.rem(my_tp + j, tp_count)}, device_id_type=MESH
        )
    for bit in bits:
        pl.semaphore_signal(
            barrier, inc=1, device_id={"dp": flip(my_dp, bit)}, device_id_type=MESH
        )
    pl.semaphore_wait(barrier, tp_count - 1 + steps)

    def step(way):
        return pltpu.make_async_remote_copy(
            src_ref=(to_right, to_left)[way],
            dst_ref=from_sides.at[way],
            send_sem=chunk_send.at[way],
            recv_sem=chunk_recv.at[way],
            device_id={"tensor": lax.rem(my_tp + (1, tp_count - 1)[way], tp_count)},
            device_id_type=MESH,
        )

    has_right, has_left = my_tp < tp_count - 1, my_tp > 0

    @pl.when(has_right)
    def _():
        step(0).start()

    @pl.when(has_left)
    def _():
        step(1).start()

    def block(j, s, owner):
        return j, pl.ds(pl.multiple_of(owner * own_rows + s * half, half), half)

    def place(k, m):
        return sum(1 << (steps - 1 - e) for e in range(k)) + m

    def fellow(s, k, m, start):
        owner = start
        for b in range(steps - 1 - k):
            if m >> b & 1:
                owner = flip(owner, orders[s][k + 1 + b])
        return owner

    def exchange_part(j, s, k, m):
        partner = flip(my_dp, orders[s][k])
        at = place(k, m)
        index, span = block(j, s, fellow(s, k, m, partner))
        return pltpu.make_async_remote_copy(
            src_ref=mine.at[index, span, :],
            dst_ref=got.at[j, s, at],
            send_sem=send.at[j, s, at],
            recv_sem=recv.at[j, s, at],
            device_id={"dp": partner},
            device_id_type=MESH,
        )

    def across(j):
        return pltpu.make_async_remote_copy(
            src_ref=mine.at[j, pl.ds(pl.multiple_of(my_dp * own_rows, own_rows), own_rows), :],
            dst_ref=got_across.at[j],
            send_sem=across_send.at[j],
            recv_sem=across_recv.at[j],
            device_id={"tensor": shard_of(j)},
            device_id_type=MESH,
        )

    def every(k):
        return [(s, m) for s in range(2) for m in range(1 << (steps - 1 - k))]

    turned[...] = rows[...].T
    for phase in range(tp_count + steps + 1):
        if phase < tp_count:
            shard = shard_of(phase)
            at = 0
            load(phase).wait()
            if phase + 1 < tp_count:
                load(phase + 1).start()
            for g, part in enumerate(parts):
                cols = part.shape[2]
                value = part[shard]
                mine[phase, :, at : at + cols] = dot_nn(turned[...], value).astype(bf16)
                product = dot_nt(value, held[phase % 2, :, at : at + cols])
                if phase == 0 and g == 0:
                    grad_rows[...] = product
                else:
                    grad_rows[...] += product
                at += cols
        for k in reversed(range(steps + 1)):
            j = phase - k
            if not 0 <= j < tp_count:
                continue
            if k > 0:
                for s, m in every(k - 1):
                    exchange_part(j, s, k - 1, m).wait_recv()
                    index, span = block(j, s, fellow(s, k - 1, m, my_dp))
                    mine[index, span, :] = (
                        mine[index, span, :].astype(f32)
                        + got[j, s, place(k - 1, m)].astype(f32)
                    ).astype(bf16)
            if k < steps:
                for s, m in every(k):
                    exchange_part(j, s, k, m).start()
            elif j < tp_count - 1:
                across(j).start()
    total = mine[
        tp_count - 1, pl.ds(pl.multiple_of(my_dp * own_rows, own_rows), own_rows), :
    ].astype(f32)
    for j in range(tp_count - 1):
        across(j).wait_recv()
        total += got_across[j].astype(f32)
    out[...] = total

    @pl.when(has_right)
    def _():
        step(0).wait_send()
        step(1).wait_recv()

    @pl.when(has_left)
    def _():
        step(1).wait_send()
        step(0).wait_recv()

    for j in range(tp_count):
        if j < tp_count - 1:
            across(j).wait_send()
        for k in range(steps):
            for s, m in every(k):
                exchange_part(j, s, k, m).wait_send()


def total_grads(rows, parts, to_right, to_left, weights, dp_count, collective_id):
    tp_count, width, cols = weights.shape
    count = rows.shape[0]
    own_rows = width // dp_count
    vmem_spec = pl.BlockSpec(memory_space=pltpu.VMEM)
    any_spec = pl.BlockSpec(memory_space=pl.ANY)
    dma = pltpu.SemaphoreType.DMA
    return pl.pallas_call(
        functools.partial(total_kernel, tp_count, dp_count, len(parts)),
        out_shape=[
            jax.ShapeDtypeStruct((own_rows, cols), f32),
            jax.ShapeDtypeStruct((count, width), f32),
            jax.ShapeDtypeStruct((2, count, width), bf16),
        ],
        in_specs=[vmem_spec] * (1 + len(parts)) + [any_spec] * 3,
        out_specs=[vmem_spec, vmem_spec, any_spec],
        scratch_shapes=[
            pltpu.VMEM((width, count), bf16),
            pltpu.VMEM((tp_count, width, cols), bf16),
            pltpu.VMEM((tp_count, 2, dp_count - 1, own_rows // 2, cols), bf16),
            pltpu.VMEM((tp_count - 1, own_rows, cols), bf16),
            pltpu.VMEM((2, width, cols), bf16),
            dma((2,)),
            dma((tp_count, 2, dp_count - 1)),
            dma((tp_count, 2, dp_count - 1)),
            dma((tp_count,)),
            dma((tp_count,)),
            dma((2,)),
            dma((2,)),
        ],
        compiler_params=pltpu.CompilerParams(
            collective_id=collective_id, has_side_effects=True, vmem_limit_bytes=62 * 1024 * 1024
        ),
        cost_estimate=pl.CostEstimate(
            flops=4 * tp_count * count * width * cols,
            bytes_accessed=16 * tp_count * width * cols,
            transcendentals=0,
        ),
        name="total_grads",
    )(rows, *parts, to_right, to_left, weights)


def rms_scale(hidden):
    return lax.rsqrt(jnp.mean(hidden * hidden, axis=1, keepdims=True) + epsilon)


def norm_back(grad_norm, hidden, scale_rows, gain):
    normed = hidden * scale_rows
    gain_part = jnp.sum(grad_norm * normed, axis=0)
    inner = grad_norm * gain
    grad_hidden = scale_rows * (inner - normed * jnp.mean(inner * normed, axis=1, keepdims=True))
    return (grad_hidden, gain_part)


def after(value, other):
    return lax.optimization_barrier((value, other))[0]


def local(
    tokens,
    upstream,
    lengths,
    positions,
    pages,
    attn_gain,
    w_query,
    w_key,
    w_value,
    w_out,
    mlp_gain,
    w_gate,
    w_up,
    w_down,
):
    dp_count = lax.axis_size("dp")
    tp_count = lax.axis_size("tensor")
    dp_index = lax.axis_index("dp")
    tp_index = lax.axis_index("tensor")
    tok_dev, width = tokens.shape
    tok_group = tok_dev * tp_count
    page_rows = tok_dev // dp_count
    group_pages = tp_count * dp_count
    page_count = pages.shape[0]
    device = dp_index * tp_count + tp_index
    everyone = ("tensor", "dp")

    local_ids = jnp.arange(dp_count, dtype=jnp.int32)
    inverse = (
        jnp.zeros((page_count,), jnp.int32).at[pages].set(jnp.arange(page_count, dtype=jnp.int32))
    )
    dealt = lax.dynamic_slice_in_dim(inverse, device * dp_count, dp_count)
    dest_group = dealt // group_pages
    send_order = jnp.zeros((dp_count,), jnp.int32).at[dest_group].set(local_ids)
    group_sources = lax.dynamic_slice_in_dim(pages, dp_index * group_pages, group_pages)
    perm = (
        (jnp.arange(group_pages, dtype=jnp.int32) // dp_count) * dp_count
        + group_sources // group_pages
    ).astype(jnp.int32)

    def reorder(rows, order):
        blocks = rows.reshape(dp_count, page_rows, rows.shape[1])
        return jnp.take(blocks, order, axis=0, mode="clip").reshape(rows.shape)

    hidden_in = reorder(tokens, send_order).astype(f32)
    grad_top = reorder(upstream, send_order).astype(f32)
    seq_lens = lengths[0]
    seq_ends = jnp.cumsum(seq_lens)
    place = (jnp.take(dealt, send_order, mode="clip") % group_pages) * page_rows
    place_rows = (place[:, None] + jnp.arange(page_rows, dtype=jnp.int32)[None, :]).reshape(-1)
    valid_rows = (place_rows < seq_ends[-1]).astype(f32)[:, None]

    row_ids = jnp.arange(tok_group, dtype=jnp.int32)
    begin = jnp.max(
        jnp.where(row_ids[:, None] >= seq_ends[None, :], seq_ends[None, :], 0), axis=1
    ).astype(jnp.int32)
    block_len = min(block_rows, tok_group)
    first_block = begin[::block_len] // min(key_rows, tok_group)
    begin = begin[None, :]
    inverse_freq = theta_base ** (-(jnp.arange(HALF, dtype=f32) * 2.0) / HD)
    angles = inverse_freq[:, None] * positions.astype(f32)
    cos_t, sin_t = jnp.cos(angles), jnp.sin(angles)

    q_cols, kv_cols = w_query.shape[1], w_key.shape[1]
    kv_heads = kv_cols // HD
    per_group = q_cols // kv_cols
    group_q = per_group * HD
    groups = range(kv_heads)
    qkv_shard = jnp.concatenate(
        [
            part
            for g in groups
            for part in (
                w_query[:, g * group_q : (g + 1) * group_q],
                w_key[:, g * HD : (g + 1) * HD],
                w_value[:, g * HD : (g + 1) * HD],
            )
        ],
        axis=1,
    )

    def trade(value):
        blocks = value.reshape(group_pages, page_rows, value.shape[-1])
        return lax.all_to_all(blocks, everyone, split_axis=0, concat_axis=0, tiled=True)

    def trade_back(value):
        return trade(value).reshape(tp_count, tok_dev, value.shape[-1])

    def pass_on(values, first, last):
        return (
            lax.ppermute(values[0], "tensor", [(t, t + 1) for t in range(*first)]),
            lax.ppermute(values[1], "tensor", [(t, t - 1) for t in range(*last)]),
        )

    grad_out = grad_top * valid_rows
    own_chunk = grad_out.astype(bf16)
    mlp_shard = jnp.concatenate([w_gate, w_up, w_down.T], axis=1)
    w_qkv, out_shards, gains, *sides = collect(
        qkv_shard, w_out.T, jnp.stack([attn_gain, mlp_gain]), own_chunk, tp_count, dp_count, 1
    )
    w_out_t = lax.all_gather(out_shards, "dp", axis=1, tiled=True)
    w_mlp = lax.all_gather(after(mlp_shard, gains), "dp", axis=0, tiled=True)
    chunks = [(sides[0], sides[1])]
    gains = gains.transpose(1, 0, 2).reshape(2, -1).astype(f32)
    gain_one, gain_two = gains[0], gains[1]

    scale_one = rms_scale(hidden_in)
    normed_one = (hidden_in * scale_one * gain_one).astype(bf16)
    slots = project(normed_one, w_qkv, dp_count, 3)
    for n in range(2, tp_count):
        passed = after(chunks[-1], slots) if n == 2 else chunks[-1]
        chunks.append(pass_on(passed, (n - 1, tp_count - 1), (1, tp_count - n + 1)))
    saved, mixed = [], []
    for g in groups:
        q_t, k_t, k_rows, v_t, v_rows = prepare(
            after(slots, (o_slots, w_out_t, chunks[1])) if g else slots, g, perm, cos_t, sin_t, per_group, 1
        )
        o_t, lse, o_slots = attend_forward(
            q_t, k_rows, v_t, begin, first_block, perm, page_rows, block_len
        )
        saved.append((q_t, k_rows, k_t, v_rows, o_t, lse))
        mixed.append(trade_back(after(o_slots, chunks[1]) if g else o_slots))
    hidden_mid = hidden_in
    mixed[-1] = after(mixed[-1], chunks[-1])
    for g in groups:
        hidden_mid = gather_sum(mixed[g], w_out_t, g, hidden_mid)

    scale_two = rms_scale(hidden_mid)
    normed_two = (hidden_mid * scale_two * gain_two).astype(bf16)
    grads_t, rows_t, inner_act, grad_gate_up, *partial_two, grad_normed_two = feed(
        normed_two, [own_chunk] + [c[0] for c in chunks] + [c[1] for c in chunks], w_mlp, tp_count
    )
    grad_normed_two = grad_normed_two.astype(f32)
    grad_mid_norm, gain_two_part = norm_back(grad_normed_two, hidden_mid, scale_two, gain_two)
    grad_mid = grad_out + grad_mid_norm

    def add_on(arrived, s):
        return tuple(
            (value.astype(f32) + partial_two[at].astype(f32)).astype(bf16)
            for value, at in zip(arrived, (s, tp_count - s))
        )

    def reduce_dp(grad):
        return lax.psum_scatter(grad.astype(bf16), "dp", scatter_dimension=0, tiled=True)

    def reduce_tensor(value):
        cols = value.shape[1] // tp_count
        total = lax.dynamic_slice_in_dim(value, tp_index * cols, cols, 1).astype(f32)
        for s in range(1, tp_count):
            target = lax.rem(tp_index + s, tp_count)
            block = lax.dynamic_slice_in_dim(value, target * cols, cols, 1)
            pairs = [(t, (t + s) % tp_count) for t in range(tp_count)]
            total = total + lax.ppermute(block, "tensor", pairs).astype(f32)
        return total

    grad_z = grad_mid.astype(bf16)
    grad_wout = outer(grad_z, mixed)
    sum_out = reduce_dp(grad_wout)
    grad_slots, grad_wmlp = weigh(
        spread(after(grad_z, grad_wout), w_out_t, 0, q_cols),
        rows_t, grads_t, grad_gate_up, inner_act, tp_count, dp_count, 2,
    )
    sum_mlp = reduce_dp(grad_wmlp)
    first_part = after((partial_two[1], partial_two[tp_count - 1]), grad_slots)
    passing = pass_on(first_part, (0, 1), (tp_count - 1, tp_count))
    grad_qkv = []
    for g in groups:
        q_t, k_rows, k_t, v_rows, o_t, lse = saved[g]
        back = attend_backward(
            after(grad_slots, (back, sum_out) if g else first_part), g, q_t, k_rows, k_t, v_rows,
            o_t, lse, begin, cos_t, sin_t, first_block, perm, page_rows, block_len,
        )
        if g == len(groups) - 1:
            steps = 2
            if tp_count > 3:
                passing = pass_on(add_on(passing, 2), (0, 2), (tp_count - 2, tp_count))
                steps = 3
            grad_qkv = [after(value, passing) for value in grad_qkv]
        grad_qkv.append(trade_back(back))
    hidden = sum_mlp.shape[1] // 3
    for s in range(steps, tp_count - 1):
        passing = pass_on(add_on(passing, s), (0, s), (tp_count - s, tp_count))
    passing = add_on(passing, tp_count - 1)
    sum_qkv, grad_normed_one, sides = total_grads(
        normed_one, grad_qkv, passing[0], passing[1], w_qkv, dp_count, 4
    )
    branch_two = jnp.where(tp_index > 0, sides[0].astype(f32), 0.0)
    branch_two += jnp.where(tp_index < tp_count - 1, sides[1].astype(f32), 0.0)
    each = group_q + 2 * HD
    sum_qkv = [sum_qkv[:, g * each : (g + 1) * each] for g in groups]
    sum_out = reduce_tensor(after(sum_out, grad_normed_one))
    result = (
        (after(hidden_mid, back) + branch_two + partial_two[0].astype(f32)) * valid_rows
    ).astype(bf16)
    grad_in_norm, gain_one_part = norm_back(grad_normed_one, hidden_in, scale_one, gain_one)
    grad_in = (grad_mid + grad_in_norm).astype(bf16)

    gain_parts = jnp.stack([gain_one_part, gain_two_part]).reshape(2, dp_count, -1)
    gain_parts = jnp.broadcast_to(
        gain_parts.transpose(1, 0, 2)[None], (tp_count, dp_count, 2, gain_parts.shape[2])
    ).reshape(group_pages, 2, -1)
    gain_sums = jnp.sum(
        lax.all_to_all(gain_parts, everyone, split_axis=0, concat_axis=0, tiled=True), axis=0
    )
    return (
        reorder(result, dest_group),
        reorder(grad_in, dest_group),
        gain_sums[0],
        jnp.concatenate([part[:, :group_q] for part in sum_qkv], axis=1),
        jnp.concatenate([part[:, group_q : group_q + HD] for part in sum_qkv], axis=1),
        jnp.concatenate([part[:, group_q + HD :] for part in sum_qkv], axis=1),
        sum_out.T,
        gain_sums[1],
        sum_mlp[:, :hidden].astype(f32),
        sum_mlp[:, hidden : 2 * hidden].astype(f32),
        sum_mlp[:, 2 * hidden :].astype(f32).T,
    )


def solution(mesh):
    rows = P(("dp", "tensor"), None)
    weight = P("dp", "tensor")
    weight_t = P("tensor", "dp")
    return jax.shard_map(
        local,
        mesh=mesh,
        in_specs=(
            rows,
            rows,
            P("dp", None),
            P("dp", None),
            P(),
            P("dp"),
            weight,
            weight,
            weight,
            weight_t,
            P("dp"),
            weight,
            weight,
            weight_t,
        ),
        out_specs=(
            rows,
            rows,
            P("dp"),
            weight,
            weight,
            weight,
            weight_t,
            P("dp"),
            weight,
            weight,
            weight_t,
        ),
        check_vma=False,
    )
```

```python
import functools

import jax
import jax.numpy as jnp
from jax import lax
from jax.experimental import pallas as pl
from jax.experimental.pallas import tpu as pltpu
from jax.sharding import PartitionSpec as P

HD = 64
HALF = HD // 2

epsilon = 1e-05
theta_base = 500000.0
masked_score = -1e30
score_scale = HD**-0.5
block_rows = 512
key_rows = 256
MESH = pl.DeviceIdType.MESH
f32 = jnp.float32
bf16 = jnp.bfloat16


def dot_nn(left, right):
    return lax.dot_general(left, right, (((1,), (0,)), ((), ())), preferred_element_type=f32)


def dot_nt(left, right):
    return lax.dot_general(left, right, (((1,), (1,)), ((), ())), preferred_element_type=f32)


def dot_tn(left, right):
    return lax.dot_general(left, right, (((0,), (0,)), ((), ())), preferred_element_type=f32)


def prep_kernel(pages_per, q_heads, kv_heads, perm, *refs):
    page_refs = refs[:pages_per]
    cos_ref, sin_ref, q_t, k_t, k_rows, v_t, v_rows = refs[pages_per:]
    rows = jnp.concatenate([r[0].astype(f32) for r in page_refs], axis=0)
    turned = rows.T
    cos, sin = cos_ref[...], sin_ref[...]

    def rope(base):
        first, second = turned[base : base + HALF], turned[base + HALF : base + HD]
        return jnp.concatenate([first * cos - second * sin, second * cos + first * sin], axis=0)

    for h in range(q_heads):
        roped = rope(h * HD).astype(bf16)
        q_t[h * HD : (h + 1) * HD, :] = (roped.astype(f32) * score_scale).astype(bf16)
    k_base = q_heads * HD
    v_base = k_base + kv_heads * HD
    for g in range(kv_heads):
        roped = rope(k_base + g * HD)
        k_t[g * HD : (g + 1) * HD, :] = roped.astype(bf16)
        k_rows[g] = roped.T.astype(bf16)
        v_t[g * HD : (g + 1) * HD, :] = turned[v_base + g * HD : v_base + (g + 1) * HD].astype(bf16)
        v_rows[g] = rows[:, v_base + g * HD : v_base + (g + 1) * HD].astype(bf16)


def prepare(slots, part, perm, cos_t, sin_t, q_heads, kv_heads):
    page_rows = slots.shape[1]
    cols = (q_heads + 2 * kv_heads) * HD
    total_rows = slots.shape[0] * page_rows
    lanes = min(256, total_rows)
    pages_per = lanes // page_rows

    def page_spec(a):
        return pl.BlockSpec(
            (1, page_rows, cols), lambda i, perm_ref, a=a: (perm_ref[i * pages_per + a], 0, part)
        )

    table = pl.BlockSpec((HALF, lanes), lambda i, perm_ref: (0, i))
    return pl.pallas_call(
        functools.partial(prep_kernel, pages_per, q_heads, kv_heads),
        grid_spec=pltpu.PrefetchScalarGridSpec(
            num_scalar_prefetch=1,
            grid=(total_rows // lanes,),
            in_specs=[page_spec(a) for a in range(pages_per)] + [table, table],
            out_specs=[
                pl.BlockSpec((q_heads * HD, lanes), lambda i, perm_ref: (0, i)),
                pl.BlockSpec((kv_heads * HD, lanes), lambda i, perm_ref: (0, i)),
                pl.BlockSpec((kv_heads, lanes, HD), lambda i, perm_ref: (0, i, 0)),
                pl.BlockSpec((kv_heads * HD, lanes), lambda i, perm_ref: (0, i)),
                pl.BlockSpec((kv_heads, lanes, HD), lambda i, perm_ref: (0, i, 0)),
            ],
        ),
        out_shape=[
            jax.ShapeDtypeStruct((q_heads * HD, total_rows), bf16),
            jax.ShapeDtypeStruct((kv_heads * HD, total_rows), bf16),
            jax.ShapeDtypeStruct((kv_heads, total_rows, HD), bf16),
            jax.ShapeDtypeStruct((kv_heads * HD, total_rows), bf16),
            jax.ShapeDtypeStruct((kv_heads, total_rows, HD), bf16),
        ],
        cost_estimate=pl.CostEstimate(
            flops=8 * slots.size, bytes_accessed=6 * slots.size, transcendentals=0
        ),
        name="prepare",
    )(perm, *([slots] * pages_per), cos_t, sin_t)


def block_bias(i, j, begin_row, block_len, key_len):
    keys = j * key_len + lax.broadcasted_iota(jnp.int32, (key_len, block_len), 0)
    queries = i * block_len + lax.broadcasted_iota(jnp.int32, (key_len, block_len), 1)
    allowed = (keys >= begin_row) & (keys <= queries)
    return jnp.where(allowed, 0.0, masked_score)


def forward_kernel(
    q_heads, kv_heads, page_rows, first_block, perm,
    q_t, k_rows, v_t, begin, o_t, lse, o_slots, acc, stage, sems,
):
    i = pl.program_id(0)
    block_len = q_t.shape[1]
    key_len = min(key_rows, k_rows.shape[1])
    per_group = q_heads // kv_heads
    acc[...] = jnp.zeros_like(acc)
    begin_row = begin[...]

    def visit(j, carry):
        bias = block_bias(i, j, begin_row, block_len, key_len)
        at = pl.ds(pl.multiple_of(j * key_len, key_len), key_len)
        scores = [
            dot_nn(k_rows[h // per_group, at, :], q_t[h * HD : (h + 1) * HD, :]) + bias
            for h in range(q_heads)
        ]
        tops = [
            jnp.maximum(carry[h][0], jnp.max(scores[h], axis=0, keepdims=True))
            for h in range(q_heads)
        ]
        weights = [jnp.exp(scores[h] - tops[h]) for h in range(q_heads)]
        fades = [jnp.exp(carry[h][0] - tops[h]) for h in range(q_heads)]
        totals = [
            carry[h][1] * fades[h] + jnp.sum(weights[h], axis=0, keepdims=True)
            for h in range(q_heads)
        ]
        for h in range(q_heads):
            g = h // per_group
            span = slice(h * HD, (h + 1) * HD)
            acc[span, :] = acc[span, :] * fades[h] + dot_nn(
                v_t[g * HD : (g + 1) * HD, at], weights[h].astype(bf16)
            )
        return tuple(zip(tops, totals))

    start = tuple(
        (jnp.full((1, block_len), masked_score, f32), jnp.zeros((1, block_len), f32))
        for _ in range(q_heads)
    )
    stats = lax.fori_loop(
        first_block[i], lax.div((i + 1) * block_len - 1, key_len) + 1, visit, start
    )
    for h in range(q_heads):
        lse[h : h + 1, :] = stats[h][0] + jnp.log(stats[h][1])
    mixed = jnp.concatenate(
        [acc[h * HD : (h + 1) * HD, :] / stats[h][1] for h in range(q_heads)], axis=0
    )
    o_t[...] = mixed.astype(bf16)
    pages = block_len // page_rows
    stage[...] = mixed.T.astype(bf16).reshape(pages, page_rows, q_heads * HD)
    copies = [
        pltpu.make_async_copy(stage.at[a], o_slots.at[perm[i * pages + a]], sems.at[a])
        for a in range(pages)
    ]
    for copy in copies:
        copy.start()
    for copy in copies:
        copy.wait()


def attend_forward(q_t, k_rows, v_t, begin, first_block, perm, page_rows, block_len):
    total_rows = q_t.shape[1]
    kv_heads = k_rows.shape[0]
    q_heads = q_t.shape[0] // HD
    pages = block_len // page_rows
    return pl.pallas_call(
        functools.partial(forward_kernel, q_heads, kv_heads, page_rows),
        grid_spec=pltpu.PrefetchScalarGridSpec(
            num_scalar_prefetch=2,
            grid=(total_rows // block_len,),
            in_specs=[
                pl.BlockSpec((q_heads * HD, block_len), lambda i, *_: (0, i)),
                pl.BlockSpec((kv_heads, total_rows, HD), lambda i, *_: (0, 0, 0)),
                pl.BlockSpec((kv_heads * HD, total_rows), lambda i, *_: (0, 0)),
                pl.BlockSpec((1, block_len), lambda i, *_: (0, i)),
            ],
            out_specs=[
                pl.BlockSpec((q_heads * HD, block_len), lambda i, *_: (0, i)),
                pl.BlockSpec((q_heads, block_len), lambda i, *_: (0, i)),
                pl.BlockSpec(memory_space=pl.ANY),
            ],
            scratch_shapes=[
                pltpu.VMEM((q_heads * HD, block_len), f32),
                pltpu.VMEM((pages, page_rows, q_heads * HD), bf16),
                pltpu.SemaphoreType.DMA((pages,)),
            ],
        ),
        out_shape=[
            jax.ShapeDtypeStruct((q_heads * HD, total_rows), bf16),
            jax.ShapeDtypeStruct((q_heads, total_rows), f32),
            jax.ShapeDtypeStruct((total_rows // page_rows, page_rows, q_heads * HD), bf16),
        ],
        cost_estimate=pl.CostEstimate(
            flops=q_heads * total_rows * total_rows * HD,
            bytes_accessed=8 * q_t.size,
            transcendentals=q_heads * total_rows * total_rows // 4,
        ),
        name="attend_forward",
    )(first_block, perm, q_t, k_rows, v_t, begin)


def backward_kernel(
    q_heads, kv_heads, page_rows, pages, first_block, perm, *refs
):
    grad_pages = refs[:pages]
    (
        q_t, k_rows, k_t, v_rows, o_t, lse, begin, cos_ref, sin_ref, cos_all, sin_all,
        out, grad_q, grad_k, grad_v, stage, kv_stage, sems, kv_sems,
    ) = refs[pages:]
    i = pl.program_id(0)
    steps = pl.num_programs(0)
    block_len = q_t.shape[1]
    key_len = min(key_rows, k_rows.shape[1])
    per_group = q_heads // kv_heads
    q_cols = q_heads * HD
    kv_cols = kv_heads * HD

    @pl.when(i == 0)
    def _():
        grad_k[...] = jnp.zeros_like(grad_k)
        grad_v[...] = jnp.zeros_like(grad_v)

    grad_rows = jnp.concatenate([r[0].astype(f32) for r in grad_pages], axis=0)
    grad_t = grad_rows.T
    grad_low = grad_t.astype(bf16)
    inner = [
        jnp.sum(
            grad_t[h * HD : (h + 1) * HD] * o_t[h * HD : (h + 1) * HD, :].astype(f32),
            axis=0,
            keepdims=True,
        )
        for h in range(q_heads)
    ]
    grad_q[...] = jnp.zeros_like(grad_q)
    begin_row = begin[...]

    def visit(j, carry):
        bias = block_bias(i, j, begin_row, block_len, key_len)
        at = pl.ds(pl.multiple_of(j * key_len, key_len), key_len)
        for g in range(kv_heads):
            kv_span = slice(g * HD, (g + 1) * HD)
            keys, vals, keys_t = k_rows[g, at, :], v_rows[g, at, :], k_t[kv_span, at]
            heads = range(g * per_group, (g + 1) * per_group)
            spans = [slice(h * HD, (h + 1) * HD) for h in heads]
            scores = [dot_nn(keys, q_t[span, :]) + bias for span in spans]
            grad_probs = [dot_nn(vals, grad_low[span]) for span in spans]
            probs = [jnp.exp(s - lse[h : h + 1, :]) for s, h in zip(scores, heads)]
            grad_scores = [
                (p * (d - inner[h])).astype(bf16) for p, d, h in zip(probs, grad_probs, heads)
            ]
            low_probs = [p.astype(bf16) for p in probs]
            grad_v[kv_span, at] += sum(
                dot_nt(grad_low[span], p) for span, p in zip(spans, low_probs)
            )
            grad_k[kv_span, at] += sum(
                dot_nt(q_t[span, :], d) for span, d in zip(spans, grad_scores)
            )
            for span, d in zip(spans, grad_scores):
                grad_q[span, :] += dot_nn(keys_t, d)
        return carry

    lax.fori_loop(first_block[i], lax.div((i + 1) * block_len - 1, key_len) + 1, visit, 0)

    def unrope(value, cos, sin):
        first, second = value[:HALF], value[HALF:]
        return jnp.concatenate([first * cos + second * sin, second * cos - first * sin], axis=0)

    cos, sin = cos_ref[...], sin_ref[...]
    parts = [
        unrope(grad_q[h * HD : (h + 1) * HD, :] * score_scale, cos, sin) for h in range(q_heads)
    ]
    stage[...] = jnp.concatenate(parts, axis=0).T.astype(bf16).reshape(pages, page_rows, q_cols)
    copies = [
        pltpu.make_async_copy(
            stage.at[a], out.at[perm[i * pages + a], :, pl.ds(0, q_cols)], sems.at[a]
        )
        for a in range(pages)
    ]
    for copy in copies:
        copy.start()
    for copy in copies:
        copy.wait()

    @pl.when(i == steps - 1)
    def _():
        all_pages = kv_stage.shape[0]
        cos, sin = cos_all[...], sin_all[...]
        parts = [unrope(grad_k[g * HD : (g + 1) * HD, :], cos, sin) for g in range(kv_heads)]
        both = jnp.concatenate(parts + [grad_v[...]], axis=0)
        kv_stage[...] = both.T.astype(bf16).reshape(all_pages, page_rows, 2 * kv_cols)
        copies = [
            pltpu.make_async_copy(
                kv_stage.at[a], out.at[perm[a], :, pl.ds(q_cols, 2 * kv_cols)], kv_sems.at[a]
            )
            for a in range(all_pages)
        ]
        for copy in copies:
            copy.start()
        for copy in copies:
            copy.wait()


def attend_backward(
    grad_slots, part, q_t, k_rows, k_t, v_rows, o_t, lse, begin, cos_t, sin_t, first_block, perm,
    page_rows, block_len,
):
    total_rows = q_t.shape[1]
    kv_heads = k_rows.shape[0]
    q_heads = q_t.shape[0] // HD
    pages = block_len // page_rows
    all_pages = total_rows // page_rows
    q_cols = q_heads * HD
    kv_cols = kv_heads * HD

    def page_spec(a):
        return pl.BlockSpec(
            (1, page_rows, q_cols),
            lambda i, first_ref, perm_ref, a=a: (perm_ref[i * pages + a], 0, part),
        )

    def whole(shape):
        return pl.BlockSpec(shape, lambda i, *_: (0,) * len(shape))

    def column(rows):
        return pl.BlockSpec((rows, block_len), lambda i, *_: (0, i))

    return pl.pallas_call(
        functools.partial(backward_kernel, q_heads, kv_heads, page_rows, pages),
        grid_spec=pltpu.PrefetchScalarGridSpec(
            num_scalar_prefetch=2,
            grid=(total_rows // block_len,),
            in_specs=[page_spec(a) for a in range(pages)]
            + [
                column(q_cols),
                whole((kv_heads, total_rows, HD)),
                whole((kv_cols, total_rows)),
                whole((kv_heads, total_rows, HD)),
                column(q_cols),
                column(q_heads),
                column(1),
                column(HALF),
                column(HALF),
                whole((HALF, total_rows)),
                whole((HALF, total_rows)),
            ],
            out_specs=pl.BlockSpec(memory_space=pl.ANY),
            scratch_shapes=[
                pltpu.VMEM((q_cols, block_len), f32),
                pltpu.VMEM((kv_cols, total_rows), f32),
                pltpu.VMEM((kv_cols, total_rows), f32),
                pltpu.VMEM((pages, page_rows, q_cols), bf16),
                pltpu.VMEM((all_pages, page_rows, 2 * kv_cols), bf16),
                pltpu.SemaphoreType.DMA((pages,)),
                pltpu.SemaphoreType.DMA((all_pages,)),
            ],
        ),
        out_shape=jax.ShapeDtypeStruct((all_pages, page_rows, q_cols + 2 * kv_cols), bf16),
        cost_estimate=pl.CostEstimate(
            flops=3 * q_heads * total_rows * total_rows * HD,
            bytes_accessed=12 * q_t.size,
            transcendentals=q_heads * total_rows * total_rows // 4,
        ),
        name="attend_backward",
    )(
        first_block, perm, *([grad_slots] * pages), q_t, k_rows, k_t, v_rows, o_t, lse, begin,
        cos_t, sin_t, cos_t, sin_t,
    )


def project_kernel(
    tp_count, dp_count, rows, weights, slots, held, stage, load_sem, own_sem, send, recv
):
    count = dp_count * tp_count
    my_dp = lax.axis_index("dp")
    my_tp = lax.axis_index("tensor")
    me = my_dp * tp_count + my_tp
    page_rows = slots.shape[1]

    def load(j):
        shard = lax.rem(my_tp + 1 + j, tp_count)
        return pltpu.make_async_copy(weights.at[shard], held.at[j % 2], load_sem.at[j % 2])

    load(0).start()
    barrier = pltpu.get_barrier_semaphore()

    def greet(j, carry):
        peer = lax.rem(me + j, count)
        pl.semaphore_signal(
            barrier,
            inc=1,
            device_id={"dp": lax.div(peer, tp_count), "tensor": lax.rem(peer, tp_count)},
            device_id_type=MESH,
        )
        return carry

    lax.fori_loop(1, count, greet, 0)
    pl.semaphore_wait(barrier, count - 1)
    home = slots.at[my_tp * dp_count + my_dp]

    def copy_to(j, off):
        p_dp = lax.rem(my_dp + off, dp_count)
        return pltpu.make_async_remote_copy(
            src_ref=stage.at[j, pl.ds(p_dp * page_rows, page_rows), :],
            dst_ref=home,
            send_sem=send.at[j, off],
            recv_sem=recv.at[j, off],
            device_id={"dp": p_dp, "tensor": lax.rem(my_tp + 1 + j, tp_count)},
            device_id_type=MESH,
        )

    def each(j, act):
        def one(off, carry):
            act(copy_to(j, off))
            return carry

        lax.fori_loop(1 if j == tp_count - 1 else 0, dp_count, one, 0)

    for j in range(tp_count):
        load(j).wait()
        if j + 1 < tp_count:
            load(j + 1).start()
        stage[j] = dot_nn(rows[...], held[j % 2]).astype(bf16)
        if j > 0:
            each(j - 1, lambda copy: copy.start())
    each(tp_count - 1, lambda copy: copy.start())
    own = pltpu.make_async_copy(
        stage.at[tp_count - 1, pl.ds(my_dp * page_rows, page_rows), :], home, own_sem
    )
    own.start()
    own.wait()
    for j in range(tp_count):
        each(j, lambda copy: copy.wait())


def project(rows, weights, dp_count, collective_id):
    tp_count, width, cols = weights.shape
    total = rows.shape[0]
    page_rows = total // dp_count
    any_spec = pl.BlockSpec(memory_space=pl.ANY)
    dma = pltpu.SemaphoreType.DMA
    return pl.pallas_call(
        functools.partial(project_kernel, tp_count, dp_count),
        out_shape=jax.ShapeDtypeStruct((tp_count * dp_count, page_rows, cols), bf16),
        in_specs=[
            pl.BlockSpec(memory_space=pltpu.VMEM),
            pl.BlockSpec(memory_space=pltpu.HBM),
        ],
        out_specs=any_spec,
        scratch_shapes=[
            pltpu.VMEM((2, width, cols), bf16),
            pltpu.VMEM((tp_count, total, cols), bf16),
            dma((2,)),
            dma,
            dma((tp_count, dp_count)),
            dma((tp_count, dp_count)),
        ],
        compiler_params=pltpu.CompilerParams(
            collective_id=collective_id, has_side_effects=True, vmem_limit_bytes=62 * 1024 * 1024
        ),
        cost_estimate=pl.CostEstimate(
            flops=2 * tp_count * total * width * cols,
            bytes_accessed=16 * tp_count * width * cols,
            transcendentals=0,
        ),
        name="project",
    )(rows, weights)


def feed_kernel(
    ring, tile, own_rows, *refs
):
    grad_rows = refs[: 2 * ring - 1]
    weights, grads_t, rows_t, act_all, grads_all = refs[2 * ring - 1 : 2 * ring + 4]
    mixed_all = refs[2 * ring + 4 : 3 * ring + 4]
    (
        grad_own, held, grads_held, acc_n, acc_m, first_part, arrived, outgoing, mixed_stage,
        final_stage, turned, load_sem, keep_sem, grad_sem, mixed_sem, final_sem,
        row_send, row_recv, sum_send, sum_recv, all_sem,
    ) = refs[3 * ring + 4 :]
    me = lax.axis_index("tensor")
    right = lax.rem(me + 1, ring)
    left = lax.rem(me + ring - 1, ring)
    hidden = weights.shape[1] // 3
    tiles = hidden // tile

    barrier = pltpu.get_barrier_semaphore()
    for neighbour in (left, right):
        pl.semaphore_signal(barrier, inc=1, device_id={"tensor": neighbour}, device_id_type=MESH)
    pl.semaphore_wait(barrier, 2)

    load = pltpu.make_async_copy(own_rows, held.at[0], load_sem)
    load.start()

    def grad_load(s):
        def copy_of(source):
            return pltpu.make_async_copy(
                grad_rows[source], grads_held.at[s % 2], grad_sem.at[s % 2]
            )

        if s == 0:
            copy_of(0).start()
            return

        @pl.when(me >= s)
        def _():
            copy_of(s).start()

        @pl.when(me < s)
        def _():
            copy_of(ring - 1 + ring - s).start()

    def grad_wait(s):
        pltpu.make_async_copy(grad_rows[0], grads_held.at[s % 2], grad_sem.at[s % 2]).wait()

    def part_of(array, s):
        count = own_rows.shape[0]
        return array.at[:, pl.ds(pl.multiple_of(s * count, 128), count)]

    def grad_keep(s):
        return pltpu.make_async_copy(turned.at[1], part_of(grads_t, s), all_sem)

    grad_load(0)
    load.wait()

    def pass_rows(s):
        return pltpu.make_async_remote_copy(
            src_ref=held.at[s],
            dst_ref=held.at[s + 1],
            send_sem=row_send.at[s],
            recv_sem=row_recv.at[s],
            device_id={"tensor": right},
            device_id_type=MESH,
        )

    def pass_sum(s):
        return pltpu.make_async_remote_copy(
            src_ref=outgoing.at[s - 1],
            dst_ref=arrived.at[s - 1],
            send_sem=sum_send.at[s - 1],
            recv_sem=sum_recv.at[s - 1],
            device_id={"tensor": right},
            device_id_type=MESH,
        )

    def keep(s):
        return pltpu.make_async_copy(turned.at[0], part_of(rows_t, s), keep_sem)

    def mixed_store(s):
        return pltpu.make_async_copy(mixed_stage, mixed_all[s], mixed_sem)

    def chunk(s, carry):
        @pl.when(s > 0)
        def _():
            pass_rows(s - 1).wait_recv()

        @pl.when(s < ring - 1)
        def _():
            pass_rows(s).start()

        @pl.when(s > 0)
        def _():
            keep(s - 1).wait()
            grad_keep(s - 1).wait()

        turned[0] = held[s].T
        keep(s).start()
        for k in range(ring):

            @pl.when(s == k)
            def _(k=k):
                grad_wait(k)
                if k < ring - 1:
                    grad_load(k + 1)

        slot = lax.rem(s, 2)
        turned[1] = grads_held[slot].T
        grad_keep(s).start()
        acc_n[...] = jnp.zeros_like(acc_n)
        acc_m[...] = jnp.zeros_like(acc_m)

        def body(w_gate, w_up, w_down, act, grad_gate, grad_up):
            rows = held[s]
            gate = dot_nn(rows, w_gate[...])
            up = dot_nn(rows, w_up[...])
            grad_act = dot_nn(grads_held[slot], w_down[...])
            sig = 1.0 / (1.0 + jnp.exp(-gate))
            silu = gate * sig
            low_act = (silu * up).astype(bf16)
            low_up = (grad_act * silu).astype(bf16)
            low_gate = (grad_act * up * sig * (1.0 + gate * (1.0 - sig))).astype(bf16)
            act[...] = low_act
            grad_gate[...] = low_gate
            grad_up[...] = low_up
            acc_m[...] += dot_nt(low_act, w_down[...])
            acc_n[...] += dot_nt(low_gate, w_gate[...]) + dot_nt(low_up, w_up[...])

        width, count = own_rows.shape[1], own_rows.shape[0]
        pltpu.emit_pipeline(
            body,
            grid=(tiles,),
            in_specs=[
                pl.BlockSpec((width, tile), lambda k: (0, k)),
                pl.BlockSpec((width, tile), lambda k: (0, k + tiles)),
                pl.BlockSpec((width, tile), lambda k: (0, k + 2 * tiles)),
            ],
            out_specs=[
                pl.BlockSpec((count, tile), lambda k: (0, k)),
                pl.BlockSpec((count, tile), lambda k: (0, k)),
                pl.BlockSpec((count, tile), lambda k: (0, k + tiles)),
            ],
        )(weights, weights, weights, act_all.at[s], grads_all.at[s], grads_all.at[s])

        @pl.when(s > 0)
        def _():
            mixed_store(0).wait()

        mixed_stage[...] = acc_m[...].astype(bf16)
        for k in range(ring):

            @pl.when(s == k)
            def _(k=k):
                mixed_store(k).start()

        @pl.when(s == 0)
        def _():
            first_part[...] = acc_n[...]

        @pl.when(s == 1)
        def _():
            outgoing[0] = acc_n[...].astype(bf16)

        @pl.when(s > 1)
        def _():
            pass_sum(s - 1).wait_recv()
            outgoing[s - 1] = (acc_n[...] + arrived[s - 2].astype(f32)).astype(bf16)

        @pl.when(s > 0)
        def _():
            pass_sum(s).start()

        return carry

    lax.fori_loop(0, ring, chunk, 0)
    mixed_store(0).wait()
    pass_sum(ring - 1).wait_recv()
    final_stage[...] = (first_part[...] + arrived[ring - 2].astype(f32)).astype(bf16)
    final = pltpu.make_async_copy(final_stage, grad_own, final_sem)
    final.start()

    def settle(s, carry):
        @pl.when(s < ring - 1)
        def _():
            pass_rows(s).wait_send()

        @pl.when(s > 0)
        def _():
            pass_sum(s).wait_send()

        return carry

    lax.fori_loop(0, ring, settle, 0)
    keep(ring - 1).wait()
    grad_keep(ring - 1).wait()
    final.wait()


def feed(own_rows, grad_rows, weights, ring, tile=256, collective_id=7):
    count, width = own_rows.shape
    hidden = weights.shape[1] // 3
    any_spec = pl.BlockSpec(memory_space=pl.ANY)
    dma = pltpu.SemaphoreType.DMA
    return pl.pallas_call(
        functools.partial(feed_kernel, ring, min(tile, hidden)),
        out_shape=[
            jax.ShapeDtypeStruct((width, ring * count), bf16),
            jax.ShapeDtypeStruct((width, ring * count), bf16),
            jax.ShapeDtypeStruct((ring, count, hidden), bf16),
            jax.ShapeDtypeStruct((ring, count, 2 * hidden), bf16),
        ]
        + [jax.ShapeDtypeStruct((count, width), bf16)] * (ring + 1),
        in_specs=[any_spec] * (1 + 2 * ring),
        out_specs=[any_spec] * (5 + ring),
        scratch_shapes=[
            pltpu.VMEM((ring, count, width), bf16),
            pltpu.VMEM((2, count, width), bf16),
            pltpu.VMEM((count, width), f32),
            pltpu.VMEM((count, width), f32),
            pltpu.VMEM((count, width), f32),
            pltpu.VMEM((ring - 1, count, width), bf16),
            pltpu.VMEM((ring - 1, count, width), bf16),
            pltpu.VMEM((count, width), bf16),
            pltpu.VMEM((count, width), bf16),
            pltpu.VMEM((2, width, count), bf16),
            dma,
            dma,
            dma((2,)),
            dma,
            dma,
            dma((ring - 1,)),
            dma((ring - 1,)),
            dma((ring - 1,)),
            dma((ring - 1,)),
            dma,
        ],
        compiler_params=pltpu.CompilerParams(
            collective_id=collective_id, has_side_effects=True, vmem_limit_bytes=64 * 1024 * 1024 - 65536,
        ),
        cost_estimate=pl.CostEstimate(
            flops=12 * ring * count * width * hidden,
            bytes_accessed=8 * ring * count * width,
            transcendentals=ring * count * hidden,
        ),
        name="feed_forward",
    )(own_rows, *grad_rows, weights)


def weigh_kernel(
    tp_count, dp_count, tile, grads, rows_t, grads_t, gate_up, act, slots, out,
    left, left_sem, own_sem, send, recv,
):
    count = dp_count * tp_count
    my_dp = lax.axis_index("dp")
    my_tp = lax.axis_index("tensor")
    me = my_dp * tp_count + my_tp
    page_rows = slots.shape[1]

    loads = [
        pltpu.make_async_copy(source, left.at[k], left_sem.at[k])
        for k, source in enumerate((rows_t, grads_t))
    ]
    for load in loads:
        load.start()

    barrier = pltpu.get_barrier_semaphore()

    def place(peer):
        return {"dp": lax.div(peer, tp_count), "tensor": lax.rem(peer, tp_count)}

    def greet(j, carry):
        peer = lax.rem(me + j, count)
        pl.semaphore_signal(barrier, inc=1, device_id=place(peer), device_id_type=MESH)
        return carry

    lax.fori_loop(1, count, greet, 0)
    pl.semaphore_wait(barrier, count - 1)

    home = slots.at[my_tp * dp_count + my_dp]

    def block(p_dp, p_tp):
        return grads.at[p_tp, pl.ds(p_dp * page_rows, page_rows), :]

    own = pltpu.make_async_copy(block(my_dp, my_tp), home, own_sem)
    own.start()

    def copy_to(j):
        peer = lax.rem(me + j, count)
        return pltpu.make_async_remote_copy(
            src_ref=block(lax.div(peer, tp_count), lax.rem(peer, tp_count)),
            dst_ref=home,
            send_sem=send.at[j],
            recv_sem=recv.at[j],
            device_id=place(peer),
            device_id_type=MESH,
        )

    def start(j, carry):
        copy_to(j).start()
        return carry

    def finish(j, carry):
        copy_to(j).wait()
        return carry

    lax.fori_loop(1, count, start, 0)

    width = rows_t.shape[0]
    step = min(512, width)

    def multiply(k, right, first):
        ring, rows, cols = right.shape

        def body(part, result):
            values = part[...].reshape(ring * rows, tile)
            for m in range(0, width, step):
                result[m : m + step, :] = dot_nn(left[k, m : m + step, :], values).astype(bf16)

        pltpu.emit_pipeline(
            body,
            grid=(cols // tile,),
            in_specs=[pl.BlockSpec((ring, rows, tile), lambda n: (0, 0, n))],
            out_specs=[pl.BlockSpec((width, tile), lambda n: (0, n + first))],
        )(right, out)

    loads[0].wait()
    multiply(0, gate_up, 0)
    loads[1].wait()
    multiply(1, act, gate_up.shape[2] // tile)
    own.wait()
    lax.fori_loop(1, count, finish, 0)


def weigh(grads, rows_t, grads_t, gate_up, act, tp_count, dp_count, collective_id):
    count = tp_count * dp_count
    cols = grads.shape[2]
    page_rows = grads.shape[1] // dp_count
    width, rows = rows_t.shape
    hidden = act.shape[2]
    any_spec = pl.BlockSpec(memory_space=pl.ANY)
    dma = pltpu.SemaphoreType.DMA
    return pl.pallas_call(
        functools.partial(weigh_kernel, tp_count, dp_count, min(512, hidden)),
        out_shape=[
            jax.ShapeDtypeStruct((count, page_rows, cols), bf16),
            jax.ShapeDtypeStruct((width, 3 * hidden), bf16),
        ],
        in_specs=[pl.BlockSpec(memory_space=pltpu.HBM)] * 5,
        out_specs=[any_spec] * 2,
        scratch_shapes=[
            pltpu.VMEM((2, width, rows), bf16),
            dma((2,)),
            dma,
            dma((count,)),
            dma((count,)),
        ],
        compiler_params=pltpu.CompilerParams(
            collective_id=collective_id, has_side_effects=True, vmem_limit_bytes=62 * 1024 * 1024
        ),
        cost_estimate=pl.CostEstimate(
            flops=6 * rows * width * hidden,
            bytes_accessed=2 * width * (2 * rows + 3 * hidden),
            transcendentals=0,
        ),
        name="weigh",
    )(grads, rows_t, grads_t, gate_up, act)


def flip(index, bit):
    return index + bit - 2 * bit * lax.rem(lax.div(index, bit), 2)


def collect_kernel(
    tp_count, dp_count, shard, second, gains, chunk, out, second_out, gains_out, from_left, from_right,
    second_send, second_recv, own_sem, ring_send, ring_recv, send, recv, gain_send, gain_recv, chunk_send, chunk_recv,
):
    my_dp = lax.axis_index("dp")
    my_tp = lax.axis_index("tensor")
    rows = shard.shape[0]
    half = rows // 2
    bits = [1 << b for b in reversed(range(dp_count.bit_length() - 1))]
    orders = [bits, bits[:-1][::-1] + bits[-1:]]
    steps = len(bits)

    barrier = pltpu.get_barrier_semaphore()
    for j in range(1, tp_count):
        pl.semaphore_signal(
            barrier, inc=1, device_id={"tensor": lax.rem(my_tp + j, tp_count)}, device_id_type=MESH
        )
    for j in range(1, dp_count):
        pl.semaphore_signal(
            barrier, inc=1, device_id={"dp": lax.rem(my_dp + j, dp_count)}, device_id_type=MESH
        )
    pl.semaphore_wait(barrier, tp_count + dp_count - 2)

    home = out.at[my_tp, pl.ds(my_dp * rows, rows), :]
    own = pltpu.make_async_copy(shard, home, own_sem.at[0])
    own.start()
    own_gain = pltpu.make_async_copy(gains, gains_out.at[my_dp], own_sem.at[1])
    own_gain.start()
    own_second = pltpu.make_async_copy(second, second_out.at[my_tp], own_sem.at[2])
    own_second.start()

    def second_copy(j):
        return pltpu.make_async_remote_copy(
            src_ref=second,
            dst_ref=second_out.at[my_tp],
            send_sem=second_send.at[j],
            recv_sem=second_recv.at[j],
            device_id={"tensor": lax.rem(my_tp + j, tp_count)},
            device_id_type=MESH,
        )

    def hand_on(way, far):
        owner = lax.rem(my_tp + (tp_count - far, far)[way], tp_count)
        spot = out.at[owner, pl.ds(my_dp * rows, rows), :]
        return pltpu.make_async_remote_copy(
            src_ref=shard if far == 0 else spot,
            dst_ref=spot,
            send_sem=ring_send.at[way, far],
            recv_sem=ring_recv.at[way, far],
            device_id={"tensor": lax.rem(my_tp + (1, tp_count - 1)[way], tp_count)},
            device_id_type=MESH,
        )

    def hands_on(way, far):
        if way == 0:
            return (my_tp >= far) & (my_tp < tp_count - 1)
        return (my_tp < tp_count - far) & (my_tp > 0)

    def relay(far):
        for way, here in ((0, my_tp >= far), (1, my_tp < tp_count - far)):

            @pl.when(here)
            def _(way=way):
                hand_on(way, far - 1).wait_recv()

                if far < tp_count - 1:

                    @pl.when(hands_on(way, far))
                    def _():
                        hand_on(way, far).start()

    def gain_copy(j):
        return pltpu.make_async_remote_copy(
            src_ref=gains,
            dst_ref=gains_out.at[my_dp],
            send_sem=gain_send.at[j],
            recv_sem=gain_recv.at[j],
            device_id={"dp": lax.rem(my_dp + j, dp_count)},
            device_id_type=MESH,
        )

    def step(way):
        return pltpu.make_async_remote_copy(
            src_ref=chunk,
            dst_ref=(from_left, from_right)[way],
            send_sem=chunk_send.at[way],
            recv_sem=chunk_recv.at[way],
            device_id={"tensor": lax.rem(my_tp + (1, tp_count - 1)[way], tp_count)},
            device_id_type=MESH,
        )

    has_right, has_left = my_tp < tp_count - 1, my_tp > 0

    def within(j, s, k, m):
        order = orders[s]
        owner = my_dp
        for b in range(k):
            if m >> b & 1:
                owner = flip(owner, order[b])
        block = out.at[
            lax.rem(my_tp - j + tp_count, tp_count), pl.ds(owner * rows + s * half, half), :
        ]
        at = (1 << k) - 1 + m
        return pltpu.make_async_remote_copy(
            src_ref=block,
            dst_ref=block,
            send_sem=send.at[j, s, at],
            recv_sem=recv.at[j, s, at],
            device_id={"dp": flip(my_dp, order[k])},
            device_id_type=MESH,
        )

    for way in range(2):

        @pl.when(hands_on(way, 0))
        def _(way=way):
            hand_on(way, 0).start()

    for j in range(1, dp_count):
        gain_copy(j).start()

    own.wait()
    for phase in range(2 * tp_count - 2 + steps):
        if 1 <= phase < tp_count:
            relay(phase)
        for k in reversed(range(steps + 1)):
            for j in range(tp_count):
                if (0 if j == 0 else tp_count - 2 + j) + k != phase:
                    continue
                for s in range(2):
                    if k > 0:
                        for m in range(1 << (k - 1)):
                            within(j, s, k - 1, m).wait_recv()
                for s in range(2):
                    if k < steps:
                        for m in range(1 << k):
                            within(j, s, k, m).start()
        if phase == tp_count - 1:

            @pl.when(has_right)
            def _():
                step(0).start()

            @pl.when(has_left)
            def _():
                step(1).start()

            for j in range(1, tp_count):
                second_copy(j).start()
    for j in range(tp_count):
        if j < tp_count - 1:
            for way in range(2):

                @pl.when(hands_on(way, j))
                def _(way=way, j=j):
                    hand_on(way, j).wait_send()

        for s in range(2):
            for k in range(steps):
                for m in range(1 << k):
                    within(j, s, k, m).wait_send()
    own_gain.wait()
    own_second.wait()
    for j in range(1, tp_count):
        second_copy(j).wait()
    for j in range(1, dp_count):
        gain_copy(j).wait()

    @pl.when(has_right)
    def _():
        step(0).wait_send()
        step(1).wait_recv()

    @pl.when(has_left)
    def _():
        step(1).wait_send()
        step(0).wait_recv()


def collect(shard, second, gains, chunk, tp_count, dp_count, collective_id):
    rows, cols = shard.shape
    dma = pltpu.SemaphoreType.DMA
    vmem_spec = pl.BlockSpec(memory_space=pltpu.VMEM)
    any_spec = pl.BlockSpec(memory_space=pl.ANY)
    return pl.pallas_call(
        functools.partial(collect_kernel, tp_count, dp_count),
        out_shape=[
            jax.ShapeDtypeStruct((tp_count, dp_count * rows, cols), shard.dtype),
            jax.ShapeDtypeStruct((tp_count,) + second.shape, second.dtype),
            jax.ShapeDtypeStruct((dp_count,) + gains.shape, gains.dtype),
            jax.ShapeDtypeStruct(chunk.shape, chunk.dtype),
            jax.ShapeDtypeStruct(chunk.shape, chunk.dtype),
        ],
        in_specs=[vmem_spec, vmem_spec, vmem_spec, any_spec],
        out_specs=[any_spec] * 5,
        scratch_shapes=[
            dma((tp_count,)),
            dma((tp_count,)),
            dma((3,)),
            dma((2, tp_count)),
            dma((2, tp_count)),
            dma((tp_count, 2, dp_count - 1)),
            dma((tp_count, 2, dp_count - 1)),
            dma((dp_count,)),
            dma((dp_count,)),
            dma((2,)),
            dma((2,)),
        ],
        compiler_params=pltpu.CompilerParams(collective_id=collective_id, has_side_effects=True),
        cost_estimate=pl.CostEstimate(
            flops=0, bytes_accessed=16 * tp_count * dp_count * shard.size, transcendentals=0
        ),
        name="collect",
    )(shard, second, gains, chunk)


def spread_kernel(rows, weight, out):
    out[0] = dot_nn(rows[...], weight[0]).astype(out.dtype)


def spread(rows, weights, part, cols):
    shards, width, _ = weights.shape
    count = rows.shape[0]
    return pl.pallas_call(
        spread_kernel,
        grid=(shards,),
        in_specs=[
            pl.BlockSpec((count, width), lambda t: (0, 0)),
            pl.BlockSpec((1, width, cols), lambda t: (t, 0, part)),
        ],
        out_specs=pl.BlockSpec((1, count, cols), lambda t: (t, 0, 0)),
        out_shape=jax.ShapeDtypeStruct((shards, count, cols), bf16),
        cost_estimate=pl.CostEstimate(
            flops=2 * shards * count * width * cols,
            bytes_accessed=2 * shards * width * cols,
            transcendentals=0,
        ),
        name="spread",
    )(rows, weights)


def gather_kernel(has_begin, part, weight, *refs):
    out = refs[-1]

    @pl.when(pl.program_id(0) == 0)
    def _():
        out[...] = refs[0][...] if has_begin else jnp.zeros_like(out)

    out[...] += dot_nt(part[0], weight[0])


def gather_sum(parts, weights, part, begin):
    shards, count, cols = parts.shape
    width = weights.shape[1]
    whole = pl.BlockSpec((count, width), lambda t: (0, 0))
    begins = [] if begin is None else [begin]
    return pl.pallas_call(
        functools.partial(gather_kernel, begin is not None),
        grid=(shards,),
        in_specs=[
            pl.BlockSpec((1, count, cols), lambda t: (t, 0, 0)),
            pl.BlockSpec((1, width, cols), lambda t: (t, 0, part)),
        ]
        + [whole] * len(begins),
        out_specs=whole,
        out_shape=jax.ShapeDtypeStruct((count, width), f32),
        cost_estimate=pl.CostEstimate(
            flops=2 * shards * count * width * cols,
            bytes_accessed=2 * shards * width * cols,
            transcendentals=0,
        ),
        name="gather_sum",
    )(parts, weights, *begins)


def outer_kernel(rows, *refs):
    parts, out, turned = refs[:-2], refs[-2], refs[-1]

    @pl.when(pl.program_id(0) == 0)
    def _():
        turned[...] = rows[...].T

    at = 0
    for part in parts:
        cols = part.shape[2]
        out[:, at : at + cols] = dot_nn(turned[...], part[0]).astype(out.dtype)
        at += cols


def outer(rows, parts):
    shards, count, _ = parts[0].shape
    cols = sum(part.shape[2] for part in parts)
    width = rows.shape[1]
    return pl.pallas_call(
        outer_kernel,
        grid=(shards,),
        in_specs=[pl.BlockSpec((count, width), lambda t: (0, 0))]
        + [pl.BlockSpec((1, count, part.shape[2]), lambda t: (t, 0, 0)) for part in parts],
        out_specs=pl.BlockSpec((width, cols), lambda t: (0, t)),
        out_shape=jax.ShapeDtypeStruct((width, shards * cols), bf16),
        scratch_shapes=[pltpu.VMEM((width, count), bf16)],
        cost_estimate=pl.CostEstimate(
            flops=2 * shards * count * width * cols,
            bytes_accessed=2 * shards * width * cols,
            transcendentals=0,
        ),
        name="outer",
    )(rows, *parts)


def total_kernel(
    tp_count, dp_count, groups, rows, *refs
):
    parts = refs[:groups]
    (
        to_right, to_left, weights, out, grad_rows, from_sides,
        turned, mine, got, got_across, held, load_sem, send, recv,
        across_send, across_recv, chunk_send, chunk_recv,
    ) = refs[groups:]
    my_dp = lax.axis_index("dp")
    my_tp = lax.axis_index("tensor")
    own_rows = out.shape[0]
    half = own_rows // 2
    bits = [1 << b for b in range(dp_count.bit_length() - 1)]
    orders = [bits, bits[:1] + bits[1:][::-1]]
    steps = len(bits)

    def shard_of(j):
        return lax.rem(my_tp + 1 + j, tp_count)

    def load(j):
        return pltpu.make_async_copy(weights.at[shard_of(j)], held.at[j % 2], load_sem.at[j % 2])

    load(0).start()
    barrier = pltpu.get_barrier_semaphore()
    for j in range(1, tp_count):
        pl.semaphore_signal(
            barrier, inc=1, device_id={"tensor": lax.rem(my_tp + j, tp_count)}, device_id_type=MESH
        )
    for bit in bits:
        pl.semaphore_signal(
            barrier, inc=1, device_id={"dp": flip(my_dp, bit)}, device_id_type=MESH
        )
    pl.semaphore_wait(barrier, tp_count - 1 + steps)

    def step(way):
        return pltpu.make_async_remote_copy(
            src_ref=(to_right, to_left)[way],
            dst_ref=from_sides.at[way],
            send_sem=chunk_send.at[way],
            recv_sem=chunk_recv.at[way],
            device_id={"tensor": lax.rem(my_tp + (1, tp_count - 1)[way], tp_count)},
            device_id_type=MESH,
        )

    has_right, has_left = my_tp < tp_count - 1, my_tp > 0

    @pl.when(has_right)
    def _():
        step(0).start()

    @pl.when(has_left)
    def _():
        step(1).start()

    def block(j, s, owner):
        return j, pl.ds(pl.multiple_of(owner * own_rows + s * half, half), half)

    def place(k, m):
        return sum(1 << (steps - 1 - e) for e in range(k)) + m

    def fellow(s, k, m, start):
        owner = start
        for b in range(steps - 1 - k):
            if m >> b & 1:
                owner = flip(owner, orders[s][k + 1 + b])
        return owner

    def exchange_part(j, s, k, m):
        partner = flip(my_dp, orders[s][k])
        at = place(k, m)
        index, span = block(j, s, fellow(s, k, m, partner))
        return pltpu.make_async_remote_copy(
            src_ref=mine.at[index, span, :],
            dst_ref=got.at[j, s, at],
            send_sem=send.at[j, s, at],
            recv_sem=recv.at[j, s, at],
            device_id={"dp": partner},
            device_id_type=MESH,
        )

    def across(j):
        return pltpu.make_async_remote_copy(
            src_ref=mine.at[j, pl.ds(pl.multiple_of(my_dp * own_rows, own_rows), own_rows), :],
            dst_ref=got_across.at[j],
            send_sem=across_send.at[j],
            recv_sem=across_recv.at[j],
            device_id={"tensor": shard_of(j)},
            device_id_type=MESH,
        )

    def every(k):
        return [(s, m) for s in range(2) for m in range(1 << (steps - 1 - k))]

    turned[...] = rows[...].T
    for phase in range(tp_count + steps + 1):
        if phase < tp_count:
            shard = shard_of(phase)
            at = 0
            load(phase).wait()
            if phase + 1 < tp_count:
                load(phase + 1).start()
            for g, part in enumerate(parts):
                cols = part.shape[2]
                value = part[shard]
                mine[phase, :, at : at + cols] = dot_nn(turned[...], value).astype(bf16)
                product = dot_nt(value, held[phase % 2, :, at : at + cols])
                if phase == 0 and g == 0:
                    grad_rows[...] = product
                else:
                    grad_rows[...] += product
                at += cols
        for k in reversed(range(steps + 1)):
            j = phase - k
            if not 0 <= j < tp_count:
                continue
            if k > 0:
                for s, m in every(k - 1):
                    exchange_part(j, s, k - 1, m).wait_recv()
                    index, span = block(j, s, fellow(s, k - 1, m, my_dp))
                    mine[index, span, :] = (
                        mine[index, span, :].astype(f32)
                        + got[j, s, place(k - 1, m)].astype(f32)
                    ).astype(bf16)
            if k < steps:
                for s, m in every(k):
                    exchange_part(j, s, k, m).start()
            elif j < tp_count - 1:
                across(j).start()
    total = mine[
        tp_count - 1, pl.ds(pl.multiple_of(my_dp * own_rows, own_rows), own_rows), :
    ].astype(f32)
    for j in range(tp_count - 1):
        across(j).wait_recv()
        total += got_across[j].astype(f32)
    out[...] = total

    @pl.when(has_right)
    def _():
        step(0).wait_send()
        step(1).wait_recv()

    @pl.when(has_left)
    def _():
        step(1).wait_send()
        step(0).wait_recv()

    for j in range(tp_count):
        if j < tp_count - 1:
            across(j).wait_send()
        for k in range(steps):
            for s, m in every(k):
                exchange_part(j, s, k, m).wait_send()


def total_grads(rows, parts, to_right, to_left, weights, dp_count, collective_id):
    tp_count, width, cols = weights.shape
    count = rows.shape[0]
    own_rows = width // dp_count
    vmem_spec = pl.BlockSpec(memory_space=pltpu.VMEM)
    any_spec = pl.BlockSpec(memory_space=pl.ANY)
    dma = pltpu.SemaphoreType.DMA
    return pl.pallas_call(
        functools.partial(total_kernel, tp_count, dp_count, len(parts)),
        out_shape=[
            jax.ShapeDtypeStruct((own_rows, cols), f32),
            jax.ShapeDtypeStruct((count, width), f32),
            jax.ShapeDtypeStruct((2, count, width), bf16),
        ],
        in_specs=[vmem_spec] * (1 + len(parts)) + [any_spec] * 3,
        out_specs=[vmem_spec, vmem_spec, any_spec],
        scratch_shapes=[
            pltpu.VMEM((width, count), bf16),
            pltpu.VMEM((tp_count, width, cols), bf16),
            pltpu.VMEM((tp_count, 2, dp_count - 1, own_rows // 2, cols), bf16),
            pltpu.VMEM((tp_count - 1, own_rows, cols), bf16),
            pltpu.VMEM((2, width, cols), bf16),
            dma((2,)),
            dma((tp_count, 2, dp_count - 1)),
            dma((tp_count, 2, dp_count - 1)),
            dma((tp_count,)),
            dma((tp_count,)),
            dma((2,)),
            dma((2,)),
        ],
        compiler_params=pltpu.CompilerParams(
            collective_id=collective_id, has_side_effects=True, vmem_limit_bytes=62 * 1024 * 1024
        ),
        cost_estimate=pl.CostEstimate(
            flops=4 * tp_count * count * width * cols,
            bytes_accessed=16 * tp_count * width * cols,
            transcendentals=0,
        ),
        name="total_grads",
    )(rows, *parts, to_right, to_left, weights)


def rms_scale(hidden):
    return lax.rsqrt(jnp.mean(hidden * hidden, axis=1, keepdims=True) + epsilon)


def norm_back(grad_norm, hidden, scale_rows, gain):
    normed = hidden * scale_rows
    gain_part = jnp.sum(grad_norm * normed, axis=0)
    inner = grad_norm * gain
    grad_hidden = scale_rows * (inner - normed * jnp.mean(inner * normed, axis=1, keepdims=True))
    return (grad_hidden, gain_part)


def after(value, other):
    return lax.optimization_barrier((value, other))[0]


def local(
    tokens,
    upstream,
    lengths,
    positions,
    pages,
    attn_gain,
    w_query,
    w_key,
    w_value,
    w_out,
    mlp_gain,
    w_gate,
    w_up,
    w_down,
):
    dp_count = lax.axis_size("dp")
    tp_count = lax.axis_size("tensor")
    dp_index = lax.axis_index("dp")
    tp_index = lax.axis_index("tensor")
    tok_dev, width = tokens.shape
    tok_group = tok_dev * tp_count
    page_rows = tok_dev // dp_count
    group_pages = tp_count * dp_count
    page_count = pages.shape[0]
    device = dp_index * tp_count + tp_index
    everyone = ("tensor", "dp")

    local_ids = jnp.arange(dp_count, dtype=jnp.int32)
    inverse = (
        jnp.zeros((page_count,), jnp.int32).at[pages].set(jnp.arange(page_count, dtype=jnp.int32))
    )
    dealt = lax.dynamic_slice_in_dim(inverse, device * dp_count, dp_count)
    dest_group = dealt // group_pages
    send_order = jnp.zeros((dp_count,), jnp.int32).at[dest_group].set(local_ids)
    group_sources = lax.dynamic_slice_in_dim(pages, dp_index * group_pages, group_pages)
    perm = (
        (jnp.arange(group_pages, dtype=jnp.int32) // dp_count) * dp_count
        + group_sources // group_pages
    ).astype(jnp.int32)

    def reorder(rows, order):
        blocks = rows.reshape(dp_count, page_rows, rows.shape[1])
        return jnp.take(blocks, order, axis=0, mode="clip").reshape(rows.shape)

    hidden_in = reorder(tokens, send_order).astype(f32)
    grad_top = reorder(upstream, send_order).astype(f32)
    seq_lens = lengths[0]
    seq_ends = jnp.cumsum(seq_lens)
    place = (jnp.take(dealt, send_order, mode="clip") % group_pages) * page_rows
    place_rows = (place[:, None] + jnp.arange(page_rows, dtype=jnp.int32)[None, :]).reshape(-1)
    valid_rows = (place_rows < seq_ends[-1]).astype(f32)[:, None]

    row_ids = jnp.arange(tok_group, dtype=jnp.int32)
    begin = jnp.max(
        jnp.where(row_ids[:, None] >= seq_ends[None, :], seq_ends[None, :], 0), axis=1
    ).astype(jnp.int32)
    block_len = min(block_rows, tok_group)
    first_block = begin[::block_len] // min(key_rows, tok_group)
    begin = begin[None, :]
    inverse_freq = theta_base ** (-(jnp.arange(HALF, dtype=f32) * 2.0) / HD)
    angles = inverse_freq[:, None] * positions.astype(f32)
    cos_t, sin_t = jnp.cos(angles), jnp.sin(angles)

    q_cols, kv_cols = w_query.shape[1], w_key.shape[1]
    kv_heads = kv_cols // HD
    per_group = q_cols // kv_cols
    group_q = per_group * HD
    groups = range(kv_heads)
    qkv_shard = jnp.concatenate(
        [
            part
            for g in groups
            for part in (
                w_query[:, g * group_q : (g + 1) * group_q],
                w_key[:, g * HD : (g + 1) * HD],
                w_value[:, g * HD : (g + 1) * HD],
            )
        ],
        axis=1,
    )

    def trade(value):
        blocks = value.reshape(group_pages, page_rows, value.shape[-1])
        return lax.all_to_all(blocks, everyone, split_axis=0, concat_axis=0, tiled=True)

    def trade_back(value):
        return trade(value).reshape(tp_count, tok_dev, value.shape[-1])

    def pass_on(values, first, last):
        return (
            lax.ppermute(values[0], "tensor", [(t, t + 1) for t in range(*first)]),
            lax.ppermute(values[1], "tensor", [(t, t - 1) for t in range(*last)]),
        )

    grad_out = grad_top * valid_rows
    own_chunk = grad_out.astype(bf16)
    mlp_shard = jnp.concatenate([w_gate, w_up, w_down.T], axis=1)
    w_qkv, out_shards, gains, *sides = collect(
        qkv_shard, w_out.T, jnp.stack([attn_gain, mlp_gain]), own_chunk, tp_count, dp_count, 1
    )
    w_out_t = lax.all_gather(out_shards, "dp", axis=1, tiled=True)
    w_mlp = lax.all_gather(after(mlp_shard, gains), "dp", axis=0, tiled=True)
    chunks = [(sides[0], sides[1])]
    gains = gains.transpose(1, 0, 2).reshape(2, -1).astype(f32)
    gain_one, gain_two = gains[0], gains[1]

    scale_one = rms_scale(hidden_in)
    normed_one = (hidden_in * scale_one * gain_one).astype(bf16)
    slots = project(normed_one, w_qkv, dp_count, 3)
    for n in range(2, tp_count):
        passed = after(chunks[-1], slots) if n == 2 else chunks[-1]
        chunks.append(pass_on(passed, (n - 1, tp_count - 1), (1, tp_count - n + 1)))
    saved, mixed = [], []
    for g in groups:
        q_t, k_t, k_rows, v_t, v_rows = prepare(
            after(slots, (o_slots, w_out_t, chunks[1])) if g else slots, g, perm, cos_t, sin_t, per_group, 1
        )
        o_t, lse, o_slots = attend_forward(
            q_t, k_rows, v_t, begin, first_block, perm, page_rows, block_len
        )
        saved.append((q_t, k_rows, k_t, v_rows, o_t, lse))
        mixed.append(trade_back(after(o_slots, chunks[1]) if g else o_slots))
    hidden_mid = hidden_in
    mixed[-1] = after(mixed[-1], chunks[-1])
    for g in groups:
        hidden_mid = gather_sum(mixed[g], w_out_t, g, hidden_mid)

    scale_two = rms_scale(hidden_mid)
    normed_two = (hidden_mid * scale_two * gain_two).astype(bf16)
    grads_t, rows_t, inner_act, grad_gate_up, *partial_two, grad_normed_two = feed(
        normed_two, [own_chunk] + [c[0] for c in chunks] + [c[1] for c in chunks], w_mlp, tp_count
    )
    grad_normed_two = grad_normed_two.astype(f32)
    grad_mid_norm, gain_two_part = norm_back(grad_normed_two, hidden_mid, scale_two, gain_two)
    grad_mid = grad_out + grad_mid_norm

    def add_on(arrived, s):
        return tuple(
            (value.astype(f32) + partial_two[at].astype(f32)).astype(bf16)
            for value, at in zip(arrived, (s, tp_count - s))
        )

    def reduce_dp(grad):
        return lax.psum_scatter(grad.astype(bf16), "dp", scatter_dimension=0, tiled=True)

    def reduce_tensor(value):
        cols = value.shape[1] // tp_count
        total = lax.dynamic_slice_in_dim(value, tp_index * cols, cols, 1).astype(f32)
        for s in range(1, tp_count):
            target = lax.rem(tp_index + s, tp_count)
            block = lax.dynamic_slice_in_dim(value, target * cols, cols, 1)
            pairs = [(t, (t + s) % tp_count) for t in range(tp_count)]
            total = total + lax.ppermute(block, "tensor", pairs).astype(f32)
        return total

    grad_z = grad_mid.astype(bf16)
    grad_wout = outer(grad_z, mixed)
    sum_out = reduce_dp(grad_wout)
    grad_slots, grad_wmlp = weigh(
        spread(after(grad_z, grad_wout), w_out_t, 0, q_cols),
        rows_t, grads_t, grad_gate_up, inner_act, tp_count, dp_count, 2,
    )
    sum_mlp = reduce_dp(grad_wmlp)
    first_part = after((partial_two[1], partial_two[tp_count - 1]), grad_slots)
    passing = pass_on(first_part, (0, 1), (tp_count - 1, tp_count))
    grad_qkv = []
    for g in groups:
        q_t, k_rows, k_t, v_rows, o_t, lse = saved[g]
        back = attend_backward(
            after(grad_slots, (back, sum_out) if g else first_part), g, q_t, k_rows, k_t, v_rows,
            o_t, lse, begin, cos_t, sin_t, first_block, perm, page_rows, block_len,
        )
        if g == len(groups) - 1:
            steps = 2
            if tp_count > 3:
                passing = pass_on(add_on(passing, 2), (0, 2), (tp_count - 2, tp_count))
                steps = 3
            grad_qkv = [after(value, passing) for value in grad_qkv]
        grad_qkv.append(trade_back(back))
    hidden = sum_mlp.shape[1] // 3
    for s in range(steps, tp_count - 1):
        passing = pass_on(add_on(passing, s), (0, s), (tp_count - s, tp_count))
    passing = add_on(passing, tp_count - 1)
    sum_qkv, grad_normed_one, sides = total_grads(
        normed_one, grad_qkv, passing[0], passing[1], w_qkv, dp_count, 4
    )
    branch_two = jnp.where(tp_index > 0, sides[0].astype(f32), 0.0)
    branch_two += jnp.where(tp_index < tp_count - 1, sides[1].astype(f32), 0.0)
    each = group_q + 2 * HD
    sum_qkv = [sum_qkv[:, g * each : (g + 1) * each] for g in groups]
    sum_out = reduce_tensor(after(sum_out, grad_normed_one))
    result = (
        (after(hidden_mid, back) + branch_two + partial_two[0].astype(f32)) * valid_rows
    ).astype(bf16)
    grad_in_norm, gain_one_part = norm_back(grad_normed_one, hidden_in, scale_one, gain_one)
    grad_in = (grad_mid + grad_in_norm).astype(bf16)

    gain_parts = jnp.stack([gain_one_part, gain_two_part]).reshape(2, dp_count, -1)
    gain_parts = jnp.broadcast_to(
        gain_parts.transpose(1, 0, 2)[None], (tp_count, dp_count, 2, gain_parts.shape[2])
    ).reshape(group_pages, 2, -1)
    gain_sums = jnp.sum(
        lax.all_to_all(gain_parts, everyone, split_axis=0, concat_axis=0, tiled=True), axis=0
    )
    return (
        reorder(result, dest_group),
        reorder(grad_in, dest_group),
        gain_sums[0],
        jnp.concatenate([part[:, :group_q] for part in sum_qkv], axis=1),
        jnp.concatenate([part[:, group_q : group_q + HD] for part in sum_qkv], axis=1),
        jnp.concatenate([part[:, group_q + HD :] for part in sum_qkv], axis=1),
        sum_out.T,
        gain_sums[1],
        sum_mlp[:, :hidden].astype(f32),
        sum_mlp[:, hidden : 2 * hidden].astype(f32),
        sum_mlp[:, 2 * hidden :].astype(f32).T,
    )


def solution(mesh):
    rows = P(("dp", "tensor"), None)
    weight = P("dp", "tensor")
    weight_t = P("tensor", "dp")
    return jax.shard_map(
        local,
        mesh=mesh,
        in_specs=(
            rows,
            rows,
            P("dp", None),
            P("dp", None),
            P(),
            P("dp"),
            weight,
            weight,
            weight,
            weight_t,
            P("dp"),
            weight,
            weight,
            weight_t,
        ),
        out_specs=(
            rows,
            rows,
            P("dp"),
            weight,
            weight,
            weight,
            weight_t,
            P("dp"),
            weight,
            weight,
            weight_t,
        ),
        check_vma=False,
    )
```

```python
import functools

import jax
import jax.numpy as jnp
from jax import lax
from jax.experimental import pallas as pl
from jax.experimental.pallas import tpu as pltpu
from jax.sharding import PartitionSpec as P

HD = 64
HALF = HD // 2

epsilon = 1e-05
theta_base = 500000.0
masked_score = -1e30
score_scale = HD**-0.5
block_rows = 512
key_rows = 256
MESH = pl.DeviceIdType.MESH
f32 = jnp.float32
bf16 = jnp.bfloat16


def dot_nn(left, right):
    return lax.dot_general(left, right, (((1,), (0,)), ((), ())), preferred_element_type=f32)


def dot_nt(left, right):
    return lax.dot_general(left, right, (((1,), (1,)), ((), ())), preferred_element_type=f32)


def dot_tn(left, right):
    return lax.dot_general(left, right, (((0,), (0,)), ((), ())), preferred_element_type=f32)


def prep_kernel(pages_per, q_heads, kv_heads, perm, *refs):
    page_refs = refs[:pages_per]
    cos_ref, sin_ref, q_t, k_t, k_rows, v_t, v_rows = refs[pages_per:]
    rows = jnp.concatenate([r[0].astype(f32) for r in page_refs], axis=0)
    turned = rows.T
    cos, sin = cos_ref[...], sin_ref[...]

    def rope(base):
        first, second = turned[base : base + HALF], turned[base + HALF : base + HD]
        return jnp.concatenate([first * cos - second * sin, second * cos + first * sin], axis=0)

    for h in range(q_heads):
        roped = rope(h * HD).astype(bf16)
        q_t[h * HD : (h + 1) * HD, :] = (roped.astype(f32) * score_scale).astype(bf16)
    k_base = q_heads * HD
    v_base = k_base + kv_heads * HD
    for g in range(kv_heads):
        roped = rope(k_base + g * HD)
        k_t[g * HD : (g + 1) * HD, :] = roped.astype(bf16)
        k_rows[g] = roped.T.astype(bf16)
        v_t[g * HD : (g + 1) * HD, :] = turned[v_base + g * HD : v_base + (g + 1) * HD].astype(bf16)
        v_rows[g] = rows[:, v_base + g * HD : v_base + (g + 1) * HD].astype(bf16)


def prepare(slots, part, perm, cos_t, sin_t, q_heads, kv_heads):
    page_rows = slots.shape[1]
    cols = (q_heads + 2 * kv_heads) * HD
    total_rows = slots.shape[0] * page_rows
    lanes = min(256, total_rows)
    pages_per = lanes // page_rows

    def page_spec(a):
        return pl.BlockSpec(
            (1, page_rows, cols), lambda i, perm_ref, a=a: (perm_ref[i * pages_per + a], 0, part)
        )

    table = pl.BlockSpec((HALF, lanes), lambda i, perm_ref: (0, i))
    return pl.pallas_call(
        functools.partial(prep_kernel, pages_per, q_heads, kv_heads),
        grid_spec=pltpu.PrefetchScalarGridSpec(
            num_scalar_prefetch=1,
            grid=(total_rows // lanes,),
            in_specs=[page_spec(a) for a in range(pages_per)] + [table, table],
            out_specs=[
                pl.BlockSpec((q_heads * HD, lanes), lambda i, perm_ref: (0, i)),
                pl.BlockSpec((kv_heads * HD, lanes), lambda i, perm_ref: (0, i)),
                pl.BlockSpec((kv_heads, lanes, HD), lambda i, perm_ref: (0, i, 0)),
                pl.BlockSpec((kv_heads * HD, lanes), lambda i, perm_ref: (0, i)),
                pl.BlockSpec((kv_heads, lanes, HD), lambda i, perm_ref: (0, i, 0)),
            ],
        ),
        out_shape=[
            jax.ShapeDtypeStruct((q_heads * HD, total_rows), bf16),
            jax.ShapeDtypeStruct((kv_heads * HD, total_rows), bf16),
            jax.ShapeDtypeStruct((kv_heads, total_rows, HD), bf16),
            jax.ShapeDtypeStruct((kv_heads * HD, total_rows), bf16),
            jax.ShapeDtypeStruct((kv_heads, total_rows, HD), bf16),
        ],
        cost_estimate=pl.CostEstimate(
            flops=8 * slots.size, bytes_accessed=6 * slots.size, transcendentals=0
        ),
        name="prepare",
    )(perm, *([slots] * pages_per), cos_t, sin_t)


def block_bias(i, j, begin_row, block_len, key_len):
    keys = j * key_len + lax.broadcasted_iota(jnp.int32, (key_len, block_len), 0)
    queries = i * block_len + lax.broadcasted_iota(jnp.int32, (key_len, block_len), 1)
    allowed = (keys >= begin_row) & (keys <= queries)
    return jnp.where(allowed, 0.0, masked_score)


def forward_kernel(
    q_heads, kv_heads, page_rows, first_block, perm,
    q_t, k_rows, v_t, begin, o_t, lse, o_slots, acc, stage, sems,
):
    i = pl.program_id(0)
    block_len = q_t.shape[1]
    key_len = min(key_rows, k_rows.shape[1])
    per_group = q_heads // kv_heads
    acc[...] = jnp.zeros_like(acc)
    begin_row = begin[...]

    def visit(j, carry):
        bias = block_bias(i, j, begin_row, block_len, key_len)
        at = pl.ds(pl.multiple_of(j * key_len, key_len), key_len)
        scores = [
            dot_nn(k_rows[h // per_group, at, :], q_t[h * HD : (h + 1) * HD, :]) + bias
            for h in range(q_heads)
        ]
        tops = [
            jnp.maximum(carry[h][0], jnp.max(scores[h], axis=0, keepdims=True))
            for h in range(q_heads)
        ]
        weights = [jnp.exp(scores[h] - tops[h]) for h in range(q_heads)]
        fades = [jnp.exp(carry[h][0] - tops[h]) for h in range(q_heads)]
        totals = [
            carry[h][1] * fades[h] + jnp.sum(weights[h], axis=0, keepdims=True)
            for h in range(q_heads)
        ]
        for h in range(q_heads):
            g = h // per_group
            span = slice(h * HD, (h + 1) * HD)
            acc[span, :] = acc[span, :] * fades[h] + dot_nn(
                v_t[g * HD : (g + 1) * HD, at], weights[h].astype(bf16)
            )
        return tuple(zip(tops, totals))

    start = tuple(
        (jnp.full((1, block_len), masked_score, f32), jnp.zeros((1, block_len), f32))
        for _ in range(q_heads)
    )
    stats = lax.fori_loop(
        first_block[i], lax.div((i + 1) * block_len - 1, key_len) + 1, visit, start
    )
    for h in range(q_heads):
        lse[h : h + 1, :] = stats[h][0] + jnp.log(stats[h][1])
    mixed = jnp.concatenate(
        [acc[h * HD : (h + 1) * HD, :] / stats[h][1] for h in range(q_heads)], axis=0
    )
    o_t[...] = mixed.astype(bf16)
    pages = block_len // page_rows
    stage[...] = mixed.T.astype(bf16).reshape(pages, page_rows, q_heads * HD)
    copies = [
        pltpu.make_async_copy(stage.at[a], o_slots.at[perm[i * pages + a]], sems.at[a])
        for a in range(pages)
    ]
    for copy in copies:
        copy.start()
    for copy in copies:
        copy.wait()


def attend_forward(q_t, k_rows, v_t, begin, first_block, perm, page_rows, block_len):
    total_rows = q_t.shape[1]
    kv_heads = k_rows.shape[0]
    q_heads = q_t.shape[0] // HD
    pages = block_len // page_rows
    return pl.pallas_call(
        functools.partial(forward_kernel, q_heads, kv_heads, page_rows),
        grid_spec=pltpu.PrefetchScalarGridSpec(
            num_scalar_prefetch=2,
            grid=(total_rows // block_len,),
            in_specs=[
                pl.BlockSpec((q_heads * HD, block_len), lambda i, *_: (0, i)),
                pl.BlockSpec((kv_heads, total_rows, HD), lambda i, *_: (0, 0, 0)),
                pl.BlockSpec((kv_heads * HD, total_rows), lambda i, *_: (0, 0)),
                pl.BlockSpec((1, block_len), lambda i, *_: (0, i)),
            ],
            out_specs=[
                pl.BlockSpec((q_heads * HD, block_len), lambda i, *_: (0, i)),
                pl.BlockSpec((q_heads, block_len), lambda i, *_: (0, i)),
                pl.BlockSpec(memory_space=pl.ANY),
            ],
            scratch_shapes=[
                pltpu.VMEM((q_heads * HD, block_len), f32),
                pltpu.VMEM((pages, page_rows, q_heads * HD), bf16),
                pltpu.SemaphoreType.DMA((pages,)),
            ],
        ),
        out_shape=[
            jax.ShapeDtypeStruct((q_heads * HD, total_rows), bf16),
            jax.ShapeDtypeStruct((q_heads, total_rows), f32),
            jax.ShapeDtypeStruct((total_rows // page_rows, page_rows, q_heads * HD), bf16),
        ],
        cost_estimate=pl.CostEstimate(
            flops=q_heads * total_rows * total_rows * HD,
            bytes_accessed=8 * q_t.size,
            transcendentals=q_heads * total_rows * total_rows // 4,
        ),
        name="attend_forward",
    )(first_block, perm, q_t, k_rows, v_t, begin)


def backward_kernel(
    q_heads, kv_heads, page_rows, pages, first_block, perm, *refs
):
    grad_pages = refs[:pages]
    (
        q_t, k_rows, k_t, v_rows, o_t, lse, begin, cos_ref, sin_ref, cos_all, sin_all,
        out, grad_q, grad_k, grad_v, stage, kv_stage, sems, kv_sems,
    ) = refs[pages:]
    i = pl.program_id(0)
    steps = pl.num_programs(0)
    block_len = q_t.shape[1]
    key_len = min(key_rows, k_rows.shape[1])
    per_group = q_heads // kv_heads
    q_cols = q_heads * HD
    kv_cols = kv_heads * HD

    @pl.when(i == 0)
    def _():
        grad_k[...] = jnp.zeros_like(grad_k)
        grad_v[...] = jnp.zeros_like(grad_v)

    grad_rows = jnp.concatenate([r[0].astype(f32) for r in grad_pages], axis=0)
    grad_t = grad_rows.T
    grad_low = grad_t.astype(bf16)
    inner = [
        jnp.sum(
            grad_t[h * HD : (h + 1) * HD] * o_t[h * HD : (h + 1) * HD, :].astype(f32),
            axis=0,
            keepdims=True,
        )
        for h in range(q_heads)
    ]
    grad_q[...] = jnp.zeros_like(grad_q)
    begin_row = begin[...]

    def visit(j, carry):
        bias = block_bias(i, j, begin_row, block_len, key_len)
        at = pl.ds(pl.multiple_of(j * key_len, key_len), key_len)
        for g in range(kv_heads):
            kv_span = slice(g * HD, (g + 1) * HD)
            keys, vals, keys_t = k_rows[g, at, :], v_rows[g, at, :], k_t[kv_span, at]
            heads = range(g * per_group, (g + 1) * per_group)
            spans = [slice(h * HD, (h + 1) * HD) for h in heads]
            scores = [dot_nn(keys, q_t[span, :]) + bias for span in spans]
            grad_probs = [dot_nn(vals, grad_low[span]) for span in spans]
            probs = [jnp.exp(s - lse[h : h + 1, :]) for s, h in zip(scores, heads)]
            grad_scores = [
                (p * (d - inner[h])).astype(bf16) for p, d, h in zip(probs, grad_probs, heads)
            ]
            low_probs = [p.astype(bf16) for p in probs]
            grad_v[kv_span, at] += sum(
                dot_nt(grad_low[span], p) for span, p in zip(spans, low_probs)
            )
            grad_k[kv_span, at] += sum(
                dot_nt(q_t[span, :], d) for span, d in zip(spans, grad_scores)
            )
            for span, d in zip(spans, grad_scores):
                grad_q[span, :] += dot_nn(keys_t, d)
        return carry

    lax.fori_loop(first_block[i], lax.div((i + 1) * block_len - 1, key_len) + 1, visit, 0)

    def unrope(value, cos, sin):
        first, second = value[:HALF], value[HALF:]
        return jnp.concatenate([first * cos + second * sin, second * cos - first * sin], axis=0)

    cos, sin = cos_ref[...], sin_ref[...]
    parts = [
        unrope(grad_q[h * HD : (h + 1) * HD, :] * score_scale, cos, sin) for h in range(q_heads)
    ]
    stage[...] = jnp.concatenate(parts, axis=0).T.astype(bf16).reshape(pages, page_rows, q_cols)
    copies = [
        pltpu.make_async_copy(
            stage.at[a], out.at[perm[i * pages + a], :, pl.ds(0, q_cols)], sems.at[a]
        )
        for a in range(pages)
    ]
    for copy in copies:
        copy.start()
    for copy in copies:
        copy.wait()

    @pl.when(i == steps - 1)
    def _():
        all_pages = kv_stage.shape[0]
        cos, sin = cos_all[...], sin_all[...]
        parts = [unrope(grad_k[g * HD : (g + 1) * HD, :], cos, sin) for g in range(kv_heads)]
        both = jnp.concatenate(parts + [grad_v[...]], axis=0)
        kv_stage[...] = both.T.astype(bf16).reshape(all_pages, page_rows, 2 * kv_cols)
        copies = [
            pltpu.make_async_copy(
                kv_stage.at[a], out.at[perm[a], :, pl.ds(q_cols, 2 * kv_cols)], kv_sems.at[a]
            )
            for a in range(all_pages)
        ]
        for copy in copies:
            copy.start()
        for copy in copies:
            copy.wait()


def attend_backward(
    grad_slots, part, q_t, k_rows, k_t, v_rows, o_t, lse, begin, cos_t, sin_t, first_block, perm,
    page_rows, block_len,
):
    total_rows = q_t.shape[1]
    kv_heads = k_rows.shape[0]
    q_heads = q_t.shape[0] // HD
    pages = block_len // page_rows
    all_pages = total_rows // page_rows
    q_cols = q_heads * HD
    kv_cols = kv_heads * HD

    def page_spec(a):
        return pl.BlockSpec(
            (1, page_rows, q_cols),
            lambda i, first_ref, perm_ref, a=a: (perm_ref[i * pages + a], 0, part),
        )

    def whole(shape):
        return pl.BlockSpec(shape, lambda i, *_: (0,) * len(shape))

    def column(rows):
        return pl.BlockSpec((rows, block_len), lambda i, *_: (0, i))

    return pl.pallas_call(
        functools.partial(backward_kernel, q_heads, kv_heads, page_rows, pages),
        grid_spec=pltpu.PrefetchScalarGridSpec(
            num_scalar_prefetch=2,
            grid=(total_rows // block_len,),
            in_specs=[page_spec(a) for a in range(pages)]
            + [
                column(q_cols),
                whole((kv_heads, total_rows, HD)),
                whole((kv_cols, total_rows)),
                whole((kv_heads, total_rows, HD)),
                column(q_cols),
                column(q_heads),
                column(1),
                column(HALF),
                column(HALF),
                whole((HALF, total_rows)),
                whole((HALF, total_rows)),
            ],
            out_specs=pl.BlockSpec(memory_space=pl.ANY),
            scratch_shapes=[
                pltpu.VMEM((q_cols, block_len), f32),
                pltpu.VMEM((kv_cols, total_rows), f32),
                pltpu.VMEM((kv_cols, total_rows), f32),
                pltpu.VMEM((pages, page_rows, q_cols), bf16),
                pltpu.VMEM((all_pages, page_rows, 2 * kv_cols), bf16),
                pltpu.SemaphoreType.DMA((pages,)),
                pltpu.SemaphoreType.DMA((all_pages,)),
            ],
        ),
        out_shape=jax.ShapeDtypeStruct((all_pages, page_rows, q_cols + 2 * kv_cols), bf16),
        cost_estimate=pl.CostEstimate(
            flops=3 * q_heads * total_rows * total_rows * HD,
            bytes_accessed=12 * q_t.size,
            transcendentals=q_heads * total_rows * total_rows // 4,
        ),
        name="attend_backward",
    )(
        first_block, perm, *([grad_slots] * pages), q_t, k_rows, k_t, v_rows, o_t, lse, begin,
        cos_t, sin_t, cos_t, sin_t,
    )


def project_kernel(
    tp_count, dp_count, rows, weights, slots, held, stage, load_sem, own_sem, send, recv
):
    count = dp_count * tp_count
    my_dp = lax.axis_index("dp")
    my_tp = lax.axis_index("tensor")
    me = my_dp * tp_count + my_tp
    page_rows = slots.shape[1]

    def load(j):
        shard = lax.rem(my_tp + 1 + j, tp_count)
        return pltpu.make_async_copy(weights.at[shard], held.at[j % 2], load_sem.at[j % 2])

    load(0).start()
    barrier = pltpu.get_barrier_semaphore()

    def greet(j, carry):
        peer = lax.rem(me + j, count)
        pl.semaphore_signal(
            barrier,
            inc=1,
            device_id={"dp": lax.div(peer, tp_count), "tensor": lax.rem(peer, tp_count)},
            device_id_type=MESH,
        )
        return carry

    lax.fori_loop(1, count, greet, 0)
    pl.semaphore_wait(barrier, count - 1)
    home = slots.at[my_tp * dp_count + my_dp]

    def copy_to(j, off):
        p_dp = lax.rem(my_dp + off, dp_count)
        return pltpu.make_async_remote_copy(
            src_ref=stage.at[j, pl.ds(p_dp * page_rows, page_rows), :],
            dst_ref=home,
            send_sem=send.at[j, off],
            recv_sem=recv.at[j, off],
            device_id={"dp": p_dp, "tensor": lax.rem(my_tp + 1 + j, tp_count)},
            device_id_type=MESH,
        )

    def each(j, act):
        def one(off, carry):
            act(copy_to(j, off))
            return carry

        lax.fori_loop(1 if j == tp_count - 1 else 0, dp_count, one, 0)

    for j in range(tp_count):
        load(j).wait()
        if j + 1 < tp_count:
            load(j + 1).start()
        stage[j] = dot_nn(rows[...], held[j % 2]).astype(bf16)
        if j > 0:
            each(j - 1, lambda copy: copy.start())
    each(tp_count - 1, lambda copy: copy.start())
    own = pltpu.make_async_copy(
        stage.at[tp_count - 1, pl.ds(my_dp * page_rows, page_rows), :], home, own_sem
    )
    own.start()
    own.wait()
    for j in range(tp_count):
        each(j, lambda copy: copy.wait())


def project(rows, weights, dp_count, collective_id):
    tp_count, width, cols = weights.shape
    total = rows.shape[0]
    page_rows = total // dp_count
    any_spec = pl.BlockSpec(memory_space=pl.ANY)
    dma = pltpu.SemaphoreType.DMA
    return pl.pallas_call(
        functools.partial(project_kernel, tp_count, dp_count),
        out_shape=jax.ShapeDtypeStruct((tp_count * dp_count, page_rows, cols), bf16),
        in_specs=[
            pl.BlockSpec(memory_space=pltpu.VMEM),
            pl.BlockSpec(memory_space=pltpu.HBM),
        ],
        out_specs=any_spec,
        scratch_shapes=[
            pltpu.VMEM((2, width, cols), bf16),
            pltpu.VMEM((tp_count, total, cols), bf16),
            dma((2,)),
            dma,
            dma((tp_count, dp_count)),
            dma((tp_count, dp_count)),
        ],
        compiler_params=pltpu.CompilerParams(
            collective_id=collective_id, has_side_effects=True, vmem_limit_bytes=62 * 1024 * 1024
        ),
        cost_estimate=pl.CostEstimate(
            flops=2 * tp_count * total * width * cols,
            bytes_accessed=16 * tp_count * width * cols,
            transcendentals=0,
        ),
        name="project",
    )(rows, weights)


def feed_kernel(
    ring, tile, own_rows, *refs
):
    grad_rows = refs[: 2 * ring - 1]
    weights, grads_t, rows_t, act_all, grads_all = refs[2 * ring - 1 : 2 * ring + 4]
    mixed_all = refs[2 * ring + 4 : 3 * ring + 4]
    (
        grad_own, held, grads_held, acc_n, acc_m, first_part, arrived, outgoing, mixed_stage,
        final_stage, turned, load_sem, keep_sem, grad_sem, mixed_sem, final_sem,
        row_send, row_recv, sum_send, sum_recv, all_sem,
    ) = refs[3 * ring + 4 :]
    me = lax.axis_index("tensor")
    right = lax.rem(me + 1, ring)
    left = lax.rem(me + ring - 1, ring)
    hidden = weights.shape[1] // 3
    tiles = hidden // tile

    barrier = pltpu.get_barrier_semaphore()
    for neighbour in (left, right):
        pl.semaphore_signal(barrier, inc=1, device_id={"tensor": neighbour}, device_id_type=MESH)
    pl.semaphore_wait(barrier, 2)

    load = pltpu.make_async_copy(own_rows, held.at[0], load_sem)
    load.start()

    def grad_load(s):
        def copy_of(source):
            return pltpu.make_async_copy(
                grad_rows[source], grads_held.at[s % 2], grad_sem.at[s % 2]
            )

        if s == 0:
            copy_of(0).start()
            return

        @pl.when(me >= s)
        def _():
            copy_of(s).start()

        @pl.when(me < s)
        def _():
            copy_of(ring - 1 + ring - s).start()

    def grad_wait(s):
        pltpu.make_async_copy(grad_rows[0], grads_held.at[s % 2], grad_sem.at[s % 2]).wait()

    def part_of(array, s):
        count = own_rows.shape[0]
        return array.at[:, pl.ds(pl.multiple_of(s * count, 128), count)]

    def grad_keep(s):
        return pltpu.make_async_copy(turned.at[1], part_of(grads_t, s), all_sem)

    grad_load(0)
    load.wait()

    def pass_rows(s):
        return pltpu.make_async_remote_copy(
            src_ref=held.at[s],
            dst_ref=held.at[s + 1],
            send_sem=row_send.at[s],
            recv_sem=row_recv.at[s],
            device_id={"tensor": right},
            device_id_type=MESH,
        )

    def pass_sum(s):
        return pltpu.make_async_remote_copy(
            src_ref=outgoing.at[s - 1],
            dst_ref=arrived.at[s - 1],
            send_sem=sum_send.at[s - 1],
            recv_sem=sum_recv.at[s - 1],
            device_id={"tensor": right},
            device_id_type=MESH,
        )

    def keep(s):
        return pltpu.make_async_copy(turned.at[0], part_of(rows_t, s), keep_sem)

    def mixed_store(s):
        return pltpu.make_async_copy(mixed_stage, mixed_all[s], mixed_sem)

    def chunk(s, carry):
        @pl.when(s > 0)
        def _():
            pass_rows(s - 1).wait_recv()

        @pl.when(s < ring - 1)
        def _():
            pass_rows(s).start()

        @pl.when(s > 0)
        def _():
            keep(s - 1).wait()
            grad_keep(s - 1).wait()

        turned[0] = held[s].T
        keep(s).start()
        for k in range(ring):

            @pl.when(s == k)
            def _(k=k):
                grad_wait(k)
                if k < ring - 1:
                    grad_load(k + 1)

        slot = lax.rem(s, 2)
        turned[1] = grads_held[slot].T
        grad_keep(s).start()
        acc_n[...] = jnp.zeros_like(acc_n)
        acc_m[...] = jnp.zeros_like(acc_m)

        def body(w_gate, w_up, w_down, act, grad_gate, grad_up):
            rows = held[s]
            gate = dot_nn(rows, w_gate[...])
            up = dot_nn(rows, w_up[...])
            grad_act = dot_nn(grads_held[slot], w_down[...])
            sig = 1.0 / (1.0 + jnp.exp(-gate))
            silu = gate * sig
            low_act = (silu * up).astype(bf16)
            low_up = (grad_act * silu).astype(bf16)
            low_gate = (grad_act * up * sig * (1.0 + gate * (1.0 - sig))).astype(bf16)
            act[...] = low_act
            grad_gate[...] = low_gate
            grad_up[...] = low_up
            acc_m[...] += dot_nt(low_act, w_down[...])
            acc_n[...] += dot_nt(low_gate, w_gate[...]) + dot_nt(low_up, w_up[...])

        width, count = own_rows.shape[1], own_rows.shape[0]
        pltpu.emit_pipeline(
            body,
            grid=(tiles,),
            in_specs=[
                pl.BlockSpec((width, tile), lambda k: (0, k)),
                pl.BlockSpec((width, tile), lambda k: (0, k + tiles)),
                pl.BlockSpec((width, tile), lambda k: (0, k + 2 * tiles)),
            ],
            out_specs=[
                pl.BlockSpec((count, tile), lambda k: (0, k)),
                pl.BlockSpec((count, tile), lambda k: (0, k)),
                pl.BlockSpec((count, tile), lambda k: (0, k + tiles)),
            ],
        )(weights, weights, weights, act_all.at[s], grads_all.at[s], grads_all.at[s])

        @pl.when(s > 0)
        def _():
            mixed_store(0).wait()

        mixed_stage[...] = acc_m[...].astype(bf16)
        for k in range(ring):

            @pl.when(s == k)
            def _(k=k):
                mixed_store(k).start()

        @pl.when(s == 0)
        def _():
            first_part[...] = acc_n[...]

        @pl.when(s == 1)
        def _():
            outgoing[0] = acc_n[...].astype(bf16)

        @pl.when(s > 1)
        def _():
            pass_sum(s - 1).wait_recv()
            outgoing[s - 1] = (acc_n[...] + arrived[s - 2].astype(f32)).astype(bf16)

        @pl.when(s > 0)
        def _():
            pass_sum(s).start()

        return carry

    lax.fori_loop(0, ring, chunk, 0)
    mixed_store(0).wait()
    pass_sum(ring - 1).wait_recv()
    final_stage[...] = (first_part[...] + arrived[ring - 2].astype(f32)).astype(bf16)
    final = pltpu.make_async_copy(final_stage, grad_own, final_sem)
    final.start()

    def settle(s, carry):
        @pl.when(s < ring - 1)
        def _():
            pass_rows(s).wait_send()

        @pl.when(s > 0)
        def _():
            pass_sum(s).wait_send()

        return carry

    lax.fori_loop(0, ring, settle, 0)
    keep(ring - 1).wait()
    grad_keep(ring - 1).wait()
    final.wait()


def feed(own_rows, grad_rows, weights, ring, tile=256, collective_id=7):
    count, width = own_rows.shape
    hidden = weights.shape[1] // 3
    any_spec = pl.BlockSpec(memory_space=pl.ANY)
    dma = pltpu.SemaphoreType.DMA
    return pl.pallas_call(
        functools.partial(feed_kernel, ring, min(tile, hidden)),
        out_shape=[
            jax.ShapeDtypeStruct((width, ring * count), bf16),
            jax.ShapeDtypeStruct((width, ring * count), bf16),
            jax.ShapeDtypeStruct((ring, count, hidden), bf16),
            jax.ShapeDtypeStruct((ring, count, 2 * hidden), bf16),
        ]
        + [jax.ShapeDtypeStruct((count, width), bf16)] * (ring + 1),
        in_specs=[any_spec] * (1 + 2 * ring),
        out_specs=[any_spec] * (5 + ring),
        scratch_shapes=[
            pltpu.VMEM((ring, count, width), bf16),
            pltpu.VMEM((2, count, width), bf16),
            pltpu.VMEM((count, width), f32),
            pltpu.VMEM((count, width), f32),
            pltpu.VMEM((count, width), f32),
            pltpu.VMEM((ring - 1, count, width), bf16),
            pltpu.VMEM((ring - 1, count, width), bf16),
            pltpu.VMEM((count, width), bf16),
            pltpu.VMEM((count, width), bf16),
            pltpu.VMEM((2, width, count), bf16),
            dma,
            dma,
            dma((2,)),
            dma,
            dma,
            dma((ring - 1,)),
            dma((ring - 1,)),
            dma((ring - 1,)),
            dma((ring - 1,)),
            dma,
        ],
        compiler_params=pltpu.CompilerParams(
            collective_id=collective_id, has_side_effects=True, vmem_limit_bytes=64 * 1024 * 1024 - 65536,
        ),
        cost_estimate=pl.CostEstimate(
            flops=12 * ring * count * width * hidden,
            bytes_accessed=8 * ring * count * width,
            transcendentals=ring * count * hidden,
        ),
        name="feed_forward",
    )(own_rows, *grad_rows, weights)


def weigh_kernel(
    tp_count, dp_count, tile, grads, rows_t, grads_t, gate_up, act, slots, out,
    left, left_sem, own_sem, send, recv,
):
    count = dp_count * tp_count
    my_dp = lax.axis_index("dp")
    my_tp = lax.axis_index("tensor")
    me = my_dp * tp_count + my_tp
    page_rows = slots.shape[1]

    loads = [
        pltpu.make_async_copy(source, left.at[k], left_sem.at[k])
        for k, source in enumerate((rows_t, grads_t))
    ]
    for load in loads:
        load.start()

    barrier = pltpu.get_barrier_semaphore()

    def place(peer):
        return {"dp": lax.div(peer, tp_count), "tensor": lax.rem(peer, tp_count)}

    def greet(j, carry):
        peer = lax.rem(me + j, count)
        pl.semaphore_signal(barrier, inc=1, device_id=place(peer), device_id_type=MESH)
        return carry

    lax.fori_loop(1, count, greet, 0)
    pl.semaphore_wait(barrier, count - 1)

    home = slots.at[my_tp * dp_count + my_dp]

    def block(p_dp, p_tp):
        return grads.at[p_tp, pl.ds(p_dp * page_rows, page_rows), :]

    own = pltpu.make_async_copy(block(my_dp, my_tp), home, own_sem)
    own.start()

    def copy_to(j):
        peer = lax.rem(me + j, count)
        return pltpu.make_async_remote_copy(
            src_ref=block(lax.div(peer, tp_count), lax.rem(peer, tp_count)),
            dst_ref=home,
            send_sem=send.at[j],
            recv_sem=recv.at[j],
            device_id=place(peer),
            device_id_type=MESH,
        )

    def start(j, carry):
        copy_to(j).start()
        return carry

    def finish(j, carry):
        copy_to(j).wait()
        return carry

    lax.fori_loop(1, count, start, 0)

    width = rows_t.shape[0]
    step = min(512, width)

    def multiply(k, right, first):
        ring, rows, cols = right.shape

        def body(part, result):
            values = part[...].reshape(ring * rows, tile)
            for m in range(0, width, step):
                result[m : m + step, :] = dot_nn(left[k, m : m + step, :], values).astype(bf16)

        pltpu.emit_pipeline(
            body,
            grid=(cols // tile,),
            in_specs=[pl.BlockSpec((ring, rows, tile), lambda n: (0, 0, n))],
            out_specs=[pl.BlockSpec((width, tile), lambda n: (0, n + first))],
        )(right, out)

    loads[0].wait()
    multiply(0, gate_up, 0)
    loads[1].wait()
    multiply(1, act, gate_up.shape[2] // tile)
    own.wait()
    lax.fori_loop(1, count, finish, 0)


def weigh(grads, rows_t, grads_t, gate_up, act, tp_count, dp_count, collective_id):
    count = tp_count * dp_count
    cols = grads.shape[2]
    page_rows = grads.shape[1] // dp_count
    width, rows = rows_t.shape
    hidden = act.shape[2]
    any_spec = pl.BlockSpec(memory_space=pl.ANY)
    dma = pltpu.SemaphoreType.DMA
    return pl.pallas_call(
        functools.partial(weigh_kernel, tp_count, dp_count, min(512, hidden)),
        out_shape=[
            jax.ShapeDtypeStruct((count, page_rows, cols), bf16),
            jax.ShapeDtypeStruct((width, 3 * hidden), bf16),
        ],
        in_specs=[pl.BlockSpec(memory_space=pltpu.HBM)] * 5,
        out_specs=[any_spec] * 2,
        scratch_shapes=[
            pltpu.VMEM((2, width, rows), bf16),
            dma((2,)),
            dma,
            dma((count,)),
            dma((count,)),
        ],
        compiler_params=pltpu.CompilerParams(
            collective_id=collective_id, has_side_effects=True, vmem_limit_bytes=62 * 1024 * 1024
        ),
        cost_estimate=pl.CostEstimate(
            flops=6 * rows * width * hidden,
            bytes_accessed=2 * width * (2 * rows + 3 * hidden),
            transcendentals=0,
        ),
        name="weigh",
    )(grads, rows_t, grads_t, gate_up, act)


def flip(index, bit):
    return index + bit - 2 * bit * lax.rem(lax.div(index, bit), 2)


def collect_kernel(
    tp_count, dp_count, shard, second, gains, chunk, out, second_out, gains_out, from_left, from_right,
    second_send, second_recv, own_sem, ring_send, ring_recv, send, recv, gain_send, gain_recv, chunk_send, chunk_recv,
):
    my_dp = lax.axis_index("dp")
    my_tp = lax.axis_index("tensor")
    rows = shard.shape[0]
    half = rows // 2
    bits = [1 << b for b in reversed(range(dp_count.bit_length() - 1))]
    orders = [bits, bits[:-1][::-1] + bits[-1:]]
    steps = len(bits)

    barrier = pltpu.get_barrier_semaphore()
    for j in range(1, tp_count):
        pl.semaphore_signal(
            barrier, inc=1, device_id={"tensor": lax.rem(my_tp + j, tp_count)}, device_id_type=MESH
        )
    for j in range(1, dp_count):
        pl.semaphore_signal(
            barrier, inc=1, device_id={"dp": lax.rem(my_dp + j, dp_count)}, device_id_type=MESH
        )
    pl.semaphore_wait(barrier, tp_count + dp_count - 2)

    home = out.at[my_tp, pl.ds(my_dp * rows, rows), :]
    own = pltpu.make_async_copy(shard, home, own_sem.at[0])
    own.start()
    own_gain = pltpu.make_async_copy(gains, gains_out.at[my_dp], own_sem.at[1])
    own_gain.start()
    own_second = pltpu.make_async_copy(second, second_out.at[my_tp], own_sem.at[2])
    own_second.start()

    def second_copy(j):
        return pltpu.make_async_remote_copy(
            src_ref=second,
            dst_ref=second_out.at[my_tp],
            send_sem=second_send.at[j],
            recv_sem=second_recv.at[j],
            device_id={"tensor": lax.rem(my_tp + j, tp_count)},
            device_id_type=MESH,
        )

    def hand_on(way, far):
        owner = lax.rem(my_tp + (tp_count - far, far)[way], tp_count)
        spot = out.at[owner, pl.ds(my_dp * rows, rows), :]
        return pltpu.make_async_remote_copy(
            src_ref=shard if far == 0 else spot,
            dst_ref=spot,
            send_sem=ring_send.at[way, far],
            recv_sem=ring_recv.at[way, far],
            device_id={"tensor": lax.rem(my_tp + (1, tp_count - 1)[way], tp_count)},
            device_id_type=MESH,
        )

    def hands_on(way, far):
        if way == 0:
            return (my_tp >= far) & (my_tp < tp_count - 1)
        return (my_tp < tp_count - far) & (my_tp > 0)

    def relay(far):
        for way, here in ((0, my_tp >= far), (1, my_tp < tp_count - far)):

            @pl.when(here)
            def _(way=way):
                hand_on(way, far - 1).wait_recv()

                if far < tp_count - 1:

                    @pl.when(hands_on(way, far))
                    def _():
                        hand_on(way, far).start()

    def gain_copy(j):
        return pltpu.make_async_remote_copy(
            src_ref=gains,
            dst_ref=gains_out.at[my_dp],
            send_sem=gain_send.at[j],
            recv_sem=gain_recv.at[j],
            device_id={"dp": lax.rem(my_dp + j, dp_count)},
            device_id_type=MESH,
        )

    def step(way):
        return pltpu.make_async_remote_copy(
            src_ref=chunk,
            dst_ref=(from_left, from_right)[way],
            send_sem=chunk_send.at[way],
            recv_sem=chunk_recv.at[way],
            device_id={"tensor": lax.rem(my_tp + (1, tp_count - 1)[way], tp_count)},
            device_id_type=MESH,
        )

    has_right, has_left = my_tp < tp_count - 1, my_tp > 0

    def within(j, s, k, m):
        order = orders[s]
        owner = my_dp
        for b in range(k):
            if m >> b & 1:
                owner = flip(owner, order[b])
        block = out.at[
            lax.rem(my_tp - j + tp_count, tp_count), pl.ds(owner * rows + s * half, half), :
        ]
        at = (1 << k) - 1 + m
        return pltpu.make_async_remote_copy(
            src_ref=block,
            dst_ref=block,
            send_sem=send.at[j, s, at],
            recv_sem=recv.at[j, s, at],
            device_id={"dp": flip(my_dp, order[k])},
            device_id_type=MESH,
        )

    for way in range(2):

        @pl.when(hands_on(way, 0))
        def _(way=way):
            hand_on(way, 0).start()

    for j in range(1, dp_count):
        gain_copy(j).start()

    own.wait()
    for phase in range(2 * tp_count - 2 + steps):
        if 1 <= phase < tp_count:
            relay(phase)
        for k in reversed(range(steps + 1)):
            for j in range(tp_count):
                if (0 if j == 0 else tp_count - 2 + j) + k != phase:
                    continue
                for s in range(2):
                    if k > 0:
                        for m in range(1 << (k - 1)):
                            within(j, s, k - 1, m).wait_recv()
                for s in range(2):
                    if k < steps:
                        for m in range(1 << k):
                            within(j, s, k, m).start()
        if phase == tp_count - 1:

            @pl.when(has_right)
            def _():
                step(0).start()

            @pl.when(has_left)
            def _():
                step(1).start()

            for j in range(1, tp_count):
                second_copy(j).start()
    for j in range(tp_count):
        if j < tp_count - 1:
            for way in range(2):

                @pl.when(hands_on(way, j))
                def _(way=way, j=j):
                    hand_on(way, j).wait_send()

        for s in range(2):
            for k in range(steps):
                for m in range(1 << k):
                    within(j, s, k, m).wait_send()
    own_gain.wait()
    own_second.wait()
    for j in range(1, tp_count):
        second_copy(j).wait()
    for j in range(1, dp_count):
        gain_copy(j).wait()

    @pl.when(has_right)
    def _():
        step(0).wait_send()
        step(1).wait_recv()

    @pl.when(has_left)
    def _():
        step(1).wait_send()
        step(0).wait_recv()


def collect(shard, second, gains, chunk, tp_count, dp_count, collective_id):
    rows, cols = shard.shape
    dma = pltpu.SemaphoreType.DMA
    vmem_spec = pl.BlockSpec(memory_space=pltpu.VMEM)
    any_spec = pl.BlockSpec(memory_space=pl.ANY)
    return pl.pallas_call(
        functools.partial(collect_kernel, tp_count, dp_count),
        out_shape=[
            jax.ShapeDtypeStruct((tp_count, dp_count * rows, cols), shard.dtype),
            jax.ShapeDtypeStruct((tp_count,) + second.shape, second.dtype),
            jax.ShapeDtypeStruct((dp_count,) + gains.shape, gains.dtype),
            jax.ShapeDtypeStruct(chunk.shape, chunk.dtype),
            jax.ShapeDtypeStruct(chunk.shape, chunk.dtype),
        ],
        in_specs=[vmem_spec, vmem_spec, vmem_spec, any_spec],
        out_specs=[any_spec] * 5,
        scratch_shapes=[
            dma((tp_count,)),
            dma((tp_count,)),
            dma((3,)),
            dma((2, tp_count)),
            dma((2, tp_count)),
            dma((tp_count, 2, dp_count - 1)),
            dma((tp_count, 2, dp_count - 1)),
            dma((dp_count,)),
            dma((dp_count,)),
            dma((2,)),
            dma((2,)),
        ],
        compiler_params=pltpu.CompilerParams(collective_id=collective_id, has_side_effects=True),
        cost_estimate=pl.CostEstimate(
            flops=0, bytes_accessed=16 * tp_count * dp_count * shard.size, transcendentals=0
        ),
        name="collect",
    )(shard, second, gains, chunk)


def spread_kernel(rows, weight, out):
    out[0] = dot_nn(rows[...], weight[0]).astype(out.dtype)


def spread(rows, weights, part, cols):
    shards, width, _ = weights.shape
    count = rows.shape[0]
    return pl.pallas_call(
        spread_kernel,
        grid=(shards,),
        in_specs=[
            pl.BlockSpec((count, width), lambda t: (0, 0)),
            pl.BlockSpec((1, width, cols), lambda t: (t, 0, part)),
        ],
        out_specs=pl.BlockSpec((1, count, cols), lambda t: (t, 0, 0)),
        out_shape=jax.ShapeDtypeStruct((shards, count, cols), bf16),
        cost_estimate=pl.CostEstimate(
            flops=2 * shards * count * width * cols,
            bytes_accessed=2 * shards * width * cols,
            transcendentals=0,
        ),
        name="spread",
    )(rows, weights)


def gather_kernel(has_begin, part, weight, *refs):
    out = refs[-1]

    @pl.when(pl.program_id(0) == 0)
    def _():
        out[...] = refs[0][...] if has_begin else jnp.zeros_like(out)

    out[...] += dot_nt(part[0], weight[0])


def gather_sum(parts, weights, part, begin):
    shards, count, cols = parts.shape
    width = weights.shape[1]
    whole = pl.BlockSpec((count, width), lambda t: (0, 0))
    begins = [] if begin is None else [begin]
    return pl.pallas_call(
        functools.partial(gather_kernel, begin is not None),
        grid=(shards,),
        in_specs=[
            pl.BlockSpec((1, count, cols), lambda t: (t, 0, 0)),
            pl.BlockSpec((1, width, cols), lambda t: (t, 0, part)),
        ]
        + [whole] * len(begins),
        out_specs=whole,
        out_shape=jax.ShapeDtypeStruct((count, width), f32),
        cost_estimate=pl.CostEstimate(
            flops=2 * shards * count * width * cols,
            bytes_accessed=2 * shards * width * cols,
            transcendentals=0,
        ),
        name="gather_sum",
    )(parts, weights, *begins)


def outer_kernel(rows, *refs):
    parts, out, turned = refs[:-2], refs[-2], refs[-1]

    @pl.when(pl.program_id(0) == 0)
    def _():
        turned[...] = rows[...].T

    at = 0
    for part in parts:
        cols = part.shape[2]
        out[:, at : at + cols] = dot_nn(turned[...], part[0]).astype(out.dtype)
        at += cols


def outer(rows, parts):
    shards, count, _ = parts[0].shape
    cols = sum(part.shape[2] for part in parts)
    width = rows.shape[1]
    return pl.pallas_call(
        outer_kernel,
        grid=(shards,),
        in_specs=[pl.BlockSpec((count, width), lambda t: (0, 0))]
        + [pl.BlockSpec((1, count, part.shape[2]), lambda t: (t, 0, 0)) for part in parts],
        out_specs=pl.BlockSpec((width, cols), lambda t: (0, t)),
        out_shape=jax.ShapeDtypeStruct((width, shards * cols), bf16),
        scratch_shapes=[pltpu.VMEM((width, count), bf16)],
        cost_estimate=pl.CostEstimate(
            flops=2 * shards * count * width * cols,
            bytes_accessed=2 * shards * width * cols,
            transcendentals=0,
        ),
        name="outer",
    )(rows, *parts)


def total_kernel(
    tp_count, dp_count, groups, rows, *refs
):
    parts = refs[:groups]
    (
        to_right, to_left, weights, out, grad_rows, from_sides,
        turned, mine, got, got_across, held, load_sem, send, recv,
        across_send, across_recv, chunk_send, chunk_recv,
    ) = refs[groups:]
    my_dp = lax.axis_index("dp")
    my_tp = lax.axis_index("tensor")
    own_rows = out.shape[0]
    half = own_rows // 2
    bits = [1 << b for b in range(dp_count.bit_length() - 1)]
    orders = [bits, bits[:1] + bits[1:][::-1]]
    steps = len(bits)

    def shard_of(j):
        return lax.rem(my_tp + 1 + j, tp_count)

    def load(j):
        return pltpu.make_async_copy(weights.at[shard_of(j)], held.at[j % 2], load_sem.at[j % 2])

    load(0).start()
    barrier = pltpu.get_barrier_semaphore()
    for j in range(1, tp_count):
        pl.semaphore_signal(
            barrier, inc=1, device_id={"tensor": lax.rem(my_tp + j, tp_count)}, device_id_type=MESH
        )
    for bit in bits:
        pl.semaphore_signal(
            barrier, inc=1, device_id={"dp": flip(my_dp, bit)}, device_id_type=MESH
        )
    pl.semaphore_wait(barrier, tp_count - 1 + steps)

    def step(way):
        return pltpu.make_async_remote_copy(
            src_ref=(to_right, to_left)[way],
            dst_ref=from_sides.at[way],
            send_sem=chunk_send.at[way],
            recv_sem=chunk_recv.at[way],
            device_id={"tensor": lax.rem(my_tp + (1, tp_count - 1)[way], tp_count)},
            device_id_type=MESH,
        )

    has_right, has_left = my_tp < tp_count - 1, my_tp > 0

    @pl.when(has_right)
    def _():
        step(0).start()

    @pl.when(has_left)
    def _():
        step(1).start()

    def block(j, s, owner):
        return j, pl.ds(pl.multiple_of(owner * own_rows + s * half, half), half)

    def place(k, m):
        return sum(1 << (steps - 1 - e) for e in range(k)) + m

    def fellow(s, k, m, start):
        owner = start
        for b in range(steps - 1 - k):
            if m >> b & 1:
                owner = flip(owner, orders[s][k + 1 + b])
        return owner

    def exchange_part(j, s, k, m):
        partner = flip(my_dp, orders[s][k])
        at = place(k, m)
        index, span = block(j, s, fellow(s, k, m, partner))
        return pltpu.make_async_remote_copy(
            src_ref=mine.at[index, span, :],
            dst_ref=got.at[j, s, at],
            send_sem=send.at[j, s, at],
            recv_sem=recv.at[j, s, at],
            device_id={"dp": partner},
            device_id_type=MESH,
        )

    def across(j):
        return pltpu.make_async_remote_copy(
            src_ref=mine.at[j, pl.ds(pl.multiple_of(my_dp * own_rows, own_rows), own_rows), :],
            dst_ref=got_across.at[j],
            send_sem=across_send.at[j],
            recv_sem=across_recv.at[j],
            device_id={"tensor": shard_of(j)},
            device_id_type=MESH,
        )

    def every(k):
        return [(s, m) for s in range(2) for m in range(1 << (steps - 1 - k))]

    turned[...] = rows[...].T
    for phase in range(tp_count + steps + 1):
        if phase < tp_count:
            shard = shard_of(phase)
            at = 0
            load(phase).wait()
            if phase + 1 < tp_count:
                load(phase + 1).start()
            for g, part in enumerate(parts):
                cols = part.shape[2]
                value = part[shard]
                mine[phase, :, at : at + cols] = dot_nn(turned[...], value).astype(bf16)
                product = dot_nt(value, held[phase % 2, :, at : at + cols])
                if phase == 0 and g == 0:
                    grad_rows[...] = product
                else:
                    grad_rows[...] += product
                at += cols
        for k in reversed(range(steps + 1)):
            j = phase - k
            if not 0 <= j < tp_count:
                continue
            if k > 0:
                for s, m in every(k - 1):
                    exchange_part(j, s, k - 1, m).wait_recv()
                    index, span = block(j, s, fellow(s, k - 1, m, my_dp))
                    mine[index, span, :] = (
                        mine[index, span, :].astype(f32)
                        + got[j, s, place(k - 1, m)].astype(f32)
                    ).astype(bf16)
            if k < steps:
                for s, m in every(k):
                    exchange_part(j, s, k, m).start()
            elif j < tp_count - 1:
                across(j).start()
    total = mine[
        tp_count - 1, pl.ds(pl.multiple_of(my_dp * own_rows, own_rows), own_rows), :
    ].astype(f32)
    for j in range(tp_count - 1):
        across(j).wait_recv()
        total += got_across[j].astype(f32)
    out[...] = total

    @pl.when(has_right)
    def _():
        step(0).wait_send()
        step(1).wait_recv()

    @pl.when(has_left)
    def _():
        step(1).wait_send()
        step(0).wait_recv()

    for j in range(tp_count):
        if j < tp_count - 1:
            across(j).wait_send()
        for k in range(steps):
            for s, m in every(k):
                exchange_part(j, s, k, m).wait_send()


def total_grads(rows, parts, to_right, to_left, weights, dp_count, collective_id):
    tp_count, width, cols = weights.shape
    count = rows.shape[0]
    own_rows = width // dp_count
    vmem_spec = pl.BlockSpec(memory_space=pltpu.VMEM)
    any_spec = pl.BlockSpec(memory_space=pl.ANY)
    dma = pltpu.SemaphoreType.DMA
    return pl.pallas_call(
        functools.partial(total_kernel, tp_count, dp_count, len(parts)),
        out_shape=[
            jax.ShapeDtypeStruct((own_rows, cols), f32),
            jax.ShapeDtypeStruct((count, width), f32),
            jax.ShapeDtypeStruct((2, count, width), bf16),
        ],
        in_specs=[vmem_spec] * (1 + len(parts)) + [any_spec] * 3,
        out_specs=[vmem_spec, vmem_spec, any_spec],
        scratch_shapes=[
            pltpu.VMEM((width, count), bf16),
            pltpu.VMEM((tp_count, width, cols), bf16),
            pltpu.VMEM((tp_count, 2, dp_count - 1, own_rows // 2, cols), bf16),
            pltpu.VMEM((tp_count - 1, own_rows, cols), bf16),
            pltpu.VMEM((2, width, cols), bf16),
            dma((2,)),
            dma((tp_count, 2, dp_count - 1)),
            dma((tp_count, 2, dp_count - 1)),
            dma((tp_count,)),
            dma((tp_count,)),
            dma((2,)),
            dma((2,)),
        ],
        compiler_params=pltpu.CompilerParams(
            collective_id=collective_id, has_side_effects=True, vmem_limit_bytes=62 * 1024 * 1024
        ),
        cost_estimate=pl.CostEstimate(
            flops=4 * tp_count * count * width * cols,
            bytes_accessed=16 * tp_count * width * cols,
            transcendentals=0,
        ),
        name="total_grads",
    )(rows, *parts, to_right, to_left, weights)


def rms_scale(hidden):
    return lax.rsqrt(jnp.mean(hidden * hidden, axis=1, keepdims=True) + epsilon)


def norm_back(grad_norm, hidden, scale_rows, gain):
    normed = hidden * scale_rows
    gain_part = jnp.sum(grad_norm * normed, axis=0)
    inner = grad_norm * gain
    grad_hidden = scale_rows * (inner - normed * jnp.mean(inner * normed, axis=1, keepdims=True))
    return (grad_hidden, gain_part)


def after(value, other):
    return lax.optimization_barrier((value, other))[0]


def local(
    tokens,
    upstream,
    lengths,
    positions,
    pages,
    attn_gain,
    w_query,
    w_key,
    w_value,
    w_out,
    mlp_gain,
    w_gate,
    w_up,
    w_down,
):
    dp_count = lax.axis_size("dp")
    tp_count = lax.axis_size("tensor")
    dp_index = lax.axis_index("dp")
    tp_index = lax.axis_index("tensor")
    tok_dev, width = tokens.shape
    tok_group = tok_dev * tp_count
    page_rows = tok_dev // dp_count
    group_pages = tp_count * dp_count
    page_count = pages.shape[0]
    device = dp_index * tp_count + tp_index
    everyone = ("tensor", "dp")

    local_ids = jnp.arange(dp_count, dtype=jnp.int32)
    own_pages = device * dp_count + local_ids
    page_ids = jnp.arange(page_count, dtype=jnp.int32)
    dealt = jnp.sum(jnp.where(pages[None, :] == own_pages[:, None], page_ids[None, :], 0), axis=1)
    dest_group = dealt // group_pages
    send_order = jnp.sum(
        jnp.where(dest_group[None, :] == local_ids[:, None], local_ids[None, :], 0), axis=1
    )
    group_sources = lax.dynamic_slice_in_dim(pages, dp_index * group_pages, group_pages)
    perm = (
        (jnp.arange(group_pages, dtype=jnp.int32) // dp_count) * dp_count
        + group_sources // group_pages
    ).astype(jnp.int32)

    def reorder(rows, order):
        blocks = rows.reshape(dp_count, page_rows, rows.shape[1])
        return jnp.take(blocks, order, axis=0, mode="clip").reshape(rows.shape)

    hidden_in = reorder(tokens, send_order).astype(f32)
    grad_top = reorder(upstream, send_order).astype(f32)
    seq_lens = lengths[0]
    seq_ends = jnp.cumsum(seq_lens)
    place = (jnp.take(dealt, send_order, mode="clip") % group_pages) * page_rows
    place_rows = (place[:, None] + jnp.arange(page_rows, dtype=jnp.int32)[None, :]).reshape(-1)
    valid_rows = (place_rows < seq_ends[-1]).astype(f32)[:, None]

    row_ids = jnp.arange(tok_group, dtype=jnp.int32)
    begin = jnp.max(
        jnp.where(row_ids[:, None] >= seq_ends[None, :], seq_ends[None, :], 0), axis=1
    ).astype(jnp.int32)
    block_len = min(block_rows, tok_group)
    first_block = begin[::block_len] // min(key_rows, tok_group)
    begin = begin[None, :]
    inverse_freq = theta_base ** (-(jnp.arange(HALF, dtype=f32) * 2.0) / HD)
    angles = inverse_freq[:, None] * positions.astype(f32)
    cos_t, sin_t = jnp.cos(angles), jnp.sin(angles)

    q_cols, kv_cols = w_query.shape[1], w_key.shape[1]
    kv_heads = kv_cols // HD
    per_group = q_cols // kv_cols
    group_q = per_group * HD
    groups = range(kv_heads)
    qkv_shard = jnp.concatenate(
        [
            part
            for g in groups
            for part in (
                w_query[:, g * group_q : (g + 1) * group_q],
                w_key[:, g * HD : (g + 1) * HD],
                w_value[:, g * HD : (g + 1) * HD],
            )
        ],
        axis=1,
    )

    def trade(value):
        blocks = value.reshape(group_pages, page_rows, value.shape[-1])
        return lax.all_to_all(blocks, everyone, split_axis=0, concat_axis=0, tiled=True)

    def trade_back(value):
        return trade(value).reshape(tp_count, tok_dev, value.shape[-1])

    def pass_on(values, first, last):
        return (
            lax.ppermute(values[0], "tensor", [(t, t + 1) for t in range(*first)]),
            lax.ppermute(values[1], "tensor", [(t, t - 1) for t in range(*last)]),
        )

    grad_out = grad_top * valid_rows
    own_chunk = grad_out.astype(bf16)
    mlp_shard = jnp.concatenate([w_gate, w_up, w_down.T], axis=1)
    w_qkv, out_shards, gains, *sides = collect(
        qkv_shard, w_out.T, jnp.stack([attn_gain, mlp_gain]), own_chunk, tp_count, dp_count, 1
    )
    w_out_t = lax.all_gather(out_shards, "dp", axis=1, tiled=True)
    w_mlp = lax.all_gather(after(mlp_shard, gains), "dp", axis=0, tiled=True)
    chunks = [(sides[0], sides[1])]
    gains = gains.transpose(1, 0, 2).reshape(2, -1).astype(f32)
    gain_one, gain_two = gains[0], gains[1]

    scale_one = rms_scale(hidden_in)
    normed_one = (hidden_in * scale_one * gain_one).astype(bf16)
    slots = project(normed_one, w_qkv, dp_count, 3)
    for n in range(2, tp_count):
        passed = after(chunks[-1], slots) if n == 2 else chunks[-1]
        chunks.append(pass_on(passed, (n - 1, tp_count - 1), (1, tp_count - n + 1)))
    saved, mixed = [], []
    for g in groups:
        q_t, k_t, k_rows, v_t, v_rows = prepare(
            after(slots, (o_slots, w_out_t, chunks[1])) if g else slots, g, perm, cos_t, sin_t, per_group, 1
        )
        o_t, lse, o_slots = attend_forward(
            q_t, k_rows, v_t, begin, first_block, perm, page_rows, block_len
        )
        saved.append((q_t, k_rows, k_t, v_rows, o_t, lse))
        mixed.append(trade_back(after(o_slots, chunks[1]) if g else o_slots))
    hidden_mid = hidden_in
    mixed[-1] = after(mixed[-1], chunks[-1])
    for g in groups:
        hidden_mid = gather_sum(mixed[g], w_out_t, g, hidden_mid)

    scale_two = rms_scale(hidden_mid)
    normed_two = (hidden_mid * scale_two * gain_two).astype(bf16)
    grads_t, rows_t, inner_act, grad_gate_up, *partial_two, grad_normed_two = feed(
        normed_two, [own_chunk] + [c[0] for c in chunks] + [c[1] for c in chunks], w_mlp, tp_count
    )
    grad_normed_two = grad_normed_two.astype(f32)
    grad_mid_norm, gain_two_part = norm_back(grad_normed_two, hidden_mid, scale_two, gain_two)
    grad_mid = grad_out + grad_mid_norm

    def add_on(arrived, s):
        return tuple(
            (value.astype(f32) + partial_two[at].astype(f32)).astype(bf16)
            for value, at in zip(arrived, (s, tp_count - s))
        )

    def reduce_dp(grad):
        return lax.psum_scatter(grad.astype(bf16), "dp", scatter_dimension=0, tiled=True)

    def reduce_tensor(value):
        cols = value.shape[1] // tp_count
        total = lax.dynamic_slice_in_dim(value, tp_index * cols, cols, 1).astype(f32)
        for s in range(1, tp_count):
            target = lax.rem(tp_index + s, tp_count)
            block = lax.dynamic_slice_in_dim(value, target * cols, cols, 1)
            pairs = [(t, (t + s) % tp_count) for t in range(tp_count)]
            total = total + lax.ppermute(block, "tensor", pairs).astype(f32)
        return total

    grad_z = grad_mid.astype(bf16)
    grad_wout = outer(grad_z, mixed)
    sum_out = reduce_dp(grad_wout)
    grad_slots, grad_wmlp = weigh(
        spread(after(grad_z, grad_wout), w_out_t, 0, q_cols),
        rows_t, grads_t, grad_gate_up, inner_act, tp_count, dp_count, 2,
    )
    sum_mlp = reduce_dp(grad_wmlp)
    first_part = after((partial_two[1], partial_two[tp_count - 1]), grad_slots)
    passing = pass_on(first_part, (0, 1), (tp_count - 1, tp_count))
    grad_qkv = []
    for g in groups:
        q_t, k_rows, k_t, v_rows, o_t, lse = saved[g]
        back = attend_backward(
            after(grad_slots, (back, sum_out) if g else first_part), g, q_t, k_rows, k_t, v_rows,
            o_t, lse, begin, cos_t, sin_t, first_block, perm, page_rows, block_len,
        )
        if g == len(groups) - 1:
            steps = 2
            if tp_count > 3:
                passing = pass_on(add_on(passing, 2), (0, 2), (tp_count - 2, tp_count))
                steps = 3
            grad_qkv = [after(value, passing) for value in grad_qkv]
        grad_qkv.append(trade_back(back))
    hidden = sum_mlp.shape[1] // 3
    for s in range(steps, tp_count - 1):
        passing = pass_on(add_on(passing, s), (0, s), (tp_count - s, tp_count))
    passing = add_on(passing, tp_count - 1)
    sum_qkv, grad_normed_one, sides = total_grads(
        normed_one, grad_qkv, passing[0], passing[1], w_qkv, dp_count, 4
    )
    branch_two = jnp.where(tp_index > 0, sides[0].astype(f32), 0.0)
    branch_two += jnp.where(tp_index < tp_count - 1, sides[1].astype(f32), 0.0)
    each = group_q + 2 * HD
    sum_qkv = [sum_qkv[:, g * each : (g + 1) * each] for g in groups]
    sum_out = reduce_tensor(after(sum_out, grad_normed_one))
    result = (
        (after(hidden_mid, back) + branch_two + partial_two[0].astype(f32)) * valid_rows
    ).astype(bf16)
    grad_in_norm, gain_one_part = norm_back(grad_normed_one, hidden_in, scale_one, gain_one)
    grad_in = (grad_mid + grad_in_norm).astype(bf16)

    gain_parts = jnp.stack([gain_one_part, gain_two_part]).reshape(2, dp_count, -1)
    gain_parts = jnp.broadcast_to(
        gain_parts.transpose(1, 0, 2)[None], (tp_count, dp_count, 2, gain_parts.shape[2])
    ).reshape(group_pages, 2, -1)
    gain_sums = jnp.sum(
        lax.all_to_all(gain_parts, everyone, split_axis=0, concat_axis=0, tiled=True), axis=0
    )
    return (
        reorder(result, dest_group),
        reorder(grad_in, dest_group),
        gain_sums[0],
        jnp.concatenate([part[:, :group_q] for part in sum_qkv], axis=1),
        jnp.concatenate([part[:, group_q : group_q + HD] for part in sum_qkv], axis=1),
        jnp.concatenate([part[:, group_q + HD :] for part in sum_qkv], axis=1),
        sum_out.T,
        gain_sums[1],
        sum_mlp[:, :hidden].astype(f32),
        sum_mlp[:, hidden : 2 * hidden].astype(f32),
        sum_mlp[:, 2 * hidden :].astype(f32).T,
    )


def solution(mesh):
    rows = P(("dp", "tensor"), None)
    weight = P("dp", "tensor")
    weight_t = P("tensor", "dp")
    return jax.shard_map(
        local,
        mesh=mesh,
        in_specs=(
            rows,
            rows,
            P("dp", None),
            P("dp", None),
            P(),
            P("dp"),
            weight,
            weight,
            weight,
            weight_t,
            P("dp"),
            weight,
            weight,
            weight_t,
        ),
        out_specs=(
            rows,
            rows,
            P("dp"),
            weight,
            weight,
            weight,
            weight_t,
            P("dp"),
            weight,
            weight,
            weight_t,
        ),
        check_vma=False,
    )
```
